32 devices in a mesh: shard: 4 (over y, x), ctx: 4 (over z), tp: 2 (over core).
Axes of the slice: x: 2, y: 2, z: 4, core: 2. Of those that a mesh axis runs over, the one named last changes fastest.
Arguments:
- tokens: bfloat16 [6144, 2048], P(('shard', 'ctx')), may hold values from -6 to 6
- lengths: int32 [4, 3], P('shard'), may hold values from 1 to 1024, 1536 in all within a row
- w_qkv: bfloat16 [1, 2048, 3, 2048], P(None, ('shard', 'ctx'), None, 'tp'), may hold values from -0.125 to 0.125
- b_qkv: bfloat16 [1, 3, 32, 64], P(None, None, 'tp', ('shard', 'ctx')), may hold values from -1.1953125 to 1.1953125
- w_out: bfloat16 [1, 2048, 2048], P(None, 'tp', ('shard', 'ctx')), may hold values from -0.5 to 0.5
- w_gateup: bfloat16 [1, 2048, 2, 5632], P(None, ('shard', 'ctx'), None, 'tp'), may hold values from -0.125 to 0.125
- w_down: bfloat16 [1, 5632, 2048], P(None, 'tp', ('shard', 'ctx')), may hold values from -0.078125 to 0.078125
- norm_gain: bfloat16 [1, 2, 2048], P(None, None, ('shard', 'ctx')), may hold values from 0.5 to 1.5
- norm_bias: bfloat16 [1, 2, 2048], P(None, None, ('shard', 'ctx')), may hold values from -1.1953125 to 1.1953125
- cotangent: bfloat16 [6144, 2048], P(('shard', 'ctx')), may hold values from -6 to 6
Outputs:
- output: bfloat16 [6144, 2048], P(('shard', 'ctx'))
- grad_tokens: float32 [6144, 2048], P(('shard', 'ctx'))
- grad_w_qkv: float32 [1, 2048, 3, 2048], P(None, ('shard', 'ctx'), None, 'tp')
- grad_b_qkv: float32 [1, 3, 32, 64], P(None, None, 'tp', ('shard', 'ctx'))
- grad_w_out: float32 [1, 2048, 2048], P(None, 'tp', ('shard', 'ctx'))
- grad_w_gateup: float32 [1, 2048, 2, 5632], P(None, ('shard', 'ctx'), None, 'tp')
- grad_w_down: float32 [1, 5632, 2048], P(None, 'tp', ('shard', 'ctx'))
- grad_norm_gain: float32 [1, 2, 2048], P(None, None, ('shard', 'ctx'))
- grad_norm_bias: float32 [1, 2, 2048], P(None, None, ('shard', 'ctx'))
The draws below stay inside these ranges and needn't reach their ends.
Inputs may be any that keep to these rules, and one draw needn't show every extreme that they name: Each row holds the lengths of a group's 3 documents; they add up to 1536, and the longest is exactly 1024.
All inputs are finite; a program needn't handle non-finite values.
Results may differ from the reference program's by a relative error of at most 0.019.
Values may be sent and summed in bfloat16 or wider, within the bound.
A program may use at most 256 MiB of HBM per device.

```python
import math
import jax
import jax.numpy as jnp
import numpy as np
from jax import lax

D = 2048
HEADS = 32
HEAD = 64
ROT = 16
FF = 5632
LAYERS = 1
DOCS = 3
PACK = 1536
GROUPS = 4
TOKENS = 6144
MOST = 1024


def steps_of(stream_key, extent, split, least, top_value):
    factor_of, own = 1.0, jax.random.fold_in(stream_key, 6)
    for axis_at, blocks in split:
        draws = jnp.exp(jax.random.uniform(jax.random.fold_in(own, axis_at), (blocks,), jnp.float32, least / len(split), top_value / len(split)))
        factor_of = factor_of * jnp.repeat(draws, extent[axis_at] // blocks).reshape([-1 if axis == axis_at else 1 for axis in range(len(extent))])
    return factor_of


def profile(count, total, limit, slope):
    weights = [(1 << 20) // math.isqrt(rank ** slope) + 1 for rank in range(2, count + 1)]
    spare, given = total - limit - (count - 1), [1] * (count - 1)
    while spare > 0:
        candidates = [i for i in range(count - 1) if given[i] < limit]
        whole, left = sum([weights[i] for i in candidates]), spare
        for i in candidates:
            addition = min(limit - given[i], max(1, left * weights[i] // whole), spare)
            given[i] = given[i] + addition
            spare = spare - addition
    return np.array([limit] + given)


def uneven_parts(own_key, count, total, most, lean):
    if count == 2:
        one = jax.random.randint(own_key, (), max(1, total - most), min(most, total - 1) + 1)
        return jnp.stack([one, total - one])
    sizes = jnp.asarray(profile(count, total, most, lean), jnp.int32)
    couples = (count - 1) // 2
    source_of, sink = sizes[1:1 + 2 * couples:2], sizes[2:2 + 2 * couples:2]
    margin = jnp.minimum(source_of - 1, most - sink)
    moved = jax.random.randint(jax.random.fold_in(own_key, 1), (couples,), 0, 1 << 20) % (margin + 1)
    sizes = sizes.at[1:1 + 2 * couples:2].set(source_of - moved).at[2:2 + 2 * couples:2].set(sink + moved)
    return sizes[jax.random.permutation(jax.random.fold_in(own_key, 2), count)]


def noise(stream_key, dims, width, reach, cuts=(), held_as=jnp.bfloat16):
    level = steps_of(stream_key, dims, cuts, -0.22, 0.18) if cuts else 1.0
    entries = jax.random.normal(stream_key, dims, jnp.float32) * width * level
    return jnp.minimum(jnp.maximum(entries, -reach), reach).astype(held_as)


def setup_inputs(seed: int = 0) -> dict:
    streams_of = jax.random.split(jax.random.key(seed), 11)
    return {
        "tokens": noise(streams_of[0], (TOKENS, D), 1.0, 6.0, ((0, 16),)),
        "lengths": jax.vmap(lambda own: uneven_parts(own, DOCS, PACK, MOST, 2))(jax.random.split(streams_of[1], GROUPS)).reshape((GROUPS, DOCS)).astype(jnp.int32),
        "w_qkv": noise(streams_of[2], (LAYERS, D, 3, D), D ** -0.5, 0.125, ((1, 16), (3, 2))),
        "b_qkv": noise(streams_of[3], (LAYERS, 3, HEADS, HEAD), 0.2, 1.1953125, ((2, 2), (3, 16))),
        "w_out": noise(streams_of[4], (LAYERS, D, D), (D // 16) ** -0.5, 0.5, ((1, 2), (2, 16))),
        "w_gateup": noise(streams_of[5], (LAYERS, D, 2, FF), D ** -0.5, 0.125, ((1, 16), (3, 2))),
        "w_down": noise(streams_of[6], (LAYERS, FF, D), FF ** -0.5, 0.078125, ((1, 2), (2, 16))),
        "norm_gain": jnp.clip(1.0 + 0.1 * jax.random.normal(streams_of[7], (LAYERS, 2, D), jnp.float32), 0.5, 1.5).astype(jnp.bfloat16),
        "norm_bias": noise(streams_of[8], (LAYERS, 2, D), 0.2, 1.1953125, ((2, 16),)),
        "cotangent": noise(streams_of[9], (TOKENS, D), 1.0, 6.0, ((0, 16),)),
    }


EPS = 1e-05
NEG = -1e+30
BASE = 10000.0
HIGH = lax.Precision.HIGHEST

@jax.custom_vjp
def low(v):
    return lax.optimization_barrier(v.astype(jnp.bfloat16)).astype(jnp.float32)

@jax.custom_vjp
def low_back(v):
    return v

def low_keep(v):
    return (low(v), None)

def low_pass(kept, grad):
    return (grad,)

def back_keep(v):
    return (v, None)

def back_low(kept, grad):
    return (low(grad),)
low.defvjp(low_keep, low_pass)
low_back.defvjp(back_keep, back_low)

def doc_table(lengths_row, row_ids):
    doc_ends = jnp.cumsum(lengths_row, dtype=jnp.int32)
    doc_begin = doc_ends - lengths_row
    doc_ids = lax.optimization_barrier(jnp.sum((row_ids[:, None] >= doc_ends[None, :]).astype(jnp.int32), axis=1, dtype=jnp.int32))
    numbers = jnp.arange(lengths_row.shape[0], dtype=jnp.int32)
    onehot = (doc_ids[:, None] == numbers[None, :]).astype(jnp.int32)
    places = row_ids - lax.optimization_barrier(jnp.sum(onehot * doc_begin[None, :], axis=1, dtype=jnp.int32))
    return (doc_ids, places)

def angles(places):
    half_rot = ROT // 2
    frequency = BASE ** (-2.0 * jnp.arange(half_rot, dtype=jnp.float32) / ROT)
    phases = places.astype(jnp.float32)[:, None] * frequency[None, :]
    return (jnp.cos(phases), jnp.sin(phases))

def rotate(values, cosine_table, sine_table, direction):
    half_rot = ROT // 2
    cosine = cosine_table[:, None, :]
    sine_part = sine_table[:, None, :]
    leading = values[..., :half_rot]
    trailing = values[..., half_rot:ROT]
    return jnp.concatenate((leading * cosine - direction * trailing * sine_part, trailing * cosine + direction * leading * sine_part, values[..., ROT:]), axis=-1)

def layer_norm(values, gain, shift):
    center = values - lax.optimization_barrier(jnp.mean(values, axis=-1, keepdims=True))
    inverse = lax.rsqrt(lax.optimization_barrier(jnp.mean(center * center, axis=-1, keepdims=True)) + EPS)
    return center * inverse * gain + shift

def attention(queries, key_rot, key_val, doc_ids):
    total_rows = queries.shape[0]
    block_size = min(512, total_rows)
    key_rows = jnp.arange(total_rows, dtype=jnp.int32)

    def one_block(offset):
        query_block = lax.dynamic_slice_in_dim(queries, offset, block_size, 0)
        block_rows = offset + jnp.arange(block_size, dtype=jnp.int32)
        block_docs = lax.dynamic_slice_in_dim(doc_ids, offset, block_size, 0)
        scores = low_back(jnp.einsum('qhe,khe->hqk', query_block, key_rot, precision=HIGH) * HEAD ** (-0.5))
        allowed = ((block_docs[:, None] == doc_ids[None, :]) & (key_rows[None, :] <= block_rows[:, None]))[None]
        masked = jnp.where(allowed, scores, NEG)
        shifted = jnp.exp(masked - lax.optimization_barrier(jnp.max(masked, axis=-1, keepdims=True)))
        shifted = jnp.where(allowed, shifted, 0.0)
        probs_full = shifted / lax.optimization_barrier(jnp.sum(shifted, axis=-1, keepdims=True))
        return jnp.einsum('hqk,khe->qhe', low(probs_full), key_val, precision=HIGH)
    offsets = block_size * jnp.arange(total_rows // block_size, dtype=jnp.int32)
    outputs = lax.map(jax.checkpoint(one_block), offsets)
    return outputs.reshape(total_rows, HEADS, HEAD)

def forward_pack(hidden, params, doc_ids, places):
    qkv_w, qkv_b, out_w, gate_up_w, down_w, norm_gains, norm_shifts = params
    cosine_table, sine_table = angles(places)
    total_rows = hidden.shape[0]
    for depth in range(LAYERS):
        normed = low(layer_norm(hidden, norm_gains[depth, 0], norm_shifts[depth, 0]))
        projected = low_back(jnp.einsum('td,dce->tce', normed, qkv_w[depth], precision=HIGH) + qkv_b[depth].reshape(3, D))
        queries = low(rotate(projected[:, 0].reshape(total_rows, HEADS, HEAD), cosine_table, sine_table, 1.0))
        key_rot = low(rotate(projected[:, 1].reshape(total_rows, HEADS, HEAD), cosine_table, sine_table, 1.0))
        key_val = low(projected[:, 2].reshape(total_rows, HEADS, HEAD))
        mixed = attention(queries, key_rot, key_val, doc_ids)
        heads_low = low(low_back(mixed.reshape(total_rows, D)))
        hidden = hidden + low_back(jnp.dot(heads_low, out_w[depth], precision=HIGH))
        normed = low(layer_norm(hidden, norm_gains[depth, 1], norm_shifts[depth, 1]))
        gate_up = low_back(jnp.einsum('td,dcf->tcf', normed, gate_up_w[depth], precision=HIGH))
        gate_part = gate_up[:, 0]
        activated = low(gate_part * jax.nn.sigmoid(gate_part) * gate_up[:, 1])
        hidden = hidden + low_back(jnp.dot(activated, down_w[depth], precision=HIGH))
    return hidden

def add_pair(left, right):
    return left + right

def reference(tokens, lengths, w_qkv, b_qkv, w_out, w_gateup, w_down, norm_gain, norm_bias, cotangent):
    params = (w_qkv.astype(jnp.float32), b_qkv.astype(jnp.float32), w_out.astype(jnp.float32), w_gateup.astype(jnp.float32), w_down.astype(jnp.float32), norm_gain.astype(jnp.float32), norm_bias.astype(jnp.float32))
    inputs = tokens.astype(jnp.float32).reshape(GROUPS, PACK, D)
    seeds = cotangent.astype(jnp.float32).reshape(GROUPS, PACK, D)
    row_ids = jnp.arange(PACK, dtype=jnp.int32)

    def per_pack(totals, pieces):
        hidden, seed_grad, lengths_row = pieces
        doc_ids, places = doc_table(lengths_row, row_ids)

        def run(hidden_in, params_in):
            return forward_pack(hidden_in, params_in, doc_ids, places)
        result, pullback = jax.vjp(run, hidden, params)
        grad_hidden, grad_params = pullback(seed_grad)
        totals = jax.tree.map(add_pair, totals, grad_params)
        return (totals, (result, grad_hidden))
    empty = jax.tree.map(jnp.zeros_like, params)
    totals, stacked = lax.scan(per_pack, empty, (inputs, seeds, lengths))
    outputs, grad_inputs = stacked
    return (outputs.reshape(TOKENS, D).astype(jnp.bfloat16), grad_inputs.reshape(TOKENS, D), totals[0], totals[1], totals[2], totals[3], totals[4], totals[5], totals[6])
```

```python
from functools import partial

import jax
import jax.numpy as jnp
from jax import lax
from jax.experimental import pallas as pl
from jax.experimental.pallas import tpu as pltpu
from jax.sharding import PartitionSpec as P

HEAD = 64
ROT = 16
EPS = 1e-05
NEG = -1e30
BASE = 10000.0
BF = jnp.bfloat16
F32 = jnp.float32
BLK = 256


def mm(a, b, ca, cb):
    return lax.dot_general(a, b, (((ca,), (cb,)), ((), ())), preferred_element_type=F32)


def turn(x, cos, lo, hi):
    n = x.shape[-1]
    return x * cos + pltpu.roll(x, n - ROT // 2, 1) * lo + pltpu.roll(x, ROT // 2, 1) * hi


def attend_kernel(
    first_ref, q_ref, k_ref, v_ref, cos_ref, lo_ref, hi_ref, begin_ref,
    qo_ref, ko_ref, vo_ref, o_ref, lse_ref, vt_ref,
):
    rows = q_ref.shape[0]
    nb = rows // BLK
    lane = lax.broadcasted_iota(jnp.int32, (BLK, 128), 1)
    left = lane < HEAD
    key_at = lax.broadcasted_iota(jnp.int32, (BLK, BLK), 0)
    query_at = lax.broadcasted_iota(jnp.int32, (1, BLK), 1)

    @pl.loop(0, nb)
    def _(i):
        r = pl.ds(pl.multiple_of(i * BLK, BLK), BLK)
        cos, lo, hi = cos_ref[r, :], lo_ref[r, :], hi_ref[r, :]
        qo_ref[r, :] = turn(q_ref[r, :], cos, lo, hi).astype(BF) * jnp.asarray(HEAD**-0.5, BF)
        ko_ref[r, :] = turn(k_ref[r, :], cos, lo, hi).astype(BF)
        v = v_ref[r, :]
        vo_ref[r, :] = v.astype(BF)
        vt_ref[:, r] = v.T.astype(BF)

    @pl.loop(0, nb)
    def _(i):
        r = pl.ds(pl.multiple_of(i * BLK, BLK), BLK)
        q = qo_ref[r, :]
        zero = jnp.zeros_like(q)
        qs = (jnp.where(left, q, zero), jnp.where(left, zero, q))
        begin = begin_ref[0:1, r]
        here = query_at + i * BLK

        def step(j, carry):
            w = pl.ds(pl.multiple_of(j * BLK, BLK), BLK)
            k, vt = ko_ref[w, :], vt_ref[:, w]
            key = key_at + j * BLK
            seen = (key <= here) & (key >= begin)
            out = []
            for h in range(2):
                m, l, acc = carry[h]
                s = jnp.where(seen, mm(k, qs[h], 1, 1), NEG)
                top = jnp.maximum(m, jnp.max(s, axis=0, keepdims=True))
                fade = jnp.exp(m - top)
                e = jnp.exp(s - top)
                out.append(
                    (top, l * fade + jnp.sum(e, axis=0, keepdims=True), acc * fade + mm(vt, e.astype(BF), 1, 0))
                )
            return tuple(out)

        start = (
            jnp.full((1, BLK), NEG, F32), jnp.zeros((1, BLK), F32), jnp.zeros((128, BLK), F32)
        )
        done = lax.fori_loop(first_ref[i], i + 1, step, (start, start))
        parts = []
        for h in range(2):
            m, l, acc = done[h]
            parts.append((acc / l).T)
            lse_ref[0, h : h + 1, r] = m + jnp.log(l)
        o_ref[r, :] = jnp.where(left, parts[0], parts[1]).astype(BF)


def attend(qkv, tables, begin, first):
    rows, wide = qkv.shape
    pairs = wide // 3 // 128
    cos, lo, hi = tables
    full = pl.BlockSpec((rows, 128), lambda j, *_: (0, 0))

    def col(base):
        return pl.BlockSpec((rows, 128), lambda j, *_: (0, base + j))

    half = jax.ShapeDtypeStruct((rows, wide // 3), BF)
    return pl.pallas_call(
        attend_kernel,
        grid_spec=pltpu.PrefetchScalarGridSpec(
            num_scalar_prefetch=1,
            grid=(pairs,),
            in_specs=[
                col(0), col(pairs), col(2 * pairs), full, full, full,
                pl.BlockSpec((1, rows), lambda j, *_: (0, 0)),
            ],
            out_specs=[col(0)] * 4 + [pl.BlockSpec((1, 2, rows), lambda j, *_: (j, 0, 0))],
            scratch_shapes=[pltpu.VMEM((128, rows), BF)],
        ),
        out_shape=[half] * 4 + [jax.ShapeDtypeStruct((pairs, 2, rows), F32)],
        compiler_params=pltpu.CompilerParams(vmem_limit_bytes=48 << 20),
        cost_estimate=pl.CostEstimate(
            flops=4 * rows * rows * wide // 3, bytes_accessed=rows * wide * 8, transcendentals=0
        ),
        name="attend",
    )(first, qkv, qkv, qkv, cos, lo, hi, begin)


def attend_back_kernel(
    first_ref, q_ref, k_ref, v_ref, o_ref, do_ref, lse_ref, cos_ref, lo_ref, hi_ref, begin_ref,
    out_ref, kt_ref, dk_ref, dv_ref,
):
    rows = q_ref.shape[0]
    nb = rows // BLK
    pair, pairs = pl.program_id(0), pl.num_programs(0)
    lane = lax.broadcasted_iota(jnp.int32, (BLK, 128), 1)
    left = lane < HEAD
    key_at = lax.broadcasted_iota(jnp.int32, (BLK, BLK), 0)
    query_at = lax.broadcasted_iota(jnp.int32, (1, BLK), 1)

    def column(base):
        return pl.ds(pl.multiple_of((base * pairs + pair) * 128, 128), 128)

    @pl.loop(0, nb)
    def _(i):
        r = pl.ds(pl.multiple_of(i * BLK, BLK), BLK)
        kt_ref[:, r] = k_ref[r, :].astype(F32).T.astype(BF)
        dk_ref[r, :] = jnp.zeros((BLK, 128), F32)
        dv_ref[r, :] = jnp.zeros((BLK, 128), F32)

    @pl.loop(0, nb)
    def _(i):
        r = pl.ds(pl.multiple_of(i * BLK, BLK), BLK)
        q, do = q_ref[r, :], do_ref[r, :]
        zero = jnp.zeros_like(q)
        qs = (jnp.where(left, q, zero), jnp.where(left, zero, q))
        dos = (jnp.where(left, do, zero), jnp.where(left, zero, do))
        prod = (do.astype(F32) * o_ref[r, :].astype(F32)).T
        deltas = (
            jnp.sum(prod[:HEAD], axis=0, keepdims=True), jnp.sum(prod[HEAD:], axis=0, keepdims=True)
        )
        lses = (lse_ref[0, 0:1, r], lse_ref[0, 1:2, r])
        begin = begin_ref[0:1, r]
        here = query_at + i * BLK

        def step(j, carry):
            w = pl.ds(pl.multiple_of(j * BLK, BLK), BLK)
            k, v, kt = k_ref[w, :], v_ref[w, :], kt_ref[:, w]
            key = key_at + j * BLK
            seen = (key <= here) & (key >= begin)
            out = []
            dk = dv = None
            for h in range(2):
                prob = jnp.exp(jnp.where(seen, mm(k, qs[h], 1, 1) - lses[h], NEG))
                ds = (prob * (mm(v, dos[h], 1, 1) - deltas[h])).astype(BF)
                out.append(carry[h] + mm(kt, ds, 1, 0))
                dk_h, dv_h = mm(ds, qs[h], 1, 0), mm(prob.astype(BF), dos[h], 1, 0)
                dk, dv = (dk_h, dv_h) if h == 0 else (dk + dk_h, dv + dv_h)
            dk_ref[w, :] += dk
            dv_ref[w, :] += dv
            return tuple(out)

        start = jnp.zeros((128, BLK), F32)
        a, b = lax.fori_loop(first_ref[i], i + 1, step, (start, start))
        dq = jnp.where(left, a.T, b.T) * (HEAD**-0.5)
        out_ref[r, column(0)] = turn(dq, cos_ref[r, :], -lo_ref[r, :], -hi_ref[r, :]).astype(BF)

    @pl.loop(0, nb)
    def _(i):
        r = pl.ds(pl.multiple_of(i * BLK, BLK), BLK)
        out_ref[r, column(1)] = turn(dk_ref[r, :], cos_ref[r, :], -lo_ref[r, :], -hi_ref[r, :]).astype(BF)
        out_ref[r, column(2)] = dv_ref[r, :].astype(BF)


def attend_back(q, k, v, o, do, lse, tables, begin, first):
    rows, wide = q.shape
    pairs = wide // 128
    cos, lo, hi = tables
    full = pl.BlockSpec((rows, 128), lambda j, *_: (0, 0))
    col = pl.BlockSpec((rows, 128), lambda j, *_: (0, j))
    return pl.pallas_call(
        attend_back_kernel,
        grid_spec=pltpu.PrefetchScalarGridSpec(
            num_scalar_prefetch=1,
            grid=(pairs,),
            in_specs=[
                col, col, col, col, col, pl.BlockSpec((1, 2, rows), lambda j, *_: (j, 0, 0)),
                full, full, full, pl.BlockSpec((1, rows), lambda j, *_: (0, 0)),
            ],
            out_specs=pl.BlockSpec((rows, 3 * wide), lambda j, *_: (0, 0)),
            scratch_shapes=[
                pltpu.VMEM((128, rows), BF), pltpu.VMEM((rows, 128), F32), pltpu.VMEM((rows, 128), F32)
            ],
        ),
        out_shape=jax.ShapeDtypeStruct((rows, 3 * wide), BF),
        compiler_params=pltpu.CompilerParams(vmem_limit_bytes=48 << 20),
        cost_estimate=pl.CostEstimate(
            flops=10 * rows * rows * wide, bytes_accessed=rows * wide * 16, transcendentals=0
        ),
        name="attend_back",
    )(first, q, k, v, o, do, lse, cos, lo, hi, begin)


def doc_tables(lengths_row, rows):
    row_ids = jnp.arange(rows, dtype=jnp.int32)
    ends = jnp.cumsum(lengths_row, dtype=jnp.int32)
    begins = ends - lengths_row
    inside = (row_ids[:, None] >= begins[None, :]) & (row_ids[:, None] < ends[None, :])
    begin = jnp.sum(jnp.where(inside, begins[None, :], 0), axis=1, dtype=jnp.int32)
    half = ROT // 2
    freq = BASE ** (-2.0 * jnp.arange(half, dtype=F32) / ROT)
    phase = (row_ids - begin).astype(F32)[:, None] * freq[None, :]
    cos, sin = jnp.cos(phase), jnp.sin(phase)
    rest = jnp.ones((rows, HEAD - ROT), F32)
    none = jnp.zeros((rows, half), F32)
    cos_t = jnp.concatenate((cos, cos, rest), axis=1)
    lo_t = jnp.concatenate((-sin, none, 0 * rest), axis=1)
    hi_t = jnp.concatenate((none, sin, 0 * rest), axis=1)
    tables = tuple(jnp.concatenate((t, t), axis=1) for t in (cos_t, lo_t, hi_t))
    return begin, tables


def layer_norm(values, gain, shift):
    center = values - jnp.mean(values, axis=-1, keepdims=True)
    inverse = lax.rsqrt(jnp.mean(center * center, axis=-1, keepdims=True) + EPS)
    normal = center * inverse
    return (normal * gain + shift, normal, inverse)


def norm_back(gradient, normal, inverse, gain):
    scaled = gradient * gain
    centered = (
        scaled
        - jnp.mean(scaled, axis=-1, keepdims=True)
        - normal * jnp.mean(scaled * normal, axis=-1, keepdims=True)
    )
    return (inverse * centered, jnp.sum(gradient * normal, axis=0), jnp.sum(gradient, axis=0))


def make_body(S, C, T):
    assert S == C

    def body(tokens, lengths, w_qkv, b_qkv, w_out, w_gateup, w_down, norm_gain, norm_bias, cotangent):
        p, z, c = lax.axis_index("shard"), lax.axis_index("ctx"), lax.axis_index("tp")
        R, D = tokens.shape
        m = R // (S * T)
        nb = D // (S * C)
        L = R * C

        def permute(x):
            return x.reshape(x.shape[0], S, C, nb).swapaxes(1, 2).reshape(x.shape)

        def unpermute(x):
            return x.reshape(x.shape[0], C, S, nb).swapaxes(1, 2).reshape(x.shape)

        def to_plane(x):
            mine = lax.dynamic_index_in_dim(x.reshape(S, T, m, D), c, 1, keepdims=False)
            moved = lax.all_to_all(mine, "shard", 0, 0, tiled=True)
            moved = lax.all_to_all(moved, "ctx", 0, 0, tiled=True)
            return permute(moved.reshape(C * m, D))

        def from_plane(x):
            x = unpermute(x).reshape(C, m, D)
            x = lax.all_to_all(x, "ctx", 0, 0, tiled=True)
            x = lax.all_to_all(x, "shard", 0, 0, tiled=True)
            x = lax.all_gather(x, "tp", axis=0)
            return x.swapaxes(0, 1).reshape(R, D)

        def gather(x):
            x = lax.all_gather(x, ("shard", "tp"), axis=0, tiled=True)
            return x.reshape(S * T, C, m, D).swapaxes(0, 1).reshape(L, D)

        def scatter(x):
            x = x.astype(BF).reshape(C, S * T, m, D).swapaxes(0, 1).reshape(L, D)
            return lax.psum_scatter(x, ("shard", "tp"), scatter_dimension=0, tiled=True).astype(F32)

        def fetch(w):
            n = w.shape[2]
            w = lax.all_to_all(w, "shard", 0, 0, tiled=True)
            return lax.all_gather(w.reshape(S * nb, n), "ctx", axis=0, tiled=True)

        def give(g):
            n = g.shape[1]
            g = lax.psum_scatter(g.astype(BF), "ctx", scatter_dimension=0, tiled=True)
            return lax.all_to_all(g.reshape(S, nb, n), "shard", 0, 0, tiled=True).astype(F32)

        hn = w_qkv.shape[3] // S
        fn = w_gateup.shape[3] // S
        heads = hn // HEAD

        small = jnp.concatenate(
            (
                norm_gain[0].astype(F32).reshape(-1),
                norm_bias[0].astype(F32).reshape(-1),
                b_qkv[0].astype(F32).reshape(-1),
                lengths[0].astype(F32),
            )
        )
        small = lax.all_gather(small, ("ctx", "shard"), axis=0)
        gains = small[:, : 2 * nb].reshape(C * S, 2, nb).swapaxes(0, 1).reshape(2, D)
        shifts = small[:, 2 * nb : 4 * nb].reshape(C * S, 2, nb).swapaxes(0, 1).reshape(2, D)
        nbias = b_qkv[0].size
        bias = small[:, 4 * nb : 4 * nb + nbias].reshape(C, S, 3, S * heads, -1)
        bias = lax.dynamic_slice_in_dim(bias, p * heads, heads, 3)
        bias = bias.transpose(2, 3, 1, 0, 4).reshape(1, 3 * hn)
        lengths_row = lax.dynamic_index_in_dim(
            small[:S, 4 * nb + nbias :], z, 0, keepdims=False
        ).astype(jnp.int32)

        begin, tables = doc_tables(lengths_row, L)
        first = begin[::BLK] // BLK
        begin = begin[None, :]

        tok = to_plane(tokens)
        wq = fetch(w_qkv[0].reshape(nb, 3, S, hn).transpose(2, 0, 1, 3).reshape(S, nb, 3 * hn))
        wo = fetch(w_out[0].reshape(S, hn, nb).swapaxes(1, 2))
        wg = fetch(w_gateup[0].reshape(nb, 2, S, fn).transpose(2, 0, 1, 3).reshape(S, nb, 2 * fn))
        wd = fetch(w_down[0].reshape(S, fn, nb).swapaxes(1, 2))

        hidden = tok.astype(F32)
        n1, normal1, inverse1 = layer_norm(hidden, gains[0], shifts[0])
        n1 = gather(n1.astype(BF))
        qkv = mm(n1, wq, 1, 0) + bias
        q, k, v, o, lse = attend(qkv, tables, begin, first)
        mid = hidden + scatter(mm(o, wo, 1, 1))
        n2, normal2, inverse2 = layer_norm(mid, gains[1], shifts[1])
        n2 = gather(n2.astype(BF))
        gu = mm(n2, wg, 1, 0)
        gate, up = gu[:, :fn], gu[:, fn:]
        logistic = jax.nn.sigmoid(gate)
        act = (gate * logistic * up).astype(BF)
        out = mid + scatter(mm(act, wd, 1, 1))
        out = from_plane(out.astype(BF))

        grad_own = to_plane(cotangent)
        gb = gather(grad_own)
        gw_down = give(mm(gb, act, 0, 0))
        dact = mm(gb, wd, 1, 0)
        dgate = dact * up * logistic * (1.0 + gate * (1.0 - logistic))
        dup = dact * gate * logistic
        dgu = jnp.concatenate((dgate, dup), axis=1).astype(BF)
        gw_gateup = give(mm(n2, dgu, 0, 0))
        dn2 = scatter(mm(dgu, wg, 1, 1))
        dmid, gain2, shift2 = norm_back(dn2, normal2, inverse2, gains[1])
        dmid = grad_own.astype(F32) + dmid
        gb1 = gather(dmid.astype(BF))
        gw_out = give(mm(gb1, o, 0, 0))
        do = mm(gb1, wo, 1, 0).astype(BF)
        dqkv = attend_back(q, k, v, o, do, lse, tables, begin, first)
        gbias = jnp.sum(dqkv.astype(F32), axis=0)
        gw_qkv = give(mm(n1, dqkv, 0, 0))
        dn1 = scatter(mm(dqkv, wq, 1, 1))
        dtok, gain1, shift1 = norm_back(dn1, normal1, inverse1, gains[0])
        gtok = from_plane((dmid + dtok).astype(BF)).astype(F32)

        slots = jnp.zeros((T * S, 3 * hn), F32)
        slots = lax.dynamic_update_slice(slots, gbias[None], (c * S + p, 0))
        sums = lax.psum(
            jnp.concatenate((gain1, gain2, shift1, shift2, slots.reshape(-1))), ("shard", "ctx", "tp")
        )
        norms = lax.dynamic_index_in_dim(
            sums[: 4 * D].reshape(4, C * S, nb), z * S + p, 1, keepdims=False
        )
        slots = lax.dynamic_index_in_dim(sums[4 * D :].reshape(T, S, 3, heads, S * C, -1), c, 0, keepdims=False)
        slots = lax.dynamic_index_in_dim(slots, p * C + z, 3, keepdims=False)
        gbias = slots.swapaxes(0, 1).reshape(3, S * heads, -1)

        return (
            out,
            gtok,
            gw_qkv.reshape(S, nb, 3, hn).transpose(1, 2, 0, 3).reshape(w_qkv.shape),
            gbias[None],
            gw_out.swapaxes(1, 2).reshape(w_out.shape),
            gw_gateup.reshape(S, nb, 2, fn).transpose(1, 2, 0, 3).reshape(w_gateup.shape),
            gw_down.swapaxes(1, 2).reshape(w_down.shape),
            norms[:2][None],
            norms[2:][None],
        )

    return body


def solution(mesh):
    both = ("shard", "ctx")
    specs = (
        P(None, both, None, "tp"),
        P(None, None, "tp", both),
        P(None, "tp", both),
        P(None, both, None, "tp"),
        P(None, "tp", both),
        P(None, None, both),
        P(None, None, both),
    )
    return jax.shard_map(
        make_body(mesh.shape["shard"], mesh.shape["ctx"], mesh.shape["tp"]),
        mesh=mesh,
        in_specs=(P(both, None), P("shard", None)) + specs + (P(both, None),),
        out_specs=(P(both, None), P(both, None)) + specs,
        check_vma=False,
    )
```

```python
import functools

import jax
import jax.numpy as jnp
from jax import lax
from jax.experimental import pallas as pl
from jax.experimental.pallas import tpu as pltpu
from jax.sharding import PartitionSpec as P

HEAD = 64
ROT = 16
EPS = 1e-05
NEG = -1e30
BASE = 10000.0
BF = jnp.bfloat16
F32 = jnp.float32
BLK = 256
MESH = pl.DeviceIdType.MESH
DMA = pltpu.SemaphoreType.DMA
ANY = pl.BlockSpec(memory_space=pl.ANY)
IN_VMEM = pl.BlockSpec(memory_space=pltpu.VMEM)


def mm(a, b, ca, cb):
    return lax.dot_general(a, b, (((ca,), (cb,)), ((), ())), preferred_element_type=F32)


def remote(src, dst, send, recv, where):
    return pltpu.make_async_remote_copy(
        src_ref=src, dst_ref=dst, send_sem=send, recv_sem=recv, device_id=where, device_id_type=MESH
    )


def greet(peers):
    barrier = pltpu.get_barrier_semaphore()
    for where in peers:
        pl.semaphore_signal(barrier, inc=1, device_id=where, device_id_type=MESH)
    pl.semaphore_wait(barrier, len(peers))


def comm(kernel, number, **call):
    return pl.pallas_call(
        kernel,
        compiler_params=pltpu.CompilerParams(
            collective_id=number, has_side_effects=True, vmem_limit_bytes=56 << 20
        ),
        **call,
    )


def exchange_kernel(S, C, T, count, small, *refs):
    ins, refs = refs[:count], refs[count:]
    if small:
        tiles, refs = refs[0], refs[1:]
    outs, refs = refs[:count], refs[count:]
    if small:
        got, refs = refs[0], refs[1:]
    send, recv, own = refs[:3]
    p, z, c = lax.axis_index("shard"), lax.axis_index("ctx"), lax.axis_index("tp")
    peers = [{"shard": (p + k) % S} for k in range(1, S)]
    everyone = [(i, j) for i in range(C) for j in range(S) if i or j]
    if small:
        greet(
            [{"shard": (p + j) % S, "ctx": (z + i) % C} for i, j in everyone] + [{"tp": 1 - c}]
        )
    else:
        greet(peers)
    copies = []
    if small:
        tsend, trecv, bsend, brecv, town = refs[3:]
        here = pltpu.make_async_copy(tiles.at[z, p], got.at[c, z, p], town)
        here.start()
        for at, (i, j) in enumerate(everyone):
            q, g = (p + j) % S, (z + i) % C
            copy = remote(
                tiles.at[g, q], got.at[c, z, p], tsend.at[at], trecv.at[at], {"shard": q, "ctx": g}
            )
            copy.start()
            copies.append((copy, got.at[c, (z - i) % C, (p - j) % S]))
    moves = []
    for n in range(count):
        for k in range(1, S):
            copy = remote(
                ins[n].at[(p + k) % S], outs[n].at[p], send.at[n, k - 1], recv.at[n, k - 1], peers[k - 1]
            )
            copy.start()
            moves.append(copy)
        local = pltpu.make_async_copy(ins[n].at[p], outs[n].at[p], own.at[n])
        local.start()
        moves.append(local)
    if small:
        here.wait()
        for copy, _ in copies:
            copy.wait()
        back = remote(got.at[c], got.at[c], bsend, brecv, {"tp": 1 - c})
        back.start()
        back.wait_send()
        remote(got.at[1 - c], got.at[1 - c], bsend, brecv, {"tp": 1 - c}).wait_recv()
    for copy in moves:
        copy.wait()


def exchange(S, C, T, number, arrays, tiles=None):
    count, small = len(arrays), tiles is not None
    shapes = [jax.ShapeDtypeStruct(x.shape, x.dtype) for x in arrays]
    scratch = [DMA((count, S - 1)), DMA((count, S - 1)), DMA((count,))]
    args = list(arrays)
    if small:
        shapes.append(jax.ShapeDtypeStruct((T,) + tiles.shape, tiles.dtype))
        scratch += [DMA((C * S - 1,)), DMA((C * S - 1,)), DMA, DMA, DMA]
        args.append(tiles)
    return comm(
        functools.partial(exchange_kernel, S, C, T, count, small),
        number,
        out_shape=shapes,
        in_specs=[IN_VMEM] * len(args),
        out_specs=[ANY] * len(shapes),
        scratch_shapes=scratch,
        name="exchange",
    )(*args)


def plane_peers(S):
    p, c = lax.axis_index("shard"), lax.axis_index("tp")
    B = S // 2
    a, b = p // B, p % B
    rows = [{"shard": a * B + (b + j) % B} for j in range(1, B)]
    col = {"shard": (1 - a) * B + b}
    return rows, col, {"tp": 1 - c}


def spread_count(S):
    B = S // 2
    return 2 * (2 + 2 * (B - 1) + 2 + 2 * (B - 1))


def spread(S, own, region, send, recv):
    p, c = lax.axis_index("shard"), lax.axis_index("tp")
    B = S // 2
    a, b = p // B, p % B
    rows, col, other = plane_peers(S)
    per = spread_count(S) // 2
    OWN, ROW, COL, VIA_COL, VIA_ROW = 0, 2, 2 + 2 * (B - 1), 4 + 2 * (B - 1), 4 + 3 * (B - 1)
    started = []

    def push(q, h, sem, where):
        view = region(q, h, c)
        copy = remote(own(h) if q is p else view, view, send.at[sem], recv.at[sem], where)
        copy.start()
        started.append(copy)

    def came(q, h, sem, core):
        view = region(q, h, core)
        remote(view, view, send.at[sem], recv.at[sem], other).wait_recv()

    for h in range(2):
        for j in range(1, B):
            push(p, h, ROW + 2 * (j - 1) + h, rows[j - 1])
    for h in (1, 0):
        push(p, h, COL + h, col)
    for h in range(2):
        push(p, h, per + OWN + h, other)

    def from_row(j, h):
        q = a * B + (b - j) % B
        came(q, h, ROW + 2 * (j - 1) + h, c)
        push(q, h, per + ROW + 2 * (j - 1) + h, other)
        return q

    def from_col(h):
        q = (1 - a) * B + b
        came(q, h, COL + h, c)
        push(q, h, per + COL + h, other)
        return q

    for j in range(1, B):
        q = from_row(j, 0)
        push(q, 0, VIA_COL + j - 1, col)
    q = from_col(1)
    for j in range(1, B):
        push(q, 1, VIA_ROW + j - 1, rows[j - 1])
    for j in range(1, B):
        from_row(j, 1)
    from_col(0)
    for j in range(1, B):
        q = (1 - a) * B + (b - j) % B
        came(q, 0, VIA_COL + j - 1, c)
        push(q, 0, per + VIA_COL + j - 1, other)
        came(q, 1, VIA_ROW + j - 1, c)
        push(q, 1, per + VIA_ROW + j - 1, other)
    for h in range(2):
        came(p, h, per + OWN + h, 1 - c)
        came((1 - a) * B + b, h, per + COL + h, 1 - c)
    for j in range(1, B):
        for h in range(2):
            came(a * B + (b - j) % B, h, per + ROW + 2 * (j - 1) + h, 1 - c)
        q = (1 - a) * B + (b - j) % B
        came(q, 0, per + VIA_COL + j - 1, 1 - c)
        came(q, 1, per + VIA_ROW + j - 1, 1 - c)
    for copy in started:
        copy.wait_send()


def gather_kernel(S, T, x_ref, out_ref, send, recv, own):
    p, c = lax.axis_index("shard"), lax.axis_index("tp")
    half = x_ref.shape[0] // 2
    rows, col, other = plane_peers(S)
    local = pltpu.make_async_copy(x_ref, out_ref.at[p * T + c], own)
    local.start()
    greet(rows + [col, other])
    spread(
        S,
        lambda h: x_ref.at[pl.ds(h * half, half)],
        lambda q, h, core: out_ref.at[q * T + core, pl.ds(h * half, half)],
        send,
        recv,
    )
    local.wait()


def gather(S, T, number, x):
    n, D = x.shape
    out = comm(
        functools.partial(gather_kernel, S, T),
        number,
        out_shape=jax.ShapeDtypeStruct((S * T, n, D), x.dtype),
        in_specs=[IN_VMEM],
        out_specs=ANY,
        scratch_shapes=[DMA((spread_count(S),)), DMA((spread_count(S),)), DMA],
        name="gather",
    )(x)
    return out.reshape(S * T * n, D)


def enter_kernel(S, C, T, count, *refs):
    xs, outs = refs[:count], refs[count : 2 * count]
    buf, s1, r1, s2, r2, s3, r3, own = refs[2 * count :]
    p, z, c = lax.axis_index("shard"), lax.axis_index("ctx"), lax.axis_index("tp")
    n, wide = outs[0].shape[2], outs[0].shape[3] // S
    rows, col, other = plane_peers(S)
    mates = [{"shard": (p + k) % S} for k in range(1, S)]
    line = [{"ctx": (z + k) % C} for k in range(1, C)]
    greet(mates + line + [other])

    def part(q):
        return pl.ds(pl.multiple_of(q * wide, 128), wide)

    sends, hops = [], []
    for t in range(count):
        mine = pl.ds(pl.multiple_of(c * n, 16), n)
        local = pltpu.make_async_copy(xs[t].at[mine, part(p)], buf.at[t, p], own.at[t, 0])
        local.start()
        hop = [local]
        for k in range(1, S):
            copy = remote(
                xs[t].at[mine, part((p + k) % S)], buf.at[t, p], s1.at[t, k - 1], r1.at[t, k - 1], mates[k - 1]
            )
            copy.start()
            hop.append(copy)
        hops.append(hop)
    lines = []
    for t in range(count):
        for copy in hops[t]:
            copy.wait()
        local = pltpu.make_async_copy(buf.at[t, z], outs[t].at[z, c, :, part(p)], own.at[t, 1])
        local.start()
        hop = [local]
        for k in range(1, C):
            copy = remote(
                buf.at[t, (z + k) % C], outs[t].at[z, c, :, part(p)], s2.at[t, k - 1], r2.at[t, k - 1], line[k - 1]
            )
            copy.start()
            hop.append(copy)
        lines.append(hop)
    for t in range(count):
        for copy in lines[t]:
            copy.wait()
        out = outs[t]

        def region(q, h, core):
            return out.at[pl.ds(h * (C // 2), C // 2), core, :, part(q)]

        spread(S, lambda h: region(p, h, c), region, s3.at[t], r3.at[t])


def enter(S, C, T, number, arrays):
    R, D = arrays[0].shape
    count = len(arrays)
    outs = comm(
        functools.partial(enter_kernel, S, C, T, count),
        number,
        out_shape=[jax.ShapeDtypeStruct((C, T, R // T, D), x.dtype) for x in arrays],
        in_specs=[ANY] * count,
        out_specs=[ANY] * count,
        scratch_shapes=[
            pltpu.VMEM((count, S, R // T, D // S), BF),
            DMA((count, S - 1)), DMA((count, S - 1)), DMA((count, C - 1)), DMA((count, C - 1)),
            DMA((count, spread_count(S))), DMA((count, spread_count(S))), DMA((count, 2)),
        ],
        name="enter",
    )(*arrays)
    return [x.reshape(C * R, D) for x in outs]


def leave_kernel(S, C, T, x_ref, out_ref, buf, buf2, s1, r1, s2, r2, s3, r3, s4, r4, own):
    p, z, c = lax.axis_index("shard"), lax.axis_index("ctx"), lax.axis_index("tp")
    wide = x_ref.shape[1] // S
    mates = [{"shard": (p + k) % S} for k in range(1, S)]
    line = [{"ctx": (z + k) % C} for k in range(1, C)]
    other = {"tp": 1 - c}
    greet(mates + line + [other])

    def part(q):
        return pl.ds(pl.multiple_of(q * wide, 128), wide)

    def turn_over(source, target, send, recv, local, extent, me, where):
        hop = [pltpu.make_async_copy(source(me), target, local)]
        hop[0].start()
        for k in range(1, extent):
            copy = remote(source((me + k) % extent), target, send.at[k - 1], recv.at[k - 1], where[k - 1])
            copy.start()
            hop.append(copy)
        for copy in hop:
            copy.wait()

    turn_over(lambda q: x_ref.at[:, part(q)], buf.at[p], s1, r1, own.at[0], S, p, mates)
    turn_over(lambda q: buf.at[q], buf2.at[z], s2, r2, own.at[1], C, z, line)
    turn_over(lambda q: buf2.at[q], out_ref.at[c, :, part(p)], s3, r3, own.at[2], S, p, mates)
    copy = remote(out_ref.at[c], out_ref.at[c], s4, r4, other)
    copy.start()
    copy.wait_send()
    remote(out_ref.at[1 - c], out_ref.at[1 - c], s4, r4, other).wait_recv()


def leave(S, C, T, number, x):
    n, D = x.shape
    out = comm(
        functools.partial(leave_kernel, S, C, T),
        number,
        out_shape=jax.ShapeDtypeStruct((T, n, D), x.dtype),
        in_specs=[ANY],
        out_specs=ANY,
        scratch_shapes=[
            pltpu.VMEM((S, n, D // S), BF), pltpu.VMEM((C, n, D // S), BF),
            DMA((S - 1,)), DMA((S - 1,)), DMA((C - 1,)), DMA((C - 1,)), DMA((S - 1,)), DMA((S - 1,)),
            DMA, DMA, DMA((3,)),
        ],
        name="leave",
    )(x)
    return out.reshape(T * n, D)


CHUNK = 512


def scatter_kernel(
    S, T, x_ref, w_ref, out_ref, away, sib, mine, row1, col1, row2, col2, to_col, to_row,
    asend, arecv, rsend, rrecv, csend, crecv, fsend, frecv,
):
    p, c = lax.axis_index("shard"), lax.axis_index("tp")
    B = S // 2
    a, b = p // B, p % B
    rows, col, other = plane_peers(S)
    n, D = out_ref.shape
    half = n // 2
    steps = D // CHUNK
    greet(rows + [col, other])

    def chip(e):
        return ((a + e // B) % 2) * B + (b + e % B) % B

    def product(e, core, store):
        x = x_ref[chip(e) * T + core]

        def column(j, _):
            w = pl.ds(pl.multiple_of(j * CHUNK, CHUNK), CHUNK)
            store(w, mm(x, w_ref[w, :], 1, 1))
            return 0

        lax.fori_loop(0, steps, column, 0)

    def to_other(e):
        return remote(away.at[e], sib.at[e], asend.at[e], arecv.at[e], other)

    def first(i, _):
        e = S - 1 - i

        def store(w, value):
            away[e, :, w] = value.astype(BF)

        product(e, 1 - c, store)
        to_other(e).start()
        return 0

    lax.fori_loop(0, S, first, 0)

    top, low = pl.ds(0, half), pl.ds(half, half)
    started = []

    def push(src, dst, send, recv, where):
        copy = remote(src, dst, send, recv, where)
        copy.start()
        started.append(copy)

    for e in range(S - 1, -1, -1):
        to_other(e).wait()

        def store(w, value):
            value = value + sib[e, :, w].astype(F32)
            if e:
                mine[e, :, w] = value.astype(BF)
            else:
                out_ref[:, w] = value

        product(e, c, store)
        j = e % B
        if e > B:
            push(mine.at[e, top], row1.at[j - 1, 1], rsend.at[j - 1, 1], rrecv.at[j - 1, 1], rows[j - 1])
            push(mine.at[e, low], col1.at[j], csend.at[j], crecv.at[j], col)
        elif e == B:
            push(mine.at[e, low], col1.at[0], csend.at[0], crecv.at[0], col)
        elif e:
            push(mine.at[e, top], row1.at[j - 1, 0], rsend.at[j - 1, 0], rrecv.at[j - 1, 0], rows[j - 1])

    def came(ref, send, recv):
        remote(ref, ref, send, recv, other).wait_recv()

    total = mine[B, top, :].astype(F32)
    for j in range(1, B):
        came(row1.at[j - 1, 1], rsend.at[j - 1, 1], rrecv.at[j - 1, 1])
        total = total + row1[j - 1, 1].astype(F32)
    to_col[...] = total.astype(BF)
    push(to_col, col2, fsend.at[0], frecv.at[0], col)
    for j in range(1, B):
        came(col1.at[j], csend.at[j], crecv.at[j])
        to_row[j - 1] = (mine[j, low, :].astype(F32) + col1[j].astype(F32)).astype(BF)
        push(to_row.at[j - 1], row2.at[j - 1], fsend.at[j], frecv.at[j], rows[j - 1])
    came(col1.at[0], csend.at[0], crecv.at[0])
    upper, lower = out_ref[top, :], out_ref[low, :] + col1[0].astype(F32)
    for j in range(1, B):
        came(row1.at[j - 1, 0], rsend.at[j - 1, 0], rrecv.at[j - 1, 0])
        upper = upper + row1[j - 1, 0].astype(F32)
    came(col2, fsend.at[0], frecv.at[0])
    out_ref[top, :] = upper + col2[...].astype(F32)
    for j in range(1, B):
        came(row2.at[j - 1], fsend.at[j], frecv.at[j])
        lower = lower + row2[j - 1].astype(F32)
    out_ref[low, :] = lower
    for copy in started:
        copy.wait_send()


def scatter(S, T, number, x, w):
    L, K = x.shape
    D = w.shape[0]
    n, B = L // (S * T), S // 2
    half = n // 2
    return comm(
        functools.partial(scatter_kernel, S, T),
        number,
        out_shape=jax.ShapeDtypeStruct((n, D), F32),
        in_specs=[IN_VMEM, IN_VMEM],
        out_specs=IN_VMEM,
        scratch_shapes=[
            pltpu.VMEM((S, n, D), BF), pltpu.VMEM((S, n, D), BF), pltpu.VMEM((S, n, D), BF),
            pltpu.VMEM((B - 1, 2, half, D), BF), pltpu.VMEM((B, half, D), BF),
            pltpu.VMEM((B - 1, half, D), BF), pltpu.VMEM((half, D), BF),
            pltpu.VMEM((half, D), BF), pltpu.VMEM((B - 1, half, D), BF),
            DMA((S,)), DMA((S,)), DMA((B - 1, 2)), DMA((B - 1, 2)), DMA((B,)), DMA((B,)), DMA((B,)), DMA((B,)),
        ],
        name="scatter",
    )(x.reshape(S * T, n, K), w)


def turn(x, cos, lo, hi):
    n = x.shape[-1]
    return x * cos + pltpu.roll(x, n - ROT // 2, 1) * lo + pltpu.roll(x, ROT // 2, 1) * hi


def attend_kernel(
    first_ref, q_ref, k_ref, v_ref, cos_ref, lo_ref, hi_ref, begin_ref,
    qo_ref, ko_ref, vo_ref, o_ref, lse_ref, vt_ref,
):
    rows = q_ref.shape[0]
    nb = rows // BLK
    lane = lax.broadcasted_iota(jnp.int32, (BLK, 128), 1)
    left = lane < HEAD
    key_at = lax.broadcasted_iota(jnp.int32, (BLK, BLK), 0)
    query_at = lax.broadcasted_iota(jnp.int32, (1, BLK), 1)

    @pl.loop(0, nb)
    def _(i):
        r = pl.ds(pl.multiple_of(i * BLK, BLK), BLK)
        cos, lo, hi = cos_ref[r, :], lo_ref[r, :], hi_ref[r, :]
        qo_ref[r, :] = turn(q_ref[r, :], cos, lo, hi).astype(BF) * jnp.asarray(HEAD**-0.5, BF)
        ko_ref[r, :] = turn(k_ref[r, :], cos, lo, hi).astype(BF)
        v = v_ref[r, :]
        vo_ref[r, :] = v.astype(BF)
        vt_ref[:, r] = v.T.astype(BF)

    @pl.loop(0, nb)
    def _(i):
        r = pl.ds(pl.multiple_of(i * BLK, BLK), BLK)
        q = qo_ref[r, :]
        zero = jnp.zeros_like(q)
        qs = (jnp.where(left, q, zero), jnp.where(left, zero, q))
        begin = begin_ref[0:1, r]
        here = query_at + i * BLK

        def step(j, carry):
            w = pl.ds(pl.multiple_of(j * BLK, BLK), BLK)
            k, vt = ko_ref[w, :], vt_ref[:, w]
            key = key_at + j * BLK
            seen = (key <= here) & (key >= begin)
            out = []
            for h in range(2):
                m, l, acc = carry[h]
                s = jnp.where(seen, mm(k, qs[h], 1, 1), NEG)
                top = jnp.maximum(m, jnp.max(s, axis=0, keepdims=True))
                fade = jnp.exp(m - top)
                e = jnp.exp(s - top)
                out.append(
                    (top, l * fade + jnp.sum(e, axis=0, keepdims=True), acc * fade + mm(vt, e.astype(BF), 1, 0))
                )
            return tuple(out)

        start = (
            jnp.full((1, BLK), NEG, F32), jnp.zeros((1, BLK), F32), jnp.zeros((128, BLK), F32)
        )
        done = lax.fori_loop(first_ref[i], i + 1, step, (start, start))
        parts = []
        for h in range(2):
            m, l, acc = done[h]
            parts.append((acc / l).T)
            lse_ref[0, h : h + 1, r] = m + jnp.log(l)
        o_ref[r, :] = jnp.where(left, parts[0], parts[1]).astype(BF)


def attend(qkv, tables, begin, first):
    rows, wide = qkv.shape
    pairs = wide // 3 // 128
    cos, lo, hi = tables
    full = pl.BlockSpec((rows, 128), lambda j, *_: (0, 0))

    def col(base):
        return pl.BlockSpec((rows, 128), lambda j, *_: (0, base + j))

    half = jax.ShapeDtypeStruct((rows, wide // 3), BF)
    return pl.pallas_call(
        attend_kernel,
        grid_spec=pltpu.PrefetchScalarGridSpec(
            num_scalar_prefetch=1,
            grid=(pairs,),
            in_specs=[
                col(0), col(pairs), col(2 * pairs), full, full, full,
                pl.BlockSpec((1, rows), lambda j, *_: (0, 0)),
            ],
            out_specs=[col(0)] * 4 + [pl.BlockSpec((1, 2, rows), lambda j, *_: (j, 0, 0))],
            scratch_shapes=[pltpu.VMEM((128, rows), BF)],
        ),
        out_shape=[half] * 4 + [jax.ShapeDtypeStruct((pairs, 2, rows), F32)],
        compiler_params=pltpu.CompilerParams(vmem_limit_bytes=48 << 20),
        cost_estimate=pl.CostEstimate(
            flops=4 * rows * rows * wide // 3, bytes_accessed=rows * wide * 8, transcendentals=0
        ),
        name="attend",
    )(first, qkv, qkv, qkv, cos, lo, hi, begin)


def attend_back_kernel(
    first_ref, q_ref, k_ref, v_ref, o_ref, do_ref, lse_ref, cos_ref, lo_ref, hi_ref, begin_ref,
    out_ref, kt_ref, dk_ref, dv_ref,
):
    rows = q_ref.shape[0]
    nb = rows // BLK
    pair, pairs = pl.program_id(0), pl.num_programs(0)
    lane = lax.broadcasted_iota(jnp.int32, (BLK, 128), 1)
    left = lane < HEAD
    key_at = lax.broadcasted_iota(jnp.int32, (BLK, BLK), 0)
    query_at = lax.broadcasted_iota(jnp.int32, (1, BLK), 1)

    def column(base):
        return pl.ds(pl.multiple_of((base * pairs + pair) * 128, 128), 128)

    @pl.loop(0, nb)
    def _(i):
        r = pl.ds(pl.multiple_of(i * BLK, BLK), BLK)
        kt_ref[:, r] = k_ref[r, :].astype(F32).T.astype(BF)
        dk_ref[r, :] = jnp.zeros((BLK, 128), F32)
        dv_ref[r, :] = jnp.zeros((BLK, 128), F32)

    @pl.loop(0, nb)
    def _(i):
        r = pl.ds(pl.multiple_of(i * BLK, BLK), BLK)
        q, do = q_ref[r, :], do_ref[r, :]
        zero = jnp.zeros_like(q)
        qs = (jnp.where(left, q, zero), jnp.where(left, zero, q))
        dos = (jnp.where(left, do, zero), jnp.where(left, zero, do))
        prod = (do.astype(F32) * o_ref[r, :].astype(F32)).T
        deltas = (
            jnp.sum(prod[:HEAD], axis=0, keepdims=True), jnp.sum(prod[HEAD:], axis=0, keepdims=True)
        )
        lses = (lse_ref[0, 0:1, r], lse_ref[0, 1:2, r])
        begin = begin_ref[0:1, r]
        here = query_at + i * BLK

        def step(j, carry):
            w = pl.ds(pl.multiple_of(j * BLK, BLK), BLK)
            k, v, kt = k_ref[w, :], v_ref[w, :], kt_ref[:, w]
            key = key_at + j * BLK
            seen = (key <= here) & (key >= begin)
            out = []
            dk = dv = None
            for h in range(2):
                prob = jnp.exp(jnp.where(seen, mm(k, qs[h], 1, 1) - lses[h], NEG))
                ds = (prob * (mm(v, dos[h], 1, 1) - deltas[h])).astype(BF)
                out.append(carry[h] + mm(kt, ds, 1, 0))
                dk_h, dv_h = mm(ds, qs[h], 1, 0), mm(prob.astype(BF), dos[h], 1, 0)
                dk, dv = (dk_h, dv_h) if h == 0 else (dk + dk_h, dv + dv_h)
            dk_ref[w, :] += dk
            dv_ref[w, :] += dv
            return tuple(out)

        start = jnp.zeros((128, BLK), F32)
        a, b = lax.fori_loop(first_ref[i], i + 1, step, (start, start))
        dq = jnp.where(left, a.T, b.T) * (HEAD**-0.5)
        out_ref[r, column(0)] = turn(dq, cos_ref[r, :], -lo_ref[r, :], -hi_ref[r, :]).astype(BF)

    @pl.loop(0, nb)
    def _(i):
        r = pl.ds(pl.multiple_of(i * BLK, BLK), BLK)
        out_ref[r, column(1)] = turn(dk_ref[r, :], cos_ref[r, :], -lo_ref[r, :], -hi_ref[r, :]).astype(BF)
        out_ref[r, column(2)] = dv_ref[r, :].astype(BF)


def attend_back(q, k, v, o, do, lse, tables, begin, first):
    rows, wide = q.shape
    pairs = wide // 128
    cos, lo, hi = tables
    full = pl.BlockSpec((rows, 128), lambda j, *_: (0, 0))
    col = pl.BlockSpec((rows, 128), lambda j, *_: (0, j))
    return pl.pallas_call(
        attend_back_kernel,
        grid_spec=pltpu.PrefetchScalarGridSpec(
            num_scalar_prefetch=1,
            grid=(pairs,),
            in_specs=[
                col, col, col, col, col, pl.BlockSpec((1, 2, rows), lambda j, *_: (j, 0, 0)),
                full, full, full, pl.BlockSpec((1, rows), lambda j, *_: (0, 0)),
            ],
            out_specs=pl.BlockSpec((rows, 3 * wide), lambda j, *_: (0, 0)),
            scratch_shapes=[
                pltpu.VMEM((128, rows), BF), pltpu.VMEM((rows, 128), F32), pltpu.VMEM((rows, 128), F32)
            ],
        ),
        out_shape=jax.ShapeDtypeStruct((rows, 3 * wide), BF),
        compiler_params=pltpu.CompilerParams(vmem_limit_bytes=48 << 20),
        cost_estimate=pl.CostEstimate(
            flops=10 * rows * rows * wide, bytes_accessed=rows * wide * 16, transcendentals=0
        ),
        name="attend_back",
    )(first, q, k, v, o, do, lse, cos, lo, hi, begin)


def doc_tables(lengths_row, rows):
    row_ids = jnp.arange(rows, dtype=jnp.int32)
    ends = jnp.cumsum(lengths_row, dtype=jnp.int32)
    begins = ends - lengths_row
    inside = (row_ids[:, None] >= begins[None, :]) & (row_ids[:, None] < ends[None, :])
    begin = jnp.sum(jnp.where(inside, begins[None, :], 0), axis=1, dtype=jnp.int32)
    half = ROT // 2
    freq = BASE ** (-2.0 * jnp.arange(half, dtype=F32) / ROT)
    phase = (row_ids - begin).astype(F32)[:, None] * freq[None, :]
    cos, sin = jnp.cos(phase), jnp.sin(phase)
    rest = jnp.ones((rows, HEAD - ROT), F32)
    none = jnp.zeros((rows, half), F32)
    cos_t = jnp.concatenate((cos, cos, rest), axis=1)
    lo_t = jnp.concatenate((-sin, none, 0 * rest), axis=1)
    hi_t = jnp.concatenate((none, sin, 0 * rest), axis=1)
    tables = tuple(jnp.concatenate((t, t), axis=1) for t in (cos_t, lo_t, hi_t))
    return begin, tables


def layer_norm(values, gain, shift):
    center = values - jnp.mean(values, axis=-1, keepdims=True)
    inverse = lax.rsqrt(jnp.mean(center * center, axis=-1, keepdims=True) + EPS)
    normal = center * inverse
    return (normal * gain + shift, normal, inverse)


def norm_back(gradient, normal, inverse, gain):
    scaled = gradient * gain
    centered = (
        scaled
        - jnp.mean(scaled, axis=-1, keepdims=True)
        - normal * jnp.mean(scaled * normal, axis=-1, keepdims=True)
    )
    return (inverse * centered, jnp.sum(gradient * normal, axis=0), jnp.sum(gradient, axis=0))


def tiles_of(parts, lead):
    flat = jnp.concatenate([x.astype(F32).reshape(lead + (-1,)) for x in parts], axis=-1)
    flat = jnp.pad(flat, ((0, 0),) * len(lead) + ((0, 1024 - flat.shape[-1]),))
    return flat.reshape(lead + (8, 128))


def make_body(S, C, T):
    assert S == C

    def body(tokens, lengths, w_qkv, b_qkv, w_out, w_gateup, w_down, norm_gain, norm_bias, cotangent):
        p, z, c = lax.axis_index("shard"), lax.axis_index("ctx"), lax.axis_index("tp")
        R, D = tokens.shape
        n = R // T
        nb = D // (S * C)
        L = R * C

        def permute(x):
            return x.reshape(x.shape[0], S, C, nb).swapaxes(1, 2).reshape(x.shape)

        def unpermute(x):
            return x.reshape(x.shape[0], C, S, nb).swapaxes(1, 2).reshape(x.shape)

        def own(x):
            return lax.dynamic_slice_in_dim(x, (p * T + c) * n, n, 0)

        def spread_out(x):
            return gather(S, T, 4, x)

        def over_ctx(w):
            return lax.all_gather(w.reshape(S * nb, -1), "ctx", axis=0, tiled=True)

        def sum_ctx(g):
            g = lax.psum_scatter(g.astype(BF), "ctx", scatter_dimension=0, tiled=True)
            return g.reshape(S, nb, -1)

        hn = w_qkv.shape[3] // S
        fn = w_gateup.shape[3] // S
        heads = hn // HEAD
        nf = HEAD // (S * C)

        tile = tiles_of((norm_gain[0].reshape(-1), norm_bias[0].reshape(-1), b_qkv[0].reshape(-1), lengths[0]), ())
        wq, small = exchange(
            S, C, T, 0,
            [w_qkv[0].reshape(nb, 3, S, hn).transpose(2, 0, 1, 3).reshape(S, nb, 3 * hn)],
            jnp.broadcast_to(tile, (C, S, 8, 128)),
        )
        wq = over_ctx(wq)
        wo, wg, wd = exchange(
            S, C, T, 1,
            [
                w_out[0].reshape(S, hn, nb).swapaxes(1, 2),
                w_gateup[0].reshape(nb, 2, S, fn).transpose(2, 0, 1, 3).reshape(S, nb, 2 * fn),
                w_down[0].reshape(S, fn, nb).swapaxes(1, 2),
            ],
        )
        wo, wg, wd = over_ctx(wo), over_ctx(wg), over_ctx(wd)
        tok, gb = enter(S, C, T, 2, [permute(tokens), permute(cotangent)])

        small = lax.dynamic_index_in_dim(small, c, 0, keepdims=False).reshape(C, S, 1024)
        norms = small[:, :, : 4 * nb].reshape(C * S, 4, nb).swapaxes(0, 1).reshape(4, D)
        gains, shifts = norms[:2], norms[2:]
        nbias = 3 * S * heads * nf
        bias = small[:, :, 4 * nb : 4 * nb + nbias].reshape(C, S, 3, S * heads, nf)
        bias = lax.dynamic_slice_in_dim(bias, p * heads, heads, 3)
        bias = bias.transpose(2, 3, 1, 0, 4).reshape(1, 3 * hn)
        docs = lengths.shape[1]
        lengths_row = lax.dynamic_index_in_dim(
            small[0, :, 4 * nb + nbias : 4 * nb + nbias + docs], z, 0, keepdims=False
        ).astype(jnp.int32)
        begin, tables = doc_tables(lengths_row, L)
        first = begin[::BLK] // BLK
        begin = begin[None, :]

        n1 = layer_norm(tok.astype(F32), gains[0], shifts[0])[0].astype(BF)
        hidden = own(tok).astype(F32)
        _, normal1, inverse1 = layer_norm(hidden, gains[0], shifts[0])
        qkv = mm(n1, wq, 1, 0) + bias
        q, k, v, o, lse = attend(qkv, tables, begin, first)
        mid = hidden + scatter(S, T, 5, o, wo)
        n2, normal2, inverse2 = layer_norm(mid, gains[1], shifts[1])
        n2 = spread_out(n2.astype(BF))
        gu = mm(n2, wg, 1, 0)
        gate, up = gu[:, :fn], gu[:, fn:]
        logistic = jax.nn.sigmoid(gate)
        act = (gate * logistic * up).astype(BF)
        gw_down = sum_ctx(mm(gb, act, 0, 0))

        dact = mm(gb, wd, 1, 0)
        dgate = dact * up * logistic * (1.0 + gate * (1.0 - logistic))
        dup = dact * gate * logistic
        dgu = jnp.concatenate((dgate, dup), axis=1).astype(BF)
        gw_gateup = sum_ctx(mm(n2, dgu, 0, 0))
        dn2 = scatter(S, T, 6, dgu, wg)
        dmid, gain2, shift2 = norm_back(dn2, normal2, inverse2, gains[1])
        dmid = own(gb).astype(F32) + dmid
        gb1 = spread_out(dmid.astype(BF))
        gw_out = sum_ctx(mm(gb1, o, 0, 0))
        do = mm(gb1, wo, 1, 0).astype(BF)
        dqkv = attend_back(q, k, v, o, do, lse, tables, begin, first)
        gw_qkv = sum_ctx(mm(n1, dqkv, 0, 0))
        dn1 = scatter(S, T, 7, dqkv, wq)
        out = mid + scatter(S, T, 8, act, wd)
        out = leave(S, C, T, 9, unpermute(out.astype(BF)))
        dtok, gain1, shift1 = norm_back(dn1, normal1, inverse1, gains[0])
        gtok = leave(S, C, T, 9, unpermute((dmid + dtok).astype(BF))).astype(F32)
        gw_out, gw_gateup, gw_down = exchange(S, C, T, 1, [gw_out, gw_gateup, gw_down])

        gbias = jnp.sum(dqkv.astype(F32), axis=0)
        tiles = tiles_of(
            (
                jnp.stack((gain1, gain2, shift1, shift2)).reshape(4, C, S, nb).transpose(1, 2, 0, 3),
                gbias.reshape(3, heads, S, C, nf).transpose(3, 2, 0, 1, 4),
            ),
            (C, S),
        )
        gw_qkv, small = exchange(S, C, T, 0, [gw_qkv], tiles)
        small = small.reshape(T, C, S, 1024)
        norms = jnp.sum(small[..., : 4 * nb], axis=(0, 1, 2)).reshape(1, 4, nb)
        gbias = lax.dynamic_index_in_dim(small, c, 0, keepdims=False)[..., 4 * nb : 4 * nb + 3 * heads * nf]
        gbias = jnp.sum(gbias, axis=0).reshape(S, 3, heads, nf).swapaxes(0, 1).reshape(b_qkv.shape)

        return (
            out,
            gtok,
            gw_qkv.astype(F32).reshape(S, nb, 3, hn).transpose(1, 2, 0, 3).reshape(w_qkv.shape),
            gbias,
            gw_out.astype(F32).swapaxes(1, 2).reshape(w_out.shape),
            gw_gateup.astype(F32).reshape(S, nb, 2, fn).transpose(1, 2, 0, 3).reshape(w_gateup.shape),
            gw_down.astype(F32).swapaxes(1, 2).reshape(w_down.shape),
            norms[:, :2],
            norms[:, 2:],
        )

    return body


def solution(mesh):
    both = ("shard", "ctx")
    specs = (
        P(None, both, None, "tp"),
        P(None, None, "tp", both),
        P(None, "tp", both),
        P(None, both, None, "tp"),
        P(None, "tp", both),
        P(None, None, both),
        P(None, None, both),
    )
    return jax.shard_map(
        make_body(mesh.shape["shard"], mesh.shape["ctx"], mesh.shape["tp"]),
        mesh=mesh,
        in_specs=(P(both, None), P("shard", None)) + specs + (P(both, None),),
        out_specs=(P(both, None), P(both, None)) + specs,
        check_vma=False,
    )
```

```python
import functools

import jax
import jax.numpy as jnp
import numpy as np
from jax import lax
from jax.experimental import pallas as pl
from jax.experimental.pallas import tpu as pltpu
from jax.sharding import PartitionSpec as P

HEAD = 64
ROT = 16
EPS = 1e-05
NEG = -1e30
BASE = 10000.0
BF = jnp.bfloat16
F32 = jnp.float32
BLK = 256
MESH = pl.DeviceIdType.MESH
DMA = pltpu.SemaphoreType.DMA
ANY = pl.BlockSpec(memory_space=pl.ANY)
IN_VMEM = pl.BlockSpec(memory_space=pltpu.VMEM)


def mm(a, b, ca, cb):
    return lax.dot_general(a, b, (((ca,), (cb,)), ((), ())), preferred_element_type=F32)


def remote(src, dst, send, recv, where):
    return pltpu.make_async_remote_copy(
        src_ref=src, dst_ref=dst, send_sem=send, recv_sem=recv, device_id=where, device_id_type=MESH
    )


def here():
    return lax.axis_index("shard"), lax.axis_index("ctx"), lax.axis_index("tp")


class Riders:
    def __init__(self, S, C, riders):
        self.S, self.C = S, C
        self.axes = [axis for axis, _ in riders]
        self.arrays = [x for _, x in riders]
        self.shapes = [jax.ShapeDtypeStruct(x.shape, x.dtype) for x in self.arrays]
        count, most = len(riders), max(S, C) - 1
        self.scratch = [DMA((count, most)), DMA((count, most)), DMA((count,))] if count else []

    def bind(self, ins, outs, sems):
        self.ins, self.outs, self.sems = ins, outs, sems

    def start(self):
        p, z, c = here()
        self.moves = []
        for n, axis in enumerate(self.axes):
            src, dst = self.ins[n], self.outs[n]
            send, recv, own = self.sems
            if axis == "tp":
                copies = [remote(src, dst, send.at[n, 0], recv.at[n, 0], {"tp": 1 - c})]
            else:
                size, me = (self.S, p) if axis == "shard" else (self.C, z)
                copies = [
                    remote(src.at[(me + k) % size], dst.at[me], send.at[n, k - 1], recv.at[n, k - 1], {axis: (me + k) % size})
                    for k in range(1, size)
                ]
                copies.append(pltpu.make_async_copy(src.at[me], dst.at[me], own.at[n]))
            for copy in copies:
                copy.start()
            self.moves += copies

    def wait(self):
        for copy in self.moves:
            copy.wait()


def greet(S, C, mates=(), line=False, other=False, axes=()):
    p, z, c = here()
    peers = [{"shard": q} for q in ([(p + k) % S for k in range(1, S)] if "shard" in axes else mates)]
    if line or "ctx" in axes:
        peers += [{"ctx": (z + k) % C} for k in range(1, C)]
    if other or "tp" in axes:
        peers.append({"tp": 1 - c})
    barrier = pltpu.get_barrier_semaphore()
    for where in peers:
        pl.semaphore_signal(barrier, inc=1, device_id=where, device_id_type=MESH)
    pl.semaphore_wait(barrier, len(peers))


def comm(kernel, S, C, number, name, args, in_specs, outs, scratch, riders=()):
    ride = Riders(S, C, riders)
    na, nr, no, ns = len(args), len(ride.axes), len(outs), len(scratch)

    def body(*refs):
        ins, refs = refs[:na], refs[na:]
        rins, refs = refs[:nr], refs[nr:]
        os, refs = refs[:no], refs[no:]
        routs, refs = refs[:nr], refs[nr:]
        ride.bind(rins, routs, refs[ns:])
        kernel(ride, ins, os, refs[:ns])

    return pl.pallas_call(
        body,
        out_shape=[shape for shape, _ in outs] + ride.shapes,
        in_specs=list(in_specs) + [IN_VMEM] * nr,
        out_specs=[spec for _, spec in outs] + [ANY] * nr,
        scratch_shapes=list(scratch) + ride.scratch,
        compiler_params=pltpu.CompilerParams(
            collective_id=number, has_side_effects=True, vmem_limit_bytes=56 << 20
        ),
        cost_estimate=pl.CostEstimate(flops=0, bytes_accessed=120_000_000, transcendentals=0),
        name=name,
    )(*args, *ride.arrays)


def exchange(S, C, T, number, riders, tiles=None):
    if tiles is None:

        def plain(ride, ins, outs, scratch):
            greet(S, C, axes=ride.axes)
            ride.start()
            ride.wait()

        return comm(plain, S, C, number, "exchange", [], [], [], [], riders)

    def kernel(ride, ins, outs, scratch):
        (tile,), (got,) = ins, outs
        send, recv, bsend, brecv, own = scratch
        p, z, c = here()
        everyone = [(i, j) for i in range(C) for j in range(S) if i or j]
        barrier = pltpu.get_barrier_semaphore()
        peers = [{"shard": (p + j) % S, "ctx": (z + i) % C} for i, j in everyone] + [{"tp": 1 - c}]
        for where in peers:
            pl.semaphore_signal(barrier, inc=1, device_id=where, device_id_type=MESH)
        pl.semaphore_wait(barrier, len(peers))
        local = pltpu.make_async_copy(tile.at[z, p], got.at[c, z, p], own)
        local.start()
        copies = []
        for at, (where, (i, j)) in enumerate(zip(peers, everyone)):
            q, g = (p + j) % S, (z + i) % C
            copies.append(remote(tile.at[g, q], got.at[c, z, p], send.at[at], recv.at[at], where))
            copies[-1].start()
        ride.start()
        local.wait()
        for copy in copies:
            copy.wait()
        back = remote(got.at[c], got.at[c], bsend, brecv, {"tp": 1 - c})
        back.start()
        back.wait_send()
        remote(got.at[1 - c], got.at[1 - c], bsend, brecv, {"tp": 1 - c}).wait_recv()
        ride.wait()

    count = C * S - 1
    return comm(
        kernel, S, C, number, "exchange", [tiles], [IN_VMEM],
        [(jax.ShapeDtypeStruct((T,) + tiles.shape, tiles.dtype), ANY)],
        [DMA((count,)), DMA((count,)), DMA, DMA, DMA],
        riders,
    )


def plane(S):
    p, _, c = here()
    B = S // 2
    a, b = p // B, p % B
    return a, b, [a * B + (b + j) % B for j in range(1, B)], (1 - a) * B + b


def spread_sems(S):
    count = 4 + 4 * (S // 2 - 1)
    return [DMA((2 * count,)), DMA((2 * count,))]


def spread(S, own, region, send, recv):
    p, _, c = here()
    B = S // 2
    a, b, rows, col = plane(S)
    rows, col, other = [{"shard": q} for q in rows], {"shard": col}, {"tp": 1 - c}
    per = 4 + 4 * (B - 1)
    OWN, ROW, COL, VIA_COL, VIA_ROW = 0, 2, 2 + 2 * (B - 1), 4 + 2 * (B - 1), 4 + 3 * (B - 1)
    started = []

    def push(q, h, sem, where, first=False):
        view = region(q, h, c)
        copy = remote(own(h) if first else view, view, send.at[sem], recv.at[sem], where)
        copy.start()
        started.append(copy)

    def came(q, h, sem, core):
        view = region(q, h, core)
        remote(view, view, send.at[sem], recv.at[sem], other).wait_recv()

    for h in range(2):
        for j in range(1, B):
            push(p, h, ROW + 2 * (j - 1) + h, rows[j - 1], True)
    for h in (1, 0):
        push(p, h, COL + h, col, True)
    for h in range(2):
        push(p, h, per + OWN + h, other, True)

    def from_row(j, h):
        q = a * B + (b - j) % B
        came(q, h, ROW + 2 * (j - 1) + h, c)
        push(q, h, per + ROW + 2 * (j - 1) + h, other)
        return q

    def from_col(h):
        q = (1 - a) * B + b
        came(q, h, COL + h, c)
        push(q, h, per + COL + h, other)
        return q

    for j in range(1, B):
        q = from_row(j, 0)
        push(q, 0, VIA_COL + j - 1, col)
    q = from_col(1)
    for j in range(1, B):
        push(q, 1, VIA_ROW + j - 1, rows[j - 1])
    for j in range(1, B):
        from_row(j, 1)
    from_col(0)
    for j in range(1, B):
        q = (1 - a) * B + (b - j) % B
        came(q, 0, VIA_COL + j - 1, c)
        push(q, 0, per + VIA_COL + j - 1, other)
        came(q, 1, VIA_ROW + j - 1, c)
        push(q, 1, per + VIA_ROW + j - 1, other)
    for h in range(2):
        came(p, h, per + OWN + h, 1 - c)
        came((1 - a) * B + b, h, per + COL + h, 1 - c)
    for j in range(1, B):
        for h in range(2):
            came(a * B + (b - j) % B, h, per + ROW + 2 * (j - 1) + h, 1 - c)
        q = (1 - a) * B + (b - j) % B
        came(q, 0, per + VIA_COL + j - 1, 1 - c)
        came(q, 1, per + VIA_ROW + j - 1, 1 - c)
    for copy in started:
        copy.wait_send()


def gather(S, C, T, number, x, riders=()):
    n, D = x.shape
    half = n // 2

    def kernel(ride, ins, outs, scratch):
        (x_ref,), (out_ref,), (send, recv, own) = ins, outs, scratch
        p, _, c = here()
        _, _, rows, col = plane(S)
        local = pltpu.make_async_copy(x_ref, out_ref.at[p * T + c], own)
        local.start()
        greet(S, C, rows + [col], other=True, axes=ride.axes)
        ride.start()
        spread(
            S,
            lambda h: x_ref.at[pl.ds(h * half, half)],
            lambda q, h, core: out_ref.at[q * T + core, pl.ds(h * half, half)],
            send,
            recv,
        )
        local.wait()
        ride.wait()

    out, *rest = comm(
        kernel, S, C, number, "gather", [x], [IN_VMEM],
        [(jax.ShapeDtypeStruct((S * T, n, D), x.dtype), ANY)], spread_sems(S) + [DMA], riders,
    )
    return [out.reshape(S * T * n, D)] + rest


def gather_columns(S, C, T, number, x, riders=()):
    _, n, wide = x.shape

    def kernel(ride, ins, outs, scratch):
        (x_ref,), (out_ref,), (send, recv, own) = ins, outs, scratch
        p, _, c = here()
        _, _, rows, col = plane(S)

        def region(q, h, core):
            part = pl.ds(pl.multiple_of(q * wide, 128), wide)
            return out_ref.at[pl.ds(h * (C // 2), C // 2), core, :, part]

        local = [
            pltpu.make_async_copy(x_ref.at[pl.ds(h * (C // 2), C // 2)], region(p, h, c), own.at[h]) for h in range(2)
        ]
        for copy in local:
            copy.start()
        greet(S, C, rows + [col], other=True, axes=ride.axes)
        ride.start()
        spread(S, lambda h: x_ref.at[pl.ds(h * (C // 2), C // 2)], region, send, recv)
        for copy in local:
            copy.wait()
        ride.wait()

    out, *rest = comm(
        kernel, S, C, number, "gather_columns", [x], [IN_VMEM],
        [(jax.ShapeDtypeStruct((C, T, n, wide * S), x.dtype), ANY)], spread_sems(S) + [DMA((2,))], riders,
    )
    return [out.reshape(C * T * n, wide * S)] + rest


def enter(S, C, T, number, x, riders=()):
    _, n, wide = x.shape

    def kernel(ride, ins, outs, scratch):
        (x_ref,), (out_ref,) = ins, outs
        buf, s1, r1, s2, r2, own, send, recv = scratch
        p, z, c = here()
        mates = [(p + k) % S for k in range(1, S)]
        line = [(z + k) % C for k in range(1, C)]
        greet(S, C, mates, line=True, other=True, axes=ride.axes)

        def part(q):
            return pl.ds(pl.multiple_of(q * wide, 128), wide)

        hop = [pltpu.make_async_copy(x_ref.at[p], buf.at[p], own.at[0])]
        for k, q in enumerate(mates):
            hop.append(remote(x_ref.at[q], buf.at[p], s1.at[k], r1.at[k], {"shard": q}))
        for copy in hop:
            copy.start()
        ride.start()
        for copy in hop:
            copy.wait()
        hop = [pltpu.make_async_copy(buf.at[z], out_ref.at[z, c, :, part(p)], own.at[1])]
        for k, g in enumerate(line):
            hop.append(remote(buf.at[g], out_ref.at[z, c, :, part(p)], s2.at[k], r2.at[k], {"ctx": g}))
        for copy in hop:
            copy.start()
        for copy in hop:
            copy.wait()

        def region(q, h, core):
            return out_ref.at[pl.ds(h * (C // 2), C // 2), core, :, part(q)]

        spread(S, lambda h: region(p, h, c), region, send, recv)
        ride.wait()

    out, *rest = comm(
        kernel, S, C, number, "enter", [x], [IN_VMEM],
        [(jax.ShapeDtypeStruct((C, T, n, wide * S), x.dtype), ANY)],
        [pltpu.VMEM((S, n, wide), BF), DMA((S - 1,)), DMA((S - 1,)), DMA((C - 1,)), DMA((C - 1,)), DMA((2,))]
        + spread_sems(S),
        riders,
    )
    return [out.reshape(C * T * n, wide * S)] + rest


def leave(S, C, T, number, x, riders=()):
    _, n, wide = x.shape

    def kernel(ride, ins, outs, scratch):
        (x_ref,), (out_ref,) = ins, outs
        buf, buf2, s1, r1, s2, r2, s3, r3, s4, r4, own = scratch
        p, z, c = here()
        mates = [(p + k) % S for k in range(1, S)]
        line = [(z + k) % C for k in range(1, C)]
        other = {"tp": 1 - c}
        greet(S, C, mates, line=True, other=True, axes=ride.axes)

        def turn_over(source, target, send, recv, local, me, axis, peers):
            hop = [pltpu.make_async_copy(source(me), target, local)]
            for k, q in enumerate(peers):
                hop.append(remote(source(q), target, send.at[k], recv.at[k], {axis: q}))
            for copy in hop:
                copy.start()
            return hop

        first = turn_over(lambda q: x_ref.at[q], buf.at[p], s1, r1, own.at[0], p, "shard", mates)
        ride.start()
        for copy in first:
            copy.wait()
        for copy in turn_over(lambda q: buf.at[q], buf2.at[z], s2, r2, own.at[1], z, "ctx", line):
            copy.wait()
        part = pl.ds(pl.multiple_of(p * wide, 128), wide)
        for copy in turn_over(lambda q: buf2.at[q], out_ref.at[c, :, part], s3, r3, own.at[2], p, "shard", mates):
            copy.wait()
        copy = remote(out_ref.at[c], out_ref.at[c], s4, r4, other)
        copy.start()
        copy.wait_send()
        remote(out_ref.at[1 - c], out_ref.at[1 - c], s4, r4, other).wait_recv()
        ride.wait()

    out, *rest = comm(
        kernel, S, C, number, "leave", [x], [IN_VMEM],
        [(jax.ShapeDtypeStruct((T, n, wide * S), x.dtype), ANY)],
        [
            pltpu.VMEM((S, n, wide), BF), pltpu.VMEM((C, n, wide), BF),
            DMA((S - 1,)), DMA((S - 1,)), DMA((C - 1,)), DMA((C - 1,)), DMA((S - 1,)), DMA((S - 1,)),
            DMA, DMA, DMA((3,)),
        ],
        riders,
    )
    return [out.reshape(T * n, wide * S)] + rest


CHUNK = 512


def scatter(S, C, T, number, x, w, riders=()):
    L, K = x.shape
    D = w.shape[0]
    n, B = L // (S * T), S // 2
    half = n // 2
    steps = D // CHUNK

    def kernel(ride, ins, outs, scratch):
        (x_ref, w_ref), (out_ref,) = ins, outs
        away, sib, mine, row1, col1, row2, col2, to_col, to_row = scratch[:9]
        asend, arecv, rsend, rrecv, csend, crecv, fsend, frecv = scratch[9:]
        p, _, c = here()
        a, b, rows, col = plane(S)
        greet(S, C, rows + [col], other=True, axes=ride.axes)
        rows, col, other = [{"shard": q} for q in rows], {"shard": col}, {"tp": 1 - c}
        ride.start()

        def chip(e):
            return ((a + e // B) % 2) * B + (b + e % B) % B

        def product(e, core, store):
            x = x_ref[chip(e) * T + core]

            def column(j, _):
                w = pl.ds(pl.multiple_of(j * CHUNK, CHUNK), CHUNK)
                store(w, mm(x, w_ref[w, :], 1, 1))
                return 0

            lax.fori_loop(0, steps, column, 0)

        def to_other(e):
            return remote(away.at[e], sib.at[e], asend.at[e], arecv.at[e], other)

        def first(i, _):
            e = S - 1 - i

            def store(w, value):
                away[e, :, w] = value.astype(BF)

            product(e, 1 - c, store)
            to_other(e).start()
            return 0

        lax.fori_loop(0, S, first, 0)

        top, low = pl.ds(0, half), pl.ds(half, half)
        started = []

        def push(src, dst, send, recv, where):
            copy = remote(src, dst, send, recv, where)
            copy.start()
            started.append(copy)

        for e in range(S - 1, -1, -1):
            to_other(e).wait()

            def store(w, value):
                value = value + sib[e, :, w].astype(F32)
                if e:
                    mine[e, :, w] = value.astype(BF)
                else:
                    out_ref[:, w] = value

            product(e, c, store)
            j = e % B
            if e > B:
                push(mine.at[e, top], row1.at[j - 1, 1], rsend.at[j - 1, 1], rrecv.at[j - 1, 1], rows[j - 1])
                push(mine.at[e, low], col1.at[j], csend.at[j], crecv.at[j], col)
            elif e == B:
                push(mine.at[e, low], col1.at[0], csend.at[0], crecv.at[0], col)
            elif e:
                push(mine.at[e, top], row1.at[j - 1, 0], rsend.at[j - 1, 0], rrecv.at[j - 1, 0], rows[j - 1])

        def came(ref, send, recv):
            remote(ref, ref, send, recv, other).wait_recv()

        total = mine[B, top, :].astype(F32)
        for j in range(1, B):
            came(row1.at[j - 1, 1], rsend.at[j - 1, 1], rrecv.at[j - 1, 1])
            total = total + row1[j - 1, 1].astype(F32)
        to_col[...] = total.astype(BF)
        push(to_col, col2, fsend.at[0], frecv.at[0], col)
        for j in range(1, B):
            came(col1.at[j], csend.at[j], crecv.at[j])
            to_row[j - 1] = (mine[j, low, :].astype(F32) + col1[j].astype(F32)).astype(BF)
            push(to_row.at[j - 1], row2.at[j - 1], fsend.at[j], frecv.at[j], rows[j - 1])
        came(col1.at[0], csend.at[0], crecv.at[0])
        upper, lower = out_ref[top, :], out_ref[low, :] + col1[0].astype(F32)
        for j in range(1, B):
            came(row1.at[j - 1, 0], rsend.at[j - 1, 0], rrecv.at[j - 1, 0])
            upper = upper + row1[j - 1, 0].astype(F32)
        came(col2, fsend.at[0], frecv.at[0])
        out_ref[top, :] = upper + col2[...].astype(F32)
        for j in range(1, B):
            came(row2.at[j - 1], fsend.at[j], frecv.at[j])
            lower = lower + row2[j - 1].astype(F32)
        out_ref[low, :] = lower
        for copy in started:
            copy.wait_send()
        ride.wait()

    def vm(*shape):
        return pltpu.VMEM(shape, BF)

    return comm(
        kernel, S, C, number, "scatter", [x.reshape(S * T, n, K), w], [IN_VMEM, IN_VMEM],
        [(jax.ShapeDtypeStruct((n, D), F32), IN_VMEM)],
        [
            vm(S, n, D), vm(S, n, D), vm(S, n, D), vm(B - 1, 2, half, D), vm(B, half, D),
            vm(B - 1, half, D), vm(half, D), vm(half, D), vm(B - 1, half, D),
            DMA((S,)), DMA((S,)), DMA((B - 1, 2)), DMA((B - 1, 2)), DMA((B,)), DMA((B,)), DMA((B,)), DMA((B,)),
        ],
        riders,
    )


def turn_tables(rows):
    feature = np.arange(128) % HEAD
    freq = np.where(feature < ROT, BASE ** (-2.0 * (feature % (ROT // 2)) / ROT), 0.0)
    near = np.arange(BLK)[:, None] * freq
    far = np.arange(0, rows, BLK)[:, None] * freq
    return [jnp.asarray(f(x), F32) for x in (near, far) for f in (np.cos, np.sin)]


def turn(x, i, tables, sign):
    cos, sin, cos_far, sin_far = tables
    far_cos, far_sin = cos_far[pl.ds(i, 1), :], sin_far[pl.ds(i, 1), :]
    cos_t = cos[...] * far_cos - sin[...] * far_sin
    sin_t = sin[...] * far_cos + cos[...] * far_sin
    ahead = lax.broadcasted_iota(jnp.int32, x.shape, 1) % HEAD < ROT // 2
    partner = jnp.where(ahead, -pltpu.roll(x, 128 - ROT // 2, 1), pltpu.roll(x, ROT // 2, 1))
    return x * cos_t + partner * (sin_t * sign)


def attend_kernel(
    first_ref, q_ref, k_ref, v_ref, cos_ref, sin_ref, cosf_ref, sinf_ref, begin_ref,
    qo_ref, ko_ref, vo_ref, o_ref, lse_ref, vt_ref,
):
    rows = q_ref.shape[0]
    nb = rows // BLK
    tables = (cos_ref, sin_ref, cosf_ref, sinf_ref)
    lane = lax.broadcasted_iota(jnp.int32, (BLK, 128), 1)
    left = lane < HEAD
    key_at = lax.broadcasted_iota(jnp.int32, (BLK, BLK), 0)
    query_at = lax.broadcasted_iota(jnp.int32, (1, BLK), 1)

    @pl.loop(0, nb)
    def _(i):
        r = pl.ds(pl.multiple_of(i * BLK, BLK), BLK)
        qo_ref[r, :] = turn(q_ref[r, :], i, tables, 1.0).astype(BF) * jnp.asarray(HEAD**-0.5, BF)
        ko_ref[r, :] = turn(k_ref[r, :], i, tables, 1.0).astype(BF)
        v = v_ref[r, :]
        vo_ref[r, :] = v.astype(BF)
        vt_ref[:, r] = v.T.astype(BF)

    @pl.loop(0, nb)
    def _(i):
        r = pl.ds(pl.multiple_of(i * BLK, BLK), BLK)
        q = qo_ref[r, :]
        zero = jnp.zeros_like(q)
        qs = (jnp.where(left, q, zero), jnp.where(left, zero, q))
        begin = begin_ref[0:1, r]
        here = query_at + i * BLK

        def step(j, carry):
            w = pl.ds(pl.multiple_of(j * BLK, BLK), BLK)
            k, vt = ko_ref[w, :], vt_ref[:, w]
            key = key_at + j * BLK
            seen = (key <= here) & (key >= begin)
            out = []
            for h in range(2):
                m, l, acc = carry[h]
                s = jnp.where(seen, mm(k, qs[h], 1, 1), NEG)
                top = jnp.maximum(m, jnp.max(s, axis=0, keepdims=True))
                fade = jnp.exp(m - top)
                e = jnp.exp(s - top)
                out.append(
                    (top, l * fade + jnp.sum(e, axis=0, keepdims=True), acc * fade + mm(vt, e.astype(BF), 1, 0))
                )
            return tuple(out)

        start = (
            jnp.full((1, BLK), NEG, F32), jnp.zeros((1, BLK), F32), jnp.zeros((128, BLK), F32)
        )
        done = lax.fori_loop(first_ref[i], i + 1, step, (start, start))
        parts = []
        for h in range(2):
            m, l, acc = done[h]
            parts.append((acc / l).T)
            lse_ref[0, h : h + 1, r] = m + jnp.log(l)
        o_ref[r, :] = jnp.where(left, parts[0], parts[1]).astype(BF)


def whole(x):
    return pl.BlockSpec(x.shape, lambda j, *_: (0, 0))


def attend(qkv, begin, first):
    rows, wide = qkv.shape
    pairs = wide // 3 // 128
    tables = turn_tables(rows)

    def col(base):
        return pl.BlockSpec((rows, 128), lambda j, *_: (0, base + j))

    half = jax.ShapeDtypeStruct((rows, wide // 3), BF)
    return pl.pallas_call(
        attend_kernel,
        grid_spec=pltpu.PrefetchScalarGridSpec(
            num_scalar_prefetch=1,
            grid=(pairs,),
            in_specs=[
                col(0), col(pairs), col(2 * pairs), *map(whole, tables), whole(begin),
            ],
            out_specs=[col(0)] * 4 + [pl.BlockSpec((1, 2, rows), lambda j, *_: (j, 0, 0))],
            scratch_shapes=[pltpu.VMEM((128, rows), BF)],
        ),
        out_shape=[half] * 4 + [jax.ShapeDtypeStruct((pairs, 2, rows), F32)],
        compiler_params=pltpu.CompilerParams(vmem_limit_bytes=48 << 20),
        cost_estimate=pl.CostEstimate(
            flops=0, bytes_accessed=27 * 3_000_000, transcendentals=0
        ),
        name="attend",
    )(first, qkv, qkv, qkv, *tables, begin)


def attend_back_kernel(
    first_ref, q_ref, k_ref, v_ref, o_ref, do_ref, lse_ref, cos_ref, sin_ref, cosf_ref, sinf_ref, begin_ref,
    out_ref, kt_ref, dk_ref, dv_ref,
):
    rows = q_ref.shape[0]
    nb = rows // BLK
    tables = (cos_ref, sin_ref, cosf_ref, sinf_ref)
    pair, pairs = pl.program_id(0), pl.num_programs(0)
    lane = lax.broadcasted_iota(jnp.int32, (BLK, 128), 1)
    left = lane < HEAD
    key_at = lax.broadcasted_iota(jnp.int32, (BLK, BLK), 0)
    query_at = lax.broadcasted_iota(jnp.int32, (1, BLK), 1)

    def column(base):
        return pl.ds(pl.multiple_of((base * pairs + pair) * 128, 128), 128)

    @pl.loop(0, nb)
    def _(i):
        r = pl.ds(pl.multiple_of(i * BLK, BLK), BLK)
        kt_ref[:, r] = k_ref[r, :].astype(F32).T.astype(BF)
        dk_ref[r, :] = jnp.zeros((BLK, 128), F32)
        dv_ref[r, :] = jnp.zeros((BLK, 128), F32)

    @pl.loop(0, nb)
    def _(i):
        r = pl.ds(pl.multiple_of(i * BLK, BLK), BLK)
        q, do = q_ref[r, :], do_ref[r, :]
        zero = jnp.zeros_like(q)
        qs = (jnp.where(left, q, zero), jnp.where(left, zero, q))
        dos = (jnp.where(left, do, zero), jnp.where(left, zero, do))
        prod = (do.astype(F32) * o_ref[r, :].astype(F32)).T
        deltas = (
            jnp.sum(prod[:HEAD], axis=0, keepdims=True), jnp.sum(prod[HEAD:], axis=0, keepdims=True)
        )
        lses = (lse_ref[0, 0:1, r], lse_ref[0, 1:2, r])
        begin = begin_ref[0:1, r]
        here = query_at + i * BLK

        def step(j, carry):
            w = pl.ds(pl.multiple_of(j * BLK, BLK), BLK)
            k, v, kt = k_ref[w, :], v_ref[w, :], kt_ref[:, w]
            key = key_at + j * BLK
            seen = (key <= here) & (key >= begin)
            out = []
            dk = dv = None
            for h in range(2):
                prob = jnp.exp(jnp.where(seen, mm(k, qs[h], 1, 1) - lses[h], NEG))
                ds = (prob * (mm(v, dos[h], 1, 1) - deltas[h])).astype(BF)
                out.append(carry[h] + mm(kt, ds, 1, 0))
                dk_h, dv_h = mm(ds, qs[h], 1, 0), mm(prob.astype(BF), dos[h], 1, 0)
                dk, dv = (dk_h, dv_h) if h == 0 else (dk + dk_h, dv + dv_h)
            dk_ref[w, :] += dk
            dv_ref[w, :] += dv
            return tuple(out)

        start = jnp.zeros((128, BLK), F32)
        a, b = lax.fori_loop(first_ref[i], i + 1, step, (start, start))
        dq = jnp.where(left, a.T, b.T) * (HEAD**-0.5)
        out_ref[r, column(0)] = turn(dq, i, tables, -1.0).astype(BF)

    @pl.loop(0, nb)
    def _(i):
        r = pl.ds(pl.multiple_of(i * BLK, BLK), BLK)
        out_ref[r, column(1)] = turn(dk_ref[r, :], i, tables, -1.0).astype(BF)
        out_ref[r, column(2)] = dv_ref[r, :].astype(BF)


def attend_back(q, k, v, o, do, lse, begin, first):
    rows, wide = q.shape
    pairs = wide // 128
    tables = turn_tables(rows)
    col = pl.BlockSpec((rows, 128), lambda j, *_: (0, j))
    return pl.pallas_call(
        attend_back_kernel,
        grid_spec=pltpu.PrefetchScalarGridSpec(
            num_scalar_prefetch=1,
            grid=(pairs,),
            in_specs=[
                col, col, col, col, col, pl.BlockSpec((1, 2, rows), lambda j, *_: (j, 0, 0)),
                *map(whole, tables), whole(begin),
            ],
            out_specs=pl.BlockSpec((rows, 3 * wide), lambda j, *_: (0, 0)),
            scratch_shapes=[
                pltpu.VMEM((128, rows), BF), pltpu.VMEM((rows, 128), F32), pltpu.VMEM((rows, 128), F32)
            ],
        ),
        out_shape=jax.ShapeDtypeStruct((rows, 3 * wide), BF),
        compiler_params=pltpu.CompilerParams(vmem_limit_bytes=48 << 20),
        cost_estimate=pl.CostEstimate(
            flops=0, bytes_accessed=32 * 3_000_000, transcendentals=0
        ),
        name="attend_back",
    )(first, q, k, v, o, do, lse, *tables, begin)


def doc_begins(lengths_row, rows):
    row_ids = jnp.arange(rows, dtype=jnp.int32)
    ends = jnp.cumsum(lengths_row, dtype=jnp.int32)
    begins = ends - lengths_row
    inside = (row_ids[:, None] >= begins[None, :]) & (row_ids[:, None] < ends[None, :])
    return jnp.sum(jnp.where(inside, begins[None, :], 0), axis=1, dtype=jnp.int32)


def layer_norm(values, gain, shift):
    center = values - jnp.mean(values, axis=-1, keepdims=True)
    inverse = lax.rsqrt(jnp.mean(center * center, axis=-1, keepdims=True) + EPS)
    normal = center * inverse
    return (normal * gain + shift, normal, inverse)


def norm_back(gradient, normal, inverse, gain):
    scaled = gradient * gain
    centered = (
        scaled
        - jnp.mean(scaled, axis=-1, keepdims=True)
        - normal * jnp.mean(scaled * normal, axis=-1, keepdims=True)
    )
    return (inverse * centered, jnp.sum(gradient * normal, axis=0), jnp.sum(gradient, axis=0))


def tiles_of(parts, lead):
    flat = jnp.concatenate([x.astype(F32).reshape(lead + (-1,)) for x in parts], axis=-1)
    flat = jnp.pad(flat, ((0, 0),) * len(lead) + ((0, 1024 - flat.shape[-1]),))
    return flat.reshape(lead + (8, 128))


def make_body(S, C, T):
    assert S == C

    def body(tokens, lengths, w_qkv, b_qkv, w_out, w_gateup, w_down, norm_gain, norm_bias, cotangent):
        p, z, c = lax.axis_index("shard"), lax.axis_index("ctx"), lax.axis_index("tp")
        R, D = tokens.shape
        n = R // T
        nb = D // (S * C)
        L = R * C

        def to_parts(x):
            return x.reshape(n, S, C, nb).transpose(2, 0, 1, 3).reshape(S, n, D // S)

        def parts(x):
            return x.reshape(n, S, D // S).swapaxes(0, 1)

        def unpermute(x):
            return x.reshape(x.shape[0], C, S, nb).swapaxes(1, 2).reshape(x.shape)

        def own(x):
            return lax.dynamic_slice_in_dim(x, (p * T + c) * n, n, 0)

        def half_of(x):
            return lax.dynamic_slice_in_dim(x, c * n, n, 0)

        def after(x, y):
            return lax.optimization_barrier((x, y))

        def over_ctx(w):
            return lax.all_gather(w.reshape(S * nb, -1), "ctx", axis=0, tiled=True)

        def sum_ctx(g):
            g = lax.psum_scatter(g.astype(BF), "ctx", scatter_dimension=0, tiled=True)
            return g.reshape(S, nb, -1)

        hn = w_qkv.shape[3] // S
        fn = w_gateup.shape[3] // S
        heads = hn // HEAD
        nf = HEAD // (S * C)

        tile = tiles_of((norm_gain[0].reshape(-1), norm_bias[0].reshape(-1), b_qkv[0].reshape(-1), lengths[0]), ())
        small, wq, cot = exchange(
            S, C, T, 0,
            [
                ("shard", w_qkv[0].reshape(nb, 3, S, hn).transpose(2, 0, 1, 3).reshape(S, nb, 3 * hn)),
                ("shard", to_parts(half_of(cotangent))),
            ],
            jnp.broadcast_to(tile, (C, S, 8, 128)),
        )
        wq = over_ctx(wq)
        tok, cot, wo, wg, wd = enter(
            S, C, T, 1, to_parts(half_of(tokens)),
            [
                ("ctx", cot),
                ("shard", w_out[0].reshape(S, hn, nb).swapaxes(1, 2)),
                ("shard", w_gateup[0].reshape(nb, 2, S, fn).transpose(2, 0, 1, 3).reshape(S, nb, 2 * fn)),
                ("shard", w_down[0].reshape(S, fn, nb).swapaxes(1, 2)),
            ],
        )
        wo, wg, wd = over_ctx(wo), over_ctx(wg), over_ctx(wd)

        small = lax.dynamic_index_in_dim(small, c, 0, keepdims=False).reshape(C, S, 1024)
        norms = small[:, :, : 4 * nb].reshape(C * S, 4, nb).swapaxes(0, 1).reshape(4, D)
        gains, shifts = norms[:2], norms[2:]
        nbias = 3 * S * heads * nf
        bias = small[:, :, 4 * nb : 4 * nb + nbias].reshape(C, S, 3, S * heads, nf)
        bias = lax.dynamic_slice_in_dim(bias, p * heads, heads, 3)
        bias = bias.transpose(2, 3, 1, 0, 4).reshape(1, 3 * hn)
        docs = lengths.shape[1]
        lengths_row = lax.dynamic_index_in_dim(
            small[0, :, 4 * nb + nbias : 4 * nb + nbias + docs], z, 0, keepdims=False
        ).astype(jnp.int32)
        begin = doc_begins(lengths_row, L)
        first = begin[::BLK] // BLK
        begin = begin[None, :]

        n1 = layer_norm(tok.astype(F32), gains[0], shifts[0])[0].astype(BF)
        hidden = own(tok).astype(F32)
        _, normal1, inverse1 = layer_norm(hidden, gains[0], shifts[0])
        qkv = mm(n1, wq, 1, 0) + bias
        q, k, v, o, lse = attend(qkv, begin, first)
        (got,) = scatter(S, C, T, 2, o, wo)
        mid = hidden + got
        n2, normal2, inverse2 = layer_norm(mid, gains[1], shifts[1])
        (n2,) = gather(S, C, T, 3, n2.astype(BF))
        cot, n2 = after(cot, n2)
        (gb,) = gather_columns(S, C, T, 4, cot)
        gu = mm(n2, wg, 1, 0)
        gate, up = gu[:, :fn], gu[:, fn:]
        logistic = jax.nn.sigmoid(gate)
        act = (gate * logistic * up).astype(BF)
        gw_down = mm(gb, act, 0, 0).astype(BF)
        wd, gw_down = after(wd, gw_down)
        gw_down = sum_ctx(gw_down)

        dact = mm(gb, wd, 1, 0)
        dgate = dact * up * logistic * (1.0 + gate * (1.0 - logistic))
        dup = dact * gate * logistic
        dgu = jnp.concatenate((dgate, dup), axis=1).astype(BF)
        gw_gateup = mm(n2, dgu, 0, 0).astype(BF)
        act, gw_gateup = after(act, gw_gateup)
        gw_gateup = sum_ctx(gw_gateup)
        (got,) = scatter(S, C, T, 5, act, wd)
        out = parts((mid + got).astype(BF))
        dgu, out = after(dgu, out)
        got, out = scatter(S, C, T, 6, dgu, wg, [("shard", out)])
        dmid, gain2, shift2 = norm_back(got, normal2, inverse2, gains[1])
        dmid = own(gb).astype(F32) + dmid
        gb1, out = gather(S, C, T, 7, dmid.astype(BF), [("ctx", out)])
        gw_out = mm(gb1, o, 0, 0).astype(BF)
        gb1, gw_out = after(gb1, gw_out)
        gw_out = sum_ctx(gw_out)
        do = mm(gb1, wo, 1, 0).astype(BF)
        dqkv = attend_back(q, k, v, o, do, lse, begin, first)
        dqkv, gw_gateup = after(dqkv, gw_gateup)
        gw_qkv = mm(n1, dqkv, 0, 0).astype(BF)
        dqkv, gw_qkv = after(dqkv, gw_qkv)
        gw_qkv = sum_ctx(gw_qkv)
        got, out, gw_gateup, gw_down = scatter(
            S, C, T, 8, dqkv, wq, [("shard", out), ("shard", gw_gateup), ("shard", gw_down)]
        )
        dtok, gain1, shift1 = norm_back(got, normal1, inverse1, gains[0])
        gtok, gw_out, mate = leave(
            S, C, T, 9, parts((dmid + dtok).astype(BF)), [("shard", gw_out), ("tp", out)]
        )
        gtok = unpermute(gtok).astype(F32)
        out = jnp.where(c == 0, jnp.stack((out, mate)), jnp.stack((mate, out)))
        out = unpermute(out.transpose(0, 2, 1, 3).reshape(R, D))

        gbias = jnp.sum(dqkv.astype(F32), axis=0)
        tiles = tiles_of(
            (
                jnp.stack((gain1, gain2, shift1, shift2)).reshape(4, C, S, nb).transpose(1, 2, 0, 3),
                gbias.reshape(3, heads, S, C, nf).transpose(3, 2, 0, 1, 4),
            ),
            (C, S),
        )
        small, gw_qkv = exchange(S, C, T, 10, [("shard", gw_qkv)], tiles)
        small = small.reshape(T, C, S, 1024)
        norms = jnp.sum(small[..., : 4 * nb], axis=(0, 1, 2)).reshape(1, 4, nb)
        gbias = lax.dynamic_index_in_dim(small, c, 0, keepdims=False)[..., 4 * nb : 4 * nb + 3 * heads * nf]
        gbias = jnp.sum(gbias, axis=0).reshape(S, 3, heads, nf).swapaxes(0, 1).reshape(b_qkv.shape)

        return (
            out,
            gtok,
            gw_qkv.astype(F32).reshape(S, nb, 3, hn).transpose(1, 2, 0, 3).reshape(w_qkv.shape),
            gbias,
            gw_out.astype(F32).swapaxes(1, 2).reshape(w_out.shape),
            gw_gateup.astype(F32).reshape(S, nb, 2, fn).transpose(1, 2, 0, 3).reshape(w_gateup.shape),
            gw_down.astype(F32).swapaxes(1, 2).reshape(w_down.shape),
            norms[:, :2],
            norms[:, 2:],
        )

    return body


def solution(mesh):
    both = ("shard", "ctx")
    specs = (
        P(None, both, None, "tp"),
        P(None, None, "tp", both),
        P(None, "tp", both),
        P(None, both, None, "tp"),
        P(None, "tp", both),
        P(None, None, both),
        P(None, None, both),
    )
    return jax.shard_map(
        make_body(mesh.shape["shard"], mesh.shape["ctx"], mesh.shape["tp"]),
        mesh=mesh,
        in_specs=(P(both, None), P("shard", None)) + specs + (P(both, None),),
        out_specs=(P(both, None), P(both, None)) + specs,
        check_vma=False,
    )
```

```python
import functools

import jax
import jax.numpy as jnp
import numpy as np
from jax import lax
from jax.experimental import pallas as pl
from jax.experimental.pallas import tpu as pltpu
from jax.sharding import PartitionSpec as P

HEAD = 64
ROT = 16
EPS = 1e-05
NEG = -1e30
BASE = 10000.0
BF = jnp.bfloat16
F32 = jnp.float32
BLK = 256
MESH = pl.DeviceIdType.MESH
DMA = pltpu.SemaphoreType.DMA
ANY = pl.BlockSpec(memory_space=pl.ANY)
IN_VMEM = pl.BlockSpec(memory_space=pltpu.VMEM)


def mm(a, b, ca, cb):
    return lax.dot_general(a, b, (((ca,), (cb,)), ((), ())), preferred_element_type=F32)


def remote(src, dst, send, recv, where):
    return pltpu.make_async_remote_copy(
        src_ref=src, dst_ref=dst, send_sem=send, recv_sem=recv, device_id=where, device_id_type=MESH
    )


def here():
    return lax.axis_index("shard"), lax.axis_index("ctx"), lax.axis_index("tp")


class Riders:
    def __init__(self, S, C, riders):
        self.S, self.C = S, C
        self.axes = [axis for axis, _ in riders]
        self.arrays = [x for _, x in riders]
        self.shapes = [jax.ShapeDtypeStruct(x.shape, x.dtype) for x in self.arrays]
        count, most = len(riders), max(S, C) - 1
        self.scratch = [DMA((count, most)), DMA((count, most)), DMA((count,))] if count else []

    def bind(self, ins, outs, sems):
        self.ins, self.outs, self.sems = ins, outs, sems

    def start(self):
        p, z, c = here()
        self.moves = []
        for n, axis in enumerate(self.axes):
            src, dst = self.ins[n], self.outs[n]
            send, recv, own = self.sems
            if axis == "tp":
                copies = [remote(src, dst, send.at[n, 0], recv.at[n, 0], {"tp": 1 - c})]
            else:
                size, me = (self.S, p) if axis == "shard" else (self.C, z)
                copies = [
                    remote(src.at[(me + k) % size], dst.at[me], send.at[n, k - 1], recv.at[n, k - 1], {axis: (me + k) % size})
                    for k in range(1, size)
                ]
                copies.append(pltpu.make_async_copy(src.at[me], dst.at[me], own.at[n]))
            for copy in copies:
                copy.start()
            self.moves += copies

    def wait(self):
        for copy in self.moves:
            copy.wait()


def greet(S, C, mates=(), line=False, other=False, axes=()):
    p, z, c = here()
    peers = [{"shard": q} for q in ([(p + k) % S for k in range(1, S)] if "shard" in axes else mates)]
    if line or "ctx" in axes:
        peers += [{"ctx": (z + k) % C} for k in range(1, C)]
    if other or "tp" in axes:
        peers.append({"tp": 1 - c})
    barrier = pltpu.get_barrier_semaphore()
    for where in peers:
        pl.semaphore_signal(barrier, inc=1, device_id=where, device_id_type=MESH)
    pl.semaphore_wait(barrier, len(peers))


def comm(kernel, S, C, number, name, args, in_specs, outs, scratch, riders=()):
    ride = Riders(S, C, riders)
    na, nr, no, ns = len(args), len(ride.axes), len(outs), len(scratch)

    def body(*refs):
        ins, refs = refs[:na], refs[na:]
        rins, refs = refs[:nr], refs[nr:]
        os, refs = refs[:no], refs[no:]
        routs, refs = refs[:nr], refs[nr:]
        ride.bind(rins, routs, refs[ns:])
        kernel(ride, ins, os, refs[:ns])

    return pl.pallas_call(
        body,
        out_shape=[shape for shape, _ in outs] + ride.shapes,
        in_specs=list(in_specs) + [IN_VMEM] * nr,
        out_specs=[spec for _, spec in outs] + [ANY] * nr,
        scratch_shapes=list(scratch) + ride.scratch,
        compiler_params=pltpu.CompilerParams(
            collective_id=number, has_side_effects=True, vmem_limit_bytes=56 << 20
        ),
        cost_estimate=pl.CostEstimate(flops=0, bytes_accessed=120_000_000, transcendentals=0),
        name=name,
    )(*args, *ride.arrays)


def exchange(S, C, T, number, riders, tiles, rows=None):
    def kernel(ride, ins, outs, scratch):
        tile, got = ins[0], outs[0]
        send, recv, bsend, brecv, own = scratch[:5]
        p, z, c = here()
        everyone = [(i, j) for i in range(C) for j in range(S) if i or j]
        barrier = pltpu.get_barrier_semaphore()
        peers = [{"shard": (p + j) % S, "ctx": (z + i) % C} for i, j in everyone] + [{"tp": 1 - c}]
        for where in peers:
            pl.semaphore_signal(barrier, inc=1, device_id=where, device_id_type=MESH)
        pl.semaphore_wait(barrier, len(peers))

        def turn_over(source, target, k, axis, size, me):
            ssem, rsem, local = scratch[5:]
            hop = [pltpu.make_async_copy(source.at[me], target.at[me], local.at[k])]
            for j in range(1, size):
                q = (me + j) % size
                hop.append(remote(source.at[q], target.at[me], ssem.at[k, j - 1], rsem.at[k, j - 1], {axis: q}))
            for copy in hop:
                copy.start()
            return hop

        if rows is not None:
            first = turn_over(ins[1], outs[1], 0, "shard", S, p)
        local = pltpu.make_async_copy(tile.at[z, p], got.at[c, z, p], own)
        local.start()
        copies = []
        for at, (where, (i, j)) in enumerate(zip(peers, everyone)):
            q, g = (p + j) % S, (z + i) % C
            copies.append(remote(tile.at[g, q], got.at[c, z, p], send.at[at], recv.at[at], where))
            copies[-1].start()
        ride.start()
        if rows is not None:
            for copy in first:
                copy.wait()
            second = turn_over(outs[1], outs[2], 1, "ctx", C, z)
        local.wait()
        for copy in copies:
            copy.wait()
        back = remote(got.at[c], got.at[c], bsend, brecv, {"tp": 1 - c})
        back.start()
        back.wait_send()
        remote(got.at[1 - c], got.at[1 - c], bsend, brecv, {"tp": 1 - c}).wait_recv()
        if rows is not None:
            for copy in second:
                copy.wait()
        ride.wait()

    count, most = C * S - 1, max(S, C) - 1
    args, outs = [tiles], [(jax.ShapeDtypeStruct((T,) + tiles.shape, tiles.dtype), ANY)]
    scratch = [DMA((count,)), DMA((count,)), DMA, DMA, DMA]
    if rows is not None:
        args.append(rows)
        outs += [(jax.ShapeDtypeStruct(rows.shape, rows.dtype), IN_VMEM)] * 2
        scratch += [DMA((2, most)), DMA((2, most)), DMA((2,))]
    return comm(kernel, S, C, number, "exchange", args, [IN_VMEM] * len(args), outs, scratch, riders)


def plane(S):
    p, _, c = here()
    B = S // 2
    a, b = p // B, p % B
    return a, b, [a * B + (b + j) % B for j in range(1, B)], (1 - a) * B + b


def spread_sems(S):
    count = 4 + 4 * (S // 2 - 1)
    return [DMA((2 * count,)), DMA((2 * count,))]


def spread(S, own, region, send, recv):
    p, _, c = here()
    B = S // 2
    a, b, rows, col = plane(S)
    rows, col, other = [{"shard": q} for q in rows], {"shard": col}, {"tp": 1 - c}
    per = 4 + 4 * (B - 1)
    OWN, ROW, COL, VIA_COL, VIA_ROW = 0, 2, 2 + 2 * (B - 1), 4 + 2 * (B - 1), 4 + 3 * (B - 1)
    started = []

    def push(q, h, sem, where, first=False):
        view = region(q, h, c)
        copy = remote(own(h) if first else view, view, send.at[sem], recv.at[sem], where)
        copy.start()
        started.append(copy)

    def came(q, h, sem, core):
        view = region(q, h, core)
        remote(view, view, send.at[sem], recv.at[sem], other).wait_recv()

    for h in range(2):
        for j in range(1, B):
            push(p, h, ROW + 2 * (j - 1) + h, rows[j - 1], True)
    for h in (1, 0):
        push(p, h, COL + h, col, True)
    for h in range(2):
        push(p, h, per + OWN + h, other, True)

    def from_row(j, h):
        q = a * B + (b - j) % B
        came(q, h, ROW + 2 * (j - 1) + h, c)
        push(q, h, per + ROW + 2 * (j - 1) + h, other)
        return q

    def from_col(h):
        q = (1 - a) * B + b
        came(q, h, COL + h, c)
        push(q, h, per + COL + h, other)
        return q

    for j in range(1, B):
        q = from_row(j, 0)
        push(q, 0, VIA_COL + j - 1, col)
    q = from_col(1)
    for j in range(1, B):
        push(q, 1, VIA_ROW + j - 1, rows[j - 1])
    for j in range(1, B):
        from_row(j, 1)
    from_col(0)
    for j in range(1, B):
        q = (1 - a) * B + (b - j) % B
        came(q, 0, VIA_COL + j - 1, c)
        push(q, 0, per + VIA_COL + j - 1, other)
        came(q, 1, VIA_ROW + j - 1, c)
        push(q, 1, per + VIA_ROW + j - 1, other)
    for h in range(2):
        came(p, h, per + OWN + h, 1 - c)
        came((1 - a) * B + b, h, per + COL + h, 1 - c)
    for j in range(1, B):
        for h in range(2):
            came(a * B + (b - j) % B, h, per + ROW + 2 * (j - 1) + h, 1 - c)
        q = (1 - a) * B + (b - j) % B
        came(q, 0, per + VIA_COL + j - 1, 1 - c)
        came(q, 1, per + VIA_ROW + j - 1, 1 - c)
    for copy in started:
        copy.wait_send()


def gather(S, C, T, number, x, riders=()):
    n, D = x.shape
    half = n // 2

    def kernel(ride, ins, outs, scratch):
        (x_ref,), (out_ref,), (send, recv, own) = ins, outs, scratch
        p, _, c = here()
        _, _, rows, col = plane(S)
        local = pltpu.make_async_copy(x_ref, out_ref.at[p * T + c], own)
        local.start()
        greet(S, C, rows + [col], other=True, axes=ride.axes)
        ride.start()
        spread(
            S,
            lambda h: x_ref.at[pl.ds(h * half, half)],
            lambda q, h, core: out_ref.at[q * T + core, pl.ds(h * half, half)],
            send,
            recv,
        )
        local.wait()
        ride.wait()

    out, *rest = comm(
        kernel, S, C, number, "gather", [x], [IN_VMEM],
        [(jax.ShapeDtypeStruct((S * T, n, D), x.dtype), ANY)], spread_sems(S) + [DMA], riders,
    )
    return [out.reshape(S * T * n, D)] + rest


def gather_columns(S, C, T, number, x, riders=()):
    _, n, wide = x.shape

    def kernel(ride, ins, outs, scratch):
        (x_ref,), (out_ref,), (send, recv, own) = ins, outs, scratch
        p, _, c = here()
        _, _, rows, col = plane(S)

        def region(q, h, core):
            part = pl.ds(pl.multiple_of(q * wide, 128), wide)
            return out_ref.at[pl.ds(h * (C // 2), C // 2), core, :, part]

        local = [
            pltpu.make_async_copy(x_ref.at[pl.ds(h * (C // 2), C // 2)], region(p, h, c), own.at[h]) for h in range(2)
        ]
        for copy in local:
            copy.start()
        greet(S, C, rows + [col], other=True, axes=ride.axes)
        ride.start()
        spread(S, lambda h: x_ref.at[pl.ds(h * (C // 2), C // 2)], region, send, recv)
        for copy in local:
            copy.wait()
        ride.wait()

    out, *rest = comm(
        kernel, S, C, number, "gather_columns", [x], [IN_VMEM],
        [(jax.ShapeDtypeStruct((C, T, n, wide * S), x.dtype), ANY)], spread_sems(S) + [DMA((2,))], riders,
    )
    return [out.reshape(C * T * n, wide * S)] + rest


def leave(S, C, T, number, x, riders=()):
    _, n, wide = x.shape

    def kernel(ride, ins, outs, scratch):
        (x_ref,), (out_ref,) = ins, outs
        buf, buf2, s1, r1, s2, r2, s3, r3, s4, r4, own = scratch
        p, z, c = here()
        mates = [(p + k) % S for k in range(1, S)]
        line = [(z + k) % C for k in range(1, C)]
        other = {"tp": 1 - c}
        greet(S, C, mates, line=True, other=True, axes=ride.axes)

        def turn_over(source, target, send, recv, local, me, axis, peers):
            hop = [pltpu.make_async_copy(source(me), target, local)]
            for k, q in enumerate(peers):
                hop.append(remote(source(q), target, send.at[k], recv.at[k], {axis: q}))
            for copy in hop:
                copy.start()
            return hop

        first = turn_over(lambda q: x_ref.at[q], buf.at[p], s1, r1, own.at[0], p, "shard", mates)
        ride.start()
        for copy in first:
            copy.wait()
        for copy in turn_over(lambda q: buf.at[q], buf2.at[z], s2, r2, own.at[1], z, "ctx", line):
            copy.wait()
        part = pl.ds(pl.multiple_of(p * wide, 128), wide)
        for copy in turn_over(lambda q: buf2.at[q], out_ref.at[c, :, part], s3, r3, own.at[2], p, "shard", mates):
            copy.wait()
        copy = remote(out_ref.at[c], out_ref.at[c], s4, r4, other)
        copy.start()
        copy.wait_send()
        remote(out_ref.at[1 - c], out_ref.at[1 - c], s4, r4, other).wait_recv()
        ride.wait()

    out, *rest = comm(
        kernel, S, C, number, "leave", [x], [IN_VMEM],
        [(jax.ShapeDtypeStruct((T, n, wide * S), x.dtype), ANY)],
        [
            pltpu.VMEM((S, n, wide), BF), pltpu.VMEM((C, n, wide), BF),
            DMA((S - 1,)), DMA((S - 1,)), DMA((C - 1,)), DMA((C - 1,)), DMA((S - 1,)), DMA((S - 1,)),
            DMA, DMA, DMA((3,)),
        ],
        riders,
    )
    return [out.reshape(T * n, wide * S)] + rest


CHUNK = 512


def scatter(S, C, T, number, x, w, riders=()):
    L, K = x.shape
    D = w.shape[0]
    n, B = L // (S * T), S // 2
    half = n // 2
    steps = D // CHUNK

    def kernel(ride, ins, outs, scratch):
        (x_ref, w_ref), (out_ref,) = ins, outs
        away, sib, mine, row1, col1, row2, col2, to_col, to_row = scratch[:9]
        asend, arecv, rsend, rrecv, csend, crecv, fsend, frecv = scratch[9:]
        p, _, c = here()
        a, b, rows, col = plane(S)
        greet(S, C, rows + [col], other=True, axes=ride.axes)
        rows, col, other = [{"shard": q} for q in rows], {"shard": col}, {"tp": 1 - c}
        ride.start()

        def chip(e):
            return ((a + e // B) % 2) * B + (b + e % B) % B

        def product(e, core, store):
            x = x_ref[chip(e) * T + core]

            def column(j, _):
                w = pl.ds(pl.multiple_of(j * CHUNK, CHUNK), CHUNK)
                store(w, mm(x, w_ref[w, :], 1, 1))
                return 0

            lax.fori_loop(0, steps, column, 0)

        def to_other(e):
            return remote(away.at[e], sib.at[e], asend.at[e], arecv.at[e], other)

        def first(i, _):
            e = S - 1 - i

            def store(w, value):
                away[e, :, w] = value.astype(BF)

            product(e, 1 - c, store)
            to_other(e).start()
            return 0

        lax.fori_loop(0, S, first, 0)

        top, low = pl.ds(0, half), pl.ds(half, half)
        started = []

        def push(src, dst, send, recv, where):
            copy = remote(src, dst, send, recv, where)
            copy.start()
            started.append(copy)

        for e in range(S - 1, -1, -1):
            to_other(e).wait()

            def store(w, value):
                value = value + sib[e, :, w].astype(F32)
                if e:
                    mine[e, :, w] = value.astype(BF)
                else:
                    out_ref[:, w] = value

            product(e, c, store)
            j = e % B
            if e > B:
                push(mine.at[e, top], row1.at[j - 1, 1], rsend.at[j - 1, 1], rrecv.at[j - 1, 1], rows[j - 1])
                push(mine.at[e, low], col1.at[j], csend.at[j], crecv.at[j], col)
            elif e == B:
                push(mine.at[e, low], col1.at[0], csend.at[0], crecv.at[0], col)
            elif e:
                push(mine.at[e, top], row1.at[j - 1, 0], rsend.at[j - 1, 0], rrecv.at[j - 1, 0], rows[j - 1])

        def came(ref, send, recv):
            remote(ref, ref, send, recv, other).wait_recv()

        total = mine[B, top, :].astype(F32)
        for j in range(1, B):
            came(row1.at[j - 1, 1], rsend.at[j - 1, 1], rrecv.at[j - 1, 1])
            total = total + row1[j - 1, 1].astype(F32)
        to_col[...] = total.astype(BF)
        push(to_col, col2, fsend.at[0], frecv.at[0], col)
        for j in range(1, B):
            came(col1.at[j], csend.at[j], crecv.at[j])
            to_row[j - 1] = (mine[j, low, :].astype(F32) + col1[j].astype(F32)).astype(BF)
            push(to_row.at[j - 1], row2.at[j - 1], fsend.at[j], frecv.at[j], rows[j - 1])
        came(col1.at[0], csend.at[0], crecv.at[0])
        upper, lower = out_ref[top, :], out_ref[low, :] + col1[0].astype(F32)
        for j in range(1, B):
            came(row1.at[j - 1, 0], rsend.at[j - 1, 0], rrecv.at[j - 1, 0])
            upper = upper + row1[j - 1, 0].astype(F32)
        came(col2, fsend.at[0], frecv.at[0])
        out_ref[top, :] = upper + col2[...].astype(F32)
        for j in range(1, B):
            came(row2.at[j - 1], fsend.at[j], frecv.at[j])
            lower = lower + row2[j - 1].astype(F32)
        out_ref[low, :] = lower
        for copy in started:
            copy.wait_send()
        ride.wait()

    def vm(*shape):
        return pltpu.VMEM(shape, BF)

    return comm(
        kernel, S, C, number, "scatter", [x.reshape(S * T, n, K), w], [IN_VMEM, IN_VMEM],
        [(jax.ShapeDtypeStruct((n, D), F32), IN_VMEM)],
        [
            vm(S, n, D), vm(S, n, D), vm(S, n, D), vm(B - 1, 2, half, D), vm(B, half, D),
            vm(B - 1, half, D), vm(half, D), vm(half, D), vm(B - 1, half, D),
            DMA((S,)), DMA((S,)), DMA((B - 1, 2)), DMA((B - 1, 2)), DMA((B,)), DMA((B,)), DMA((B,)), DMA((B,)),
        ],
        riders,
    )


def turn_tables(rows):
    feature = np.arange(128) % HEAD
    freq = np.where(feature < ROT, BASE ** (-2.0 * (feature % (ROT // 2)) / ROT), 0.0)
    near = np.arange(BLK)[:, None] * freq
    far = np.arange(0, rows, BLK)[:, None] * freq
    return [jnp.asarray(f(x), F32) for x in (near, far) for f in (np.cos, np.sin)]


def turn(x, i, tables, sign):
    cos, sin, cos_far, sin_far = tables
    far_cos, far_sin = cos_far[pl.ds(i, 1), :], sin_far[pl.ds(i, 1), :]
    cos_t = cos[...] * far_cos - sin[...] * far_sin
    sin_t = sin[...] * far_cos + cos[...] * far_sin
    ahead = lax.broadcasted_iota(jnp.int32, x.shape, 1) % HEAD < ROT // 2
    partner = jnp.where(ahead, -pltpu.roll(x, 128 - ROT // 2, 1), pltpu.roll(x, ROT // 2, 1))
    return x * cos_t + partner * (sin_t * sign)


def two_heads(x, left):
    zero = jnp.zeros_like(x)
    return [jnp.where(left, x, zero), jnp.where(left, zero, x)]


def block_of(rows):
    return next(size for size in (512, 256) if rows % size == 0)


def attend_kernel(
    first_ref, qkv_ref, cos_ref, sin_ref, cosf_ref, sinf_ref, begin_ref,
    qo_ref, ko_ref, vo_ref, o_ref, lse_ref, vt_ref,
):
    rows, wide = qo_ref.shape
    pairs, size = wide // 128, block_of(rows)
    tables = (cos_ref, sin_ref, cosf_ref, sinf_ref)
    left = lax.broadcasted_iota(jnp.int32, (size, 128), 1) < HEAD
    key_at = lax.broadcasted_iota(jnp.int32, (size, size), 0)
    query_at = lax.broadcasted_iota(jnp.int32, (1, size), 1)

    @pl.loop(0, rows // BLK)
    def _(i):
        r = pl.ds(pl.multiple_of(i * BLK, BLK), BLK)
        for t in range(pairs):
            w = pl.ds(t * 128, 128)
            q, k, v = (qkv_ref[r, pl.ds(part * wide + t * 128, 128)] for part in range(3))
            qo_ref[r, w] = turn(q, i, tables, 1.0).astype(BF) * jnp.asarray(HEAD**-0.5, BF)
            ko_ref[r, w] = turn(k, i, tables, 1.0).astype(BF)
            vo_ref[r, w] = v.astype(BF)
            vt_ref[w, r] = v.T.astype(BF)

    @pl.loop(0, rows // size)
    def _(i):
        r = pl.ds(pl.multiple_of(i * size, size), size)
        qs = sum((two_heads(qo_ref[r, pl.ds(t * 128, 128)], left) for t in range(pairs)), [])
        begin = begin_ref[0:1, r]
        here = query_at + i * size

        def step(j, carry):
            w = pl.ds(pl.multiple_of(j * size, size), size)
            key = key_at + j * size
            seen = (key <= here) & (key >= begin)
            out = []
            for h in range(2 * pairs):
                m, l, acc = carry[h]
                s = jnp.where(seen, mm(ko_ref[w, pl.ds(h // 2 * 128, 128)], qs[h], 1, 1), NEG)
                top = jnp.maximum(m, jnp.max(s, axis=0, keepdims=True))
                fade = jnp.exp(m - top)
                e = jnp.exp(s - top)
                acc = acc * fade + mm(vt_ref[pl.ds(h * HEAD, HEAD), w], e.astype(BF), 1, 0)
                out.append((top, l * fade + jnp.sum(e, axis=0, keepdims=True), acc))
            return tuple(out)

        start = (
            jnp.full((1, size), NEG, F32), jnp.zeros((1, size), F32), jnp.zeros((HEAD, size), F32)
        )
        done = lax.fori_loop(first_ref[i], i + 1, step, (start,) * (2 * pairs))
        for t in range(pairs):
            both = []
            for h in (2 * t, 2 * t + 1):
                m, l, acc = done[h]
                both.append(acc / l)
                lse_ref[h : h + 1, r] = m + jnp.log(l)
            o_ref[r, pl.ds(t * 128, 128)] = jnp.concatenate(both, axis=0).T.astype(BF)


def attend(qkv, begin):
    rows, wide = qkv.shape[0], qkv.shape[1] // 3
    size = block_of(rows)
    half = jax.ShapeDtypeStruct((rows, wide), BF)
    return pl.pallas_call(
        attend_kernel,
        in_specs=[pl.BlockSpec(memory_space=pltpu.SMEM)] + [IN_VMEM] * 6,
        out_specs=[IN_VMEM] * 5,
        out_shape=[half] * 4 + [jax.ShapeDtypeStruct((wide // HEAD, rows), F32)],
        scratch_shapes=[pltpu.VMEM((wide, rows), BF)],
        compiler_params=pltpu.CompilerParams(vmem_limit_bytes=48 << 20),
        name="attend",
    )(begin[0, ::size] // size, qkv, *turn_tables(rows), begin)


def attend_back_work(ins, out_ref, scratch):
    q_ref, k_ref, v_ref, o_ref, do_ref, lse_ref, cos_ref, sin_ref, cosf_ref, sinf_ref, begin_ref = ins
    kt_ref, dq_ref, dk_ref, dv_ref = scratch
    rows, wide = q_ref.shape
    pairs, size = wide // 128, block_of(rows)
    tables = (cos_ref, sin_ref, cosf_ref, sinf_ref)
    left = lax.broadcasted_iota(jnp.int32, (size, 128), 1) < HEAD
    key_at = lax.broadcasted_iota(jnp.int32, (size, size), 0)
    query_at = lax.broadcasted_iota(jnp.int32, (1, size), 1)

    @pl.loop(0, rows // BLK)
    def _(i):
        r = pl.ds(pl.multiple_of(i * BLK, BLK), BLK)
        for t in range(pairs):
            w = pl.ds(t * 128, 128)
            kt_ref[w, r] = k_ref[r, w].astype(F32).T.astype(BF)
            dk_ref[r, w] = jnp.zeros((BLK, 128), F32)
            dv_ref[r, w] = jnp.zeros((BLK, 128), F32)

    @pl.loop(0, rows // size)
    def _(i):
        r = pl.ds(pl.multiple_of(i * size, size), size)
        qs, dos, deltas, lses = [], [], [], []
        for t in range(pairs):
            w = pl.ds(t * 128, 128)
            do = do_ref[r, w]
            qs += two_heads(q_ref[r, w], left)
            dos += two_heads(do, left)
            prod = (do.astype(F32) * o_ref[r, w].astype(F32)).T
            deltas += [jnp.sum(prod[:HEAD], axis=0, keepdims=True), jnp.sum(prod[HEAD:], axis=0, keepdims=True)]
            lses += [lse_ref[2 * t : 2 * t + 1, r], lse_ref[2 * t + 1 : 2 * t + 2, r]]
        begin = begin_ref[0:1, r]
        here = query_at + i * size

        def step(j, carry):
            w = pl.ds(pl.multiple_of(j * size, size), size)
            key = key_at + j * size
            seen = (key <= here) & (key >= begin)
            out = []
            for t in range(pairs):
                lanes = pl.ds(t * 128, 128)
                k, v = k_ref[w, lanes], v_ref[w, lanes]
                dk = dv = None
                for h in (2 * t, 2 * t + 1):
                    prob = jnp.exp(jnp.where(seen, mm(k, qs[h], 1, 1) - lses[h], NEG))
                    ds = (prob * (mm(v, dos[h], 1, 1) - deltas[h])).astype(BF)
                    out.append(carry[h] + mm(kt_ref[pl.ds(h * HEAD, HEAD), w], ds, 1, 0))
                    dk_h, dv_h = mm(ds, qs[h], 1, 0), mm(prob.astype(BF), dos[h], 1, 0)
                    dk, dv = (dk_h, dv_h) if dk is None else (dk + dk_h, dv + dv_h)
                dk_ref[w, lanes] += dk
                dv_ref[w, lanes] += dv
            return tuple(out)

        done = lax.fori_loop(0, i + 1, step, (jnp.zeros((HEAD, size), F32),) * (2 * pairs))
        for t in range(pairs):
            both = jnp.concatenate(done[2 * t : 2 * t + 2], axis=0)
            dq_ref[r, pl.ds(t * 128, 128)] = both.T * (HEAD**-0.5)

    @pl.loop(0, rows // BLK)
    def _(i):
        r = pl.ds(pl.multiple_of(i * BLK, BLK), BLK)
        for t in range(pairs):
            w = pl.ds(t * 128, 128)
            for part, value in enumerate((turn(dq_ref[r, w], i, tables, -1.0), turn(dk_ref[r, w], i, tables, -1.0), dv_ref[r, w])):
                out_ref[r, pl.ds(part * wide + t * 128, 128)] = value.astype(BF)


def attend_back(S, C, number, q, k, v, o, do, lse, begin, riders):
    rows, wide = q.shape

    def kernel(ride, ins, outs, scratch):
        greet(S, C, axes=ride.axes)
        ride.start()
        attend_back_work(ins, outs[0], scratch)
        ride.wait()

    args = [q, k, v, o, do, lse, *turn_tables(rows), begin]
    return comm(
        kernel, S, C, number, "attend_back", args, [IN_VMEM] * len(args),
        [(jax.ShapeDtypeStruct((rows, 3 * wide), BF), IN_VMEM)],
        [pltpu.VMEM((wide, rows), BF)] + [pltpu.VMEM((rows, wide), F32)] * 3,
        riders,
    )


def doc_begins(lengths_row, rows):
    row_ids = jnp.arange(rows, dtype=jnp.int32)
    ends = jnp.cumsum(lengths_row, dtype=jnp.int32)
    begins = ends - lengths_row
    inside = (row_ids[:, None] >= begins[None, :]) & (row_ids[:, None] < ends[None, :])
    return jnp.sum(jnp.where(inside, begins[None, :], 0), axis=1, dtype=jnp.int32)


def layer_norm(values, gain, shift):
    center = values - jnp.mean(values, axis=-1, keepdims=True)
    inverse = lax.rsqrt(jnp.mean(center * center, axis=-1, keepdims=True) + EPS)
    normal = center * inverse
    return (normal * gain + shift, normal, inverse)


def norm_back(gradient, normal, inverse, gain):
    scaled = gradient * gain
    centered = (
        scaled
        - jnp.mean(scaled, axis=-1, keepdims=True)
        - normal * jnp.mean(scaled * normal, axis=-1, keepdims=True)
    )
    return (inverse * centered, jnp.sum(gradient * normal, axis=0), jnp.sum(gradient, axis=0))


def tiles_of(parts, lead):
    flat = jnp.concatenate([x.astype(F32).reshape(lead + (-1,)) for x in parts], axis=-1)
    flat = jnp.pad(flat, ((0, 0),) * len(lead) + ((0, 1024 - flat.shape[-1]),))
    return flat.reshape(lead + (8, 128))


def make_body(S, C, T):
    assert S == C

    def body(tokens, lengths, w_qkv, b_qkv, w_out, w_gateup, w_down, norm_gain, norm_bias, cotangent):
        p, z, c = lax.axis_index("shard"), lax.axis_index("ctx"), lax.axis_index("tp")
        R, D = tokens.shape
        n = R // T
        nb = D // (S * C)
        L = R * C

        def to_parts(x):
            return x.reshape(n, S, C, nb).transpose(2, 0, 1, 3).reshape(S, n, D // S)

        def parts(x):
            return x.reshape(n, S, D // S).swapaxes(0, 1)

        def unpermute(x):
            return x.reshape(x.shape[0], C, S, nb).swapaxes(1, 2).reshape(x.shape)

        def own(x):
            return lax.dynamic_slice_in_dim(x, (p * T + c) * n, n, 0)

        def half_of(x):
            return lax.dynamic_slice_in_dim(x, c * n, n, 0)

        def after(x, y):
            return lax.optimization_barrier((x, y))

        def over_ctx(w):
            return lax.all_gather(w.reshape(S * nb, -1), "ctx", axis=0, tiled=True)

        def sum_ctx(g):
            g = lax.psum_scatter(g.astype(BF), "ctx", scatter_dimension=0, tiled=True)
            return g.reshape(S, nb, -1)

        hn = w_qkv.shape[3] // S
        fn = w_gateup.shape[3] // S
        heads = hn // HEAD
        nf = HEAD // (S * C)

        tile = tiles_of((norm_gain[0].reshape(-1), norm_bias[0].reshape(-1), b_qkv[0].reshape(-1), lengths[0]), ())
        small, _, tok, wq = exchange(
            S, C, T, 0,
            [("shard", w_qkv[0].reshape(nb, 3, S, hn).transpose(2, 0, 1, 3).reshape(S, nb, 3 * hn))],
            jnp.broadcast_to(tile, (C, S, 8, 128)),
            to_parts(half_of(tokens)),
        )
        wq = over_ctx(wq)
        tok, wo, wg, wd, cot = gather_columns(
            S, C, T, 1, tok,
            [
                ("shard", w_out[0].reshape(S, hn, nb).swapaxes(1, 2)),
                ("shard", w_gateup[0].reshape(nb, 2, S, fn).transpose(2, 0, 1, 3).reshape(S, nb, 2 * fn)),
                ("shard", w_down[0].reshape(S, fn, nb).swapaxes(1, 2)),
                ("shard", to_parts(half_of(cotangent))),
            ],
        )
        wo, wg, wd = over_ctx(wo), over_ctx(wg), over_ctx(wd)

        small = lax.dynamic_index_in_dim(small, c, 0, keepdims=False).reshape(C, S, 1024)
        norms = small[:, :, : 4 * nb].reshape(C * S, 4, nb).swapaxes(0, 1).reshape(4, D)
        gains, shifts = norms[:2], norms[2:]
        nbias = 3 * S * heads * nf
        bias = small[:, :, 4 * nb : 4 * nb + nbias].reshape(C, S, 3, S * heads, nf)
        bias = lax.dynamic_slice_in_dim(bias, p * heads, heads, 3)
        bias = bias.transpose(2, 3, 1, 0, 4).reshape(1, 3 * hn)
        docs = lengths.shape[1]
        lengths_row = lax.dynamic_index_in_dim(
            small[0, :, 4 * nb + nbias : 4 * nb + nbias + docs], z, 0, keepdims=False
        ).astype(jnp.int32)
        begin = doc_begins(lengths_row, L)
        begin = begin[None, :]

        n1 = layer_norm(tok.astype(F32), gains[0], shifts[0])[0].astype(BF)
        hidden = own(tok).astype(F32)
        _, normal1, inverse1 = layer_norm(hidden, gains[0], shifts[0])
        qkv = mm(n1, wq, 1, 0) + bias
        q, k, v, o, lse = attend(qkv, begin)
        got, cot = scatter(S, C, T, 2, o, wo, [("ctx", cot)])
        mid = hidden + got
        n2, normal2, inverse2 = layer_norm(mid, gains[1], shifts[1])
        (n2,) = gather(S, C, T, 3, n2.astype(BF))
        cot, n2 = after(cot, n2)
        (gb,) = gather_columns(S, C, T, 4, cot)
        gu = mm(n2, wg, 1, 0)
        gate, up = gu[:, :fn], gu[:, fn:]
        logistic = jax.nn.sigmoid(gate)
        act = (gate * logistic * up).astype(BF)
        gw_down = mm(gb, act, 0, 0).astype(BF)
        wd, gw_down = after(wd, gw_down)
        gw_down = sum_ctx(gw_down)

        dact = mm(gb, wd, 1, 0)
        dgate = dact * up * logistic * (1.0 + gate * (1.0 - logistic))
        dup = dact * gate * logistic
        dgu = jnp.concatenate((dgate, dup), axis=1).astype(BF)
        gw_gateup = mm(n2, dgu, 0, 0).astype(BF)
        act, gw_gateup = after(act, gw_gateup)
        gw_gateup = sum_ctx(gw_gateup)
        (got,) = scatter(S, C, T, 5, act, wd)
        out = parts((mid + got).astype(BF))
        dgu, out = after(dgu, out)
        got, out = scatter(S, C, T, 6, dgu, wg, [("shard", out)])
        dmid, gain2, shift2 = norm_back(got, normal2, inverse2, gains[1])
        dmid = own(gb).astype(F32) + dmid
        gb1, out = gather(S, C, T, 7, dmid.astype(BF), [("ctx", out)])
        gw_out = mm(gb1, o, 0, 0).astype(BF)
        gb1, gw_out = after(gb1, gw_out)
        gw_out = sum_ctx(gw_out)
        do = mm(gb1, wo, 1, 0).astype(BF)
        dqkv, gw_gateup, gw_down = attend_back(
            S, C, 11, q, k, v, o, do, lse, begin, [("shard", gw_gateup), ("shard", gw_down)]
        )
        gw_qkv = mm(n1, dqkv, 0, 0).astype(BF)
        dqkv, gw_qkv = after(dqkv, gw_qkv)
        gw_qkv = sum_ctx(gw_qkv)
        got, out = scatter(S, C, T, 8, dqkv, wq, [("shard", out)])
        dtok, gain1, shift1 = norm_back(got, normal1, inverse1, gains[0])
        gtok, gw_out, mate = leave(
            S, C, T, 9, parts((dmid + dtok).astype(BF)), [("shard", gw_out), ("tp", out)]
        )
        gtok = unpermute(gtok).astype(F32)
        out = jnp.where(c == 0, jnp.stack((out, mate)), jnp.stack((mate, out)))
        out = unpermute(out.transpose(0, 2, 1, 3).reshape(R, D))

        gbias = jnp.sum(dqkv.astype(F32), axis=0)
        tiles = tiles_of(
            (
                jnp.stack((gain1, gain2, shift1, shift2)).reshape(4, C, S, nb).transpose(1, 2, 0, 3),
                gbias.reshape(3, heads, S, C, nf).transpose(3, 2, 0, 1, 4),
            ),
            (C, S),
        )
        small, gw_qkv = exchange(S, C, T, 10, [("shard", gw_qkv)], tiles)
        small = small.reshape(T, C, S, 1024)
        norms = jnp.sum(small[..., : 4 * nb], axis=(0, 1, 2)).reshape(1, 4, nb)
        gbias = lax.dynamic_index_in_dim(small, c, 0, keepdims=False)[..., 4 * nb : 4 * nb + 3 * heads * nf]
        gbias = jnp.sum(gbias, axis=0).reshape(S, 3, heads, nf).swapaxes(0, 1).reshape(b_qkv.shape)

        return (
            out,
            gtok,
            gw_qkv.astype(F32).reshape(S, nb, 3, hn).transpose(1, 2, 0, 3).reshape(w_qkv.shape),
            gbias,
            gw_out.astype(F32).swapaxes(1, 2).reshape(w_out.shape),
            gw_gateup.astype(F32).reshape(S, nb, 2, fn).transpose(1, 2, 0, 3).reshape(w_gateup.shape),
            gw_down.astype(F32).swapaxes(1, 2).reshape(w_down.shape),
            norms[:, :2],
            norms[:, 2:],
        )

    return body


def solution(mesh):
    both = ("shard", "ctx")
    specs = (
        P(None, both, None, "tp"),
        P(None, None, "tp", both),
        P(None, "tp", both),
        P(None, both, None, "tp"),
        P(None, "tp", both),
        P(None, None, both),
        P(None, None, both),
    )
    return jax.shard_map(
        make_body(mesh.shape["shard"], mesh.shape["ctx"], mesh.shape["tp"]),
        mesh=mesh,
        in_specs=(P(both, None), P("shard", None)) + specs + (P(both, None),),
        out_specs=(P(both, None), P(both, None)) + specs,
        check_vma=False,
    )
```

```python
import functools

import jax
import jax.numpy as jnp
import numpy as np
from jax import lax
from jax.experimental import pallas as pl
from jax.experimental.pallas import tpu as pltpu
from jax.sharding import PartitionSpec as P

HEAD = 64
ROT = 16
EPS = 1e-05
NEG = -1e30
BASE = 10000.0
BF = jnp.bfloat16
F32 = jnp.float32
BLK = 256
MESH = pl.DeviceIdType.MESH
DMA = pltpu.SemaphoreType.DMA
ANY = pl.BlockSpec(memory_space=pl.ANY)
IN_VMEM = pl.BlockSpec(memory_space=pltpu.VMEM)


def mm(a, b, ca, cb):
    return lax.dot_general(a, b, (((ca,), (cb,)), ((), ())), preferred_element_type=F32)


def remote(src, dst, send, recv, where):
    return pltpu.make_async_remote_copy(
        src_ref=src, dst_ref=dst, send_sem=send, recv_sem=recv, device_id=where, device_id_type=MESH
    )


def here():
    return lax.axis_index("shard"), lax.axis_index("ctx"), lax.axis_index("tp")


class Riders:
    def __init__(self, S, C, riders):
        self.S, self.C = S, C
        self.axes = [axis for axis, _ in riders]
        self.arrays = [x for _, x in riders]
        self.shapes = [
            jax.ShapeDtypeStruct((C,) + x.shape if axis == "all" else x.shape, x.dtype) for axis, x in riders
        ]
        count, most = len(riders), max(S, C) - 1
        self.scratch = [DMA((count, most)), DMA((count, most)), DMA((count,))] if count else []

    def bind(self, ins, outs, sems):
        self.ins, self.outs, self.sems = ins, outs, sems

    def start(self):
        p, z, c = here()
        self.moves = []
        for n, axis in enumerate(self.axes):
            src, dst = self.ins[n], self.outs[n]
            send, recv, own = self.sems
            if axis == "tp":
                copies = [remote(src, dst, send.at[n, 0], recv.at[n, 0], {"tp": 1 - c})]
            elif axis == "all":
                copies = [
                    remote(src, dst.at[z], send.at[n, k - 1], recv.at[n, k - 1], {"ctx": (z + k) % self.C})
                    for k in range(1, self.C)
                ]
                copies.append(pltpu.make_async_copy(src, dst.at[z], own.at[n]))
            else:
                size, me = (self.S, p) if axis == "shard" else (self.C, z)
                copies = [
                    remote(src.at[(me + k) % size], dst.at[me], send.at[n, k - 1], recv.at[n, k - 1], {axis: (me + k) % size})
                    for k in range(1, size)
                ]
                copies.append(pltpu.make_async_copy(src.at[me], dst.at[me], own.at[n]))
            for copy in copies:
                copy.start()
            self.moves += copies

    def wait(self):
        for copy in self.moves:
            copy.wait()


def greet(S, C, mates=(), line=False, other=False, axes=()):
    p, z, c = here()
    peers = [{"shard": q} for q in ([(p + k) % S for k in range(1, S)] if "shard" in axes else mates)]
    if line or "ctx" in axes or "all" in axes:
        peers += [{"ctx": (z + k) % C} for k in range(1, C)]
    if other or "tp" in axes:
        peers.append({"tp": 1 - c})
    barrier = pltpu.get_barrier_semaphore()
    for where in peers:
        pl.semaphore_signal(barrier, inc=1, device_id=where, device_id_type=MESH)
    pl.semaphore_wait(barrier, len(peers))


def comm(kernel, S, C, number, name, args, in_specs, outs, scratch, riders=()):
    ride = Riders(S, C, riders)
    na, nr, no, ns = len(args), len(ride.axes), len(outs), len(scratch)

    def body(*refs):
        ins, refs = refs[:na], refs[na:]
        rins, refs = refs[:nr], refs[nr:]
        os, refs = refs[:no], refs[no:]
        routs, refs = refs[:nr], refs[nr:]
        ride.bind(rins, routs, refs[ns:])
        kernel(ride, ins, os, refs[:ns])

    return pl.pallas_call(
        body,
        out_shape=[shape for shape, _ in outs] + ride.shapes,
        in_specs=list(in_specs) + [IN_VMEM] * nr,
        out_specs=[spec for _, spec in outs] + [ANY] * nr,
        scratch_shapes=list(scratch) + ride.scratch,
        compiler_params=pltpu.CompilerParams(
            collective_id=number, has_side_effects=True, vmem_limit_bytes=56 << 20
        ),
        cost_estimate=pl.CostEstimate(flops=0, bytes_accessed=120_000_000, transcendentals=0),
        name=name,
    )(*args, *ride.arrays)


def exchange(S, C, T, number, riders, tiles, rows=None):
    def kernel(ride, ins, outs, scratch):
        tile, got = ins[0], outs[0]
        send, recv, bsend, brecv, own = scratch[:5]
        p, z, c = here()
        everyone = [(i, j) for i in range(C) for j in range(S) if i or j]
        barrier = pltpu.get_barrier_semaphore()
        peers = [{"shard": (p + j) % S, "ctx": (z + i) % C} for i, j in everyone] + [{"tp": 1 - c}]
        for where in peers:
            pl.semaphore_signal(barrier, inc=1, device_id=where, device_id_type=MESH)
        pl.semaphore_wait(barrier, len(peers))

        def turn_over(source, target, k, axis, size, me):
            ssem, rsem, local = scratch[5:]
            hop = [pltpu.make_async_copy(source.at[me], target.at[me], local.at[k])]
            for j in range(1, size):
                q = (me + j) % size
                hop.append(remote(source.at[q], target.at[me], ssem.at[k, j - 1], rsem.at[k, j - 1], {axis: q}))
            for copy in hop:
                copy.start()
            return hop

        if rows is not None:
            first = turn_over(ins[1], outs[1], 0, "shard", S, p)
        local = pltpu.make_async_copy(tile.at[z, p], got.at[c, z, p], own)
        local.start()
        copies = []
        for at, (where, (i, j)) in enumerate(zip(peers, everyone)):
            q, g = (p + j) % S, (z + i) % C
            copies.append(remote(tile.at[g, q], got.at[c, z, p], send.at[at], recv.at[at], where))
            copies[-1].start()
        ride.start()
        if rows is not None:
            for copy in first:
                copy.wait()
            second = turn_over(outs[1], outs[2], 1, "ctx", C, z)
        local.wait()
        for copy in copies:
            copy.wait()
        back = remote(got.at[c], got.at[c], bsend, brecv, {"tp": 1 - c})
        back.start()
        back.wait_send()
        remote(got.at[1 - c], got.at[1 - c], bsend, brecv, {"tp": 1 - c}).wait_recv()
        if rows is not None:
            for copy in second:
                copy.wait()
        ride.wait()

    count, most = C * S - 1, max(S, C) - 1
    args, outs = [tiles], [(jax.ShapeDtypeStruct((T,) + tiles.shape, tiles.dtype), ANY)]
    scratch = [DMA((count,)), DMA((count,)), DMA, DMA, DMA]
    if rows is not None:
        args.append(rows)
        outs += [(jax.ShapeDtypeStruct(rows.shape, rows.dtype), IN_VMEM)] * 2
        scratch += [DMA((2, most)), DMA((2, most)), DMA((2,))]
    return comm(kernel, S, C, number, "exchange", args, [IN_VMEM] * len(args), outs, scratch, riders)


def plane(S):
    p, _, c = here()
    B = S // 2
    a, b = p // B, p % B
    return a, b, [a * B + (b + j) % B for j in range(1, B)], (1 - a) * B + b


def spread_sems(S):
    count = 4 + 4 * (S // 2 - 1)
    return [DMA((2 * count,)), DMA((2 * count,))]


def spread(S, own, region, send, recv):
    p, _, c = here()
    B = S // 2
    a, b, rows, col = plane(S)
    rows, col, other = [{"shard": q} for q in rows], {"shard": col}, {"tp": 1 - c}
    per = 4 + 4 * (B - 1)
    OWN, ROW, COL, VIA_COL, VIA_ROW = 0, 2, 2 + 2 * (B - 1), 4 + 2 * (B - 1), 4 + 3 * (B - 1)
    started = []

    def push(q, h, sem, where, first=False):
        view = region(q, h, c)
        copy = remote(own(h) if first else view, view, send.at[sem], recv.at[sem], where)
        copy.start()
        started.append(copy)

    def came(q, h, sem, core):
        view = region(q, h, core)
        remote(view, view, send.at[sem], recv.at[sem], other).wait_recv()

    for h in range(2):
        for j in range(1, B):
            push(p, h, ROW + 2 * (j - 1) + h, rows[j - 1], True)
    for h in (1, 0):
        push(p, h, COL + h, col, True)
    for h in range(2):
        push(p, h, per + OWN + h, other, True)

    def from_row(j, h):
        q = a * B + (b - j) % B
        came(q, h, ROW + 2 * (j - 1) + h, c)
        push(q, h, per + ROW + 2 * (j - 1) + h, other)
        return q

    def from_col(h):
        q = (1 - a) * B + b
        came(q, h, COL + h, c)
        push(q, h, per + COL + h, other)
        return q

    for j in range(1, B):
        q = from_row(j, 0)
        push(q, 0, VIA_COL + j - 1, col)
    q = from_col(1)
    for j in range(1, B):
        push(q, 1, VIA_ROW + j - 1, rows[j - 1])
    for j in range(1, B):
        from_row(j, 1)
    from_col(0)
    for j in range(1, B):
        q = (1 - a) * B + (b - j) % B
        came(q, 0, VIA_COL + j - 1, c)
        push(q, 0, per + VIA_COL + j - 1, other)
        came(q, 1, VIA_ROW + j - 1, c)
        push(q, 1, per + VIA_ROW + j - 1, other)
    for h in range(2):
        came(p, h, per + OWN + h, 1 - c)
        came((1 - a) * B + b, h, per + COL + h, 1 - c)
    for j in range(1, B):
        for h in range(2):
            came(a * B + (b - j) % B, h, per + ROW + 2 * (j - 1) + h, 1 - c)
        q = (1 - a) * B + (b - j) % B
        came(q, 0, per + VIA_COL + j - 1, 1 - c)
        came(q, 1, per + VIA_ROW + j - 1, 1 - c)
    for copy in started:
        copy.wait_send()


def gather_columns(S, C, T, number, x, riders=()):
    _, n, wide = x.shape

    def kernel(ride, ins, outs, scratch):
        (x_ref,), (out_ref,), (send, recv, own) = ins, outs, scratch
        p, _, c = here()
        _, _, rows, col = plane(S)

        def region(q, h, core):
            part = pl.ds(pl.multiple_of(q * wide, 128), wide)
            return out_ref.at[pl.ds(h * (C // 2), C // 2), core, :, part]

        local = [
            pltpu.make_async_copy(x_ref.at[pl.ds(h * (C // 2), C // 2)], region(p, h, c), own.at[h]) for h in range(2)
        ]
        for copy in local:
            copy.start()
        greet(S, C, rows + [col], other=True, axes=ride.axes)
        ride.start()
        spread(S, lambda h: x_ref.at[pl.ds(h * (C // 2), C // 2)], region, send, recv)
        for copy in local:
            copy.wait()
        ride.wait()

    out, *rest = comm(
        kernel, S, C, number, "gather_columns", [x], [IN_VMEM],
        [(jax.ShapeDtypeStruct((C, T, n, wide * S), x.dtype), ANY)], spread_sems(S) + [DMA((2,))], riders,
    )
    return [out.reshape(C * T * n, wide * S)] + rest


CHUNK = 512
ROWS = 32


def sum_scratch(S, n, D):
    half, B = n // 2, S // 2

    def vm(*shape):
        return pltpu.VMEM(shape, BF)

    return [
        vm(S, n, D), vm(S, n, D), vm(S, n, D), vm(B - 1, 2, half, D), vm(B, half, D),
        vm(B - 1, half, D), vm(half, D), vm(half, D), vm(B - 1, half, D),
        DMA((S,)), DMA((S,)), DMA((B - 1, 2)), DMA((B - 1, 2)), DMA((B,)), DMA((B,)), DMA((B,)), DMA((B,)),
    ]


def sum_over_plane(S, T, x_ref, w_ref, out_ref, scratch):
    away, sib, mine, row1, col1, row2, col2, to_col, to_row = scratch[:9]
    asend, arecv, rsend, rrecv, csend, crecv, fsend, frecv = scratch[9:]
    n, D = out_ref.shape
    half, B = n // 2, S // 2
    _, _, c = here()
    a, b, rows, col = plane(S)
    rows, col, other = [{"shard": q} for q in rows], {"shard": col}, {"tp": 1 - c}

    def chip(e):
        return ((a + e // B) % 2) * B + (b + e % B) % B

    def product(e, core, store):
        x = x_ref[chip(e) * T + core]

        def column(j, _):
            w = pl.ds(pl.multiple_of(j * CHUNK, CHUNK), CHUNK)
            store(w, mm(x, w_ref[w, :], 1, 1))
            return 0

        lax.fori_loop(0, D // CHUNK, column, 0)

    def to_other(e):
        return remote(away.at[e], sib.at[e], asend.at[e], arecv.at[e], other)

    def first(i, _):
        e = S - 1 - i

        def store(w, value):
            away[e, :, w] = value.astype(BF)

        product(e, 1 - c, store)
        to_other(e).start()
        return 0

    lax.fori_loop(0, S, first, 0)

    top, low = pl.ds(0, half), pl.ds(half, half)
    started = []

    def push(src, dst, send, recv, where):
        copy = remote(src, dst, send, recv, where)
        copy.start()
        started.append(copy)

    for e in range(S - 1, -1, -1):
        to_other(e).wait()

        def store(w, value):
            value = value + sib[e, :, w].astype(F32)
            if e:
                mine[e, :, w] = value.astype(BF)
            else:
                out_ref[:, w] = value

        product(e, c, store)
        j = e % B
        if e > B:
            push(mine.at[e, top], row1.at[j - 1, 1], rsend.at[j - 1, 1], rrecv.at[j - 1, 1], rows[j - 1])
            push(mine.at[e, low], col1.at[j], csend.at[j], crecv.at[j], col)
        elif e == B:
            push(mine.at[e, low], col1.at[0], csend.at[0], crecv.at[0], col)
        elif e:
            push(mine.at[e, top], row1.at[j - 1, 0], rsend.at[j - 1, 0], rrecv.at[j - 1, 0], rows[j - 1])

    def came(ref, send, recv):
        remote(ref, ref, send, recv, other).wait_recv()

    total = mine[B, top, :].astype(F32)
    for j in range(1, B):
        came(row1.at[j - 1, 1], rsend.at[j - 1, 1], rrecv.at[j - 1, 1])
        total = total + row1[j - 1, 1].astype(F32)
    to_col[...] = total.astype(BF)
    push(to_col, col2, fsend.at[0], frecv.at[0], col)
    for j in range(1, B):
        came(col1.at[j], csend.at[j], crecv.at[j])
        to_row[j - 1] = (mine[j, low, :].astype(F32) + col1[j].astype(F32)).astype(BF)
        push(to_row.at[j - 1], row2.at[j - 1], fsend.at[j], frecv.at[j], rows[j - 1])
    came(col1.at[0], csend.at[0], crecv.at[0])
    upper, lower = out_ref[top, :], out_ref[low, :] + col1[0].astype(F32)
    for j in range(1, B):
        came(row1.at[j - 1, 0], rsend.at[j - 1, 0], rrecv.at[j - 1, 0])
        upper = upper + row1[j - 1, 0].astype(F32)
    came(col2, fsend.at[0], frecv.at[0])
    out_ref[top, :] = upper + col2[...].astype(F32)
    for j in range(1, B):
        came(row2.at[j - 1], fsend.at[j], frecv.at[j])
        lower = lower + row2[j - 1].astype(F32)
    out_ref[low, :] = lower
    for copy in started:
        copy.wait_send()


def scatter(S, C, T, number, x, w, riders=()):
    L, K = x.shape
    D, n = w.shape[0], L // (S * T)

    def kernel(ride, ins, outs, scratch):
        _, _, rows, col = plane(S)
        greet(S, C, rows + [col], other=True, axes=ride.axes)
        ride.start()
        sum_over_plane(S, T, ins[0], ins[1], outs[0], scratch)
        ride.wait()

    return comm(
        kernel, S, C, number, "scatter", [x.reshape(S * T, n, K), w], [IN_VMEM, IN_VMEM],
        [(jax.ShapeDtypeStruct((n, D), F32), IN_VMEM)], sum_scratch(S, n, D), riders,
    )


def row_blocks(n, work):
    @pl.loop(0, n // ROWS)
    def _(i):
        work(pl.ds(pl.multiple_of(i * ROWS, ROWS), ROWS))


def norm_of(v):
    center = v - jnp.mean(v, axis=-1, keepdims=True)
    inverse = lax.rsqrt(jnp.mean(center * center, axis=-1, keepdims=True) + EPS)
    return center * inverse, inverse


def norm_back(v, g, gain, stats_ref):
    normal, inverse = norm_of(v)
    e = g * gain
    stats_ref[0:1, :] += jnp.sum(g * normal, axis=0, keepdims=True)
    stats_ref[1:2, :] += jnp.sum(g, axis=0, keepdims=True)
    return inverse * (
        e - jnp.mean(e, axis=-1, keepdims=True) - normal * jnp.mean(e * normal, axis=-1, keepdims=True)
    )


def spread_rows(S, T, src, out_ref, send, recv, own):
    p, _, c = here()
    half = src.shape[0] // 2
    local = pltpu.make_async_copy(src, out_ref.at[p * T + c], own)
    local.start()
    spread(
        S,
        lambda h: src.at[pl.ds(h * half, half)],
        lambda q, h, core: out_ref.at[q * T + core, pl.ds(h * half, half)],
        send,
        recv,
    )
    local.wait()


def sum_norm_gather(S, C, T, number, x, w, residual, gain, shift, riders=()):
    L, K = x.shape
    D, n = w.shape[0], L // (S * T)

    def kernel(ride, ins, outs, scratch):
        x_ref, w_ref, res_ref, gain_ref, shift_ref = ins
        v_ref, out_ref = outs
        acc, low, send, recv, own = scratch[:5]
        _, _, rows, col = plane(S)
        greet(S, C, rows + [col], other=True, axes=ride.axes)
        ride.start()
        sum_over_plane(S, T, x_ref, w_ref, acc, scratch[5:])

        def work(r):
            v = res_ref[r, :].astype(F32) + acc[r, :]
            v_ref[r, :] = v
            low[r, :] = (norm_of(v)[0] * gain_ref[...] + shift_ref[...]).astype(BF)

        row_blocks(n, work)
        spread_rows(S, T, low, out_ref, send, recv, own)
        ride.wait()

    v, out, *rest = comm(
        kernel, S, C, number, "sum_norm_gather", [x.reshape(S * T, n, K), w, residual, gain, shift], [IN_VMEM] * 5,
        [(jax.ShapeDtypeStruct((n, D), F32), IN_VMEM), (jax.ShapeDtypeStruct((S * T, n, D), BF), ANY)],
        [pltpu.VMEM((n, D), F32), pltpu.VMEM((n, D), BF)] + spread_sems(S) + [DMA] + sum_scratch(S, n, D),
        riders,
    )
    return [v, out.reshape(L, D)] + rest


def sum_back_gather(S, C, T, number, x, w, v, residual, gain, riders=()):
    L, K = x.shape
    D, n = w.shape[0], L // (S * T)

    def kernel(ride, ins, outs, scratch):
        x_ref, w_ref, in_ref, res_ref, gain_ref = ins
        v_ref, out_ref, stats = outs
        acc, low, send, recv, own = scratch[:5]
        _, _, rows, col = plane(S)
        greet(S, C, rows + [col], other=True, axes=ride.axes)
        ride.start()
        sum_over_plane(S, T, x_ref, w_ref, acc, scratch[5:])
        stats[...] = jnp.zeros_like(stats)

        def work(r):
            g = res_ref[r, :].astype(F32) + norm_back(in_ref[r, :], acc[r, :], gain_ref[...], stats)
            v_ref[r, :] = g
            low[r, :] = g.astype(BF)

        row_blocks(n, work)
        spread_rows(S, T, low, out_ref, send, recv, own)
        ride.wait()

    g, out, stats, *rest = comm(
        kernel, S, C, number, "sum_back_gather", [x.reshape(S * T, n, K), w, v, residual, gain], [IN_VMEM] * 5,
        [
            (jax.ShapeDtypeStruct((n, D), F32), IN_VMEM), (jax.ShapeDtypeStruct((S * T, n, D), BF), ANY),
            (jax.ShapeDtypeStruct((2, D), F32), IN_VMEM),
        ],
        [pltpu.VMEM((n, D), F32), pltpu.VMEM((n, D), BF)] + spread_sems(S) + [DMA] + sum_scratch(S, n, D),
        riders,
    )
    return [g, out.reshape(L, D), stats] + rest


def sum_back_leave(S, C, T, number, x, w, v, residual, gain, riders=()):
    L, K = x.shape
    D, n = w.shape[0], L // (S * T)
    wide = D // S

    def kernel(ride, ins, outs, scratch):
        x_ref, w_ref, in_ref, res_ref, gain_ref = ins
        out_ref, stats = outs
        acc, low, buf, buf2, s1, r1, s2, r2, s3, r3, s4, r4, own = scratch[:13]
        p, z, c = here()
        mates = [(p + k) % S for k in range(1, S)]
        line = [(z + k) % C for k in range(1, C)]
        other = {"tp": 1 - c}
        greet(S, C, mates, line=True, other=True, axes=ride.axes)
        ride.start()
        sum_over_plane(S, T, x_ref, w_ref, acc, scratch[13:])
        stats[...] = jnp.zeros_like(stats)

        def work(r):
            g = res_ref[r, :] + norm_back(in_ref[r, :].astype(F32), acc[r, :], gain_ref[...], stats)
            low[r, :] = g.astype(BF)

        row_blocks(n, work)

        def part(q):
            return pl.ds(pl.multiple_of(q * wide, 128), wide)

        def turn_over(source, target, send, recv, local, me, axis, peers):
            hop = [pltpu.make_async_copy(source(me), target, local)]
            for k, q in enumerate(peers):
                hop.append(remote(source(q), target, send.at[k], recv.at[k], {axis: q}))
            for copy in hop:
                copy.start()
            for copy in hop:
                copy.wait()

        turn_over(lambda q: low.at[:, part(q)], buf.at[p], s1, r1, own.at[0], p, "shard", mates)
        turn_over(lambda q: buf.at[q], buf2.at[z], s2, r2, own.at[1], z, "ctx", line)
        turn_over(lambda q: buf2.at[q], out_ref.at[c, :, part(p)], s3, r3, own.at[2], p, "shard", mates)
        copy = remote(out_ref.at[c], out_ref.at[c], s4, r4, other)
        copy.start()
        copy.wait_send()
        remote(out_ref.at[1 - c], out_ref.at[1 - c], s4, r4, other).wait_recv()
        ride.wait()

    out, stats, *rest = comm(
        kernel, S, C, number, "sum_back_leave", [x.reshape(S * T, n, K), w, v, residual, gain], [IN_VMEM] * 5,
        [(jax.ShapeDtypeStruct((T, n, D), BF), ANY), (jax.ShapeDtypeStruct((2, D), F32), IN_VMEM)],
        [
            pltpu.VMEM((n, D), F32), pltpu.VMEM((n, D), BF), pltpu.VMEM((S, n, wide), BF), pltpu.VMEM((C, n, wide), BF),
            DMA((S - 1,)), DMA((S - 1,)), DMA((C - 1,)), DMA((C - 1,)), DMA((S - 1,)), DMA((S - 1,)), DMA, DMA, DMA((3,)),
        ]
        + sum_scratch(S, n, D),
        riders,
    )
    return [out.reshape(T * n, D), stats] + rest


def turn_tables(rows):
    feature = np.arange(128) % HEAD
    freq = np.where(feature < ROT, BASE ** (-2.0 * (feature % (ROT // 2)) / ROT), 0.0)
    near = np.arange(BLK)[:, None] * freq
    far = np.arange(0, rows, BLK)[:, None] * freq
    return [jnp.asarray(f(x), F32) for x in (near, far) for f in (np.cos, np.sin)]


def turn(x, i, tables, sign):
    cos, sin, cos_far, sin_far = tables
    far_cos, far_sin = cos_far[pl.ds(i, 1), :], sin_far[pl.ds(i, 1), :]
    cos_t = cos[...] * far_cos - sin[...] * far_sin
    sin_t = sin[...] * far_cos + cos[...] * far_sin
    ahead = lax.broadcasted_iota(jnp.int32, x.shape, 1) % HEAD < ROT // 2
    partner = jnp.where(ahead, -pltpu.roll(x, 128 - ROT // 2, 1), pltpu.roll(x, ROT // 2, 1))
    return x * cos_t + partner * (sin_t * sign)


def two_heads(x, left):
    zero = jnp.zeros_like(x)
    return [jnp.where(left, x, zero), jnp.where(left, zero, x)]


def block_of(rows):
    return next(size for size in (512, 256) if rows % size == 0)


def attend_kernel(
    first_ref, qkv_ref, cos_ref, sin_ref, cosf_ref, sinf_ref, begin_ref,
    qo_ref, ko_ref, vo_ref, o_ref, lse_ref, vt_ref,
):
    rows, wide = qo_ref.shape
    pairs, size = wide // 128, block_of(rows)
    tables = (cos_ref, sin_ref, cosf_ref, sinf_ref)
    left = lax.broadcasted_iota(jnp.int32, (size, 128), 1) < HEAD
    key_at = lax.broadcasted_iota(jnp.int32, (size, size), 0)
    query_at = lax.broadcasted_iota(jnp.int32, (1, size), 1)

    @pl.loop(0, rows // BLK)
    def _(i):
        r = pl.ds(pl.multiple_of(i * BLK, BLK), BLK)
        for t in range(pairs):
            w = pl.ds(t * 128, 128)
            q, k, v = (qkv_ref[r, pl.ds(part * wide + t * 128, 128)] for part in range(3))
            qo_ref[r, w] = turn(q, i, tables, 1.0).astype(BF) * jnp.asarray(HEAD**-0.5, BF)
            ko_ref[r, w] = turn(k, i, tables, 1.0).astype(BF)
            vo_ref[r, w] = v.astype(BF)
            vt_ref[w, r] = v.T.astype(BF)

    @pl.loop(0, rows // size)
    def _(i):
        r = pl.ds(pl.multiple_of(i * size, size), size)
        qs = sum((two_heads(qo_ref[r, pl.ds(t * 128, 128)], left) for t in range(pairs)), [])
        begin = begin_ref[0:1, r]
        here = query_at + i * size

        def step(j, carry):
            w = pl.ds(pl.multiple_of(j * size, size), size)
            key = key_at + j * size
            seen = (key <= here) & (key >= begin)
            out = []
            for h in range(2 * pairs):
                m, l, acc = carry[h]
                s = jnp.where(seen, mm(ko_ref[w, pl.ds(h // 2 * 128, 128)], qs[h], 1, 1), NEG)
                top = jnp.maximum(m, jnp.max(s, axis=0, keepdims=True))
                fade = jnp.exp(m - top)
                e = jnp.exp(s - top)
                acc = acc * fade + mm(vt_ref[pl.ds(h * HEAD, HEAD), w], e.astype(BF), 1, 0)
                out.append((top, l * fade + jnp.sum(e, axis=0, keepdims=True), acc))
            return tuple(out)

        start = (
            jnp.full((1, size), NEG, F32), jnp.zeros((1, size), F32), jnp.zeros((HEAD, size), F32)
        )
        done = lax.fori_loop(first_ref[i], i + 1, step, (start,) * (2 * pairs))
        for t in range(pairs):
            both = []
            for h in (2 * t, 2 * t + 1):
                m, l, acc = done[h]
                both.append(acc / l)
                lse_ref[h : h + 1, r] = m + jnp.log(l)
            o_ref[r, pl.ds(t * 128, 128)] = jnp.concatenate(both, axis=0).T.astype(BF)


def attend(qkv, begin):
    rows, wide = qkv.shape[0], qkv.shape[1] // 3
    size = block_of(rows)
    half = jax.ShapeDtypeStruct((rows, wide), BF)
    return pl.pallas_call(
        attend_kernel,
        in_specs=[pl.BlockSpec(memory_space=pltpu.SMEM)] + [IN_VMEM] * 6,
        out_specs=[IN_VMEM] * 5,
        out_shape=[half] * 4 + [jax.ShapeDtypeStruct((wide // HEAD, rows), F32)],
        scratch_shapes=[pltpu.VMEM((wide, rows), BF)],
        compiler_params=pltpu.CompilerParams(vmem_limit_bytes=48 << 20),
        name="attend",
    )(begin[0, ::size] // size, qkv, *turn_tables(rows), begin)


def attend_back_work(ins, out_ref, scratch):
    q_ref, k_ref, v_ref, o_ref, do_ref, lse_ref, cos_ref, sin_ref, cosf_ref, sinf_ref, begin_ref = ins
    kt_ref, dq_ref, dk_ref, dv_ref = scratch
    rows, wide = q_ref.shape
    pairs, size = wide // 128, block_of(rows)
    tables = (cos_ref, sin_ref, cosf_ref, sinf_ref)
    left = lax.broadcasted_iota(jnp.int32, (size, 128), 1) < HEAD
    key_at = lax.broadcasted_iota(jnp.int32, (size, size), 0)
    query_at = lax.broadcasted_iota(jnp.int32, (1, size), 1)

    @pl.loop(0, rows // BLK)
    def _(i):
        r = pl.ds(pl.multiple_of(i * BLK, BLK), BLK)
        for t in range(pairs):
            w = pl.ds(t * 128, 128)
            kt_ref[w, r] = k_ref[r, w].astype(F32).T.astype(BF)
            dk_ref[r, w] = jnp.zeros((BLK, 128), F32)
            dv_ref[r, w] = jnp.zeros((BLK, 128), F32)

    @pl.loop(0, rows // size)
    def _(i):
        r = pl.ds(pl.multiple_of(i * size, size), size)
        qs, dos, deltas, lses = [], [], [], []
        for t in range(pairs):
            w = pl.ds(t * 128, 128)
            do = do_ref[r, w]
            qs += two_heads(q_ref[r, w], left)
            dos += two_heads(do, left)
            prod = (do.astype(F32) * o_ref[r, w].astype(F32)).T
            deltas += [jnp.sum(prod[:HEAD], axis=0, keepdims=True), jnp.sum(prod[HEAD:], axis=0, keepdims=True)]
            lses += [lse_ref[2 * t : 2 * t + 1, r], lse_ref[2 * t + 1 : 2 * t + 2, r]]
        begin = begin_ref[0:1, r]
        here = query_at + i * size

        def step(j, carry):
            w = pl.ds(pl.multiple_of(j * size, size), size)
            key = key_at + j * size
            seen = (key <= here) & (key >= begin)
            out = []
            for t in range(pairs):
                lanes = pl.ds(t * 128, 128)
                k, v = k_ref[w, lanes], v_ref[w, lanes]
                dk = dv = None
                for h in (2 * t, 2 * t + 1):
                    prob = jnp.exp(jnp.where(seen, mm(k, qs[h], 1, 1) - lses[h], NEG))
                    ds = (prob * (mm(v, dos[h], 1, 1) - deltas[h])).astype(BF)
                    out.append(carry[h] + mm(kt_ref[pl.ds(h * HEAD, HEAD), w], ds, 1, 0))
                    dk_h, dv_h = mm(ds, qs[h], 1, 0), mm(prob.astype(BF), dos[h], 1, 0)
                    dk, dv = (dk_h, dv_h) if dk is None else (dk + dk_h, dv + dv_h)
                dk_ref[w, lanes] += dk
                dv_ref[w, lanes] += dv
            return tuple(out)

        done = lax.fori_loop(0, i + 1, step, (jnp.zeros((HEAD, size), F32),) * (2 * pairs))
        for t in range(pairs):
            both = jnp.concatenate(done[2 * t : 2 * t + 2], axis=0)
            dq_ref[r, pl.ds(t * 128, 128)] = both.T * (HEAD**-0.5)

    @pl.loop(0, rows // BLK)
    def _(i):
        r = pl.ds(pl.multiple_of(i * BLK, BLK), BLK)
        for t in range(pairs):
            w = pl.ds(t * 128, 128)
            for part, value in enumerate((turn(dq_ref[r, w], i, tables, -1.0), turn(dk_ref[r, w], i, tables, -1.0), dv_ref[r, w])):
                out_ref[r, pl.ds(part * wide + t * 128, 128)] = value.astype(BF)


def attend_back(S, C, number, q, k, v, o, do, lse, begin, riders):
    rows, wide = q.shape

    def kernel(ride, ins, outs, scratch):
        greet(S, C, axes=ride.axes)
        ride.start()
        attend_back_work(ins, outs[0], scratch)
        ride.wait()

    args = [q, k, v, o, do, lse, *turn_tables(rows), begin]
    return comm(
        kernel, S, C, number, "attend_back", args, [IN_VMEM] * len(args),
        [(jax.ShapeDtypeStruct((rows, 3 * wide), BF), IN_VMEM)],
        [pltpu.VMEM((wide, rows), BF)] + [pltpu.VMEM((rows, wide), F32)] * 3,
        riders,
    )


def doc_begins(lengths_row, rows):
    row_ids = jnp.arange(rows, dtype=jnp.int32)
    ends = jnp.cumsum(lengths_row, dtype=jnp.int32)
    begins = ends - lengths_row
    inside = (row_ids[:, None] >= begins[None, :]) & (row_ids[:, None] < ends[None, :])
    return jnp.sum(jnp.where(inside, begins[None, :], 0), axis=1, dtype=jnp.int32)


def tiles_of(parts, lead):
    flat = jnp.concatenate([x.astype(F32).reshape(lead + (-1,)) for x in parts], axis=-1)
    flat = jnp.pad(flat, ((0, 0),) * len(lead) + ((0, 1024 - flat.shape[-1]),))
    return flat.reshape(lead + (8, 128))


def make_body(S, C, T):
    assert S == C

    def body(tokens, lengths, w_qkv, b_qkv, w_out, w_gateup, w_down, norm_gain, norm_bias, cotangent):
        p, z, c = lax.axis_index("shard"), lax.axis_index("ctx"), lax.axis_index("tp")
        R, D = tokens.shape
        n = R // T
        nb = D // (S * C)
        L = R * C

        def to_parts(x):
            return x.reshape(n, S, C, nb).transpose(2, 0, 1, 3).reshape(S, n, D // S)

        def parts(x):
            return x.reshape(n, S, D // S).swapaxes(0, 1)

        def unpermute(x):
            return x.reshape(x.shape[0], C, S, nb).swapaxes(1, 2).reshape(x.shape)

        def own(x):
            return lax.dynamic_slice_in_dim(x, (p * T + c) * n, n, 0)

        def half_of(x):
            return lax.dynamic_slice_in_dim(x, c * n, n, 0)

        def after(x, y):
            return lax.optimization_barrier((x, y))

        def over_ctx(w):
            return lax.all_gather(w.reshape(S * nb, -1), "ctx", axis=0, tiled=True)

        def sum_ctx(g):
            g = lax.psum_scatter(g.astype(BF), "ctx", scatter_dimension=0, tiled=True)
            return g.reshape(S, nb, -1)

        hn = w_qkv.shape[3] // S
        fn = w_gateup.shape[3] // S
        heads = hn // HEAD
        nf = HEAD // (S * C)

        tile = tiles_of((norm_gain[0].reshape(-1), norm_bias[0].reshape(-1), b_qkv[0].reshape(-1), lengths[0]), ())
        small, _, tok, wq, wo = exchange(
            S, C, T, 0,
            [
                ("shard", w_qkv[0].reshape(nb, 3, S, hn).transpose(2, 0, 1, 3).reshape(S, nb, 3 * hn)),
                ("shard", w_out[0].reshape(S, hn, nb).swapaxes(1, 2)),
            ],
            jnp.broadcast_to(tile, (C, S, 8, 128)),
            to_parts(half_of(tokens)),
        )
        wq = over_ctx(wq)
        tok, wo, wg, wd, cot = gather_columns(
            S, C, T, 1, tok,
            [
                ("all", wo.reshape(S * nb, hn)),
                ("shard", w_gateup[0].reshape(nb, 2, S, fn).transpose(2, 0, 1, 3).reshape(S, nb, 2 * fn)),
                ("shard", w_down[0].reshape(S, fn, nb).swapaxes(1, 2)),
                ("shard", to_parts(half_of(cotangent))),
            ],
        )
        wo, wg, wd = wo.reshape(D, hn), over_ctx(wg), over_ctx(wd)

        small = lax.dynamic_index_in_dim(small, c, 0, keepdims=False).reshape(C, S, 1024)
        norms = small[:, :, : 4 * nb].reshape(C * S, 4, nb).swapaxes(0, 1).reshape(4, D)
        gains, shifts = norms[:2], norms[2:]
        nbias = 3 * S * heads * nf
        bias = small[:, :, 4 * nb : 4 * nb + nbias].reshape(C, S, 3, S * heads, nf)
        bias = lax.dynamic_slice_in_dim(bias, p * heads, heads, 3)
        bias = bias.transpose(2, 3, 1, 0, 4).reshape(1, 3 * hn)
        docs = lengths.shape[1]
        lengths_row = lax.dynamic_index_in_dim(
            small[0, :, 4 * nb + nbias : 4 * nb + nbias + docs], z, 0, keepdims=False
        ).astype(jnp.int32)
        begin = doc_begins(lengths_row, L)
        begin = begin[None, :]

        n1 = (norm_of(tok.astype(F32))[0] * gains[0] + shifts[0]).astype(BF)
        own_tok = own(tok)
        qkv = mm(n1, wq, 1, 0) + bias
        q, k, v, o, lse = attend(qkv, begin)
        mid, n2, cot = sum_norm_gather(S, C, T, 2, o, wo, own_tok, gains[1:], shifts[1:], [("ctx", cot)])
        cot, n2 = after(cot, n2)
        (gb,) = gather_columns(S, C, T, 4, cot)
        gu = mm(n2, wg, 1, 0)
        gate, up = gu[:, :fn], gu[:, fn:]
        logistic = jax.nn.sigmoid(gate)
        act = (gate * logistic * up).astype(BF)
        gw_down = mm(gb, act, 0, 0).astype(BF)
        wd, gw_down = after(wd, gw_down)
        gw_down = sum_ctx(gw_down)

        dact = mm(gb, wd, 1, 0)
        dgate = dact * up * logistic * (1.0 + gate * (1.0 - logistic))
        dup = dact * gate * logistic
        dgu = jnp.concatenate((dgate, dup), axis=1).astype(BF)
        gw_gateup = mm(n2, dgu, 0, 0).astype(BF)
        act, gw_gateup = after(act, gw_gateup)
        gw_gateup = sum_ctx(gw_gateup)
        (got,) = scatter(S, C, T, 5, act, wd)
        out = parts((mid + got).astype(BF))
        dgu, out = after(dgu, out)
        dmid, gb1, stats2, out = sum_back_gather(
            S, C, T, 6, dgu, wg, mid, own(gb), gains[1:], [("shard", out)]
        )
        gw_out = mm(gb1, o, 0, 0).astype(BF)
        gb1, gw_out = after(gb1, gw_out)
        gw_out = sum_ctx(gw_out)
        do = mm(gb1, wo, 1, 0).astype(BF)
        dqkv, gw_gateup, gw_down, out = attend_back(
            S, C, 11, q, k, v, o, do, lse, begin, [("shard", gw_gateup), ("shard", gw_down), ("ctx", out)]
        )
        gw_qkv = mm(n1, dqkv, 0, 0).astype(BF)
        dqkv, gw_qkv = after(dqkv, gw_qkv)
        gw_qkv = sum_ctx(gw_qkv)
        gtok, stats1, gw_out, out = sum_back_leave(
            S, C, T, 8, dqkv, wq, own_tok, dmid, gains[:1], [("shard", gw_out), ("shard", out)]
        )
        gtok = unpermute(gtok).astype(F32)
        gbias = jnp.sum(dqkv.astype(F32), axis=0)
        tiles = tiles_of(
            (
                jnp.stack((stats1[0], stats2[0], stats1[1], stats2[1])).reshape(4, C, S, nb).transpose(1, 2, 0, 3),
                gbias.reshape(3, heads, S, C, nf).transpose(3, 2, 0, 1, 4),
            ),
            (C, S),
        )
        small, gw_qkv, mate = exchange(S, C, T, 10, [("shard", gw_qkv), ("tp", out)], tiles)
        out = jnp.where(c == 0, jnp.stack((out, mate)), jnp.stack((mate, out)))
        out = unpermute(out.transpose(0, 2, 1, 3).reshape(R, D))
        small = small.reshape(T, C, S, 1024)
        norms = jnp.sum(small[..., : 4 * nb], axis=(0, 1, 2)).reshape(1, 4, nb)
        gbias = lax.dynamic_index_in_dim(small, c, 0, keepdims=False)[..., 4 * nb : 4 * nb + 3 * heads * nf]
        gbias = jnp.sum(gbias, axis=0).reshape(S, 3, heads, nf).swapaxes(0, 1).reshape(b_qkv.shape)

        return (
            out,
            gtok,
            gw_qkv.astype(F32).reshape(S, nb, 3, hn).transpose(1, 2, 0, 3).reshape(w_qkv.shape),
            gbias,
            gw_out.astype(F32).swapaxes(1, 2).reshape(w_out.shape),
            gw_gateup.astype(F32).reshape(S, nb, 2, fn).transpose(1, 2, 0, 3).reshape(w_gateup.shape),
            gw_down.astype(F32).swapaxes(1, 2).reshape(w_down.shape),
            norms[:, :2],
            norms[:, 2:],
        )

    return body


def solution(mesh):
    both = ("shard", "ctx")
    specs = (
        P(None, both, None, "tp"),
        P(None, None, "tp", both),
        P(None, "tp", both),
        P(None, both, None, "tp"),
        P(None, "tp", both),
        P(None, None, both),
        P(None, None, both),
    )
    return jax.shard_map(
        make_body(mesh.shape["shard"], mesh.shape["ctx"], mesh.shape["tp"]),
        mesh=mesh,
        in_specs=(P(both, None), P("shard", None)) + specs + (P(both, None),),
        out_specs=(P(both, None), P(both, None)) + specs,
        check_vma=False,
    )
```

```python
import functools

import jax
import jax.numpy as jnp
import numpy as np
from jax import lax
from jax.experimental import pallas as pl
from jax.experimental.pallas import tpu as pltpu
from jax.sharding import PartitionSpec as P

HEAD = 64
ROT = 16
EPS = 1e-05
NEG = -1e30
BASE = 10000.0
BF = jnp.bfloat16
F32 = jnp.float32
BLK = 256
MESH = pl.DeviceIdType.MESH
DMA = pltpu.SemaphoreType.DMA
ANY = pl.BlockSpec(memory_space=pl.ANY)
IN_VMEM = pl.BlockSpec(memory_space=pltpu.VMEM)


def mm(a, b, ca, cb):
    return lax.dot_general(a, b, (((ca,), (cb,)), ((), ())), preferred_element_type=F32)


def remote(src, dst, send, recv, where):
    return pltpu.make_async_remote_copy(
        src_ref=src, dst_ref=dst, send_sem=send, recv_sem=recv, device_id=where, device_id_type=MESH
    )


def here():
    return lax.axis_index("shard"), lax.axis_index("ctx"), lax.axis_index("tp")


class Riders:
    def __init__(self, S, C, riders):
        self.S, self.C = S, C
        self.axes = [axis for axis, _ in riders]
        self.arrays = [x for _, x in riders]
        self.shapes = [
            jax.ShapeDtypeStruct((C,) + x.shape if axis == "all" else x.shape, x.dtype) for axis, x in riders
        ]
        count, most = len(riders), max(S, C) - 1
        self.scratch = [DMA((count, most)), DMA((count, most)), DMA((count,))] if count else []

    def bind(self, ins, outs, sems):
        self.ins, self.outs, self.sems = ins, outs, sems

    def start(self):
        p, z, c = here()
        self.moves = []
        for n, axis in enumerate(self.axes):
            src, dst = self.ins[n], self.outs[n]
            send, recv, own = self.sems
            if axis == "tp":
                copies = [remote(src, dst, send.at[n, 0], recv.at[n, 0], {"tp": 1 - c})]
            elif axis == "all":
                copies = [
                    remote(src, dst.at[z], send.at[n, k - 1], recv.at[n, k - 1], {"ctx": (z + k) % self.C})
                    for k in range(1, self.C)
                ]
                copies.append(pltpu.make_async_copy(src, dst.at[z], own.at[n]))
            else:
                size, me = (self.S, p) if axis == "shard" else (self.C, z)
                copies = [
                    remote(src.at[(me + k) % size], dst.at[me], send.at[n, k - 1], recv.at[n, k - 1], {axis: (me + k) % size})
                    for k in range(1, size)
                ]
                copies.append(pltpu.make_async_copy(src.at[me], dst.at[me], own.at[n]))
            for copy in copies:
                copy.start()
            self.moves += copies

    def wait(self):
        for copy in self.moves:
            copy.wait()


def greet(S, C, mates=(), line=False, other=False, axes=()):
    p, z, c = here()
    peers = [{"shard": q} for q in ([(p + k) % S for k in range(1, S)] if "shard" in axes else mates)]
    if line or "ctx" in axes or "all" in axes:
        peers += [{"ctx": (z + k) % C} for k in range(1, C)]
    if other or "tp" in axes:
        peers.append({"tp": 1 - c})
    barrier = pltpu.get_barrier_semaphore()
    for where in peers:
        pl.semaphore_signal(barrier, inc=1, device_id=where, device_id_type=MESH)
    pl.semaphore_wait(barrier, len(peers))


def comm(kernel, S, C, number, name, args, in_specs, outs, scratch, riders=()):
    ride = Riders(S, C, riders)
    na, nr, no, ns = len(args), len(ride.axes), len(outs), len(scratch)

    def body(*refs):
        ins, refs = refs[:na], refs[na:]
        rins, refs = refs[:nr], refs[nr:]
        os, refs = refs[:no], refs[no:]
        routs, refs = refs[:nr], refs[nr:]
        ride.bind(rins, routs, refs[ns:])
        kernel(ride, ins, os, refs[:ns])

    return pl.pallas_call(
        body,
        out_shape=[shape for shape, _ in outs] + ride.shapes,
        in_specs=list(in_specs) + [IN_VMEM] * nr,
        out_specs=[spec for _, spec in outs] + [ANY] * nr,
        scratch_shapes=list(scratch) + ride.scratch,
        compiler_params=pltpu.CompilerParams(
            collective_id=number, has_side_effects=True, vmem_limit_bytes=56 << 20
        ),
        cost_estimate=pl.CostEstimate(flops=0, bytes_accessed=120_000_000, transcendentals=0),
        name=name,
    )(*args, *ride.arrays)


def exchange(S, C, T, number, riders, tiles, rows=None):
    def kernel(ride, ins, outs, scratch):
        tile, got = ins[0], outs[0]
        send, recv, bsend, brecv, own = scratch[:5]
        p, z, c = here()
        everyone = [(i, j) for i in range(C) for j in range(S) if i or j]
        barrier = pltpu.get_barrier_semaphore()
        peers = [{"shard": (p + j) % S, "ctx": (z + i) % C} for i, j in everyone] + [{"tp": 1 - c}]
        for where in peers:
            pl.semaphore_signal(barrier, inc=1, device_id=where, device_id_type=MESH)
        pl.semaphore_wait(barrier, len(peers))

        def turn_over(source, target, k, axis, size, me):
            ssem, rsem, local = scratch[5:]
            hop = [pltpu.make_async_copy(source.at[me], target.at[me], local.at[k])]
            for j in range(1, size):
                q = (me + j) % size
                hop.append(remote(source.at[q], target.at[me], ssem.at[k, j - 1], rsem.at[k, j - 1], {axis: q}))
            for copy in hop:
                copy.start()
            return hop

        if rows is not None:
            first = turn_over(ins[1], outs[1], 0, "shard", S, p)
        local = pltpu.make_async_copy(tile.at[z, p], got.at[c, z, p], own)
        local.start()
        copies = []
        for at, (where, (i, j)) in enumerate(zip(peers, everyone)):
            q, g = (p + j) % S, (z + i) % C
            copies.append(remote(tile.at[g, q], got.at[c, z, p], send.at[at], recv.at[at], where))
            copies[-1].start()
        ride.start()
        if rows is not None:
            for copy in first:
                copy.wait()
            second = turn_over(outs[1], outs[2], 1, "ctx", C, z)
        local.wait()
        for copy in copies:
            copy.wait()
        back = remote(got.at[c], got.at[c], bsend, brecv, {"tp": 1 - c})
        back.start()
        back.wait_send()
        remote(got.at[1 - c], got.at[1 - c], bsend, brecv, {"tp": 1 - c}).wait_recv()
        if rows is not None:
            for copy in second:
                copy.wait()
        ride.wait()

    count, most = C * S - 1, max(S, C) - 1
    args, outs = [tiles], [(jax.ShapeDtypeStruct((T,) + tiles.shape, tiles.dtype), ANY)]
    scratch = [DMA((count,)), DMA((count,)), DMA, DMA, DMA]
    if rows is not None:
        args.append(rows)
        outs += [(jax.ShapeDtypeStruct(rows.shape, rows.dtype), IN_VMEM)] * 2
        scratch += [DMA((2, most)), DMA((2, most)), DMA((2,))]
    return comm(kernel, S, C, number, "exchange", args, [IN_VMEM] * len(args), outs, scratch, riders)


def plane(S):
    p, _, c = here()
    B = S // 2
    a, b = p // B, p % B
    return a, b, [a * B + (b + j) % B for j in range(1, B)], (1 - a) * B + b


def spread_sems(S):
    count = 4 + 4 * (S // 2 - 1)
    return [DMA((2 * count,)), DMA((2 * count,))]


def spread(S, own, region, send, recv):
    p, _, c = here()
    B = S // 2
    a, b, rows, col = plane(S)
    rows, col, other = [{"shard": q} for q in rows], {"shard": col}, {"tp": 1 - c}
    per = 4 + 4 * (B - 1)
    OWN, ROW, COL, VIA_COL, VIA_ROW = 0, 2, 2 + 2 * (B - 1), 4 + 2 * (B - 1), 4 + 3 * (B - 1)
    started = []

    def push(q, h, sem, where, first=False):
        view = region(q, h, c)
        copy = remote(own(h) if first else view, view, send.at[sem], recv.at[sem], where)
        copy.start()
        started.append(copy)

    def came(q, h, sem, core):
        view = region(q, h, core)
        remote(view, view, send.at[sem], recv.at[sem], other).wait_recv()

    for h in range(2):
        for j in range(1, B):
            push(p, h, ROW + 2 * (j - 1) + h, rows[j - 1], True)
    for h in (1, 0):
        push(p, h, COL + h, col, True)
    for h in range(2):
        push(p, h, per + OWN + h, other, True)

    def from_row(j, h):
        q = a * B + (b - j) % B
        came(q, h, ROW + 2 * (j - 1) + h, c)
        push(q, h, per + ROW + 2 * (j - 1) + h, other)
        return q

    def from_col(h):
        q = (1 - a) * B + b
        came(q, h, COL + h, c)
        push(q, h, per + COL + h, other)
        return q

    for j in range(1, B):
        q = from_row(j, 0)
        push(q, 0, VIA_COL + j - 1, col)
    q = from_col(1)
    for j in range(1, B):
        push(q, 1, VIA_ROW + j - 1, rows[j - 1])
    for j in range(1, B):
        from_row(j, 1)
    from_col(0)
    for j in range(1, B):
        q = (1 - a) * B + (b - j) % B
        came(q, 0, VIA_COL + j - 1, c)
        push(q, 0, per + VIA_COL + j - 1, other)
        came(q, 1, VIA_ROW + j - 1, c)
        push(q, 1, per + VIA_ROW + j - 1, other)
    for h in range(2):
        came(p, h, per + OWN + h, 1 - c)
        came((1 - a) * B + b, h, per + COL + h, 1 - c)
    for j in range(1, B):
        for h in range(2):
            came(a * B + (b - j) % B, h, per + ROW + 2 * (j - 1) + h, 1 - c)
        q = (1 - a) * B + (b - j) % B
        came(q, 0, per + VIA_COL + j - 1, 1 - c)
        came(q, 1, per + VIA_ROW + j - 1, 1 - c)
    for copy in started:
        copy.wait_send()


def gather_columns(S, C, T, number, x, riders=()):
    _, n, wide = x.shape

    def kernel(ride, ins, outs, scratch):
        (x_ref,), (out_ref,), (send, recv, own) = ins, outs, scratch
        p, _, c = here()
        _, _, rows, col = plane(S)

        def region(q, h, core):
            part = pl.ds(pl.multiple_of(q * wide, 128), wide)
            return out_ref.at[pl.ds(h * (C // 2), C // 2), core, :, part]

        local = [
            pltpu.make_async_copy(x_ref.at[pl.ds(h * (C // 2), C // 2)], region(p, h, c), own.at[h]) for h in range(2)
        ]
        for copy in local:
            copy.start()
        greet(S, C, rows + [col], other=True, axes=ride.axes)
        ride.start()
        spread(S, lambda h: x_ref.at[pl.ds(h * (C // 2), C // 2)], region, send, recv)
        for copy in local:
            copy.wait()
        ride.wait()

    out, *rest = comm(
        kernel, S, C, number, "gather_columns", [x], [IN_VMEM],
        [(jax.ShapeDtypeStruct((C, T, n, wide * S), x.dtype), ANY)], spread_sems(S) + [DMA((2,))], riders,
    )
    return [out.reshape(C * T * n, wide * S)] + rest


CHUNK = 512
ROWS = 32


def sum_scratch(S, n, D):
    half, B = n // 2, S // 2

    def vm(*shape):
        return pltpu.VMEM(shape, BF)

    return [
        vm(S, n, D), vm(S, n, D), vm(S, n, D), vm(B - 1, 2, half, D), vm(B, half, D),
        vm(B - 1, half, D), vm(half, D), vm(half, D), vm(B - 1, half, D),
        DMA((S,)), DMA((S,)), DMA((B - 1, 2)), DMA((B - 1, 2)), DMA((B,)), DMA((B,)), DMA((B,)), DMA((B,)),
    ]


def sum_over_plane(S, T, x_ref, w_ref, out_ref, scratch, meanwhile=None):
    away, sib, mine, row1, col1, row2, col2, to_col, to_row = scratch[:9]
    asend, arecv, rsend, rrecv, csend, crecv, fsend, frecv = scratch[9:]
    n, D = out_ref.shape
    half, B = n // 2, S // 2
    _, _, c = here()
    a, b, rows, col = plane(S)
    rows, col, other = [{"shard": q} for q in rows], {"shard": col}, {"tp": 1 - c}

    def chip(e):
        return ((a + e // B) % 2) * B + (b + e % B) % B

    def product(e, core, store):
        x = x_ref[chip(e) * T + core]

        def column(j, _):
            w = pl.ds(pl.multiple_of(j * CHUNK, CHUNK), CHUNK)
            store(w, mm(x, w_ref[w, :], 1, 1))
            return 0

        lax.fori_loop(0, D // CHUNK, column, 0)

    def to_other(e):
        return remote(away.at[e], sib.at[e], asend.at[e], arecv.at[e], other)

    def first(i, _):
        e = S - 1 - i

        def store(w, value):
            away[e, :, w] = value.astype(BF)

        product(e, 1 - c, store)
        to_other(e).start()
        return 0

    lax.fori_loop(0, S, first, 0)

    top, low = pl.ds(0, half), pl.ds(half, half)
    started = []

    def push(src, dst, send, recv, where):
        copy = remote(src, dst, send, recv, where)
        copy.start()
        started.append(copy)

    for e in range(S - 1, -1, -1):
        to_other(e).wait()

        def store(w, value):
            value = value + sib[e, :, w].astype(F32)
            if e:
                mine[e, :, w] = value.astype(BF)
            else:
                out_ref[:, w] = value

        product(e, c, store)
        j = e % B
        if e > B:
            push(mine.at[e, top], row1.at[j - 1, 1], rsend.at[j - 1, 1], rrecv.at[j - 1, 1], rows[j - 1])
            push(mine.at[e, low], col1.at[j], csend.at[j], crecv.at[j], col)
        elif e == B:
            push(mine.at[e, low], col1.at[0], csend.at[0], crecv.at[0], col)
        elif e:
            push(mine.at[e, top], row1.at[j - 1, 0], rsend.at[j - 1, 0], rrecv.at[j - 1, 0], rows[j - 1])

    def came(ref, send, recv):
        remote(ref, ref, send, recv, other).wait_recv()

    if meanwhile is not None:
        meanwhile()
    total = mine[B, top, :].astype(F32)
    for j in range(1, B):
        came(row1.at[j - 1, 1], rsend.at[j - 1, 1], rrecv.at[j - 1, 1])
        total = total + row1[j - 1, 1].astype(F32)
    to_col[...] = total.astype(BF)
    push(to_col, col2, fsend.at[0], frecv.at[0], col)
    for j in range(1, B):
        came(col1.at[j], csend.at[j], crecv.at[j])
        to_row[j - 1] = (mine[j, low, :].astype(F32) + col1[j].astype(F32)).astype(BF)
        push(to_row.at[j - 1], row2.at[j - 1], fsend.at[j], frecv.at[j], rows[j - 1])
    came(col1.at[0], csend.at[0], crecv.at[0])
    upper, lower = out_ref[top, :], out_ref[low, :] + col1[0].astype(F32)
    for j in range(1, B):
        came(row1.at[j - 1, 0], rsend.at[j - 1, 0], rrecv.at[j - 1, 0])
        upper = upper + row1[j - 1, 0].astype(F32)
    came(col2, fsend.at[0], frecv.at[0])
    out_ref[top, :] = upper + col2[...].astype(F32)
    for j in range(1, B):
        came(row2.at[j - 1], fsend.at[j], frecv.at[j])
        lower = lower + row2[j - 1].astype(F32)
    out_ref[low, :] = lower
    for copy in started:
        copy.wait_send()


def sum_and_gates(S, C, T, number, act, wd, gb, gu):
    L, K = act.shape
    D, n = wd.shape[0], L // (S * T)

    def kernel(ride, ins, outs, scratch):
        act_ref, wd_ref, gb_ref, gu_ref = ins
        out_ref, dgu_ref = outs
        _, _, rows, col = plane(S)
        greet(S, C, rows + [col], other=True)

        def meanwhile():
            @pl.loop(0, L // BLK)
            def _(i):
                r = pl.ds(pl.multiple_of(i * BLK, BLK), BLK)
                dact = mm(gb_ref[r, :], wd_ref[...], 1, 0)
                both = gu_ref[r, :]
                gate, up = both[:, :K], both[:, K:]
                s = jax.nn.sigmoid(gate)
                dgate = dact * up * s * (1.0 + gate * (1.0 - s))
                dgu_ref[r, :] = jnp.concatenate((dgate, dact * gate * s), axis=1).astype(BF)

        sum_over_plane(S, T, act_ref, wd_ref, out_ref, scratch, meanwhile)

    return comm(
        kernel, S, C, number, "sum_and_gates", [act.reshape(S * T, n, K), wd, gb, gu], [IN_VMEM] * 4,
        [(jax.ShapeDtypeStruct((n, D), F32), IN_VMEM), (jax.ShapeDtypeStruct((L, 2 * K), BF), IN_VMEM)],
        sum_scratch(S, n, D),
    )


def row_blocks(n, work):
    @pl.loop(0, n // ROWS)
    def _(i):
        work(pl.ds(pl.multiple_of(i * ROWS, ROWS), ROWS))


def norm_of(v):
    center = v - jnp.mean(v, axis=-1, keepdims=True)
    inverse = lax.rsqrt(jnp.mean(center * center, axis=-1, keepdims=True) + EPS)
    return center * inverse, inverse


def norm_back(v, g, gain, stats_ref):
    normal, inverse = norm_of(v)
    e = g * gain
    stats_ref[0:1, :] += jnp.sum(g * normal, axis=0, keepdims=True)
    stats_ref[1:2, :] += jnp.sum(g, axis=0, keepdims=True)
    return inverse * (
        e - jnp.mean(e, axis=-1, keepdims=True) - normal * jnp.mean(e * normal, axis=-1, keepdims=True)
    )


def spread_rows(S, T, src, out_ref, send, recv, own):
    p, _, c = here()
    half = src.shape[0] // 2
    local = pltpu.make_async_copy(src, out_ref.at[p * T + c], own)
    local.start()
    spread(
        S,
        lambda h: src.at[pl.ds(h * half, half)],
        lambda q, h, core: out_ref.at[q * T + core, pl.ds(h * half, half)],
        send,
        recv,
    )
    local.wait()


def sum_norm_gather(S, C, T, number, x, w, residual, gain, shift, riders=()):
    L, K = x.shape
    D, n = w.shape[0], L // (S * T)

    def kernel(ride, ins, outs, scratch):
        x_ref, w_ref, res_ref, gain_ref, shift_ref = ins
        v_ref, out_ref = outs
        acc, low, send, recv, own = scratch[:5]
        _, _, rows, col = plane(S)
        greet(S, C, rows + [col], other=True, axes=ride.axes)
        ride.start()
        sum_over_plane(S, T, x_ref, w_ref, acc, scratch[5:])

        def work(r):
            v = res_ref[r, :].astype(F32) + acc[r, :]
            v_ref[r, :] = v
            low[r, :] = (norm_of(v)[0] * gain_ref[...] + shift_ref[...]).astype(BF)

        row_blocks(n, work)
        spread_rows(S, T, low, out_ref, send, recv, own)
        ride.wait()

    v, out, *rest = comm(
        kernel, S, C, number, "sum_norm_gather", [x.reshape(S * T, n, K), w, residual, gain, shift], [IN_VMEM] * 5,
        [(jax.ShapeDtypeStruct((n, D), F32), IN_VMEM), (jax.ShapeDtypeStruct((S * T, n, D), BF), ANY)],
        [pltpu.VMEM((n, D), F32), pltpu.VMEM((n, D), BF)] + spread_sems(S) + [DMA] + sum_scratch(S, n, D),
        riders,
    )
    return [v, out.reshape(L, D)] + rest


def sum_back_gather(S, C, T, number, x, w, v, residual, gain, riders=()):
    L, K = x.shape
    D, n = w.shape[0], L // (S * T)

    def kernel(ride, ins, outs, scratch):
        x_ref, w_ref, in_ref, res_ref, gain_ref = ins
        v_ref, out_ref, stats = outs
        acc, low, send, recv, own = scratch[:5]
        _, _, rows, col = plane(S)
        greet(S, C, rows + [col], other=True, axes=ride.axes)
        ride.start()
        sum_over_plane(S, T, x_ref, w_ref, acc, scratch[5:])
        stats[...] = jnp.zeros_like(stats)

        def work(r):
            g = res_ref[r, :].astype(F32) + norm_back(in_ref[r, :], acc[r, :], gain_ref[...], stats)
            v_ref[r, :] = g
            low[r, :] = g.astype(BF)

        row_blocks(n, work)
        spread_rows(S, T, low, out_ref, send, recv, own)
        ride.wait()

    g, out, stats, *rest = comm(
        kernel, S, C, number, "sum_back_gather", [x.reshape(S * T, n, K), w, v, residual, gain], [IN_VMEM] * 5,
        [
            (jax.ShapeDtypeStruct((n, D), F32), IN_VMEM), (jax.ShapeDtypeStruct((S * T, n, D), BF), ANY),
            (jax.ShapeDtypeStruct((2, D), F32), IN_VMEM),
        ],
        [pltpu.VMEM((n, D), F32), pltpu.VMEM((n, D), BF)] + spread_sems(S) + [DMA] + sum_scratch(S, n, D),
        riders,
    )
    return [g, out.reshape(L, D), stats] + rest


def sum_back(S, C, T, number, x, w, v, residual, gain, riders=()):
    L, K = x.shape
    D, n = w.shape[0], L // (S * T)

    def kernel(ride, ins, outs, scratch):
        x_ref, w_ref, in_ref, res_ref, gain_ref = ins
        low, stats = outs
        acc = scratch[0]
        _, _, rows, col = plane(S)
        greet(S, C, rows + [col], other=True, axes=ride.axes)
        ride.start()
        sum_over_plane(S, T, x_ref, w_ref, acc, scratch[1:])
        stats[...] = jnp.zeros_like(stats)

        def work(r):
            g = res_ref[r, :] + norm_back(in_ref[r, :].astype(F32), acc[r, :], gain_ref[...], stats)
            low[r, :] = g.astype(BF)

        row_blocks(n, work)
        ride.wait()

    return comm(
        kernel, S, C, number, "sum_back", [x.reshape(S * T, n, K), w, v, residual, gain], [IN_VMEM] * 5,
        [(jax.ShapeDtypeStruct((n, D), BF), IN_VMEM), (jax.ShapeDtypeStruct((2, D), F32), IN_VMEM)],
        [pltpu.VMEM((n, D), F32)] + sum_scratch(S, n, D),
        riders,
    )


def finish(S, C, T, number, x, stats, bias, riders):
    n, D = x.shape
    wide, lines = D // S, bias.shape[1] // 128
    nb = D // (S * C)
    count = sum(y.shape[0] for y in stats)
    tall = -(-(count + lines) // 8) * 8
    many = C * S - 1

    def kernel(ride, ins, outs, scratch):
        x_ref, stat_refs, bias_ref = ins[0], ins[1:-1], ins[-1]
        out_ref, got = outs
        buf, buf2, tile, s1, r1, s2, r2, s3, r3, s4, r4, own, tsend, trecv, bsend, brecv = scratch
        p, z, c = here()
        other = {"tp": 1 - c}
        everyone = [(i, j) for i in range(C) for j in range(S) if i or j]
        peers = [{"shard": (p + j) % S, "ctx": (z + i) % C} for i, j in everyone]
        barrier = pltpu.get_barrier_semaphore()
        for where in peers + [other]:
            pl.semaphore_signal(barrier, inc=1, device_id=where, device_id_type=MESH)
        pl.semaphore_wait(barrier, len(peers) + 1)

        def part(q):
            return pl.ds(pl.multiple_of(q * wide, 128), wide)

        def turn_over(source, target, send, recv, local, size, me, axis):
            hop = [pltpu.make_async_copy(source(me), target, local)]
            for k in range(1, size):
                q = (me + k) % size
                hop.append(remote(source(q), target, send.at[k - 1], recv.at[k - 1], {axis: q}))
            for copy in hop:
                copy.start()
            return hop

        hop = turn_over(lambda q: x_ref.at[:, part(q)], buf.at[p], s1, r1, own.at[0], S, p, "shard")
        ride.start()
        tile[...] = jnp.zeros_like(tile)
        at = 0
        for ref in stat_refs:
            tile[at : at + ref.shape[0], :] = ref[...]
            at += ref.shape[0]
        for k in range(lines):
            for block in range(D // 128):
                tile[at + k : at + k + 1, pl.ds(block * 128, 128)] = bias_ref[:, pl.ds(k * 128, 128)]

        def columns(g, q):
            return tile.at[:, pl.ds(pl.multiple_of((g * S + q) * nb // 128 * 128, 128), 128)]

        small = [pltpu.make_async_copy(columns(z, p), got.at[c, z, p], own.at[3])]
        for k, (where, (i, j)) in enumerate(zip(peers, everyone)):
            small.append(
                remote(columns((z + i) % C, (p + j) % S), got.at[c, z, p], tsend.at[k], trecv.at[k], where)
            )
        for copy in small:
            copy.start()
        for copy in hop:
            copy.wait()
        hop = turn_over(lambda q: buf.at[q], buf2.at[z], s2, r2, own.at[1], C, z, "ctx")
        for copy in small:
            copy.wait()
        back = remote(got.at[c], got.at[c], bsend, brecv, other)
        back.start()
        for copy in hop:
            copy.wait()
        for copy in turn_over(lambda q: buf2.at[q], out_ref.at[c, :, part(p)], s3, r3, own.at[2], S, p, "shard"):
            copy.wait()
        last = remote(out_ref.at[c], out_ref.at[c], s4, r4, other)
        last.start()
        back.wait_send()
        remote(got.at[1 - c], got.at[1 - c], bsend, brecv, other).wait_recv()
        last.wait_send()
        remote(out_ref.at[1 - c], out_ref.at[1 - c], s4, r4, other).wait_recv()
        ride.wait()

    args = [x, *stats, bias]
    out, got, *rest = comm(
        kernel, S, C, number, "finish", args, [IN_VMEM] * len(args),
        [(jax.ShapeDtypeStruct((T, n, D), BF), ANY), (jax.ShapeDtypeStruct((T, C, S, tall, 128), F32), ANY)],
        [
            pltpu.VMEM((S, n, wide), BF), pltpu.VMEM((C, n, wide), BF), pltpu.VMEM((tall, D), F32),
            DMA((S - 1,)), DMA((S - 1,)), DMA((C - 1,)), DMA((C - 1,)), DMA((S - 1,)), DMA((S - 1,)),
            DMA, DMA, DMA((4,)), DMA((many,)), DMA((many,)), DMA, DMA,
        ],
        riders,
    )
    return [out.reshape(T * n, D), got] + rest


def turn_tables(rows):
    feature = np.arange(128) % HEAD
    freq = np.where(feature < ROT, BASE ** (-2.0 * (feature % (ROT // 2)) / ROT), 0.0)
    near = np.arange(BLK)[:, None] * freq
    far = np.arange(0, rows, BLK)[:, None] * freq
    return [jnp.asarray(f(x), F32) for x in (near, far) for f in (np.cos, np.sin)]


def turn(x, i, tables, sign):
    cos, sin, cos_far, sin_far = tables
    far_cos, far_sin = cos_far[pl.ds(i, 1), :], sin_far[pl.ds(i, 1), :]
    cos_t = cos[...] * far_cos - sin[...] * far_sin
    sin_t = sin[...] * far_cos + cos[...] * far_sin
    ahead = lax.broadcasted_iota(jnp.int32, x.shape, 1) % HEAD < ROT // 2
    partner = jnp.where(ahead, -pltpu.roll(x, 128 - ROT // 2, 1), pltpu.roll(x, ROT // 2, 1))
    return x * cos_t + partner * (sin_t * sign)


def two_heads(x, left):
    zero = jnp.zeros_like(x)
    return [jnp.where(left, x, zero), jnp.where(left, zero, x)]


def block_of(rows):
    return next(size for size in (512, 256) if rows % size == 0)


def attend_kernel(
    first_ref, qkv_ref, cos_ref, sin_ref, cosf_ref, sinf_ref, begin_ref,
    qo_ref, ko_ref, vo_ref, o_ref, lse_ref, vt_ref,
):
    rows, wide = qo_ref.shape
    pairs, size = wide // 128, block_of(rows)
    tables = (cos_ref, sin_ref, cosf_ref, sinf_ref)
    left = lax.broadcasted_iota(jnp.int32, (size, 128), 1) < HEAD
    key_at = lax.broadcasted_iota(jnp.int32, (size, size), 0)
    query_at = lax.broadcasted_iota(jnp.int32, (1, size), 1)

    @pl.loop(0, rows // BLK)
    def _(i):
        r = pl.ds(pl.multiple_of(i * BLK, BLK), BLK)
        for t in range(pairs):
            w = pl.ds(t * 128, 128)
            q, k, v = (qkv_ref[r, pl.ds(part * wide + t * 128, 128)] for part in range(3))
            qo_ref[r, w] = turn(q, i, tables, 1.0).astype(BF) * jnp.asarray(HEAD**-0.5, BF)
            ko_ref[r, w] = turn(k, i, tables, 1.0).astype(BF)
            vo_ref[r, w] = v.astype(BF)
            vt_ref[w, r] = v.T.astype(BF)

    @pl.loop(0, rows // size)
    def _(i):
        r = pl.ds(pl.multiple_of(i * size, size), size)
        qs = sum((two_heads(qo_ref[r, pl.ds(t * 128, 128)], left) for t in range(pairs)), [])
        begin = begin_ref[0:1, r]
        here = query_at + i * size

        def step(j, carry):
            w = pl.ds(pl.multiple_of(j * size, size), size)
            key = key_at + j * size
            seen = (key <= here) & (key >= begin)
            out = []
            for h in range(2 * pairs):
                m, l, acc = carry[h]
                s = jnp.where(seen, mm(ko_ref[w, pl.ds(h // 2 * 128, 128)], qs[h], 1, 1), NEG)
                top = jnp.maximum(m, jnp.max(s, axis=0, keepdims=True))
                fade = jnp.exp(m - top)
                e = jnp.exp(s - top)
                acc = acc * fade + mm(vt_ref[pl.ds(h * HEAD, HEAD), w], e.astype(BF), 1, 0)
                out.append((top, l * fade + jnp.sum(e, axis=0, keepdims=True), acc))
            return tuple(out)

        start = (
            jnp.full((1, size), NEG, F32), jnp.zeros((1, size), F32), jnp.zeros((HEAD, size), F32)
        )
        done = lax.fori_loop(first_ref[i], i + 1, step, (start,) * (2 * pairs))
        for t in range(pairs):
            both = []
            for h in (2 * t, 2 * t + 1):
                m, l, acc = done[h]
                both.append(acc / l)
                lse_ref[h : h + 1, r] = m + jnp.log(l)
            o_ref[r, pl.ds(t * 128, 128)] = jnp.concatenate(both, axis=0).T.astype(BF)


def attend(qkv, begin):
    rows, wide = qkv.shape[0], qkv.shape[1] // 3
    size = block_of(rows)
    half = jax.ShapeDtypeStruct((rows, wide), BF)
    return pl.pallas_call(
        attend_kernel,
        in_specs=[pl.BlockSpec(memory_space=pltpu.SMEM)] + [IN_VMEM] * 6,
        out_specs=[IN_VMEM] * 5,
        out_shape=[half] * 4 + [jax.ShapeDtypeStruct((wide // HEAD, rows), F32)],
        scratch_shapes=[pltpu.VMEM((wide, rows), BF)],
        compiler_params=pltpu.CompilerParams(vmem_limit_bytes=48 << 20),
        name="attend",
    )(begin[0, ::size] // size, qkv, *turn_tables(rows), begin)


def attend_back_work(ins, out_ref, bias_ref, scratch):
    q_ref, k_ref, v_ref, o_ref, do_ref, lse_ref, cos_ref, sin_ref, cosf_ref, sinf_ref, begin_ref = ins
    kt_ref, dq_ref, dk_ref, dv_ref = scratch
    rows, wide = q_ref.shape
    pairs, size = wide // 128, block_of(rows)
    tables = (cos_ref, sin_ref, cosf_ref, sinf_ref)
    left = lax.broadcasted_iota(jnp.int32, (size, 128), 1) < HEAD
    key_at = lax.broadcasted_iota(jnp.int32, (size, size), 0)
    query_at = lax.broadcasted_iota(jnp.int32, (1, size), 1)

    @pl.loop(0, rows // BLK)
    def _(i):
        r = pl.ds(pl.multiple_of(i * BLK, BLK), BLK)
        for t in range(pairs):
            w = pl.ds(t * 128, 128)
            kt_ref[w, r] = k_ref[r, w].astype(F32).T.astype(BF)
            dk_ref[r, w] = jnp.zeros((BLK, 128), F32)
            dv_ref[r, w] = jnp.zeros((BLK, 128), F32)

    @pl.loop(0, rows // size)
    def _(i):
        r = pl.ds(pl.multiple_of(i * size, size), size)
        qs, dos, deltas, lses = [], [], [], []
        for t in range(pairs):
            w = pl.ds(t * 128, 128)
            do = do_ref[r, w]
            qs += two_heads(q_ref[r, w], left)
            dos += two_heads(do, left)
            prod = (do.astype(F32) * o_ref[r, w].astype(F32)).T
            deltas += [jnp.sum(prod[:HEAD], axis=0, keepdims=True), jnp.sum(prod[HEAD:], axis=0, keepdims=True)]
            lses += [lse_ref[2 * t : 2 * t + 1, r], lse_ref[2 * t + 1 : 2 * t + 2, r]]
        begin = begin_ref[0:1, r]
        here = query_at + i * size

        def step(j, carry):
            w = pl.ds(pl.multiple_of(j * size, size), size)
            key = key_at + j * size
            seen = (key <= here) & (key >= begin)
            out = []
            for t in range(pairs):
                lanes = pl.ds(t * 128, 128)
                k, v = k_ref[w, lanes], v_ref[w, lanes]
                dk = dv = None
                for h in (2 * t, 2 * t + 1):
                    prob = jnp.exp(jnp.where(seen, mm(k, qs[h], 1, 1) - lses[h], NEG))
                    ds = (prob * (mm(v, dos[h], 1, 1) - deltas[h])).astype(BF)
                    out.append(carry[h] + mm(kt_ref[pl.ds(h * HEAD, HEAD), w], ds, 1, 0))
                    dk_h, dv_h = mm(ds, qs[h], 1, 0), mm(prob.astype(BF), dos[h], 1, 0)
                    dk, dv = (dk_h, dv_h) if dk is None else (dk + dk_h, dv + dv_h)
                dk_ref[w, lanes] += dk
                dv_ref[w, lanes] += dv
            return tuple(out)

        done = lax.fori_loop(0, i + 1, step, (jnp.zeros((HEAD, size), F32),) * (2 * pairs))
        for t in range(pairs):
            both = jnp.concatenate(done[2 * t : 2 * t + 2], axis=0)
            dq_ref[r, pl.ds(t * 128, 128)] = both.T * (HEAD**-0.5)

    bias_ref[...] = jnp.zeros_like(bias_ref)

    @pl.loop(0, rows // BLK)
    def _(i):
        r = pl.ds(pl.multiple_of(i * BLK, BLK), BLK)
        for t in range(pairs):
            w = pl.ds(t * 128, 128)
            for part, value in enumerate((turn(dq_ref[r, w], i, tables, -1.0), turn(dk_ref[r, w], i, tables, -1.0), dv_ref[r, w])):
                lanes = pl.ds(part * wide + t * 128, 128)
                value = value.astype(BF)
                out_ref[r, lanes] = value
                bias_ref[:, lanes] += jnp.sum(value.astype(F32), axis=0, keepdims=True)


def attend_back(S, C, number, q, k, v, o, do, lse, begin, riders):
    rows, wide = q.shape

    def kernel(ride, ins, outs, scratch):
        greet(S, C, axes=ride.axes)
        ride.start()
        attend_back_work(ins, outs[0], outs[1], scratch)
        ride.wait()

    args = [q, k, v, o, do, lse, *turn_tables(rows), begin]
    return comm(
        kernel, S, C, number, "attend_back", args, [IN_VMEM] * len(args),
        [(jax.ShapeDtypeStruct((rows, 3 * wide), BF), IN_VMEM), (jax.ShapeDtypeStruct((1, 3 * wide), F32), IN_VMEM)],
        [pltpu.VMEM((wide, rows), BF)] + [pltpu.VMEM((rows, wide), F32)] * 3,
        riders,
    )


def doc_begins(lengths_row, rows):
    row_ids = jnp.arange(rows, dtype=jnp.int32)
    ends = jnp.cumsum(lengths_row, dtype=jnp.int32)
    begins = ends - lengths_row
    inside = (row_ids[:, None] >= begins[None, :]) & (row_ids[:, None] < ends[None, :])
    return jnp.sum(jnp.where(inside, begins[None, :], 0), axis=1, dtype=jnp.int32)


def tiles_of(parts, lead):
    flat = jnp.concatenate([x.astype(F32).reshape(lead + (-1,)) for x in parts], axis=-1)
    flat = jnp.pad(flat, ((0, 0),) * len(lead) + ((0, 1024 - flat.shape[-1]),))
    return flat.reshape(lead + (8, 128))


def make_body(S, C, T):
    assert S == C

    def body(tokens, lengths, w_qkv, b_qkv, w_out, w_gateup, w_down, norm_gain, norm_bias, cotangent):
        p, z, c = lax.axis_index("shard"), lax.axis_index("ctx"), lax.axis_index("tp")
        R, D = tokens.shape
        n = R // T
        nb = D // (S * C)
        L = R * C

        def to_parts(x):
            return x.reshape(n, S, C, nb).transpose(2, 0, 1, 3).reshape(S, n, D // S)

        def parts(x):
            return x.reshape(n, S, D // S).swapaxes(0, 1)

        def unpermute(x):
            return x.reshape(x.shape[0], C, S, nb).swapaxes(1, 2).reshape(x.shape)

        def own(x):
            return lax.dynamic_slice_in_dim(x, (p * T + c) * n, n, 0)

        def half_of(x):
            return lax.dynamic_slice_in_dim(x, c * n, n, 0)

        def after(x, y):
            return lax.optimization_barrier((x, y))

        def over_ctx(w):
            return lax.all_gather(w.reshape(S * nb, -1), "ctx", axis=0, tiled=True)

        def sum_ctx(g):
            g = lax.psum_scatter(g.astype(BF), "ctx", scatter_dimension=0, tiled=True)
            return g.reshape(S, nb, -1)

        hn = w_qkv.shape[3] // S
        fn = w_gateup.shape[3] // S
        heads = hn // HEAD
        nf = HEAD // (S * C)

        tile = tiles_of((norm_gain[0].reshape(-1), norm_bias[0].reshape(-1), b_qkv[0].reshape(-1), lengths[0]), ())
        small, _, tok, wq, wo = exchange(
            S, C, T, 0,
            [
                ("shard", w_qkv[0].reshape(nb, 3, S, hn).transpose(2, 0, 1, 3).reshape(S, nb, 3 * hn)),
                ("shard", w_out[0].reshape(S, hn, nb).swapaxes(1, 2)),
            ],
            jnp.broadcast_to(tile, (C, S, 8, 128)),
            to_parts(half_of(tokens)),
        )
        wq = over_ctx(wq)
        tok, wo, wg, wd, cot = gather_columns(
            S, C, T, 1, tok,
            [
                ("all", wo.reshape(S * nb, hn)),
                ("shard", w_gateup[0].reshape(nb, 2, S, fn).transpose(2, 0, 1, 3).reshape(S, nb, 2 * fn)),
                ("shard", w_down[0].reshape(S, fn, nb).swapaxes(1, 2)),
                ("shard", to_parts(half_of(cotangent))),
            ],
        )
        wo, wg, wd = wo.reshape(D, hn), over_ctx(wg), over_ctx(wd)

        small = lax.dynamic_index_in_dim(small, c, 0, keepdims=False).reshape(C, S, 1024)
        norms = small[:, :, : 4 * nb].reshape(C * S, 4, nb).swapaxes(0, 1).reshape(4, D)
        gains, shifts = norms[:2], norms[2:]
        nbias = 3 * S * heads * nf
        bias = small[:, :, 4 * nb : 4 * nb + nbias].reshape(C, S, 3, S * heads, nf)
        bias = lax.dynamic_slice_in_dim(bias, p * heads, heads, 3)
        bias = bias.transpose(2, 3, 1, 0, 4).reshape(1, 3 * hn)
        docs = lengths.shape[1]
        lengths_row = lax.dynamic_index_in_dim(
            small[0, :, 4 * nb + nbias : 4 * nb + nbias + docs], z, 0, keepdims=False
        ).astype(jnp.int32)
        begin = doc_begins(lengths_row, L)
        begin = begin[None, :]

        n1 = (norm_of(tok.astype(F32))[0] * gains[0] + shifts[0]).astype(BF)
        own_tok = own(tok)
        qkv = mm(n1, wq, 1, 0) + bias
        q, k, v, o, lse = attend(qkv, begin)
        mid, n2, cot = sum_norm_gather(S, C, T, 2, o, wo, own_tok, gains[1:], shifts[1:], [("ctx", cot)])
        cot, n2 = after(cot, n2)
        (gb,) = gather_columns(S, C, T, 4, cot)
        gu = mm(n2, wg, 1, 0)
        gate, up = gu[:, :fn], gu[:, fn:]
        logistic = jax.nn.sigmoid(gate)
        act = (gate * logistic * up).astype(BF)
        gw_down = mm(gb, act, 0, 0).astype(BF)
        wd, gw_down = after(wd, gw_down)
        gw_down = sum_ctx(gw_down)

        got, dgu = sum_and_gates(S, C, T, 5, act, wd, gb, gu)
        gw_gateup = mm(n2, dgu, 0, 0).astype(BF)
        dgu, gw_gateup = after(dgu, gw_gateup)
        gw_gateup = sum_ctx(gw_gateup)
        out = parts((mid + got).astype(BF))
        dmid, gb1, stats2, out = sum_back_gather(
            S, C, T, 6, dgu, wg, mid, own(gb), gains[1:], [("shard", out)]
        )
        gw_out = mm(gb1, o, 0, 0).astype(BF)
        gb1, gw_out = after(gb1, gw_out)
        gw_out = sum_ctx(gw_out)
        do = mm(gb1, wo, 1, 0).astype(BF)
        dqkv, gbias, gw_gateup, gw_down, out = attend_back(
            S, C, 11, q, k, v, o, do, lse, begin, [("shard", gw_gateup), ("shard", gw_down), ("ctx", out)]
        )
        gw_qkv = mm(n1, dqkv, 0, 0).astype(BF)
        dqkv, gw_qkv = after(dqkv, gw_qkv)
        gw_qkv = sum_ctx(gw_qkv)
        low, stats1, out = sum_back(S, C, T, 8, dqkv, wq, own_tok, dmid, gains[:1], [("shard", out)])
        gtok, small, gw_qkv, gw_out, mate = finish(
            S, C, T, 10, low, [stats1, stats2], gbias, [("shard", gw_qkv), ("shard", gw_out), ("tp", out)]
        )
        gtok = unpermute(gtok).astype(F32)
        out = jnp.where(c == 0, jnp.stack((out, mate)), jnp.stack((mate, out)))
        out = unpermute(out.transpose(0, 2, 1, 3).reshape(R, D))
        norms = lax.dynamic_slice_in_dim(jnp.sum(small[..., :4, :], axis=(0, 1, 2)), (z * S + p) * nb % 128, nb, 1)
        gbias = lax.dynamic_index_in_dim(small, c, 0, keepdims=False)[:, :, 4 : 4 + 3 * hn // 128]
        gbias = jnp.sum(gbias, axis=0).reshape(S, 3, heads, S * C, nf)
        gbias = lax.dynamic_index_in_dim(gbias, p * C + z, 3, keepdims=False)
        gbias = gbias.swapaxes(0, 1).reshape(b_qkv.shape)

        return (
            out,
            gtok,
            gw_qkv.astype(F32).reshape(S, nb, 3, hn).transpose(1, 2, 0, 3).reshape(w_qkv.shape),
            gbias,
            gw_out.astype(F32).swapaxes(1, 2).reshape(w_out.shape),
            gw_gateup.astype(F32).reshape(S, nb, 2, fn).transpose(1, 2, 0, 3).reshape(w_gateup.shape),
            gw_down.astype(F32).swapaxes(1, 2).reshape(w_down.shape),
            jnp.stack((norms[0], norms[2]))[None],
            jnp.stack((norms[1], norms[3]))[None],
        )

    return body


def solution(mesh):
    both = ("shard", "ctx")
    specs = (
        P(None, both, None, "tp"),
        P(None, None, "tp", both),
        P(None, "tp", both),
        P(None, both, None, "tp"),
        P(None, "tp", both),
        P(None, None, both),
        P(None, None, both),
    )
    return jax.shard_map(
        make_body(mesh.shape["shard"], mesh.shape["ctx"], mesh.shape["tp"]),
        mesh=mesh,
        in_specs=(P(both, None), P("shard", None)) + specs + (P(both, None),),
        out_specs=(P(both, None), P(both, None)) + specs,
        check_vma=False,
    )
```

```python
import functools

import jax
import jax.numpy as jnp
import numpy as np
from jax import lax
from jax.experimental import pallas as pl
from jax.experimental.pallas import tpu as pltpu
from jax.sharding import PartitionSpec as P

HEAD = 64
ROT = 16
EPS = 1e-05
NEG = -1e30
BASE = 10000.0
BF = jnp.bfloat16
F32 = jnp.float32
BLK = 256
MESH = pl.DeviceIdType.MESH
DMA = pltpu.SemaphoreType.DMA
ANY = pl.BlockSpec(memory_space=pl.ANY)
IN_VMEM = pl.BlockSpec(memory_space=pltpu.VMEM)


def mm(a, b, ca, cb):
    return lax.dot_general(a, b, (((ca,), (cb,)), ((), ())), preferred_element_type=F32)


def remote(src, dst, send, recv, where):
    return pltpu.make_async_remote_copy(
        src_ref=src, dst_ref=dst, send_sem=send, recv_sem=recv, device_id=where, device_id_type=MESH
    )


def here():
    return lax.axis_index("shard"), lax.axis_index("ctx"), lax.axis_index("tp")


class Riders:
    def __init__(self, S, C, riders):
        self.S, self.C = S, C
        self.axes = [axis for axis, _ in riders]
        self.arrays = [x for _, x in riders]
        self.shapes = [
            jax.ShapeDtypeStruct((C,) + x.shape if axis == "all" else x.shape, x.dtype) for axis, x in riders
        ]
        count, most = len(riders), max(S, C) - 1
        self.scratch = [DMA((count, most)), DMA((count, most)), DMA((count,))] if count else []

    def bind(self, ins, outs, sems):
        self.ins, self.outs, self.sems = ins, outs, sems

    def start(self):
        p, z, c = here()
        self.moves = []
        for n, axis in enumerate(self.axes):
            src, dst = self.ins[n], self.outs[n]
            send, recv, own = self.sems
            if axis == "tp":
                copies = [remote(src, dst, send.at[n, 0], recv.at[n, 0], {"tp": 1 - c})]
            elif axis == "all":
                copies = [
                    remote(src, dst.at[z], send.at[n, k - 1], recv.at[n, k - 1], {"ctx": (z + k) % self.C})
                    for k in range(1, self.C)
                ]
                copies.append(pltpu.make_async_copy(src, dst.at[z], own.at[n]))
            else:
                size, me = (self.S, p) if axis == "shard" else (self.C, z)
                copies = [
                    remote(src.at[(me + k) % size], dst.at[me], send.at[n, k - 1], recv.at[n, k - 1], {axis: (me + k) % size})
                    for k in range(1, size)
                ]
                copies.append(pltpu.make_async_copy(src.at[me], dst.at[me], own.at[n]))
            for copy in copies:
                copy.start()
            self.moves += copies

    def wait(self):
        for copy in self.moves:
            copy.wait()


def greet(S, C, mates=(), line=False, other=False, axes=()):
    p, z, c = here()
    peers = [{"shard": q} for q in ([(p + k) % S for k in range(1, S)] if "shard" in axes else mates)]
    if line or "ctx" in axes or "all" in axes:
        peers += [{"ctx": (z + k) % C} for k in range(1, C)]
    if other or "tp" in axes:
        peers.append({"tp": 1 - c})
    barrier = pltpu.get_barrier_semaphore()
    for where in peers:
        pl.semaphore_signal(barrier, inc=1, device_id=where, device_id_type=MESH)
    pl.semaphore_wait(barrier, len(peers))


def comm(kernel, S, C, number, name, args, in_specs, outs, scratch, riders=()):
    ride = Riders(S, C, riders)
    na, nr, no, ns = len(args), len(ride.axes), len(outs), len(scratch)

    def body(*refs):
        ins, refs = refs[:na], refs[na:]
        rins, refs = refs[:nr], refs[nr:]
        os, refs = refs[:no], refs[no:]
        routs, refs = refs[:nr], refs[nr:]
        ride.bind(rins, routs, refs[ns:])
        kernel(ride, ins, os, refs[:ns])

    return pl.pallas_call(
        body,
        out_shape=[shape for shape, _ in outs] + ride.shapes,
        in_specs=list(in_specs) + [IN_VMEM] * nr,
        out_specs=[spec for _, spec in outs] + [ANY] * nr,
        scratch_shapes=list(scratch) + ride.scratch,
        compiler_params=pltpu.CompilerParams(
            collective_id=number, has_side_effects=True, vmem_limit_bytes=56 << 20
        ),
        cost_estimate=pl.CostEstimate(flops=0, bytes_accessed=120_000_000, transcendentals=0),
        name=name,
    )(*args, *ride.arrays)


def exchange(S, C, T, number, riders, tiles, rows=None):
    def kernel(ride, ins, outs, scratch):
        tile, got = ins[0], outs[0]
        send, recv, bsend, brecv, own = scratch[:5]
        p, z, c = here()
        everyone = [(i, j) for i in range(C) for j in range(S) if i or j]
        barrier = pltpu.get_barrier_semaphore()
        peers = [{"shard": (p + j) % S, "ctx": (z + i) % C} for i, j in everyone] + [{"tp": 1 - c}]
        for where in peers:
            pl.semaphore_signal(barrier, inc=1, device_id=where, device_id_type=MESH)
        pl.semaphore_wait(barrier, len(peers))

        def turn_over(source, target, k, axis, size, me):
            ssem, rsem, local = scratch[5:]
            hop = [pltpu.make_async_copy(source.at[me], target.at[me], local.at[k])]
            for j in range(1, size):
                q = (me + j) % size
                hop.append(remote(source.at[q], target.at[me], ssem.at[k, j - 1], rsem.at[k, j - 1], {axis: q}))
            for copy in hop:
                copy.start()
            return hop

        if rows is not None:
            first = turn_over(ins[1], outs[1], 0, "shard", S, p)
        local = pltpu.make_async_copy(tile.at[z, p], got.at[c, z, p], own)
        local.start()
        copies = []
        for at, (where, (i, j)) in enumerate(zip(peers, everyone)):
            q, g = (p + j) % S, (z + i) % C
            copies.append(remote(tile.at[g, q], got.at[c, z, p], send.at[at], recv.at[at], where))
            copies[-1].start()
        ride.start()
        if rows is not None:
            for copy in first:
                copy.wait()
            second = turn_over(outs[1], outs[2], 1, "ctx", C, z)
        local.wait()
        for copy in copies:
            copy.wait()
        back = remote(got.at[c], got.at[c], bsend, brecv, {"tp": 1 - c})
        back.start()
        back.wait_send()
        remote(got.at[1 - c], got.at[1 - c], bsend, brecv, {"tp": 1 - c}).wait_recv()
        if rows is not None:
            for copy in second:
                copy.wait()
        ride.wait()

    count, most = C * S - 1, max(S, C) - 1
    args, outs = [tiles], [(jax.ShapeDtypeStruct((T,) + tiles.shape, tiles.dtype), ANY)]
    scratch = [DMA((count,)), DMA((count,)), DMA, DMA, DMA]
    if rows is not None:
        args.append(rows)
        outs += [(jax.ShapeDtypeStruct(rows.shape, rows.dtype), IN_VMEM)] * 2
        scratch += [DMA((2, most)), DMA((2, most)), DMA((2,))]
    return comm(kernel, S, C, number, "exchange", args, [IN_VMEM] * len(args), outs, scratch, riders)


def plane(S):
    p, _, c = here()
    B = S // 2
    a, b = p // B, p % B
    return a, b, [a * B + (b + j) % B for j in range(1, B)], (1 - a) * B + b


def spread_sems(S):
    count = 4 + 4 * (S // 2 - 1)
    return [DMA((2 * count,)), DMA((2 * count,))]


def spread(S, own, region, send, recv):
    p, _, c = here()
    B = S // 2
    a, b, rows, col = plane(S)
    rows, col, other = [{"shard": q} for q in rows], {"shard": col}, {"tp": 1 - c}
    per = 4 + 4 * (B - 1)
    OWN, ROW, COL, VIA_COL, VIA_ROW = 0, 2, 2 + 2 * (B - 1), 4 + 2 * (B - 1), 4 + 3 * (B - 1)
    started = []

    def push(q, h, sem, where, first=False):
        view = region(q, h, c)
        copy = remote(own(h) if first else view, view, send.at[sem], recv.at[sem], where)
        copy.start()
        started.append(copy)

    def came(q, h, sem, core):
        view = region(q, h, core)
        remote(view, view, send.at[sem], recv.at[sem], other).wait_recv()

    for h in range(2):
        for j in range(1, B):
            push(p, h, ROW + 2 * (j - 1) + h, rows[j - 1], True)
    for h in (1, 0):
        push(p, h, COL + h, col, True)
    for h in range(2):
        push(p, h, per + OWN + h, other, True)

    def from_row(j, h):
        q = a * B + (b - j) % B
        came(q, h, ROW + 2 * (j - 1) + h, c)
        push(q, h, per + ROW + 2 * (j - 1) + h, other)
        return q

    def from_col(h):
        q = (1 - a) * B + b
        came(q, h, COL + h, c)
        push(q, h, per + COL + h, other)
        return q

    for j in range(1, B):
        q = from_row(j, 0)
        push(q, 0, VIA_COL + j - 1, col)
    q = from_col(1)
    for j in range(1, B):
        push(q, 1, VIA_ROW + j - 1, rows[j - 1])
    for j in range(1, B):
        from_row(j, 1)
    from_col(0)
    for j in range(1, B):
        q = (1 - a) * B + (b - j) % B
        came(q, 0, VIA_COL + j - 1, c)
        push(q, 0, per + VIA_COL + j - 1, other)
        came(q, 1, VIA_ROW + j - 1, c)
        push(q, 1, per + VIA_ROW + j - 1, other)
    for h in range(2):
        came(p, h, per + OWN + h, 1 - c)
        came((1 - a) * B + b, h, per + COL + h, 1 - c)
    for j in range(1, B):
        for h in range(2):
            came(a * B + (b - j) % B, h, per + ROW + 2 * (j - 1) + h, 1 - c)
        q = (1 - a) * B + (b - j) % B
        came(q, 0, per + VIA_COL + j - 1, 1 - c)
        came(q, 1, per + VIA_ROW + j - 1, 1 - c)
    for copy in started:
        copy.wait_send()


def gather_columns(S, C, T, number, x, riders=()):
    _, n, wide = x.shape

    def kernel(ride, ins, outs, scratch):
        (x_ref,), (out_ref,), (send, recv, own) = ins, outs, scratch
        p, _, c = here()
        _, _, rows, col = plane(S)

        def region(q, h, core):
            part = pl.ds(pl.multiple_of(q * wide, 128), wide)
            return out_ref.at[pl.ds(h * (C // 2), C // 2), core, :, part]

        local = [
            pltpu.make_async_copy(x_ref.at[pl.ds(h * (C // 2), C // 2)], region(p, h, c), own.at[h]) for h in range(2)
        ]
        for copy in local:
            copy.start()
        greet(S, C, rows + [col], other=True, axes=ride.axes)
        ride.start()
        spread(S, lambda h: x_ref.at[pl.ds(h * (C // 2), C // 2)], region, send, recv)
        for copy in local:
            copy.wait()
        ride.wait()

    out, *rest = comm(
        kernel, S, C, number, "gather_columns", [x], [IN_VMEM],
        [(jax.ShapeDtypeStruct((C, T, n, wide * S), x.dtype), ANY)], spread_sems(S) + [DMA((2,))], riders,
    )
    return [out.reshape(C * T * n, wide * S)] + rest


CHUNK = 512
ROWS = 32


def sum_scratch(S, n, D):
    half, B = n // 2, S // 2

    def vm(*shape):
        return pltpu.VMEM(shape, BF)

    return [
        vm(S, n, D), vm(S, n, D), vm(S, n, D), vm(B - 1, 2, half, D), vm(B, half, D),
        vm(B - 1, half, D), vm(half, D), vm(half, D), vm(B - 1, half, D),
        DMA((S,)), DMA((S,)), DMA((B - 1, 2)), DMA((B - 1, 2)), DMA((B,)), DMA((B,)), DMA((B,)), DMA((B,)),
    ]


def sum_over_plane(S, T, x_ref, w_ref, out_ref, scratch, meanwhile=None):
    away, sib, mine, row1, col1, row2, col2, to_col, to_row = scratch[:9]
    asend, arecv, rsend, rrecv, csend, crecv, fsend, frecv = scratch[9:]
    n, D = out_ref.shape
    half, B = n // 2, S // 2
    _, _, c = here()
    a, b, rows, col = plane(S)
    rows, col, other = [{"shard": q} for q in rows], {"shard": col}, {"tp": 1 - c}

    def chip(e):
        return ((a + e // B) % 2) * B + (b + e % B) % B

    def product(e, core, store):
        x = x_ref[chip(e) * T + core]

        def column(j, _):
            w = pl.ds(pl.multiple_of(j * CHUNK, CHUNK), CHUNK)
            store(w, mm(x, w_ref[w, :], 1, 1))
            return 0

        lax.fori_loop(0, D // CHUNK, column, 0)

    def to_other(e):
        return remote(away.at[e], sib.at[e], asend.at[e], arecv.at[e], other)

    def first(i, _):
        e = S - 1 - i

        def store(w, value):
            away[e, :, w] = value.astype(BF)

        product(e, 1 - c, store)
        to_other(e).start()
        return 0

    lax.fori_loop(0, S, first, 0)

    top, low = pl.ds(0, half), pl.ds(half, half)
    started = []

    def push(src, dst, send, recv, where):
        copy = remote(src, dst, send, recv, where)
        copy.start()
        started.append(copy)

    for e in range(S - 1, -1, -1):
        to_other(e).wait()

        def store(w, value):
            value = value + sib[e, :, w].astype(F32)
            if e:
                mine[e, :, w] = value.astype(BF)
            else:
                out_ref[:, w] = value

        product(e, c, store)
        j = e % B
        if e > B:
            push(mine.at[e, top], row1.at[j - 1, 1], rsend.at[j - 1, 1], rrecv.at[j - 1, 1], rows[j - 1])
            push(mine.at[e, low], col1.at[j], csend.at[j], crecv.at[j], col)
        elif e == B:
            push(mine.at[e, low], col1.at[0], csend.at[0], crecv.at[0], col)
        elif e:
            push(mine.at[e, top], row1.at[j - 1, 0], rsend.at[j - 1, 0], rrecv.at[j - 1, 0], rows[j - 1])

    def came(ref, send, recv):
        remote(ref, ref, send, recv, other).wait_recv()

    if meanwhile is not None:
        meanwhile()
    total = mine[B, top, :].astype(F32)
    for j in range(1, B):
        came(row1.at[j - 1, 1], rsend.at[j - 1, 1], rrecv.at[j - 1, 1])
        total = total + row1[j - 1, 1].astype(F32)
    to_col[...] = total.astype(BF)
    push(to_col, col2, fsend.at[0], frecv.at[0], col)
    for j in range(1, B):
        came(col1.at[j], csend.at[j], crecv.at[j])
        to_row[j - 1] = (mine[j, low, :].astype(F32) + col1[j].astype(F32)).astype(BF)
        push(to_row.at[j - 1], row2.at[j - 1], fsend.at[j], frecv.at[j], rows[j - 1])
    came(col1.at[0], csend.at[0], crecv.at[0])
    upper, lower = out_ref[top, :], out_ref[low, :] + col1[0].astype(F32)
    for j in range(1, B):
        came(row1.at[j - 1, 0], rsend.at[j - 1, 0], rrecv.at[j - 1, 0])
        upper = upper + row1[j - 1, 0].astype(F32)
    came(col2, fsend.at[0], frecv.at[0])
    out_ref[top, :] = upper + col2[...].astype(F32)
    for j in range(1, B):
        came(row2.at[j - 1], fsend.at[j], frecv.at[j])
        lower = lower + row2[j - 1].astype(F32)
    out_ref[low, :] = lower
    for copy in started:
        copy.wait_send()


def gates_kernel(n2_ref, wg_ref, gu_ref, act_ref):
    both = mm(n2_ref[...], wg_ref[...], 1, 0)
    gu_ref[...] = both
    width = act_ref.shape[1]
    gate, up = both[:, :width], both[:, width:]
    act_ref[...] = (gate * jax.nn.sigmoid(gate) * up).astype(BF)


def gates_back_kernel(gb_ref, wd_ref, gu_ref, dgu_ref):
    dact = mm(gb_ref[...], wd_ref[...], 1, 0)
    both, width = gu_ref[...], dact.shape[1]
    gate, up = both[:, :width], both[:, width:]
    s = jax.nn.sigmoid(gate)
    dgate = dact * up * s * (1.0 + gate * (1.0 - s))
    dgu_ref[...] = jnp.concatenate((dgate, dact * gate * s), axis=1).astype(BF)


def by_rows(kernel, name, arrays, outs):
    L = outs[0].shape[0]

    def spec(width):
        return pl.BlockSpec((BLK, width), lambda i: (i, 0))

    return pl.pallas_call(
        kernel,
        grid=(L // BLK,),
        in_specs=[spec(x.shape[1]) if rows else pl.BlockSpec(x.shape, lambda i: (0, 0)) for rows, x in arrays],
        out_specs=[spec(x.shape[1]) for x in outs],
        out_shape=outs,
        compiler_params=pltpu.CompilerParams(vmem_limit_bytes=48 << 20),
        name=name,
    )(*[x for _, x in arrays])


def row_blocks(n, work):
    @pl.loop(0, n // ROWS)
    def _(i):
        work(pl.ds(pl.multiple_of(i * ROWS, ROWS), ROWS))


def norm_of(v):
    center = v - jnp.mean(v, axis=-1, keepdims=True)
    inverse = lax.rsqrt(jnp.mean(center * center, axis=-1, keepdims=True) + EPS)
    return center * inverse, inverse


def norm_back(v, g, gain, stats_ref):
    normal, inverse = norm_of(v)
    e = g * gain
    stats_ref[0:1, :] += jnp.sum(g * normal, axis=0, keepdims=True)
    stats_ref[1:2, :] += jnp.sum(g, axis=0, keepdims=True)
    return inverse * (
        e - jnp.mean(e, axis=-1, keepdims=True) - normal * jnp.mean(e * normal, axis=-1, keepdims=True)
    )


def spread_rows(S, T, src, out_ref, send, recv, own):
    p, _, c = here()
    half = src.shape[0] // 2
    local = pltpu.make_async_copy(src, out_ref.at[p * T + c], own)
    local.start()
    spread(
        S,
        lambda h: src.at[pl.ds(h * half, half)],
        lambda q, h, core: out_ref.at[q * T + core, pl.ds(h * half, half)],
        send,
        recv,
    )
    local.wait()


def sum_norm_gather(S, C, T, number, x, w, residual, gain, shift, riders=()):
    L, K = x.shape
    D, n = w.shape[0], L // (S * T)

    def kernel(ride, ins, outs, scratch):
        x_ref, w_ref, res_ref, gain_ref, shift_ref = ins
        v_ref, out_ref = outs
        acc, low, send, recv, own = scratch[:5]
        _, _, rows, col = plane(S)
        greet(S, C, rows + [col], other=True, axes=ride.axes)
        ride.start()
        sum_over_plane(S, T, x_ref, w_ref, acc, scratch[5:])

        def work(r):
            v = res_ref[r, :].astype(F32) + acc[r, :]
            v_ref[r, :] = v
            low[r, :] = (norm_of(v)[0] * gain_ref[...] + shift_ref[...]).astype(BF)

        row_blocks(n, work)
        spread_rows(S, T, low, out_ref, send, recv, own)
        ride.wait()

    v, out, *rest = comm(
        kernel, S, C, number, "sum_norm_gather", [x.reshape(S * T, n, K), w, residual, gain, shift], [IN_VMEM] * 5,
        [(jax.ShapeDtypeStruct((n, D), F32), IN_VMEM), (jax.ShapeDtypeStruct((S * T, n, D), BF), ANY)],
        [pltpu.VMEM((n, D), F32), pltpu.VMEM((n, D), BF)] + spread_sems(S) + [DMA] + sum_scratch(S, n, D),
        riders,
    )
    return [v, out.reshape(L, D)] + rest


def sum_back_gather(S, C, T, number, x, w, v, residual, gain, riders=()):
    L, K = x.shape
    D, n = w.shape[0], L // (S * T)

    def kernel(ride, ins, outs, scratch):
        x_ref, w_ref, in_ref, res_ref, gain_ref = ins
        v_ref, out_ref, stats = outs
        acc, low, send, recv, own = scratch[:5]
        _, _, rows, col = plane(S)
        greet(S, C, rows + [col], other=True, axes=ride.axes)
        ride.start()
        sum_over_plane(S, T, x_ref, w_ref, acc, scratch[5:])
        stats[...] = jnp.zeros_like(stats)

        def work(r):
            g = res_ref[r, :].astype(F32) + norm_back(in_ref[r, :], acc[r, :], gain_ref[...], stats)
            v_ref[r, :] = g
            low[r, :] = g.astype(BF)

        row_blocks(n, work)
        spread_rows(S, T, low, out_ref, send, recv, own)
        ride.wait()

    g, out, stats, *rest = comm(
        kernel, S, C, number, "sum_back_gather", [x.reshape(S * T, n, K), w, v, residual, gain], [IN_VMEM] * 5,
        [
            (jax.ShapeDtypeStruct((n, D), F32), IN_VMEM), (jax.ShapeDtypeStruct((S * T, n, D), BF), ANY),
            (jax.ShapeDtypeStruct((2, D), F32), IN_VMEM),
        ],
        [pltpu.VMEM((n, D), F32), pltpu.VMEM((n, D), BF)] + spread_sems(S) + [DMA] + sum_scratch(S, n, D),
        riders,
    )
    return [g, out.reshape(L, D), stats] + rest


def sum_back(S, C, T, number, x, w, v, residual, gain, riders=()):
    L, K = x.shape
    D, n = w.shape[0], L // (S * T)

    def kernel(ride, ins, outs, scratch):
        x_ref, w_ref, in_ref, res_ref, gain_ref = ins
        low, stats = outs
        acc = scratch[0]
        _, _, rows, col = plane(S)
        greet(S, C, rows + [col], other=True, axes=ride.axes)
        ride.start()
        sum_over_plane(S, T, x_ref, w_ref, acc, scratch[1:])
        stats[...] = jnp.zeros_like(stats)

        def work(r):
            g = res_ref[r, :] + norm_back(in_ref[r, :].astype(F32), acc[r, :], gain_ref[...], stats)
            low[r, :] = g.astype(BF)

        row_blocks(n, work)
        ride.wait()

    return comm(
        kernel, S, C, number, "sum_back", [x.reshape(S * T, n, K), w, v, residual, gain], [IN_VMEM] * 5,
        [(jax.ShapeDtypeStruct((n, D), BF), IN_VMEM), (jax.ShapeDtypeStruct((2, D), F32), IN_VMEM)],
        [pltpu.VMEM((n, D), F32)] + sum_scratch(S, n, D),
        riders,
    )


def finish(S, C, T, number, x, y, stats, bias, riders):
    n, D = x.shape
    wide, lines = D // S, bias.shape[1] // 128
    nb = D // (S * C)
    count = sum(z.shape[0] for z in stats)
    tall = -(-(count + lines) // 8) * 8
    many = C * S - 1
    pieces = S if ordered(D, S, C) else 1

    def kernel(ride, ins, outs, scratch):
        x_ref, y_ref, stat_refs, bias_ref = ins[0], ins[1], ins[2:-1], ins[-1]
        x_out, y_out, got = outs
        xbuf, xbuf2, ybuf2, tile, send, recv, own, psend, precv, pown, lsend, lrecv, tsend, trecv = scratch
        p, z, c = here()
        other = {"tp": 1 - c}
        everyone = [(i, j) for i in range(C) for j in range(S) if i or j]
        peers = [{"shard": (p + j) % S, "ctx": (z + i) % C} for i, j in everyone]
        barrier = pltpu.get_barrier_semaphore()
        for where in peers + [other]:
            pl.semaphore_signal(barrier, inc=1, device_id=where, device_id_type=MESH)
        pl.semaphore_wait(barrier, len(peers) + 1)

        def part(q):
            return pl.ds(pl.multiple_of(q * wide, 128), wide)

        def turn_over(source, target, at, size, me, axis):
            hop = [pltpu.make_async_copy(source(me), target, own.at[at])]
            for k in range(1, size):
                q = (me + k) % size
                hop.append(remote(source(q), target, send.at[at, k - 1], recv.at[at, k - 1], {axis: q}))
            for copy in hop:
                copy.start()
            return hop

        def arrive(buf, out, at):
            hop = []
            for i in range(pieces):
                src = pl.ds(i * (wide // pieces), wide // pieces)
                first = (i * C + p) * nb if pieces > 1 else p * wide
                dst = out.at[c, :, pl.ds(pl.multiple_of(first, 128), wide // pieces)]
                hop.append(pltpu.make_async_copy(buf.at[p, :, src], dst, pown.at[at, i]))
                for k in range(1, S):
                    q = (p + k) % S
                    hop.append(
                        remote(buf.at[q, :, src], dst, psend.at[at, k - 1, i], precv.at[at, k - 1, i], {"shard": q})
                    )
            for copy in hop:
                copy.start()
            return hop

        def both(ref, at):
            copy = remote(ref.at[c], ref.at[c], lsend.at[at], lrecv.at[at], other)
            copy.start()
            return copy

        def settle(ref, at, copy):
            copy.wait_send()
            remote(ref.at[1 - c], ref.at[1 - c], lsend.at[at], lrecv.at[at], other).wait_recv()

        x_hop = turn_over(lambda q: x_ref.at[:, part(q)], xbuf.at[p], 0, S, p, "shard")
        y_hop = turn_over(lambda q: y_ref.at[q], ybuf2.at[z], 1, C, z, "ctx")
        ride.start()
        tile[...] = jnp.zeros_like(tile)
        at = 0
        for ref in stat_refs:
            tile[at : at + ref.shape[0], :] = ref[...]
            at += ref.shape[0]
        for k in range(lines):
            for block in range(D // 128):
                tile[at + k : at + k + 1, pl.ds(block * 128, 128)] = bias_ref[:, pl.ds(k * 128, 128)]

        def columns(g, q):
            return tile.at[:, pl.ds(pl.multiple_of((g * S + q) * nb // 128 * 128, 128), 128)]

        small = [pltpu.make_async_copy(columns(z, p), got.at[c, z, p], own.at[3])]
        for k, (where, (i, j)) in enumerate(zip(peers, everyone)):
            small.append(
                remote(columns((z + i) % C, (p + j) % S), got.at[c, z, p], tsend.at[k], trecv.at[k], where)
            )
        for copy in small:
            copy.start()
        for copy in x_hop:
            copy.wait()
        x_hop = turn_over(lambda q: xbuf.at[q], xbuf2.at[z], 2, C, z, "ctx")
        for copy in y_hop:
            copy.wait()
        y_hop = arrive(ybuf2, y_out, 0)
        for copy in small:
            copy.wait()
        small_last = both(got, 0)
        for copy in x_hop:
            copy.wait()
        x_hop = arrive(xbuf2, x_out, 1)
        for copy in y_hop:
            copy.wait()
        y_last = both(y_out, 1)
        for copy in x_hop:
            copy.wait()
        x_last = both(x_out, 2)
        settle(got, 0, small_last)
        settle(y_out, 1, y_last)
        settle(x_out, 2, x_last)
        ride.wait()

    args = [x, y, *stats, bias]
    most = max(S, C) - 1
    home = (jax.ShapeDtypeStruct((T, n, D), BF), ANY)
    x, y, got, *rest = comm(
        kernel, S, C, number, "finish", args, [IN_VMEM] * len(args),
        [home, home, (jax.ShapeDtypeStruct((T, C, S, tall, 128), F32), ANY)],
        [
            pltpu.VMEM((S, n, wide), BF), pltpu.VMEM((C, n, wide), BF), pltpu.VMEM((C, n, wide), BF),
            pltpu.VMEM((tall, D), F32), DMA((3, most)), DMA((3, most)), DMA((4,)),
            DMA((2, S - 1, pieces)), DMA((2, S - 1, pieces)), DMA((2, pieces)), DMA((3,)), DMA((3,)),
            DMA((many,)), DMA((many,)),
        ],
        riders,
    )
    return [x.reshape(T * n, D), y.reshape(T * n, D), got] + rest


def ordered(D, S, C):
    return D // (S * C) % 128 == 0


def turn_tables(rows):
    feature = np.arange(128) % HEAD
    freq = np.where(feature < ROT, BASE ** (-2.0 * (feature % (ROT // 2)) / ROT), 0.0)
    near = np.arange(BLK)[:, None] * freq
    far = np.arange(0, rows, BLK)[:, None] * freq
    return [jnp.asarray(f(x), F32) for x in (near, far) for f in (np.cos, np.sin)]


def turn(x, i, tables, sign):
    cos, sin, cos_far, sin_far = tables
    far_cos, far_sin = cos_far[pl.ds(i, 1), :], sin_far[pl.ds(i, 1), :]
    cos_t = cos[...] * far_cos - sin[...] * far_sin
    sin_t = sin[...] * far_cos + cos[...] * far_sin
    ahead = lax.broadcasted_iota(jnp.int32, x.shape, 1) % HEAD < ROT // 2
    partner = jnp.where(ahead, -pltpu.roll(x, 128 - ROT // 2, 1), pltpu.roll(x, ROT // 2, 1))
    return x * cos_t + partner * (sin_t * sign)


def two_heads(x, left):
    zero = jnp.zeros_like(x)
    return [jnp.where(left, x, zero), jnp.where(left, zero, x)]


def block_of(rows):
    return next(size for size in (512, 256) if rows % size == 0)


def attend_kernel(
    first_ref, qkv_ref, cos_ref, sin_ref, cosf_ref, sinf_ref, begin_ref,
    qo_ref, ko_ref, vo_ref, o_ref, lse_ref, vt_ref,
):
    rows, wide = qo_ref.shape
    pairs, size = wide // 128, block_of(rows)
    tables = (cos_ref, sin_ref, cosf_ref, sinf_ref)
    left = lax.broadcasted_iota(jnp.int32, (size, 128), 1) < HEAD
    key_at = lax.broadcasted_iota(jnp.int32, (size, size), 0)
    query_at = lax.broadcasted_iota(jnp.int32, (1, size), 1)

    @pl.loop(0, rows // BLK)
    def _(i):
        r = pl.ds(pl.multiple_of(i * BLK, BLK), BLK)
        for t in range(pairs):
            w = pl.ds(t * 128, 128)
            q, k, v = (qkv_ref[r, pl.ds(part * wide + t * 128, 128)] for part in range(3))
            qo_ref[r, w] = turn(q, i, tables, 1.0).astype(BF) * jnp.asarray(HEAD**-0.5, BF)
            ko_ref[r, w] = turn(k, i, tables, 1.0).astype(BF)
            vo_ref[r, w] = v.astype(BF)
            vt_ref[w, r] = v.T.astype(BF)

    @pl.loop(0, rows // size)
    def _(i):
        r = pl.ds(pl.multiple_of(i * size, size), size)
        qs = sum((two_heads(qo_ref[r, pl.ds(t * 128, 128)], left) for t in range(pairs)), [])
        begin = begin_ref[0:1, r]
        here = query_at + i * size

        def step(j, carry):
            w = pl.ds(pl.multiple_of(j * size, size), size)
            key = key_at + j * size
            seen = (key <= here) & (key >= begin)
            out = []
            for h in range(2 * pairs):
                m, l, acc = carry[h]
                s = jnp.where(seen, mm(ko_ref[w, pl.ds(h // 2 * 128, 128)], qs[h], 1, 1), NEG)
                top = jnp.maximum(m, jnp.max(s, axis=0, keepdims=True))
                fade = jnp.exp(m - top)
                e = jnp.exp(s - top)
                acc = acc * fade + mm(vt_ref[pl.ds(h * HEAD, HEAD), w], e.astype(BF), 1, 0)
                out.append((top, l * fade + jnp.sum(e, axis=0, keepdims=True), acc))
            return tuple(out)

        start = (
            jnp.full((1, size), NEG, F32), jnp.zeros((1, size), F32), jnp.zeros((HEAD, size), F32)
        )
        done = lax.fori_loop(first_ref[i], i + 1, step, (start,) * (2 * pairs))
        for t in range(pairs):
            both = []
            for h in (2 * t, 2 * t + 1):
                m, l, acc = done[h]
                both.append(acc / l)
                lse_ref[h : h + 1, r] = m + jnp.log(l)
            o_ref[r, pl.ds(t * 128, 128)] = jnp.concatenate(both, axis=0).T.astype(BF)


def attend(qkv, begin):
    rows, wide = qkv.shape[0], qkv.shape[1] // 3
    size = block_of(rows)
    half = jax.ShapeDtypeStruct((rows, wide), BF)
    return pl.pallas_call(
        attend_kernel,
        in_specs=[pl.BlockSpec(memory_space=pltpu.SMEM)] + [IN_VMEM] * 6,
        out_specs=[IN_VMEM] * 5,
        out_shape=[half] * 4 + [jax.ShapeDtypeStruct((wide // HEAD, rows), F32)],
        scratch_shapes=[pltpu.VMEM((wide, rows), BF)],
        compiler_params=pltpu.CompilerParams(vmem_limit_bytes=48 << 20),
        name="attend",
    )(begin[0, ::size] // size, qkv, *turn_tables(rows), begin)


def attend_back_work(ins, out_ref, bias_ref, scratch):
    q_ref, k_ref, v_ref, o_ref, do_ref, lse_ref, cos_ref, sin_ref, cosf_ref, sinf_ref, begin_ref = ins
    kt_ref, dq_ref, dk_ref, dv_ref = scratch
    rows, wide = q_ref.shape
    pairs, size = wide // 128, block_of(rows)
    tables = (cos_ref, sin_ref, cosf_ref, sinf_ref)
    left = lax.broadcasted_iota(jnp.int32, (size, 128), 1) < HEAD
    key_at = lax.broadcasted_iota(jnp.int32, (size, size), 0)
    query_at = lax.broadcasted_iota(jnp.int32, (1, size), 1)

    @pl.loop(0, rows // BLK)
    def _(i):
        r = pl.ds(pl.multiple_of(i * BLK, BLK), BLK)
        for t in range(pairs):
            w = pl.ds(t * 128, 128)
            kt_ref[w, r] = k_ref[r, w].astype(F32).T.astype(BF)
            dk_ref[r, w] = jnp.zeros((BLK, 128), F32)
            dv_ref[r, w] = jnp.zeros((BLK, 128), F32)

    @pl.loop(0, rows // size)
    def _(i):
        r = pl.ds(pl.multiple_of(i * size, size), size)
        qs, dos, deltas, lses = [], [], [], []
        for t in range(pairs):
            w = pl.ds(t * 128, 128)
            do = do_ref[r, w]
            qs += two_heads(q_ref[r, w], left)
            dos += two_heads(do, left)
            prod = (do.astype(F32) * o_ref[r, w].astype(F32)).T
            deltas += [jnp.sum(prod[:HEAD], axis=0, keepdims=True), jnp.sum(prod[HEAD:], axis=0, keepdims=True)]
            lses += [lse_ref[2 * t : 2 * t + 1, r], lse_ref[2 * t + 1 : 2 * t + 2, r]]
        begin = begin_ref[0:1, r]
        here = query_at + i * size

        def step(j, carry):
            w = pl.ds(pl.multiple_of(j * size, size), size)
            key = key_at + j * size
            seen = (key <= here) & (key >= begin)
            out = []
            for t in range(pairs):
                lanes = pl.ds(t * 128, 128)
                k, v = k_ref[w, lanes], v_ref[w, lanes]
                dk = dv = None
                for h in (2 * t, 2 * t + 1):
                    prob = jnp.exp(jnp.where(seen, mm(k, qs[h], 1, 1) - lses[h], NEG))
                    ds = (prob * (mm(v, dos[h], 1, 1) - deltas[h])).astype(BF)
                    out.append(carry[h] + mm(kt_ref[pl.ds(h * HEAD, HEAD), w], ds, 1, 0))
                    dk_h, dv_h = mm(ds, qs[h], 1, 0), mm(prob.astype(BF), dos[h], 1, 0)
                    dk, dv = (dk_h, dv_h) if dk is None else (dk + dk_h, dv + dv_h)
                dk_ref[w, lanes] += dk
                dv_ref[w, lanes] += dv
            return tuple(out)

        done = lax.fori_loop(0, i + 1, step, (jnp.zeros((HEAD, size), F32),) * (2 * pairs))
        for t in range(pairs):
            both = jnp.concatenate(done[2 * t : 2 * t + 2], axis=0)
            dq_ref[r, pl.ds(t * 128, 128)] = both.T * (HEAD**-0.5)

    bias_ref[...] = jnp.zeros_like(bias_ref)

    @pl.loop(0, rows // BLK)
    def _(i):
        r = pl.ds(pl.multiple_of(i * BLK, BLK), BLK)
        for t in range(pairs):
            w = pl.ds(t * 128, 128)
            for part, value in enumerate((turn(dq_ref[r, w], i, tables, -1.0), turn(dk_ref[r, w], i, tables, -1.0), dv_ref[r, w])):
                lanes = pl.ds(part * wide + t * 128, 128)
                value = value.astype(BF)
                out_ref[r, lanes] = value
                bias_ref[:, lanes] += jnp.sum(value.astype(F32), axis=0, keepdims=True)


def attend_back(S, C, T, number, q, k, v, o, do, lse, begin, act, wd, riders):
    rows, wide = q.shape
    K, D, n = act.shape[1], wd.shape[0], rows // (S * T)

    def kernel(ride, ins, outs, scratch):
        _, _, row, col = plane(S)
        greet(S, C, row + [col], other=True, axes=ride.axes)

        def meanwhile():
            ride.start()
            attend_back_work(ins[2:], outs[0], outs[1], scratch[:4])

        sum_over_plane(S, T, ins[0], ins[1], outs[2], scratch[4:], meanwhile)
        ride.wait()

    args = [act.reshape(S * T, n, K), wd, q, k, v, o, do, lse, *turn_tables(rows), begin]
    return comm(
        kernel, S, C, number, "attend_back", args, [IN_VMEM] * len(args),
        [(jax.ShapeDtypeStruct((rows, 3 * wide), BF), IN_VMEM), (jax.ShapeDtypeStruct((1, 3 * wide), F32), IN_VMEM),
         (jax.ShapeDtypeStruct((n, D), F32), IN_VMEM)],
        [pltpu.VMEM((wide, rows), BF)] + [pltpu.VMEM((rows, wide), F32)] * 3 + sum_scratch(S, n, D),
        riders,
    )


def doc_begins(lengths_row, rows):
    row_ids = jnp.arange(rows, dtype=jnp.int32)
    ends = jnp.cumsum(lengths_row, dtype=jnp.int32)
    begins = ends - lengths_row
    inside = (row_ids[:, None] >= begins[None, :]) & (row_ids[:, None] < ends[None, :])
    return jnp.sum(jnp.where(inside, begins[None, :], 0), axis=1, dtype=jnp.int32)


def tiles_of(parts, lead):
    flat = jnp.concatenate([x.astype(F32).reshape(lead + (-1,)) for x in parts], axis=-1)
    flat = jnp.pad(flat, ((0, 0),) * len(lead) + ((0, 1024 - flat.shape[-1]),))
    return flat.reshape(lead + (8, 128))


def make_body(S, C, T):
    assert S == C

    def body(tokens, lengths, w_qkv, b_qkv, w_out, w_gateup, w_down, norm_gain, norm_bias, cotangent):
        p, z, c = lax.axis_index("shard"), lax.axis_index("ctx"), lax.axis_index("tp")
        R, D = tokens.shape
        n = R // T
        nb = D // (S * C)
        L = R * C

        def to_parts(x):
            return x.reshape(n, S, C, nb).transpose(2, 0, 1, 3).reshape(S, n, D // S)

        def parts(x):
            return x.reshape(n, S, D // S).swapaxes(0, 1)

        def unpermute(x):
            return x.reshape(x.shape[0], C, S, nb).swapaxes(1, 2).reshape(x.shape)

        def own(x):
            return lax.dynamic_slice_in_dim(x, (p * T + c) * n, n, 0)

        def half_of(x):
            return lax.dynamic_slice_in_dim(x, c * n, n, 0)

        def after(x, y):
            return lax.optimization_barrier((x, y))

        def over_ctx(w):
            return lax.all_gather(w.reshape(S * nb, -1), "ctx", axis=0, tiled=True)

        def sum_ctx(g):
            g = lax.psum_scatter(g.astype(BF), "ctx", scatter_dimension=0, tiled=True)
            return g.reshape(S, nb, -1)

        hn = w_qkv.shape[3] // S
        fn = w_gateup.shape[3] // S
        heads = hn // HEAD
        nf = HEAD // (S * C)

        tile = tiles_of((norm_gain[0].reshape(-1), norm_bias[0].reshape(-1), b_qkv[0].reshape(-1), lengths[0]), ())
        small, _, tok, wq, wo = exchange(
            S, C, T, 0,
            [
                ("shard", w_qkv[0].reshape(nb, 3, S, hn).transpose(2, 0, 1, 3).reshape(S, nb, 3 * hn)),
                ("shard", w_out[0].reshape(S, hn, nb).swapaxes(1, 2)),
            ],
            jnp.broadcast_to(tile, (C, S, 8, 128)),
            to_parts(half_of(tokens)),
        )
        wq = over_ctx(wq)
        tok, wo, wg, wd, cot = gather_columns(
            S, C, T, 1, tok,
            [
                ("all", wo.reshape(S * nb, hn)),
                ("shard", w_gateup[0].reshape(nb, 2, S, fn).transpose(2, 0, 1, 3).reshape(S, nb, 2 * fn)),
                ("shard", w_down[0].reshape(S, fn, nb).swapaxes(1, 2)),
                ("shard", to_parts(half_of(cotangent))),
            ],
        )
        wo, wg, wd = wo.reshape(D, hn), over_ctx(wg), over_ctx(wd)

        small = lax.dynamic_index_in_dim(small, c, 0, keepdims=False).reshape(C, S, 1024)
        norms = small[:, :, : 4 * nb].reshape(C * S, 4, nb).swapaxes(0, 1).reshape(4, D)
        gains, shifts = norms[:2], norms[2:]
        nbias = 3 * S * heads * nf
        bias = small[:, :, 4 * nb : 4 * nb + nbias].reshape(C, S, 3, S * heads, nf)
        bias = lax.dynamic_slice_in_dim(bias, p * heads, heads, 3)
        bias = bias.transpose(2, 3, 1, 0, 4).reshape(1, 3 * hn)
        docs = lengths.shape[1]
        lengths_row = lax.dynamic_index_in_dim(
            small[0, :, 4 * nb + nbias : 4 * nb + nbias + docs], z, 0, keepdims=False
        ).astype(jnp.int32)
        begin = doc_begins(lengths_row, L)
        begin = begin[None, :]

        n1 = (norm_of(tok.astype(F32))[0] * gains[0] + shifts[0]).astype(BF)
        own_tok = own(tok)
        qkv = mm(n1, wq, 1, 0) + bias
        q, k, v, o, lse = attend(qkv, begin)
        mid, n2, cot = sum_norm_gather(S, C, T, 2, o, wo, own_tok, gains[1:], shifts[1:], [("ctx", cot)])
        cot, n2 = after(cot, n2)
        (gb,) = gather_columns(S, C, T, 4, cot)
        gu, act = by_rows(
            gates_kernel, "gates", [(True, n2), (False, wg)],
            [jax.ShapeDtypeStruct((L, 2 * fn), F32), jax.ShapeDtypeStruct((L, fn), BF)],
        )
        gw_down = mm(gb, act, 0, 0).astype(BF)
        wd, gw_down = after(wd, gw_down)
        gw_down = sum_ctx(gw_down)

        (dgu,) = by_rows(
            gates_back_kernel, "gates_back", [(True, gb), (False, wd), (True, gu)],
            [jax.ShapeDtypeStruct((L, 2 * fn), BF)],
        )
        gw_gateup = mm(n2, dgu, 0, 0).astype(BF)
        dgu, gw_gateup = after(dgu, gw_gateup)
        gw_gateup = sum_ctx(gw_gateup)
        dmid, gb1, stats2 = sum_back_gather(S, C, T, 6, dgu, wg, mid, own(gb), gains[1:])
        gw_out = mm(gb1, o, 0, 0).astype(BF)
        gb1, gw_out = after(gb1, gw_out)
        gw_out = sum_ctx(gw_out)
        do = mm(gb1, wo, 1, 0).astype(BF)
        dqkv, gbias, got, gw_down = attend_back(
            S, C, T, 11, q, k, v, o, do, lse, begin, act, wd, [("shard", gw_down)]
        )
        out = parts((mid + got).astype(BF))
        gw_qkv = mm(n1, dqkv, 0, 0).astype(BF)
        dqkv, gw_qkv = after(dqkv, gw_qkv)
        gw_qkv = sum_ctx(gw_qkv)
        low, stats1, out, gw_gateup = sum_back(
            S, C, T, 8, dqkv, wq, own_tok, dmid, gains[:1], [("shard", out), ("shard", gw_gateup)]
        )
        low, gw_gateup, gw_down = lax.optimization_barrier((low, gw_gateup, gw_down))
        gw_gateup = gw_gateup.astype(F32).reshape(S, nb, 2, fn).transpose(1, 2, 0, 3).reshape(w_gateup.shape)
        gw_down = gw_down.astype(F32).swapaxes(1, 2).reshape(w_down.shape)
        low, gw_gateup, gw_down = lax.optimization_barrier((low, gw_gateup, gw_down))
        gtok, out, small, gw_qkv, gw_out = finish(
            S, C, T, 10, low, out, [stats1, stats2], gbias, [("shard", gw_qkv), ("shard", gw_out)]
        )
        if not ordered(D, S, C):
            gtok, out = unpermute(gtok), unpermute(out)
        gtok = gtok.astype(F32)
        norms = lax.dynamic_slice_in_dim(jnp.sum(small[..., :4, :], axis=(0, 1, 2)), (z * S + p) * nb % 128, nb, 1)
        gbias = lax.dynamic_index_in_dim(small, c, 0, keepdims=False)[:, :, 4 : 4 + 3 * hn // 128]
        gbias = jnp.sum(gbias, axis=0).reshape(S, 3, heads, S * C, nf)
        gbias = lax.dynamic_index_in_dim(gbias, p * C + z, 3, keepdims=False)
        gbias = gbias.swapaxes(0, 1).reshape(b_qkv.shape)

        return (
            out,
            gtok,
            gw_qkv.astype(F32).reshape(S, nb, 3, hn).transpose(1, 2, 0, 3).reshape(w_qkv.shape),
            gbias,
            gw_out.astype(F32).swapaxes(1, 2).reshape(w_out.shape),
            gw_gateup,
            gw_down,
            jnp.stack((norms[0], norms[2]))[None],
            jnp.stack((norms[1], norms[3]))[None],
        )

    return body


def solution(mesh):
    both = ("shard", "ctx")
    specs = (
        P(None, both, None, "tp"),
        P(None, None, "tp", both),
        P(None, "tp", both),
        P(None, both, None, "tp"),
        P(None, "tp", both),
        P(None, None, both),
        P(None, None, both),
    )
    return jax.shard_map(
        make_body(mesh.shape["shard"], mesh.shape["ctx"], mesh.shape["tp"]),
        mesh=mesh,
        in_specs=(P(both, None), P("shard", None)) + specs + (P(both, None),),
        out_specs=(P(both, None), P(both, None)) + specs,
        check_vma=False,
    )
```

```python
import functools

import jax
import jax.numpy as jnp
import numpy as np
from jax import lax
from jax.experimental import pallas as pl
from jax.experimental.pallas import tpu as pltpu
from jax.sharding import PartitionSpec as P

HEAD = 64
ROT = 16
EPS = 1e-05
NEG = -1e30
BASE = 10000.0
BF = jnp.bfloat16
F32 = jnp.float32
BLK = 256
MESH = pl.DeviceIdType.MESH
DMA = pltpu.SemaphoreType.DMA
ANY = pl.BlockSpec(memory_space=pl.ANY)
IN_VMEM = pl.BlockSpec(memory_space=pltpu.VMEM)


def mm(a, b, ca, cb):
    return lax.dot_general(a, b, (((ca,), (cb,)), ((), ())), preferred_element_type=F32)


def remote(src, dst, send, recv, where):
    return pltpu.make_async_remote_copy(
        src_ref=src, dst_ref=dst, send_sem=send, recv_sem=recv, device_id=where, device_id_type=MESH
    )


def here():
    return lax.axis_index("shard"), lax.axis_index("ctx"), lax.axis_index("tp")


class Riders:
    def __init__(self, S, C, riders):
        self.S, self.C = S, C
        self.axes = [axis for axis, _ in riders]
        self.arrays = [x for _, x in riders]
        self.shapes = [
            jax.ShapeDtypeStruct((C,) + x.shape if axis == "all" else x.shape, x.dtype) for axis, x in riders
        ]
        count, most = len(riders), max(S, C) - 1
        self.scratch = [DMA((count, most)), DMA((count, most)), DMA((count,))] if count else []

    def bind(self, ins, outs, sems):
        self.ins, self.outs, self.sems = ins, outs, sems

    def start(self):
        p, z, c = here()
        self.moves = []
        for n, axis in enumerate(self.axes):
            src, dst = self.ins[n], self.outs[n]
            send, recv, own = self.sems
            if axis == "tp":
                copies = [remote(src, dst, send.at[n, 0], recv.at[n, 0], {"tp": 1 - c})]
            elif axis == "all":
                copies = [
                    remote(src, dst.at[z], send.at[n, k - 1], recv.at[n, k - 1], {"ctx": (z + k) % self.C})
                    for k in range(1, self.C)
                ]
                copies.append(pltpu.make_async_copy(src, dst.at[z], own.at[n]))
            else:
                size, me = (self.S, p) if axis == "shard" else (self.C, z)
                copies = [
                    remote(src.at[(me + k) % size], dst.at[me], send.at[n, k - 1], recv.at[n, k - 1], {axis: (me + k) % size})
                    for k in range(1, size)
                ]
                copies.append(pltpu.make_async_copy(src.at[me], dst.at[me], own.at[n]))
            for copy in copies:
                copy.start()
            self.moves += copies

    def wait(self):
        for copy in self.moves:
            copy.wait()


def greet(S, C, mates=(), line=False, other=False, axes=()):
    p, z, c = here()
    peers = [{"shard": q} for q in ([(p + k) % S for k in range(1, S)] if "shard" in axes else mates)]
    if line or "ctx" in axes or "all" in axes:
        peers += [{"ctx": (z + k) % C} for k in range(1, C)]
    if other or "tp" in axes:
        peers.append({"tp": 1 - c})
    barrier = pltpu.get_barrier_semaphore()
    for where in peers:
        pl.semaphore_signal(barrier, inc=1, device_id=where, device_id_type=MESH)
    pl.semaphore_wait(barrier, len(peers))


def comm(kernel, S, C, number, name, args, in_specs, outs, scratch, riders=()):
    ride = Riders(S, C, riders)
    na, nr, no, ns = len(args), len(ride.axes), len(outs), len(scratch)

    def body(*refs):
        ins, refs = refs[:na], refs[na:]
        rins, refs = refs[:nr], refs[nr:]
        os, refs = refs[:no], refs[no:]
        routs, refs = refs[:nr], refs[nr:]
        ride.bind(rins, routs, refs[ns:])
        kernel(ride, ins, os, refs[:ns])

    return pl.pallas_call(
        body,
        out_shape=[shape for shape, _ in outs] + ride.shapes,
        in_specs=list(in_specs) + [IN_VMEM] * nr,
        out_specs=[spec for _, spec in outs] + [ANY] * nr,
        scratch_shapes=list(scratch) + ride.scratch,
        compiler_params=pltpu.CompilerParams(
            collective_id=number, has_side_effects=True, vmem_limit_bytes=56 << 20
        ),
        cost_estimate=pl.CostEstimate(flops=0, bytes_accessed=120_000_000, transcendentals=0),
        name=name,
    )(*args, *ride.arrays)


def exchange(S, C, T, number, riders, tiles, rows=None):
    def kernel(ride, ins, outs, scratch):
        tile, got = ins[0], outs[0]
        send, recv, bsend, brecv, own = scratch[:5]
        p, z, c = here()
        everyone = [(i, j) for i in range(C) for j in range(S) if i or j]
        barrier = pltpu.get_barrier_semaphore()
        peers = [{"shard": (p + j) % S, "ctx": (z + i) % C} for i, j in everyone] + [{"tp": 1 - c}]
        for where in peers:
            pl.semaphore_signal(barrier, inc=1, device_id=where, device_id_type=MESH)
        pl.semaphore_wait(barrier, len(peers))

        def turn_over(source, target, k, axis, size, me):
            ssem, rsem, local = scratch[5:]
            hop = [pltpu.make_async_copy(source.at[me], target.at[me], local.at[k])]
            for j in range(1, size):
                q = (me + j) % size
                hop.append(remote(source.at[q], target.at[me], ssem.at[k, j - 1], rsem.at[k, j - 1], {axis: q}))
            for copy in hop:
                copy.start()
            return hop

        if rows is not None:
            first = turn_over(ins[1], outs[1], 0, "shard", S, p)
        local = pltpu.make_async_copy(tile.at[z, p], got.at[c, z, p], own)
        local.start()
        copies = []
        for at, (where, (i, j)) in enumerate(zip(peers, everyone)):
            q, g = (p + j) % S, (z + i) % C
            copies.append(remote(tile.at[g, q], got.at[c, z, p], send.at[at], recv.at[at], where))
            copies[-1].start()
        ride.start()
        if rows is not None:
            for copy in first:
                copy.wait()
            second = turn_over(outs[1], outs[2], 1, "ctx", C, z)
        local.wait()
        for copy in copies:
            copy.wait()
        back = remote(got.at[c], got.at[c], bsend, brecv, {"tp": 1 - c})
        back.start()
        back.wait_send()
        remote(got.at[1 - c], got.at[1 - c], bsend, brecv, {"tp": 1 - c}).wait_recv()
        if rows is not None:
            for copy in second:
                copy.wait()
        ride.wait()

    count, most = C * S - 1, max(S, C) - 1
    args, outs = [tiles], [(jax.ShapeDtypeStruct((T,) + tiles.shape, tiles.dtype), ANY)]
    scratch = [DMA((count,)), DMA((count,)), DMA, DMA, DMA]
    if rows is not None:
        args.append(rows)
        outs += [(jax.ShapeDtypeStruct(rows.shape, rows.dtype), IN_VMEM)] * 2
        scratch += [DMA((2, most)), DMA((2, most)), DMA((2,))]
    return comm(kernel, S, C, number, "exchange", args, [IN_VMEM] * len(args), outs, scratch, riders)


def plane(S):
    p, _, c = here()
    B = S // 2
    a, b = p // B, p % B
    return a, b, [a * B + (b + j) % B for j in range(1, B)], (1 - a) * B + b


def spread_sems(S):
    count = 4 + 4 * (S // 2 - 1)
    return [DMA((2 * count,)), DMA((2 * count,))]


def spread(S, own, region, send, recv):
    p, _, c = here()
    B = S // 2
    a, b, rows, col = plane(S)
    rows, col, other = [{"shard": q} for q in rows], {"shard": col}, {"tp": 1 - c}
    per = 4 + 4 * (B - 1)
    OWN, ROW, COL, VIA_COL, VIA_ROW = 0, 2, 2 + 2 * (B - 1), 4 + 2 * (B - 1), 4 + 3 * (B - 1)
    started = []

    def push(q, h, sem, where, first=False):
        view = region(q, h, c)
        copy = remote(own(h) if first else view, view, send.at[sem], recv.at[sem], where)
        copy.start()
        started.append(copy)

    def came(q, h, sem, core):
        view = region(q, h, core)
        remote(view, view, send.at[sem], recv.at[sem], other).wait_recv()

    for h in range(2):
        for j in range(1, B):
            push(p, h, ROW + 2 * (j - 1) + h, rows[j - 1], True)
    for h in (1, 0):
        push(p, h, COL + h, col, True)
    for h in range(2):
        push(p, h, per + OWN + h, other, True)

    def from_row(j, h):
        q = a * B + (b - j) % B
        came(q, h, ROW + 2 * (j - 1) + h, c)
        push(q, h, per + ROW + 2 * (j - 1) + h, other)
        return q

    def from_col(h):
        q = (1 - a) * B + b
        came(q, h, COL + h, c)
        push(q, h, per + COL + h, other)
        return q

    for j in range(1, B):
        q = from_row(j, 0)
        push(q, 0, VIA_COL + j - 1, col)
    q = from_col(1)
    for j in range(1, B):
        push(q, 1, VIA_ROW + j - 1, rows[j - 1])
    for j in range(1, B):
        from_row(j, 1)
    from_col(0)
    for j in range(1, B):
        q = (1 - a) * B + (b - j) % B
        came(q, 0, VIA_COL + j - 1, c)
        push(q, 0, per + VIA_COL + j - 1, other)
        came(q, 1, VIA_ROW + j - 1, c)
        push(q, 1, per + VIA_ROW + j - 1, other)
    for h in range(2):
        came(p, h, per + OWN + h, 1 - c)
        came((1 - a) * B + b, h, per + COL + h, 1 - c)
    for j in range(1, B):
        for h in range(2):
            came(a * B + (b - j) % B, h, per + ROW + 2 * (j - 1) + h, 1 - c)
        q = (1 - a) * B + (b - j) % B
        came(q, 0, per + VIA_COL + j - 1, 1 - c)
        came(q, 1, per + VIA_ROW + j - 1, 1 - c)
    for copy in started:
        copy.wait_send()


def gather_columns(S, C, T, number, x, riders=()):
    _, n, wide = x.shape

    def kernel(ride, ins, outs, scratch):
        (x_ref,), (out_ref,), (send, recv, own) = ins, outs, scratch
        p, _, c = here()
        _, _, rows, col = plane(S)

        def region(q, h, core):
            part = pl.ds(pl.multiple_of(q * wide, 128), wide)
            return out_ref.at[pl.ds(h * (C // 2), C // 2), core, :, part]

        local = [
            pltpu.make_async_copy(x_ref.at[pl.ds(h * (C // 2), C // 2)], region(p, h, c), own.at[h]) for h in range(2)
        ]
        for copy in local:
            copy.start()
        greet(S, C, rows + [col], other=True, axes=ride.axes)
        ride.start()
        spread(S, lambda h: x_ref.at[pl.ds(h * (C // 2), C // 2)], region, send, recv)
        for copy in local:
            copy.wait()
        ride.wait()

    out, *rest = comm(
        kernel, S, C, number, "gather_columns", [x], [IN_VMEM],
        [(jax.ShapeDtypeStruct((C, T, n, wide * S), x.dtype), ANY)], spread_sems(S) + [DMA((2,))], riders,
    )
    return [out.reshape(C * T * n, wide * S)] + rest


CHUNK = 512
ROWS = 32


def sum_scratch(S, n, D):
    half, B = n // 2, S // 2

    def vm(*shape):
        return pltpu.VMEM(shape, BF)

    return [
        vm(S, n, D), vm(S, n, D), vm(S, n, D), vm(B - 1, 2, half, D), vm(B, half, D),
        vm(B - 1, half, D), vm(half, D), vm(half, D), vm(B - 1, half, D),
        DMA((S,)), DMA((S,)), DMA((B - 1, 2)), DMA((B - 1, 2)), DMA((B,)), DMA((B,)), DMA((B,)), DMA((B,)),
    ]


def sum_over_plane(S, T, x_ref, w_ref, out_ref, scratch, meanwhile=None):
    away, sib, mine, row1, col1, row2, col2, to_col, to_row = scratch[:9]
    asend, arecv, rsend, rrecv, csend, crecv, fsend, frecv = scratch[9:]
    n, D = out_ref.shape
    half, B = n // 2, S // 2
    _, _, c = here()
    a, b, rows, col = plane(S)
    rows, col, other = [{"shard": q} for q in rows], {"shard": col}, {"tp": 1 - c}

    def chip(e):
        return ((a + e // B) % 2) * B + (b + e % B) % B

    def product(e, core, store):
        x = x_ref[chip(e) * T + core]

        def column(j, _):
            w = pl.ds(pl.multiple_of(j * CHUNK, CHUNK), CHUNK)
            store(w, mm(x, w_ref[w, :], 1, 1))
            return 0

        lax.fori_loop(0, D // CHUNK, column, 0)

    def to_other(e):
        return remote(away.at[e], sib.at[e], asend.at[e], arecv.at[e], other)

    def first(i, _):
        e = S - 1 - i

        def store(w, value):
            away[e, :, w] = value.astype(BF)

        product(e, 1 - c, store)
        to_other(e).start()
        return 0

    lax.fori_loop(0, S, first, 0)

    top, low = pl.ds(0, half), pl.ds(half, half)
    started = []

    def push(src, dst, send, recv, where):
        copy = remote(src, dst, send, recv, where)
        copy.start()
        started.append(copy)

    for e in range(S - 1, -1, -1):
        to_other(e).wait()

        def store(w, value):
            value = value + sib[e, :, w].astype(F32)
            if e:
                mine[e, :, w] = value.astype(BF)
            else:
                out_ref[:, w] = value

        product(e, c, store)
        j = e % B
        if e > B:
            push(mine.at[e, top], row1.at[j - 1, 1], rsend.at[j - 1, 1], rrecv.at[j - 1, 1], rows[j - 1])
            push(mine.at[e, low], col1.at[j], csend.at[j], crecv.at[j], col)
        elif e == B:
            push(mine.at[e, low], col1.at[0], csend.at[0], crecv.at[0], col)
        elif e:
            push(mine.at[e, top], row1.at[j - 1, 0], rsend.at[j - 1, 0], rrecv.at[j - 1, 0], rows[j - 1])

    def came(ref, send, recv):
        remote(ref, ref, send, recv, other).wait_recv()

    if meanwhile is not None:
        meanwhile()
    total = mine[B, top, :].astype(F32)
    for j in range(1, B):
        came(row1.at[j - 1, 1], rsend.at[j - 1, 1], rrecv.at[j - 1, 1])
        total = total + row1[j - 1, 1].astype(F32)
    to_col[...] = total.astype(BF)
    push(to_col, col2, fsend.at[0], frecv.at[0], col)
    for j in range(1, B):
        came(col1.at[j], csend.at[j], crecv.at[j])
        to_row[j - 1] = (mine[j, low, :].astype(F32) + col1[j].astype(F32)).astype(BF)
        push(to_row.at[j - 1], row2.at[j - 1], fsend.at[j], frecv.at[j], rows[j - 1])
    came(col1.at[0], csend.at[0], crecv.at[0])
    upper, lower = out_ref[top, :], out_ref[low, :] + col1[0].astype(F32)
    for j in range(1, B):
        came(row1.at[j - 1, 0], rsend.at[j - 1, 0], rrecv.at[j - 1, 0])
        upper = upper + row1[j - 1, 0].astype(F32)
    came(col2, fsend.at[0], frecv.at[0])
    out_ref[top, :] = upper + col2[...].astype(F32)
    for j in range(1, B):
        came(row2.at[j - 1], fsend.at[j], frecv.at[j])
        lower = lower + row2[j - 1].astype(F32)
    out_ref[low, :] = lower
    for copy in started:
        copy.wait_send()


def project(S, C, T, number, tok, raw, gain, shift, bias):
    L, D = tok.shape
    _, parts, nb, wide = raw.shape
    hn = wide // S
    most = S - 1

    def kernel(ride, ins, outs, scratch):
        tok_ref, raw_ref, gain_ref, shift_ref, bias_ref = ins
        n_ref, out_ref, w_ref = outs
        send, recv, own = scratch
        p, _, _ = here()
        mates = [(p + k) % S for k in range(1, S)]
        greet(S, C, mates)

        def lanes(q):
            return pl.ds(pl.multiple_of(q * hn, 128), hn)

        copies = []
        for part in range(parts):
            dst = w_ref.at[:, p, :, pl.ds(part * hn, hn)]
            for k, q in enumerate(mates):
                copies.append(
                    remote(raw_ref.at[:, part, :, lanes(q)], dst, send.at[k, part], recv.at[k, part], {"shard": q})
                )
            copies.append(pltpu.make_async_copy(raw_ref.at[:, part, :, lanes(p)], dst, own.at[part]))
        for copy in copies:
            copy.start()

        def normed(r):
            n_ref[r, :] = (norm_of(tok_ref[r, :].astype(F32))[0] * gain_ref[...] + shift_ref[...]).astype(BF)

        row_blocks(L, normed)
        for copy in copies:
            copy.wait()
        w = w_ref[...].reshape(D, parts * hn)

        @pl.loop(0, L // BLK)
        def _(i):
            r = pl.ds(pl.multiple_of(i * BLK, BLK), BLK)
            out_ref[r, :] = mm(n_ref[r, :], w, 1, 0) + bias_ref[...]

    n, out, w = comm(
        kernel, S, C, number, "project", [tok, raw, gain, shift, bias], [IN_VMEM] * 5,
        [
            (jax.ShapeDtypeStruct((L, D), BF), IN_VMEM), (jax.ShapeDtypeStruct((L, parts * hn), F32), IN_VMEM),
            (jax.ShapeDtypeStruct((C, S, nb, parts * hn), BF), IN_VMEM),
        ],
        [DMA((most, parts)), DMA((most, parts)), DMA((parts,))],
    )
    return n, out, w.reshape(D, parts * hn)


def gates_kernel(n2_ref, wg_ref, gu_ref, act_ref):
    both = mm(n2_ref[...], wg_ref[...], 1, 0)
    gu_ref[...] = both
    width = act_ref.shape[1]
    gate, up = both[:, :width], both[:, width:]
    act_ref[...] = (gate * jax.nn.sigmoid(gate) * up).astype(BF)


def gates_back_kernel(gb_ref, wd_ref, gu_ref, dgu_ref):
    dact = mm(gb_ref[...], wd_ref[...], 1, 0)
    both, width = gu_ref[...], dact.shape[1]
    gate, up = both[:, :width], both[:, width:]
    s = jax.nn.sigmoid(gate)
    dgate = dact * up * s * (1.0 + gate * (1.0 - s))
    dgu_ref[...] = jnp.concatenate((dgate, dact * gate * s), axis=1).astype(BF)


def by_rows(kernel, name, arrays, outs):
    L = outs[0].shape[0]

    def spec(width):
        return pl.BlockSpec((BLK, width), lambda i: (i, 0))

    return pl.pallas_call(
        kernel,
        grid=(L // BLK,),
        in_specs=[spec(x.shape[1]) if rows else pl.BlockSpec(x.shape, lambda i: (0, 0)) for rows, x in arrays],
        out_specs=[spec(x.shape[1]) for x in outs],
        out_shape=outs,
        compiler_params=pltpu.CompilerParams(vmem_limit_bytes=48 << 20),
        name=name,
    )(*[x for _, x in arrays])


def row_blocks(n, work):
    @pl.loop(0, n // ROWS)
    def _(i):
        work(pl.ds(pl.multiple_of(i * ROWS, ROWS), ROWS))


def norm_of(v):
    center = v - jnp.mean(v, axis=-1, keepdims=True)
    inverse = lax.rsqrt(jnp.mean(center * center, axis=-1, keepdims=True) + EPS)
    return center * inverse, inverse


def norm_back(v, g, gain, stats_ref):
    normal, inverse = norm_of(v)
    e = g * gain
    stats_ref[0:1, :] += jnp.sum(g * normal, axis=0, keepdims=True)
    stats_ref[1:2, :] += jnp.sum(g, axis=0, keepdims=True)
    return inverse * (
        e - jnp.mean(e, axis=-1, keepdims=True) - normal * jnp.mean(e * normal, axis=-1, keepdims=True)
    )


def spread_rows(S, T, src, out_ref, send, recv, own):
    p, _, c = here()
    half = src.shape[0] // 2
    local = pltpu.make_async_copy(src, out_ref.at[p * T + c], own)
    local.start()
    spread(
        S,
        lambda h: src.at[pl.ds(h * half, half)],
        lambda q, h, core: out_ref.at[q * T + core, pl.ds(h * half, half)],
        send,
        recv,
    )
    local.wait()


def sum_norm_gather(S, C, T, number, x, w, residual, gain, shift, riders=()):
    L, K = x.shape
    D, n = w.shape[0], L // (S * T)

    def kernel(ride, ins, outs, scratch):
        x_ref, w_ref, res_ref, gain_ref, shift_ref = ins
        v_ref, out_ref = outs
        acc, low, send, recv, own = scratch[:5]
        _, _, rows, col = plane(S)
        greet(S, C, rows + [col], other=True, axes=ride.axes)
        ride.start()
        sum_over_plane(S, T, x_ref, w_ref, acc, scratch[5:])

        def work(r):
            v = res_ref[r, :].astype(F32) + acc[r, :]
            v_ref[r, :] = v
            low[r, :] = (norm_of(v)[0] * gain_ref[...] + shift_ref[...]).astype(BF)

        row_blocks(n, work)
        spread_rows(S, T, low, out_ref, send, recv, own)
        ride.wait()

    v, out, *rest = comm(
        kernel, S, C, number, "sum_norm_gather", [x.reshape(S * T, n, K), w, residual, gain, shift], [IN_VMEM] * 5,
        [(jax.ShapeDtypeStruct((n, D), F32), IN_VMEM), (jax.ShapeDtypeStruct((S * T, n, D), BF), ANY)],
        [pltpu.VMEM((n, D), F32), pltpu.VMEM((n, D), BF)] + spread_sems(S) + [DMA] + sum_scratch(S, n, D),
        riders,
    )
    return [v, out.reshape(L, D)] + rest


def sum_back_gather(S, C, T, number, x, w, v, residual, gain, riders=()):
    L, K = x.shape
    D, n = w.shape[0], L // (S * T)

    def kernel(ride, ins, outs, scratch):
        x_ref, w_ref, in_ref, res_ref, gain_ref = ins
        v_ref, out_ref, stats = outs
        acc, low, send, recv, own = scratch[:5]
        _, _, rows, col = plane(S)
        greet(S, C, rows + [col], other=True, axes=ride.axes)
        ride.start()
        sum_over_plane(S, T, x_ref, w_ref, acc, scratch[5:])
        stats[...] = jnp.zeros_like(stats)

        def work(r):
            g = res_ref[r, :].astype(F32) + norm_back(in_ref[r, :], acc[r, :], gain_ref[...], stats)
            v_ref[r, :] = g
            low[r, :] = g.astype(BF)

        row_blocks(n, work)
        spread_rows(S, T, low, out_ref, send, recv, own)
        ride.wait()

    g, out, stats, *rest = comm(
        kernel, S, C, number, "sum_back_gather", [x.reshape(S * T, n, K), w, v, residual, gain], [IN_VMEM] * 5,
        [
            (jax.ShapeDtypeStruct((n, D), F32), IN_VMEM), (jax.ShapeDtypeStruct((S * T, n, D), BF), ANY),
            (jax.ShapeDtypeStruct((2, D), F32), IN_VMEM),
        ],
        [pltpu.VMEM((n, D), F32), pltpu.VMEM((n, D), BF)] + spread_sems(S) + [DMA] + sum_scratch(S, n, D),
        riders,
    )
    return [g, out.reshape(L, D), stats] + rest


def sum_back(S, C, T, number, x, w, v, residual, gain, riders=()):
    L, K = x.shape
    D, n = w.shape[0], L // (S * T)

    def kernel(ride, ins, outs, scratch):
        x_ref, w_ref, in_ref, res_ref, gain_ref = ins
        low, stats = outs
        acc = scratch[0]
        _, _, rows, col = plane(S)
        greet(S, C, rows + [col], other=True, axes=ride.axes)
        ride.start()
        sum_over_plane(S, T, x_ref, w_ref, acc, scratch[1:])
        stats[...] = jnp.zeros_like(stats)

        def work(r):
            g = res_ref[r, :] + norm_back(in_ref[r, :].astype(F32), acc[r, :], gain_ref[...], stats)
            low[r, :] = g.astype(BF)

        row_blocks(n, work)
        ride.wait()

    return comm(
        kernel, S, C, number, "sum_back", [x.reshape(S * T, n, K), w, v, residual, gain], [IN_VMEM] * 5,
        [(jax.ShapeDtypeStruct((n, D), BF), IN_VMEM), (jax.ShapeDtypeStruct((2, D), F32), IN_VMEM)],
        [pltpu.VMEM((n, D), F32)] + sum_scratch(S, n, D),
        riders,
    )


def finish(S, C, T, number, x, y, stats, bias, gateup, down, qkv, out):
    n, D = x.shape
    fn, hn = down.shape[2], out.shape[2]
    wide, lines = D // S, bias.shape[1] // 128
    nb = D // (S * C)
    count = sum(z.shape[0] for z in stats)
    tall = -(-(count + lines) // 8) * 8
    many = C * S - 1
    pieces = S if ordered(D, S, C) else 1

    def kernel(ride, ins, outs, scratch):
        x_ref, y_ref, stat_refs, bias_ref = ins[0], ins[1], ins[2:-5], ins[-5]
        gateup_ref, down_ref, qkv_ref, o_ref = ins[-4:]
        x_out, y_out, got, gateup_out, down_out, qkv_out, o_out = outs
        xbuf, xbuf2, ybuf2, tile, send, recv, own, psend, precv, pown, lsend, lrecv, tsend, trecv = scratch[:14]
        qkv_buf, o_buf, gsend, grecv, gown = scratch[14:]
        p, z, c = here()
        other = {"tp": 1 - c}
        everyone = [(i, j) for i in range(C) for j in range(S) if i or j]
        peers = [{"shard": (p + j) % S, "ctx": (z + i) % C} for i, j in everyone]
        barrier = pltpu.get_barrier_semaphore()
        for where in peers + [other]:
            pl.semaphore_signal(barrier, inc=1, device_id=where, device_id_type=MESH)
        pl.semaphore_wait(barrier, len(peers) + 1)

        def part(q):
            return pl.ds(pl.multiple_of(q * wide, 128), wide)

        def turn_over(source, target, at, size, me, axis):
            hop = [pltpu.make_async_copy(source(me), target, own.at[at])]
            for k in range(1, size):
                q = (me + k) % size
                hop.append(remote(source(q), target, send.at[at, k - 1], recv.at[at, k - 1], {axis: q}))
            for copy in hop:
                copy.start()
            return hop

        def arrive(buf, out, at):
            hop = []
            for i in range(pieces):
                src = pl.ds(i * (wide // pieces), wide // pieces)
                first = (i * C + p) * nb if pieces > 1 else p * wide
                dst = out.at[c, :, pl.ds(pl.multiple_of(first, 128), wide // pieces)]
                hop.append(pltpu.make_async_copy(buf.at[p, :, src], dst, pown.at[at, i]))
                for k in range(1, S):
                    q = (p + k) % S
                    hop.append(
                        remote(buf.at[q, :, src], dst, psend.at[at, k - 1, i], precv.at[at, k - 1, i], {"shard": q})
                    )
            for copy in hop:
                copy.start()
            return hop

        def both(ref, at):
            copy = remote(ref.at[c], ref.at[c], lsend.at[at], lrecv.at[at], other)
            copy.start()
            return copy

        def settle(ref, at, copy):
            copy.wait_send()
            remote(ref.at[1 - c], ref.at[1 - c], lsend.at[at], lrecv.at[at], other).wait_recv()

        x_hop = turn_over(lambda q: x_ref.at[:, part(q)], xbuf.at[p], 0, S, p, "shard")
        y_hop = turn_over(lambda q: y_ref.at[q], ybuf2.at[z], 1, C, z, "ctx")
        moves = []
        for i, (src, dst) in enumerate(((qkv_ref, qkv_buf), (o_ref, o_buf))):
            moves.append(pltpu.make_async_copy(src.at[p], dst.at[p], gown.at[i]))
            for k in range(1, S):
                q = (p + k) % S
                moves.append(remote(src.at[q], dst.at[p], gsend.at[i, k - 1], grecv.at[i, k - 1], {"shard": q}))
        for copy in moves:
            copy.start()
        tile[...] = jnp.zeros_like(tile)
        at = 0
        for ref in stat_refs:
            tile[at : at + ref.shape[0], :] = ref[...]
            at += ref.shape[0]
        for k in range(lines):
            for block in range(D // 128):
                tile[at + k : at + k + 1, pl.ds(block * 128, 128)] = bias_ref[:, pl.ds(k * 128, 128)]

        def columns(g, q):
            return tile.at[:, pl.ds(pl.multiple_of((g * S + q) * nb // 128 * 128, 128), 128)]

        small = [pltpu.make_async_copy(columns(z, p), got.at[c, z, p], own.at[3])]
        for k, (where, (i, j)) in enumerate(zip(peers, everyone)):
            small.append(
                remote(columns((z + i) % C, (p + j) % S), got.at[c, z, p], tsend.at[k], trecv.at[k], where)
            )
        for copy in small:
            copy.start()
        for copy in x_hop:
            copy.wait()
        x_hop = turn_over(lambda q: xbuf.at[q], xbuf2.at[z], 2, C, z, "ctx")
        for q in range(S):
            down_out[q * fn : (q + 1) * fn, :] = down_ref[q].astype(F32).T
        for copy in y_hop:
            copy.wait()
        y_hop = arrive(ybuf2, y_out, 0)
        for copy in small:
            copy.wait()
        small_last = both(got, 0)
        for i in range(2):
            for q in range(S):
                gateup_out[:, i, q * fn : (q + 1) * fn] = gateup_ref[q, :, i * fn : (i + 1) * fn].astype(F32)
        for copy in moves:
            copy.wait()
        for q in range(S):
            o_out[q * hn : (q + 1) * hn, :] = o_buf[q].astype(F32).T
            for i in range(3):
                qkv_out[i, :, q * hn : (q + 1) * hn] = qkv_buf[q, :, i * hn : (i + 1) * hn].astype(F32)
        for copy in x_hop:
            copy.wait()
        x_hop = arrive(xbuf2, x_out, 1)
        for copy in y_hop:
            copy.wait()
        y_last = both(y_out, 1)
        for copy in x_hop:
            copy.wait()
        x_last = both(x_out, 2)
        settle(got, 0, small_last)
        settle(y_out, 1, y_last)
        settle(x_out, 2, x_last)

    args = [x, y, *stats, bias, gateup, down, qkv, out]
    most = max(S, C) - 1
    home = (jax.ShapeDtypeStruct((T, n, D), BF), ANY)
    x, y, got, *rest = comm(
        kernel, S, C, number, "finish", args, [IN_VMEM] * len(args),
        [home, home, (jax.ShapeDtypeStruct((T, C, S, tall, 128), F32), ANY)]
        + [
            (jax.ShapeDtypeStruct(shape, F32), IN_VMEM)
            for shape in ((nb, 2, S * fn), (S * fn, nb), (3, nb, S * hn), (S * hn, nb))
        ],
        [
            pltpu.VMEM((S, n, wide), BF), pltpu.VMEM((C, n, wide), BF), pltpu.VMEM((C, n, wide), BF),
            pltpu.VMEM((tall, D), F32), DMA((3, most)), DMA((3, most)), DMA((4,)),
            DMA((2, S - 1, pieces)), DMA((2, S - 1, pieces)), DMA((2, pieces)), DMA((3,)), DMA((3,)),
            DMA((many,)), DMA((many,)),
            pltpu.VMEM(qkv.shape, BF), pltpu.VMEM(out.shape, BF), DMA((2, S - 1)), DMA((2, S - 1)), DMA((2,)),
        ],
    )
    return [x.reshape(T * n, D), y.reshape(T * n, D), got] + rest


def ordered(D, S, C):
    return D // (S * C) % 128 == 0


def turn_tables(rows):
    feature = np.arange(128) % HEAD
    freq = np.where(feature < ROT, BASE ** (-2.0 * (feature % (ROT // 2)) / ROT), 0.0)
    near = np.arange(BLK)[:, None] * freq
    far = np.arange(0, rows, BLK)[:, None] * freq
    return [jnp.asarray(f(x), F32) for x in (near, far) for f in (np.cos, np.sin)]


def turn(x, i, tables, sign):
    cos, sin, cos_far, sin_far = tables
    far_cos, far_sin = cos_far[pl.ds(i, 1), :], sin_far[pl.ds(i, 1), :]
    cos_t = cos[...] * far_cos - sin[...] * far_sin
    sin_t = sin[...] * far_cos + cos[...] * far_sin
    ahead = lax.broadcasted_iota(jnp.int32, x.shape, 1) % HEAD < ROT // 2
    partner = jnp.where(ahead, -pltpu.roll(x, 128 - ROT // 2, 1), pltpu.roll(x, ROT // 2, 1))
    return x * cos_t + partner * (sin_t * sign)


def two_heads(x, left):
    zero = jnp.zeros_like(x)
    return [jnp.where(left, x, zero), jnp.where(left, zero, x)]


def block_of(rows):
    return next(size for size in (512, 256) if rows % size == 0)


def attend_kernel(
    first_ref, qkv_ref, cos_ref, sin_ref, cosf_ref, sinf_ref, begin_ref,
    qo_ref, ko_ref, vo_ref, o_ref, lse_ref, vt_ref,
):
    rows, wide = qo_ref.shape
    pairs, size = wide // 128, block_of(rows)
    tables = (cos_ref, sin_ref, cosf_ref, sinf_ref)
    left = lax.broadcasted_iota(jnp.int32, (size, 128), 1) < HEAD
    key_at = lax.broadcasted_iota(jnp.int32, (size, size), 0)
    query_at = lax.broadcasted_iota(jnp.int32, (1, size), 1)

    @pl.loop(0, rows // BLK)
    def _(i):
        r = pl.ds(pl.multiple_of(i * BLK, BLK), BLK)
        for t in range(pairs):
            w = pl.ds(t * 128, 128)
            q, k, v = (qkv_ref[r, pl.ds(part * wide + t * 128, 128)] for part in range(3))
            qo_ref[r, w] = turn(q, i, tables, 1.0).astype(BF) * jnp.asarray(HEAD**-0.5, BF)
            ko_ref[r, w] = turn(k, i, tables, 1.0).astype(BF)
            vo_ref[r, w] = v.astype(BF)
            vt_ref[w, r] = v.T.astype(BF)

    @pl.loop(0, rows // size)
    def _(i):
        r = pl.ds(pl.multiple_of(i * size, size), size)
        qs = sum((two_heads(qo_ref[r, pl.ds(t * 128, 128)], left) for t in range(pairs)), [])
        begin = begin_ref[0:1, r]
        here = query_at + i * size

        def step(j, carry):
            w = pl.ds(pl.multiple_of(j * size, size), size)
            key = key_at + j * size
            seen = (key <= here) & (key >= begin)
            out = []
            for h in range(2 * pairs):
                m, l, acc = carry[h]
                s = jnp.where(seen, mm(ko_ref[w, pl.ds(h // 2 * 128, 128)], qs[h], 1, 1), NEG)
                top = jnp.maximum(m, jnp.max(s, axis=0, keepdims=True))
                fade = jnp.exp(m - top)
                e = jnp.exp(s - top)
                acc = acc * fade + mm(vt_ref[pl.ds(h * HEAD, HEAD), w], e.astype(BF), 1, 0)
                out.append((top, l * fade + jnp.sum(e, axis=0, keepdims=True), acc))
            return tuple(out)

        start = (
            jnp.full((1, size), NEG, F32), jnp.zeros((1, size), F32), jnp.zeros((HEAD, size), F32)
        )
        done = lax.fori_loop(first_ref[i], i + 1, step, (start,) * (2 * pairs))
        for t in range(pairs):
            both = []
            for h in (2 * t, 2 * t + 1):
                m, l, acc = done[h]
                both.append(acc / l)
                lse_ref[h : h + 1, r] = m + jnp.log(l)
            o_ref[r, pl.ds(t * 128, 128)] = jnp.concatenate(both, axis=0).T.astype(BF)


def attend(qkv, begin):
    rows, wide = qkv.shape[0], qkv.shape[1] // 3
    size = block_of(rows)
    half = jax.ShapeDtypeStruct((rows, wide), BF)
    return pl.pallas_call(
        attend_kernel,
        in_specs=[pl.BlockSpec(memory_space=pltpu.SMEM)] + [IN_VMEM] * 6,
        out_specs=[IN_VMEM] * 5,
        out_shape=[half] * 4 + [jax.ShapeDtypeStruct((wide // HEAD, rows), F32)],
        scratch_shapes=[pltpu.VMEM((wide, rows), BF)],
        compiler_params=pltpu.CompilerParams(vmem_limit_bytes=48 << 20),
        name="attend",
    )(begin[0, ::size] // size, qkv, *turn_tables(rows), begin)


def attend_back_work(ins, out_ref, bias_ref, scratch):
    q_ref, k_ref, v_ref, o_ref, do_ref, lse_ref, cos_ref, sin_ref, cosf_ref, sinf_ref, begin_ref = ins
    kt_ref, dq_ref, dk_ref, dv_ref = scratch
    rows, wide = q_ref.shape
    pairs, size = wide // 128, block_of(rows)
    tables = (cos_ref, sin_ref, cosf_ref, sinf_ref)
    left = lax.broadcasted_iota(jnp.int32, (size, 128), 1) < HEAD
    key_at = lax.broadcasted_iota(jnp.int32, (size, size), 0)
    query_at = lax.broadcasted_iota(jnp.int32, (1, size), 1)

    @pl.loop(0, rows // BLK)
    def _(i):
        r = pl.ds(pl.multiple_of(i * BLK, BLK), BLK)
        for t in range(pairs):
            w = pl.ds(t * 128, 128)
            kt_ref[w, r] = k_ref[r, w].astype(F32).T.astype(BF)
            dk_ref[r, w] = jnp.zeros((BLK, 128), F32)
            dv_ref[r, w] = jnp.zeros((BLK, 128), F32)

    @pl.loop(0, rows // size)
    def _(i):
        r = pl.ds(pl.multiple_of(i * size, size), size)
        qs, dos, deltas, lses = [], [], [], []
        for t in range(pairs):
            w = pl.ds(t * 128, 128)
            do = do_ref[r, w]
            qs += two_heads(q_ref[r, w], left)
            dos += two_heads(do, left)
            prod = (do.astype(F32) * o_ref[r, w].astype(F32)).T
            deltas += [jnp.sum(prod[:HEAD], axis=0, keepdims=True), jnp.sum(prod[HEAD:], axis=0, keepdims=True)]
            lses += [lse_ref[2 * t : 2 * t + 1, r], lse_ref[2 * t + 1 : 2 * t + 2, r]]
        begin = begin_ref[0:1, r]
        here = query_at + i * size

        def step(j, carry):
            w = pl.ds(pl.multiple_of(j * size, size), size)
            key = key_at + j * size
            seen = (key <= here) & (key >= begin)
            out = []
            for t in range(pairs):
                lanes = pl.ds(t * 128, 128)
                k, v = k_ref[w, lanes], v_ref[w, lanes]
                dk = dv = None
                for h in (2 * t, 2 * t + 1):
                    prob = jnp.exp(jnp.where(seen, mm(k, qs[h], 1, 1) - lses[h], NEG))
                    ds = (prob * (mm(v, dos[h], 1, 1) - deltas[h])).astype(BF)
                    out.append(carry[h] + mm(kt_ref[pl.ds(h * HEAD, HEAD), w], ds, 1, 0))
                    dk_h, dv_h = mm(ds, qs[h], 1, 0), mm(prob.astype(BF), dos[h], 1, 0)
                    dk, dv = (dk_h, dv_h) if dk is None else (dk + dk_h, dv + dv_h)
                dk_ref[w, lanes] += dk
                dv_ref[w, lanes] += dv
            return tuple(out)

        done = lax.fori_loop(0, i + 1, step, (jnp.zeros((HEAD, size), F32),) * (2 * pairs))
        for t in range(pairs):
            both = jnp.concatenate(done[2 * t : 2 * t + 2], axis=0)
            dq_ref[r, pl.ds(t * 128, 128)] = both.T * (HEAD**-0.5)

    bias_ref[...] = jnp.zeros_like(bias_ref)

    @pl.loop(0, rows // BLK)
    def _(i):
        r = pl.ds(pl.multiple_of(i * BLK, BLK), BLK)
        for t in range(pairs):
            w = pl.ds(t * 128, 128)
            for part, value in enumerate((turn(dq_ref[r, w], i, tables, -1.0), turn(dk_ref[r, w], i, tables, -1.0), dv_ref[r, w])):
                lanes = pl.ds(part * wide + t * 128, 128)
                value = value.astype(BF)
                out_ref[r, lanes] = value
                bias_ref[:, lanes] += jnp.sum(value.astype(F32), axis=0, keepdims=True)


def attend_back(S, C, T, number, q, k, v, o, do, lse, begin, act, wd, riders):
    rows, wide = q.shape
    K, D, n = act.shape[1], wd.shape[0], rows // (S * T)

    def kernel(ride, ins, outs, scratch):
        _, _, row, col = plane(S)
        greet(S, C, row + [col], other=True, axes=ride.axes)

        def meanwhile():
            ride.start()
            attend_back_work(ins[2:], outs[0], outs[1], scratch[:4])

        sum_over_plane(S, T, ins[0], ins[1], outs[2], scratch[4:], meanwhile)
        ride.wait()

    args = [act.reshape(S * T, n, K), wd, q, k, v, o, do, lse, *turn_tables(rows), begin]
    return comm(
        kernel, S, C, number, "attend_back", args, [IN_VMEM] * len(args),
        [(jax.ShapeDtypeStruct((rows, 3 * wide), BF), IN_VMEM), (jax.ShapeDtypeStruct((1, 3 * wide), F32), IN_VMEM),
         (jax.ShapeDtypeStruct((n, D), F32), IN_VMEM)],
        [pltpu.VMEM((wide, rows), BF)] + [pltpu.VMEM((rows, wide), F32)] * 3 + sum_scratch(S, n, D),
        riders,
    )


def doc_begins(lengths_row, rows):
    row_ids = jnp.arange(rows, dtype=jnp.int32)
    ends = jnp.cumsum(lengths_row, dtype=jnp.int32)
    begins = ends - lengths_row
    inside = (row_ids[:, None] >= begins[None, :]) & (row_ids[:, None] < ends[None, :])
    return jnp.sum(jnp.where(inside, begins[None, :], 0), axis=1, dtype=jnp.int32)


def tiles_of(parts, lead):
    flat = jnp.concatenate([x.astype(F32).reshape(lead + (-1,)) for x in parts], axis=-1)
    flat = jnp.pad(flat, ((0, 0),) * len(lead) + ((0, 1024 - flat.shape[-1]),))
    return flat.reshape(lead + (8, 128))


def make_body(S, C, T):
    assert S == C

    def body(tokens, lengths, w_qkv, b_qkv, w_out, w_gateup, w_down, norm_gain, norm_bias, cotangent):
        p, z, c = lax.axis_index("shard"), lax.axis_index("ctx"), lax.axis_index("tp")
        R, D = tokens.shape
        n = R // T
        nb = D // (S * C)
        L = R * C

        def to_parts(x):
            return x.reshape(n, S, C, nb).transpose(2, 0, 1, 3).reshape(S, n, D // S)

        def parts(x):
            return x.reshape(n, S, D // S).swapaxes(0, 1)

        def unpermute(x):
            return x.reshape(x.shape[0], C, S, nb).swapaxes(1, 2).reshape(x.shape)

        def own(x):
            return lax.dynamic_slice_in_dim(x, (p * T + c) * n, n, 0)

        def half_of(x):
            return lax.dynamic_slice_in_dim(x, c * n, n, 0)

        def after(x, y):
            return lax.optimization_barrier((x, y))

        def over_ctx(w):
            return lax.all_gather(w.reshape(S * nb, -1), "ctx", axis=0, tiled=True)

        def sum_ctx(g):
            g = lax.psum_scatter(g.astype(BF), "ctx", scatter_dimension=0, tiled=True)
            return g.reshape(S, nb, -1)

        hn = w_qkv.shape[3] // S
        fn = w_gateup.shape[3] // S
        heads = hn // HEAD
        nf = HEAD // (S * C)

        tile = tiles_of((norm_gain[0].reshape(-1), norm_bias[0].reshape(-1), b_qkv[0].reshape(-1), lengths[0]), ())
        raw = lax.all_gather(w_qkv[0].swapaxes(0, 1).reshape(3 * nb, -1), "ctx", axis=0, tiled=True)
        small, _, tok, wo, wg, wd, cot = exchange(
            S, C, T, 0,
            [
                ("shard", w_out[0].reshape(S, hn, nb).swapaxes(1, 2)),
                ("shard", w_gateup[0].reshape(nb, 2, S, fn).transpose(2, 0, 1, 3).reshape(S, nb, 2 * fn)),
                ("shard", w_down[0].reshape(S, fn, nb).swapaxes(1, 2)),
                ("shard", to_parts(half_of(cotangent))),
            ],
            jnp.broadcast_to(tile, (C, S, 8, 128)),
            to_parts(half_of(tokens)),
        )
        tok, wo = gather_columns(S, C, T, 1, tok, [("all", wo.reshape(S * nb, hn))])
        wo, wg, wd = wo.reshape(D, hn), over_ctx(wg), over_ctx(wd)

        small = lax.dynamic_index_in_dim(small, c, 0, keepdims=False).reshape(C, S, 1024)
        norms = small[:, :, : 4 * nb].reshape(C * S, 4, nb).swapaxes(0, 1).reshape(4, D)
        gains, shifts = norms[:2], norms[2:]
        nbias = 3 * S * heads * nf
        bias = small[:, :, 4 * nb : 4 * nb + nbias].reshape(C, S, 3, S * heads, nf)
        bias = lax.dynamic_slice_in_dim(bias, p * heads, heads, 3)
        bias = bias.transpose(2, 3, 1, 0, 4).reshape(1, 3 * hn)
        docs = lengths.shape[1]
        lengths_row = lax.dynamic_index_in_dim(
            small[0, :, 4 * nb + nbias : 4 * nb + nbias + docs], z, 0, keepdims=False
        ).astype(jnp.int32)
        begin = doc_begins(lengths_row, L)
        begin = begin[None, :]

        n1, qkv, wq = project(S, C, T, 12, tok, raw.reshape(C, 3, nb, -1), gains[:1], shifts[:1], bias)
        own_tok = own(tok)
        q, k, v, o, lse = attend(qkv, begin)
        mid, n2, cot = sum_norm_gather(S, C, T, 2, o, wo, own_tok, gains[1:], shifts[1:], [("ctx", cot)])
        cot, n2 = after(cot, n2)
        (gb,) = gather_columns(S, C, T, 4, cot)
        gu, act = by_rows(
            gates_kernel, "gates", [(True, n2), (False, wg)],
            [jax.ShapeDtypeStruct((L, 2 * fn), F32), jax.ShapeDtypeStruct((L, fn), BF)],
        )
        gw_down = mm(gb, act, 0, 0).astype(BF)
        wd, gw_down = after(wd, gw_down)
        gw_down = sum_ctx(gw_down)

        (dgu,) = by_rows(
            gates_back_kernel, "gates_back", [(True, gb), (False, wd), (True, gu)],
            [jax.ShapeDtypeStruct((L, 2 * fn), BF)],
        )
        gw_gateup = mm(n2, dgu, 0, 0).astype(BF)
        dgu, gw_gateup = after(dgu, gw_gateup)
        gw_gateup = sum_ctx(gw_gateup)
        dmid, gb1, stats2 = sum_back_gather(S, C, T, 6, dgu, wg, mid, own(gb), gains[1:])
        gw_out = mm(gb1, o, 0, 0).astype(BF)
        gb1, gw_out = after(gb1, gw_out)
        gw_out = sum_ctx(gw_out)
        do = mm(gb1, wo, 1, 0).astype(BF)
        dqkv, gbias, got, gw_down = attend_back(
            S, C, T, 11, q, k, v, o, do, lse, begin, act, wd, [("shard", gw_down)]
        )
        out = parts((mid + got).astype(BF))
        gw_qkv = mm(n1, dqkv, 0, 0).astype(BF)
        dqkv, gw_qkv = after(dqkv, gw_qkv)
        gw_qkv = sum_ctx(gw_qkv)
        low, stats1, out, gw_gateup = sum_back(
            S, C, T, 8, dqkv, wq, own_tok, dmid, gains[:1], [("shard", out), ("shard", gw_gateup)]
        )
        gtok, out, small, gw_gateup, gw_down, gw_qkv, gw_out = finish(
            S, C, T, 10, low, out, [stats1, stats2], gbias, gw_gateup, gw_down, gw_qkv, gw_out
        )
        if not ordered(D, S, C):
            gtok, out = unpermute(gtok), unpermute(out)
        gtok = gtok.astype(F32)
        norms = lax.dynamic_slice_in_dim(jnp.sum(small[..., :4, :], axis=(0, 1, 2)), (z * S + p) * nb % 128, nb, 1)
        gbias = lax.dynamic_index_in_dim(small, c, 0, keepdims=False)[:, :, 4 : 4 + 3 * hn // 128]
        gbias = jnp.sum(gbias, axis=0).reshape(S, 3, heads, S * C, nf)
        gbias = lax.dynamic_index_in_dim(gbias, p * C + z, 3, keepdims=False)
        gbias = gbias.swapaxes(0, 1).reshape(b_qkv.shape)

        return (
            out,
            gtok,
            gw_qkv.swapaxes(0, 1).reshape(w_qkv.shape),
            gbias,
            gw_out.reshape(w_out.shape),
            gw_gateup.reshape(w_gateup.shape),
            gw_down.reshape(w_down.shape),
            jnp.stack((norms[0], norms[2]))[None],
            jnp.stack((norms[1], norms[3]))[None],
        )

    return body


def solution(mesh):
    both = ("shard", "ctx")
    specs = (
        P(None, both, None, "tp"),
        P(None, None, "tp", both),
        P(None, "tp", both),
        P(None, both, None, "tp"),
        P(None, "tp", both),
        P(None, None, both),
        P(None, None, both),
    )
    return jax.shard_map(
        make_body(mesh.shape["shard"], mesh.shape["ctx"], mesh.shape["tp"]),
        mesh=mesh,
        in_specs=(P(both, None), P("shard", None)) + specs + (P(both, None),),
        out_specs=(P(both, None), P(both, None)) + specs,
        check_vma=False,
    )
```

```python
import functools

import jax
import jax.numpy as jnp
import numpy as np
from jax import lax
from jax.experimental import pallas as pl
from jax.experimental.pallas import tpu as pltpu
from jax.sharding import PartitionSpec as P

HEAD = 64
ROT = 16
EPS = 1e-05
NEG = -1e30
BASE = 10000.0
BF = jnp.bfloat16
F32 = jnp.float32
BLK = 256
MESH = pl.DeviceIdType.MESH
DMA = pltpu.SemaphoreType.DMA
ANY = pl.BlockSpec(memory_space=pl.ANY)
IN_VMEM = pl.BlockSpec(memory_space=pltpu.VMEM)


def mm(a, b, ca, cb):
    return lax.dot_general(a, b, (((ca,), (cb,)), ((), ())), preferred_element_type=F32)


def remote(src, dst, send, recv, where):
    return pltpu.make_async_remote_copy(
        src_ref=src, dst_ref=dst, send_sem=send, recv_sem=recv, device_id=where, device_id_type=MESH
    )


def here():
    return lax.axis_index("shard"), lax.axis_index("ctx"), lax.axis_index("tp")


class Riders:
    def __init__(self, S, C, riders):
        self.S, self.C = S, C
        self.axes = [axis for axis, _ in riders]
        self.arrays = [x for _, x in riders]
        self.shapes = [
            jax.ShapeDtypeStruct((C,) + x.shape if axis == "all" else x.shape, x.dtype) for axis, x in riders
        ]
        count, most = len(riders), max(S, C) - 1
        self.scratch = [DMA((count, most)), DMA((count, most)), DMA((count,))] if count else []

    def bind(self, ins, outs, sems):
        self.ins, self.outs, self.sems = ins, outs, sems

    def start(self):
        p, z, c = here()
        self.moves = []
        for n, axis in enumerate(self.axes):
            src, dst = self.ins[n], self.outs[n]
            send, recv, own = self.sems
            if axis == "tp":
                copies = [remote(src, dst, send.at[n, 0], recv.at[n, 0], {"tp": 1 - c})]
            elif axis == "all":
                copies = [
                    remote(src, dst.at[z], send.at[n, k - 1], recv.at[n, k - 1], {"ctx": (z + k) % self.C})
                    for k in range(1, self.C)
                ]
                copies.append(pltpu.make_async_copy(src, dst.at[z], own.at[n]))
            else:
                size, me = (self.S, p) if axis == "shard" else (self.C, z)
                copies = [
                    remote(src.at[(me + k) % size], dst.at[me], send.at[n, k - 1], recv.at[n, k - 1], {axis: (me + k) % size})
                    for k in range(1, size)
                ]
                copies.append(pltpu.make_async_copy(src.at[me], dst.at[me], own.at[n]))
            for copy in copies:
                copy.start()
            self.moves += copies

    def wait(self):
        for copy in self.moves:
            copy.wait()


def greet(S, C, mates=(), line=False, other=False, axes=()):
    p, z, c = here()
    peers = [{"shard": q} for q in ([(p + k) % S for k in range(1, S)] if "shard" in axes else mates)]
    if line or "ctx" in axes or "all" in axes:
        peers += [{"ctx": (z + k) % C} for k in range(1, C)]
    if other or "tp" in axes:
        peers.append({"tp": 1 - c})
    barrier = pltpu.get_barrier_semaphore()
    for where in peers:
        pl.semaphore_signal(barrier, inc=1, device_id=where, device_id_type=MESH)
    pl.semaphore_wait(barrier, len(peers))


def comm(kernel, S, C, number, name, args, in_specs, outs, scratch, riders=()):
    ride = Riders(S, C, riders)
    na, nr, no, ns = len(args), len(ride.axes), len(outs), len(scratch)

    def body(*refs):
        ins, refs = refs[:na], refs[na:]
        rins, refs = refs[:nr], refs[nr:]
        os, refs = refs[:no], refs[no:]
        routs, refs = refs[:nr], refs[nr:]
        ride.bind(rins, routs, refs[ns:])
        kernel(ride, ins, os, refs[:ns])

    return pl.pallas_call(
        body,
        out_shape=[shape for shape, _ in outs] + ride.shapes,
        in_specs=list(in_specs) + [IN_VMEM] * nr,
        out_specs=[spec for _, spec in outs] + [ANY] * nr,
        scratch_shapes=list(scratch) + ride.scratch,
        compiler_params=pltpu.CompilerParams(
            collective_id=number, has_side_effects=True, vmem_limit_bytes=56 << 20
        ),
        cost_estimate=pl.CostEstimate(flops=0, bytes_accessed=120_000_000, transcendentals=0),
        name=name,
    )(*args, *ride.arrays)


def exchange(S, C, T, number, riders, tiles, rows=None):
    def kernel(ride, ins, outs, scratch):
        tile, got = ins[0], outs[0]
        send, recv, bsend, brecv, own = scratch[:5]
        p, z, c = here()
        everyone = [(i, j) for i in range(C) for j in range(S) if i or j]
        barrier = pltpu.get_barrier_semaphore()
        peers = [{"shard": (p + j) % S, "ctx": (z + i) % C} for i, j in everyone] + [{"tp": 1 - c}]
        for where in peers:
            pl.semaphore_signal(barrier, inc=1, device_id=where, device_id_type=MESH)
        pl.semaphore_wait(barrier, len(peers))

        def turn_over(source, target, k, axis, size, me):
            ssem, rsem, local = scratch[5:]
            hop = [pltpu.make_async_copy(source.at[me], target.at[me], local.at[k])]
            for j in range(1, size):
                q = (me + j) % size
                hop.append(remote(source.at[q], target.at[me], ssem.at[k, j - 1], rsem.at[k, j - 1], {axis: q}))
            for copy in hop:
                copy.start()
            return hop

        if rows is not None:
            first = turn_over(ins[1], outs[1], 0, "shard", S, p)
        local = pltpu.make_async_copy(tile.at[z, p], got.at[c, z, p], own)
        local.start()
        copies = []
        for at, (where, (i, j)) in enumerate(zip(peers, everyone)):
            q, g = (p + j) % S, (z + i) % C
            copies.append(remote(tile.at[g, q], got.at[c, z, p], send.at[at], recv.at[at], where))
            copies[-1].start()
        ride.start()
        if rows is not None:
            for copy in first:
                copy.wait()
            second = turn_over(outs[1], outs[2], 1, "ctx", C, z)
        local.wait()
        for copy in copies:
            copy.wait()
        back = remote(got.at[c], got.at[c], bsend, brecv, {"tp": 1 - c})
        back.start()
        back.wait_send()
        remote(got.at[1 - c], got.at[1 - c], bsend, brecv, {"tp": 1 - c}).wait_recv()
        if rows is not None:
            for copy in second:
                copy.wait()
        ride.wait()

    count, most = C * S - 1, max(S, C) - 1
    args, outs = [tiles], [(jax.ShapeDtypeStruct((T,) + tiles.shape, tiles.dtype), ANY)]
    scratch = [DMA((count,)), DMA((count,)), DMA, DMA, DMA]
    if rows is not None:
        args.append(rows)
        outs += [(jax.ShapeDtypeStruct(rows.shape, rows.dtype), IN_VMEM)] * 2
        scratch += [DMA((2, most)), DMA((2, most)), DMA((2,))]
    return comm(kernel, S, C, number, "exchange", args, [IN_VMEM] * len(args), outs, scratch, riders)


def plane(S):
    p, _, c = here()
    B = S // 2
    a, b = p // B, p % B
    return a, b, [a * B + (b + j) % B for j in range(1, B)], (1 - a) * B + b


def spread_sems(S):
    count = 4 + 4 * (S // 2 - 1)
    return [DMA((2 * count,)), DMA((2 * count,))]


def spread(S, own, region, send, recv, work=(None, None)):
    p, _, c = here()
    B = S // 2
    a, b, rows, col = plane(S)
    rows, col, other = [{"shard": q} for q in rows], {"shard": col}, {"tp": 1 - c}
    per = 4 + 4 * (B - 1)
    OWN, ROW, COL, VIA_COL, VIA_ROW = 0, 2, 2 + 2 * (B - 1), 4 + 2 * (B - 1), 4 + 3 * (B - 1)
    started = []

    def push(q, h, sem, where, first=False):
        view = region(q, h, c)
        copy = remote(own(h) if first else view, view, send.at[sem], recv.at[sem], where)
        copy.start()
        started.append(copy)

    def came(q, h, sem, core):
        view = region(q, h, core)
        remote(view, view, send.at[sem], recv.at[sem], other).wait_recv()

    for h in range(2):
        for j in range(1, B):
            push(p, h, ROW + 2 * (j - 1) + h, rows[j - 1], True)
    for h in (1, 0):
        push(p, h, COL + h, col, True)
    for h in range(2):
        push(p, h, per + OWN + h, other, True)

    def from_row(j, h):
        q = a * B + (b - j) % B
        came(q, h, ROW + 2 * (j - 1) + h, c)
        push(q, h, per + ROW + 2 * (j - 1) + h, other)
        return q

    def from_col(h):
        q = (1 - a) * B + b
        came(q, h, COL + h, c)
        push(q, h, per + COL + h, other)
        return q

    if work[0] is not None:
        work[0]()
    for j in range(1, B):
        q = from_row(j, 0)
        push(q, 0, VIA_COL + j - 1, col)
    q = from_col(1)
    for j in range(1, B):
        push(q, 1, VIA_ROW + j - 1, rows[j - 1])
    if work[1] is not None:
        work[1]()
    for j in range(1, B):
        from_row(j, 1)
    from_col(0)
    for j in range(1, B):
        q = (1 - a) * B + (b - j) % B
        came(q, 0, VIA_COL + j - 1, c)
        push(q, 0, per + VIA_COL + j - 1, other)
        came(q, 1, VIA_ROW + j - 1, c)
        push(q, 1, per + VIA_ROW + j - 1, other)
    for h in range(2):
        came(p, h, per + OWN + h, 1 - c)
        came((1 - a) * B + b, h, per + COL + h, 1 - c)
    for j in range(1, B):
        for h in range(2):
            came(a * B + (b - j) % B, h, per + ROW + 2 * (j - 1) + h, 1 - c)
        q = (1 - a) * B + (b - j) % B
        came(q, 0, per + VIA_COL + j - 1, 1 - c)
        came(q, 1, per + VIA_ROW + j - 1, 1 - c)
    for copy in started:
        copy.wait_send()


def gather_columns(S, C, T, number, x, riders=(), extra=None):
    _, n, wide = x.shape
    more, more_specs, more_outs, more_scratch, task = extra or ((), (), (), (), None)

    def kernel(ride, ins, outs, scratch):
        x_ref, out_ref = ins[0], outs[0]
        send, recv, own = scratch[:3]
        p, _, c = here()
        _, _, rows, col = plane(S)

        def region(q, h, core):
            part = pl.ds(pl.multiple_of(q * wide, 128), wide)
            return out_ref.at[pl.ds(h * (C // 2), C // 2), core, :, part]

        local = [
            pltpu.make_async_copy(x_ref.at[pl.ds(h * (C // 2), C // 2)], region(p, h, c), own.at[h]) for h in range(2)
        ]
        for copy in local:
            copy.start()
        greet(S, C, rows + [col], other=True, axes=ride.axes)
        ride.start()
        work = [None, None]
        if task is not None:
            work = [functools.partial(task, ins[1:], outs[1:], scratch[3:], piece) for piece in range(2)]
        spread(S, lambda h: x_ref.at[pl.ds(h * (C // 2), C // 2)], region, send, recv, work)
        for copy in local:
            copy.wait()
        ride.wait()

    out, *rest = comm(
        kernel, S, C, number, "gather_columns", [x, *more], [IN_VMEM, *more_specs],
        [(jax.ShapeDtypeStruct((C, T, n, wide * S), x.dtype), ANY), *more_outs],
        spread_sems(S) + [DMA((2,)), *more_scratch], riders,
    )
    return [out.reshape(C * T * n, wide * S)] + rest


CHUNK = 512
ROWS = 32


def sum_scratch(S, n, D):
    half, B = n // 2, S // 2

    def vm(*shape):
        return pltpu.VMEM(shape, BF)

    return [
        vm(S, n, D), vm(S, n, D), vm(S, n, D), vm(B - 1, 2, half, D), vm(B, half, D),
        vm(B - 1, half, D), vm(half, D), vm(half, D), vm(B - 1, half, D),
        DMA((S,)), DMA((S,)), DMA((B - 1, 2)), DMA((B - 1, 2)), DMA((B,)), DMA((B,)), DMA((B,)), DMA((B,)),
    ]


def sum_over_plane(S, T, x_ref, w_ref, out_ref, scratch, meanwhile=None):
    away, sib, mine, row1, col1, row2, col2, to_col, to_row = scratch[:9]
    asend, arecv, rsend, rrecv, csend, crecv, fsend, frecv = scratch[9:]
    n, D = out_ref.shape
    half, B = n // 2, S // 2
    _, _, c = here()
    a, b, rows, col = plane(S)
    rows, col, other = [{"shard": q} for q in rows], {"shard": col}, {"tp": 1 - c}

    def chip(e):
        return ((a + e // B) % 2) * B + (b + e % B) % B

    def product(e, core, store):
        x = x_ref[chip(e) * T + core]

        def column(j, _):
            w = pl.ds(pl.multiple_of(j * CHUNK, CHUNK), CHUNK)
            store(w, mm(x, w_ref[w, :], 1, 1))
            return 0

        lax.fori_loop(0, D // CHUNK, column, 0)

    def to_other(e):
        return remote(away.at[e], sib.at[e], asend.at[e], arecv.at[e], other)

    def first(i, _):
        e = S - 1 - i

        def store(w, value):
            away[e, :, w] = value.astype(BF)

        product(e, 1 - c, store)
        to_other(e).start()
        return 0

    lax.fori_loop(0, S, first, 0)

    top, low = pl.ds(0, half), pl.ds(half, half)
    started = []

    def push(src, dst, send, recv, where):
        copy = remote(src, dst, send, recv, where)
        copy.start()
        started.append(copy)

    for e in range(S - 1, -1, -1):
        to_other(e).wait()

        def store(w, value):
            value = value + sib[e, :, w].astype(F32)
            if e:
                mine[e, :, w] = value.astype(BF)
            else:
                out_ref[:, w] = value

        product(e, c, store)
        j = e % B
        if e > B:
            push(mine.at[e, top], row1.at[j - 1, 1], rsend.at[j - 1, 1], rrecv.at[j - 1, 1], rows[j - 1])
            push(mine.at[e, low], col1.at[j], csend.at[j], crecv.at[j], col)
        elif e == B:
            push(mine.at[e, low], col1.at[0], csend.at[0], crecv.at[0], col)
        elif e:
            push(mine.at[e, top], row1.at[j - 1, 0], rsend.at[j - 1, 0], rrecv.at[j - 1, 0], rows[j - 1])

    def came(ref, send, recv):
        remote(ref, ref, send, recv, other).wait_recv()

    if meanwhile is not None:
        meanwhile()
    total = mine[B, top, :].astype(F32)
    for j in range(1, B):
        came(row1.at[j - 1, 1], rsend.at[j - 1, 1], rrecv.at[j - 1, 1])
        total = total + row1[j - 1, 1].astype(F32)
    to_col[...] = total.astype(BF)
    push(to_col, col2, fsend.at[0], frecv.at[0], col)
    for j in range(1, B):
        came(col1.at[j], csend.at[j], crecv.at[j])
        to_row[j - 1] = (mine[j, low, :].astype(F32) + col1[j].astype(F32)).astype(BF)
        push(to_row.at[j - 1], row2.at[j - 1], fsend.at[j], frecv.at[j], rows[j - 1])
    came(col1.at[0], csend.at[0], crecv.at[0])
    upper, lower = out_ref[top, :], out_ref[low, :] + col1[0].astype(F32)
    for j in range(1, B):
        came(row1.at[j - 1, 0], rsend.at[j - 1, 0], rrecv.at[j - 1, 0])
        upper = upper + row1[j - 1, 0].astype(F32)
    came(col2, fsend.at[0], frecv.at[0])
    out_ref[top, :] = upper + col2[...].astype(F32)
    for j in range(1, B):
        came(row2.at[j - 1], fsend.at[j], frecv.at[j])
        lower = lower + row2[j - 1].astype(F32)
    out_ref[low, :] = lower
    for copy in started:
        copy.wait_send()


def project(S, C, T, number, tok, raw, gain, shift, bias, riders):
    L, D = tok.shape
    _, parts, nb, wide = raw.shape
    hn = wide // S
    most = S - 1

    def kernel(ride, ins, outs, scratch):
        tok_ref, raw_ref, gain_ref, shift_ref, bias_ref = ins
        n_ref, out_ref, w_ref = outs
        send, recv, own = scratch
        p, _, _ = here()
        mates = [(p + k) % S for k in range(1, S)]
        greet(S, C, mates, axes=ride.axes)

        def lanes(q):
            return pl.ds(pl.multiple_of(q * hn, 128), hn)

        copies = []
        for part in range(parts):
            dst = w_ref.at[:, p, :, pl.ds(part * hn, hn)]
            for k, q in enumerate(mates):
                copies.append(
                    remote(raw_ref.at[:, part, :, lanes(q)], dst, send.at[k, part], recv.at[k, part], {"shard": q})
                )
            copies.append(pltpu.make_async_copy(raw_ref.at[:, part, :, lanes(p)], dst, own.at[part]))
        for copy in copies:
            copy.start()
        ride.start()

        def normed(r):
            n_ref[r, :] = (norm_of(tok_ref[r, :].astype(F32))[0] * gain_ref[...] + shift_ref[...]).astype(BF)

        row_blocks(L, normed)
        for copy in copies:
            copy.wait()
        w = w_ref[...].reshape(D, parts * hn)

        @pl.loop(0, L // BLK)
        def _(i):
            r = pl.ds(pl.multiple_of(i * BLK, BLK), BLK)
            out_ref[r, :] = mm(n_ref[r, :], w, 1, 0) + bias_ref[...]

        ride.wait()

    n, out, w, *rest = comm(
        kernel, S, C, number, "project", [tok, raw, gain, shift, bias], [IN_VMEM] * 5,
        [
            (jax.ShapeDtypeStruct((L, D), BF), IN_VMEM), (jax.ShapeDtypeStruct((L, parts * hn), F32), IN_VMEM),
            (jax.ShapeDtypeStruct((C, S, nb, parts * hn), BF), IN_VMEM),
        ],
        [DMA((most, parts)), DMA((most, parts)), DMA((parts,))],
        riders,
    )
    return [n, out, w.reshape(D, parts * hn)] + rest


def gates_kernel(n2_ref, wg_ref, gu_ref, act_ref):
    both = mm(n2_ref[...], wg_ref[...], 1, 0)
    gu_ref[...] = both
    width = act_ref.shape[1]
    gate, up = both[:, :width], both[:, width:]
    act_ref[...] = (gate * jax.nn.sigmoid(gate) * up).astype(BF)


def gates_back_kernel(gb_ref, wd_ref, gu_ref, dgu_ref):
    dact = mm(gb_ref[...], wd_ref[...], 1, 0)
    both, width = gu_ref[...], dact.shape[1]
    gate, up = both[:, :width], both[:, width:]
    s = jax.nn.sigmoid(gate)
    dgate = dact * up * s * (1.0 + gate * (1.0 - s))
    dgu_ref[...] = jnp.concatenate((dgate, dact * gate * s), axis=1).astype(BF)


def by_rows(kernel, name, arrays, outs):
    L = outs[0].shape[0]
    size = L // 2

    def spec(width):
        return pl.BlockSpec((size, width), lambda i: (i, 0))

    return pl.pallas_call(
        kernel,
        grid=(L // size,),
        in_specs=[spec(x.shape[1]) if rows else pl.BlockSpec(x.shape, lambda i: (0, 0)) for rows, x in arrays],
        out_specs=[spec(x.shape[1]) for x in outs],
        out_shape=outs,
        compiler_params=pltpu.CompilerParams(vmem_limit_bytes=60 << 20),
        name=name,
    )(*[x for _, x in arrays])


def row_blocks(n, work):
    @pl.loop(0, n // ROWS)
    def _(i):
        work(pl.ds(pl.multiple_of(i * ROWS, ROWS), ROWS))


def own_rows(T, x_ref, row_ref, sem):
    p, _, c = here()
    copy = pltpu.make_async_copy(x_ref.at[p * T + c], row_ref, sem)
    copy.start()
    return copy


def norm_of(v):
    center = v - jnp.mean(v, axis=-1, keepdims=True)
    inverse = lax.rsqrt(jnp.mean(center * center, axis=-1, keepdims=True) + EPS)
    return center * inverse, inverse


def norm_back(v, g, gain, stats_ref):
    normal, inverse = norm_of(v)
    e = g * gain
    stats_ref[0:1, :] += jnp.sum(g * normal, axis=0, keepdims=True)
    stats_ref[1:2, :] += jnp.sum(g, axis=0, keepdims=True)
    return inverse * (
        e - jnp.mean(e, axis=-1, keepdims=True) - normal * jnp.mean(e * normal, axis=-1, keepdims=True)
    )


def spread_rows(S, T, src, out_ref, send, recv, own):
    p, _, c = here()
    half = src.shape[0] // 2
    local = pltpu.make_async_copy(src, out_ref.at[p * T + c], own)
    local.start()
    spread(
        S,
        lambda h: src.at[pl.ds(h * half, half)],
        lambda q, h, core: out_ref.at[q * T + core, pl.ds(h * half, half)],
        send,
        recv,
    )
    local.wait()


def sum_norm_gather(S, C, T, number, x, w, residual, gain, shift, riders=()):
    L, K = x.shape
    D, n = w.shape[0], L // (S * T)

    def kernel(ride, ins, outs, scratch):
        x_ref, w_ref, all_ref, gain_ref, shift_ref = ins
        v_ref, out_ref = outs
        acc, low, send, recv, own, res_ref, sem = scratch[:7]
        _, _, rows, col = plane(S)
        rest = own_rows(T, all_ref, res_ref, sem)
        greet(S, C, rows + [col], other=True, axes=ride.axes)
        ride.start()
        sum_over_plane(S, T, x_ref, w_ref, acc, scratch[7:])
        rest.wait()

        def work(r):
            v = res_ref[r, :].astype(F32) + acc[r, :]
            v_ref[r, :] = v
            low[r, :] = (norm_of(v)[0] * gain_ref[...] + shift_ref[...]).astype(BF)

        row_blocks(n, work)
        spread_rows(S, T, low, out_ref, send, recv, own)
        ride.wait()

    v, out, *rest = comm(
        kernel, S, C, number, "sum_norm_gather", [x.reshape(S * T, n, K), w, residual.reshape(S * T, n, D), gain, shift],
        [IN_VMEM, IN_VMEM, ANY, IN_VMEM, IN_VMEM],
        [(jax.ShapeDtypeStruct((n, D), F32), IN_VMEM), (jax.ShapeDtypeStruct((S * T, n, D), BF), ANY)],
        [pltpu.VMEM((n, D), F32), pltpu.VMEM((n, D), BF)] + spread_sems(S)
        + [DMA, pltpu.VMEM((n, D), BF), DMA] + sum_scratch(S, n, D),
        riders,
    )
    return [v, out.reshape(L, D)] + rest


def sum_back_gather(S, C, T, number, x, w, v, residual, gain, riders=()):
    L, K = x.shape
    D, n = w.shape[0], L // (S * T)

    def kernel(ride, ins, outs, scratch):
        x_ref, w_ref, in_ref, all_ref, gain_ref = ins
        v_ref, out_ref, stats = outs
        acc, low, send, recv, own, res_ref, sem = scratch[:7]
        _, _, rows, col = plane(S)
        rest = own_rows(T, all_ref, res_ref, sem)
        greet(S, C, rows + [col], other=True, axes=ride.axes)
        ride.start()
        sum_over_plane(S, T, x_ref, w_ref, acc, scratch[7:])
        rest.wait()
        stats[...] = jnp.zeros_like(stats)

        def work(r):
            g = res_ref[r, :].astype(F32) + norm_back(in_ref[r, :], acc[r, :], gain_ref[...], stats)
            v_ref[r, :] = g
            low[r, :] = g.astype(BF)

        row_blocks(n, work)
        spread_rows(S, T, low, out_ref, send, recv, own)
        ride.wait()

    g, out, stats, *rest = comm(
        kernel, S, C, number, "sum_back_gather", [x.reshape(S * T, n, K), w, v, residual.reshape(S * T, n, D), gain],
        [IN_VMEM, IN_VMEM, IN_VMEM, ANY, IN_VMEM],
        [
            (jax.ShapeDtypeStruct((n, D), F32), IN_VMEM), (jax.ShapeDtypeStruct((S * T, n, D), BF), ANY),
            (jax.ShapeDtypeStruct((2, D), F32), IN_VMEM),
        ],
        [pltpu.VMEM((n, D), F32), pltpu.VMEM((n, D), BF)] + spread_sems(S)
        + [DMA, pltpu.VMEM((n, D), BF), DMA] + sum_scratch(S, n, D),
        riders,
    )
    return [g, out.reshape(L, D), stats] + rest


def sum_back(S, C, T, number, x, w, v, residual, gain, riders=()):
    L, K = x.shape
    D, n = w.shape[0], L // (S * T)

    def kernel(ride, ins, outs, scratch):
        x_ref, w_ref, all_ref, res_ref, gain_ref = ins
        low, stats = outs
        acc, in_ref, sem = scratch[:3]
        _, _, rows, col = plane(S)
        rest = own_rows(T, all_ref, in_ref, sem)
        greet(S, C, rows + [col], other=True, axes=ride.axes)
        ride.start()
        sum_over_plane(S, T, x_ref, w_ref, acc, scratch[3:])
        rest.wait()
        stats[...] = jnp.zeros_like(stats)

        def work(r):
            g = res_ref[r, :] + norm_back(in_ref[r, :].astype(F32), acc[r, :], gain_ref[...], stats)
            low[r, :] = g.astype(BF)

        row_blocks(n, work)
        ride.wait()

    return comm(
        kernel, S, C, number, "sum_back", [x.reshape(S * T, n, K), w, v.reshape(S * T, n, D), residual, gain],
        [IN_VMEM, IN_VMEM, ANY, IN_VMEM, IN_VMEM],
        [(jax.ShapeDtypeStruct((n, D), BF), IN_VMEM), (jax.ShapeDtypeStruct((2, D), F32), IN_VMEM)],
        [pltpu.VMEM((n, D), F32), pltpu.VMEM((n, D), BF), DMA] + sum_scratch(S, n, D),
        riders,
    )


def finish(S, C, T, number, x, y, stats, bias, gateup, down, qkv, out):
    n, D = x.shape
    fn, hn = down.shape[2], out.shape[2]
    wide, lines = D // S, bias.shape[1] // 128
    nb = D // (S * C)
    count = sum(z.shape[0] for z in stats)
    tall = -(-(count + lines) // 8) * 8
    many = C * S - 1
    pieces = S if ordered(D, S, C) else 1

    def kernel(ride, ins, outs, scratch):
        x_ref, y_ref, stat_refs, bias_ref = ins[0], ins[1], ins[2:-5], ins[-5]
        gateup_ref, down_ref, qkv_ref, o_ref = ins[-4:]
        x_out, y_out, norm_out, bias_out, gateup_out, down_out, qkv_out, o_out = outs
        xbuf, xbuf2, ybuf2, tile, send, recv, own, psend, precv, pown, lsend, lrecv, tsend, trecv = scratch[:14]
        qkv_buf, o_buf, gsend, grecv, gown, got = scratch[14:]
        p, z, c = here()
        other = {"tp": 1 - c}
        everyone = [(i, j) for i in range(C) for j in range(S) if i or j]
        peers = [{"shard": (p + j) % S, "ctx": (z + i) % C} for i, j in everyone]
        barrier = pltpu.get_barrier_semaphore()
        for where in peers + [other]:
            pl.semaphore_signal(barrier, inc=1, device_id=where, device_id_type=MESH)
        pl.semaphore_wait(barrier, len(peers) + 1)

        def part(q):
            return pl.ds(pl.multiple_of(q * wide, 128), wide)

        def turn_over(source, target, at, size, me, axis):
            hop = [pltpu.make_async_copy(source(me), target, own.at[at])]
            for k in range(1, size):
                q = (me + k) % size
                hop.append(remote(source(q), target, send.at[at, k - 1], recv.at[at, k - 1], {axis: q}))
            for copy in hop:
                copy.start()
            return hop

        def arrive(buf, out, at):
            hop = []
            for i in range(pieces):
                src = pl.ds(i * (wide // pieces), wide // pieces)
                first = (i * C + p) * nb if pieces > 1 else p * wide
                dst = out.at[c, :, pl.ds(pl.multiple_of(first, 128), wide // pieces)]
                hop.append(pltpu.make_async_copy(buf.at[p, :, src], dst, pown.at[at, i]))
                for k in range(1, S):
                    q = (p + k) % S
                    hop.append(
                        remote(buf.at[q, :, src], dst, psend.at[at, k - 1, i], precv.at[at, k - 1, i], {"shard": q})
                    )
            for copy in hop:
                copy.start()
            return hop

        def both(ref, at):
            copy = remote(ref.at[c], ref.at[c], lsend.at[at], lrecv.at[at], other)
            copy.start()
            return copy

        def settle(ref, at, copy):
            copy.wait_send()
            remote(ref.at[1 - c], ref.at[1 - c], lsend.at[at], lrecv.at[at], other).wait_recv()

        x_hop = turn_over(lambda q: x_ref.at[:, part(q)], xbuf.at[p], 0, S, p, "shard")
        y_hop = turn_over(lambda q: y_ref.at[q], ybuf2.at[z], 1, C, z, "ctx")
        moves = []
        for i, (src, dst) in enumerate(((qkv_ref, qkv_buf), (o_ref, o_buf))):
            moves.append(pltpu.make_async_copy(src.at[p], dst.at[p], gown.at[i]))
            for k in range(1, S):
                q = (p + k) % S
                moves.append(remote(src.at[q], dst.at[p], gsend.at[i, k - 1], grecv.at[i, k - 1], {"shard": q}))
        for copy in moves:
            copy.start()
        tile[...] = jnp.zeros_like(tile)
        at = count
        for i, ref in enumerate(stat_refs):
            for j in range(2):
                tile[j * len(stat_refs) + i : j * len(stat_refs) + i + 1, :] = ref[j : j + 1, :]
        for k in range(lines):
            for block in range(D // 128):
                tile[at + k : at + k + 1, pl.ds(block * 128, 128)] = bias_ref[:, pl.ds(k * 128, 128)]

        def columns(g, q):
            return tile.at[:, pl.ds(pl.multiple_of((g * S + q) * nb // 128 * 128, 128), 128)]

        small = [pltpu.make_async_copy(columns(z, p), got.at[c, z, p], own.at[3])]
        for k, (where, (i, j)) in enumerate(zip(peers, everyone)):
            small.append(
                remote(columns((z + i) % C, (p + j) % S), got.at[c, z, p], tsend.at[k], trecv.at[k], where)
            )
        for copy in small:
            copy.start()
        for copy in x_hop:
            copy.wait()
        x_hop = turn_over(lambda q: xbuf.at[q], xbuf2.at[z], 2, C, z, "ctx")
        for q in range(S):
            down_out[q * fn : (q + 1) * fn, :] = down_ref[q].astype(F32).T
        for copy in y_hop:
            copy.wait()
        y_hop = arrive(ybuf2, y_out, 0)
        for copy in small:
            copy.wait()
        small_last = both(got, 0)
        bias_out[...] = jnp.sum(got[c, :, :, count : count + lines, :], axis=0)
        for i in range(2):
            for q in range(S):
                gateup_out[:, i, q * fn : (q + 1) * fn] = gateup_ref[q, :, i * fn : (i + 1) * fn].astype(F32)
        for copy in moves:
            copy.wait()
        for q in range(S):
            o_out[q * hn : (q + 1) * hn, :] = o_buf[q].astype(F32).T
            for i in range(3):
                qkv_out[i, :, q * hn : (q + 1) * hn] = qkv_buf[q, :, i * hn : (i + 1) * hn].astype(F32)
        for copy in x_hop:
            copy.wait()
        x_hop = arrive(xbuf2, x_out, 1)
        for copy in y_hop:
            copy.wait()
        y_last = both(y_out, 1)
        for copy in x_hop:
            copy.wait()
        x_last = both(x_out, 2)
        settle(got, 0, small_last)
        norm_out[...] = jnp.sum(got[:, :, :, :count, :], axis=(0, 1, 2))
        settle(y_out, 1, y_last)
        settle(x_out, 2, x_last)

    args = [x, y, *stats, bias, gateup, down, qkv, out]
    most = max(S, C) - 1
    home = (jax.ShapeDtypeStruct((T, n, D), BF), ANY)
    x, y, *rest = comm(
        kernel, S, C, number, "finish", args, [IN_VMEM] * len(args),
        [home, home]
        + [
            (jax.ShapeDtypeStruct(shape, F32), IN_VMEM)
            for shape in ((count, 128), (S, lines, 128), (nb, 2, S * fn), (S * fn, nb), (3, nb, S * hn), (S * hn, nb))
        ],
        [
            pltpu.VMEM((S, n, wide), BF), pltpu.VMEM((C, n, wide), BF), pltpu.VMEM((C, n, wide), BF),
            pltpu.VMEM((tall, D), F32), DMA((3, most)), DMA((3, most)), DMA((4,)),
            DMA((2, S - 1, pieces)), DMA((2, S - 1, pieces)), DMA((2, pieces)), DMA((3,)), DMA((3,)),
            DMA((many,)), DMA((many,)),
            pltpu.VMEM(qkv.shape, BF), pltpu.VMEM(out.shape, BF), DMA((2, S - 1)), DMA((2, S - 1)), DMA((2,)),
            pltpu.VMEM((T, C, S, tall, 128), F32),
        ],
    )
    return [x.reshape(T * n, D), y.reshape(T * n, D)] + rest


def ordered(D, S, C):
    return D // (S * C) % 128 == 0


def turn_tables(rows):
    feature = np.arange(128) % HEAD
    freq = np.where(feature < ROT, BASE ** (-2.0 * (feature % (ROT // 2)) / ROT), 0.0)
    near = np.arange(BLK)[:, None] * freq
    far = np.arange(0, rows, BLK)[:, None] * freq
    return [jnp.asarray(f(x), F32) for x in (near, far) for f in (np.cos, np.sin)]


def turn(x, i, tables, sign):
    cos, sin, cos_far, sin_far = tables
    far_cos, far_sin = cos_far[pl.ds(i, 1), :], sin_far[pl.ds(i, 1), :]
    cos_t = cos[...] * far_cos - sin[...] * far_sin
    sin_t = sin[...] * far_cos + cos[...] * far_sin
    ahead = lax.broadcasted_iota(jnp.int32, x.shape, 1) % HEAD < ROT // 2
    partner = jnp.where(ahead, -pltpu.roll(x, 128 - ROT // 2, 1), pltpu.roll(x, ROT // 2, 1))
    return x * cos_t + partner * (sin_t * sign)


def two_heads(x, left):
    zero = jnp.zeros_like(x)
    return [jnp.where(left, x, zero), jnp.where(left, zero, x)]


def block_of(rows):
    return next(size for size in (512, 256) if rows % size == 0)


def attend_work(ins, outs, scratch, piece):
    qkv_ref, cos_ref, sin_ref, cosf_ref, sinf_ref, begin_ref = ins
    qo_ref, ko_ref, vo_ref, o_ref, lse_ref = outs
    (vt_ref,) = scratch
    rows, wide = qo_ref.shape
    pairs, size = wide // 128, block_of(rows)
    tables = (cos_ref, sin_ref, cosf_ref, sinf_ref)
    left = lax.broadcasted_iota(jnp.int32, (size, 128), 1) < HEAD
    key_at = lax.broadcasted_iota(jnp.int32, (size, size), 0)
    query_at = lax.broadcasted_iota(jnp.int32, (1, size), 1)

    if piece == 0:

        @pl.loop(0, rows // BLK)
        def _(i):
            r = pl.ds(pl.multiple_of(i * BLK, BLK), BLK)
            for t in range(pairs):
                w = pl.ds(t * 128, 128)
                q, k, v = (qkv_ref[r, pl.ds(part * wide + t * 128, 128)] for part in range(3))
                qo_ref[r, w] = turn(q, i, tables, 1.0).astype(BF) * jnp.asarray(HEAD**-0.5, BF)
                ko_ref[r, w] = turn(k, i, tables, 1.0).astype(BF)
                vo_ref[r, w] = v.astype(BF)
                vt_ref[w, r] = v.T.astype(BF)

    last = rows // size - 1

    @pl.loop(0 if piece == 0 else last, last if piece == 0 else last + 1)
    def _(i):
        r = pl.ds(pl.multiple_of(i * size, size), size)
        qs = sum((two_heads(qo_ref[r, pl.ds(t * 128, 128)], left) for t in range(pairs)), [])
        begin = begin_ref[0:1, r]
        here = query_at + i * size

        def step(j, carry):
            w = pl.ds(pl.multiple_of(j * size, size), size)
            key = key_at + j * size
            seen = (key <= here) & (key >= begin)
            out = []
            for h in range(2 * pairs):
                m, l, acc = carry[h]
                s = jnp.where(seen, mm(ko_ref[w, pl.ds(h // 2 * 128, 128)], qs[h], 1, 1), NEG)
                top = jnp.maximum(m, jnp.max(s, axis=0, keepdims=True))
                fade = jnp.exp(m - top)
                e = jnp.exp(s - top)
                acc = acc * fade + mm(vt_ref[pl.ds(h * HEAD, HEAD), w], e.astype(BF), 1, 0)
                out.append((top, l * fade + jnp.sum(e, axis=0, keepdims=True), acc))
            return tuple(out)

        start = (
            jnp.full((1, size), NEG, F32), jnp.zeros((1, size), F32), jnp.zeros((HEAD, size), F32)
        )
        done = lax.fori_loop(0, i + 1, step, (start,) * (2 * pairs))
        for t in range(pairs):
            both = []
            for h in (2 * t, 2 * t + 1):
                m, l, acc = done[h]
                both.append(acc / l)
                lse_ref[h : h + 1, r] = m + jnp.log(l)
            o_ref[r, pl.ds(t * 128, 128)] = jnp.concatenate(both, axis=0).T.astype(BF)


def attend(S, C, T, number, qkv, begin, x):
    rows, wide = qkv.shape[0], qkv.shape[1] // 3
    half = jax.ShapeDtypeStruct((rows, wide), BF)
    args = [qkv, *turn_tables(rows), begin]
    outs = [half] * 4 + [jax.ShapeDtypeStruct((wide // HEAD, rows), F32)]
    return gather_columns(
        S, C, T, number, x, (),
        (args, [IN_VMEM] * len(args), [(shape, IN_VMEM) for shape in outs], [pltpu.VMEM((wide, rows), BF)], attend_work),
    )


def attend_back_work(ins, out_ref, bias_ref, scratch):
    q_ref, k_ref, v_ref, o_ref, do_ref, lse_ref, cos_ref, sin_ref, cosf_ref, sinf_ref, begin_ref = ins
    kt_ref, dq_ref, dk_ref, dv_ref = scratch
    rows, wide = q_ref.shape
    pairs, size = wide // 128, block_of(rows)
    tables = (cos_ref, sin_ref, cosf_ref, sinf_ref)
    left = lax.broadcasted_iota(jnp.int32, (size, 128), 1) < HEAD
    key_at = lax.broadcasted_iota(jnp.int32, (size, size), 0)
    query_at = lax.broadcasted_iota(jnp.int32, (1, size), 1)

    @pl.loop(0, rows // BLK)
    def _(i):
        r = pl.ds(pl.multiple_of(i * BLK, BLK), BLK)
        for t in range(pairs):
            w = pl.ds(t * 128, 128)
            kt_ref[w, r] = k_ref[r, w].astype(F32).T.astype(BF)
            dk_ref[r, w] = jnp.zeros((BLK, 128), F32)
            dv_ref[r, w] = jnp.zeros((BLK, 128), F32)

    @pl.loop(0, rows // size)
    def _(i):
        r = pl.ds(pl.multiple_of(i * size, size), size)
        qs, dos, deltas, lses = [], [], [], []
        for t in range(pairs):
            w = pl.ds(t * 128, 128)
            do = do_ref[r, w]
            qs += two_heads(q_ref[r, w], left)
            dos += two_heads(do, left)
            prod = (do.astype(F32) * o_ref[r, w].astype(F32)).T
            deltas += [jnp.sum(prod[:HEAD], axis=0, keepdims=True), jnp.sum(prod[HEAD:], axis=0, keepdims=True)]
            lses += [lse_ref[2 * t : 2 * t + 1, r], lse_ref[2 * t + 1 : 2 * t + 2, r]]
        begin = begin_ref[0:1, r]
        here = query_at + i * size

        def step(j, carry):
            w = pl.ds(pl.multiple_of(j * size, size), size)
            key = key_at + j * size
            seen = (key <= here) & (key >= begin)
            out = []
            for t in range(pairs):
                lanes = pl.ds(t * 128, 128)
                k, v = k_ref[w, lanes], v_ref[w, lanes]
                dk = dv = None
                for h in (2 * t, 2 * t + 1):
                    prob = jnp.exp(jnp.where(seen, mm(k, qs[h], 1, 1) - lses[h], NEG))
                    ds = (prob * (mm(v, dos[h], 1, 1) - deltas[h])).astype(BF)
                    out.append(carry[h] + mm(kt_ref[pl.ds(h * HEAD, HEAD), w], ds, 1, 0))
                    dk_h, dv_h = mm(ds, qs[h], 1, 0), mm(prob.astype(BF), dos[h], 1, 0)
                    dk, dv = (dk_h, dv_h) if dk is None else (dk + dk_h, dv + dv_h)
                dk_ref[w, lanes] += dk
                dv_ref[w, lanes] += dv
            return tuple(out)

        done = lax.fori_loop(0, i + 1, step, (jnp.zeros((HEAD, size), F32),) * (2 * pairs))
        for t in range(pairs):
            both = jnp.concatenate(done[2 * t : 2 * t + 2], axis=0)
            dq_ref[r, pl.ds(t * 128, 128)] = both.T * (HEAD**-0.5)

    bias_ref[...] = jnp.zeros_like(bias_ref)

    @pl.loop(0, rows // BLK)
    def _(i):
        r = pl.ds(pl.multiple_of(i * BLK, BLK), BLK)
        for t in range(pairs):
            w = pl.ds(t * 128, 128)
            for part, value in enumerate((turn(dq_ref[r, w], i, tables, -1.0), turn(dk_ref[r, w], i, tables, -1.0), dv_ref[r, w])):
                lanes = pl.ds(part * wide + t * 128, 128)
                value = value.astype(BF)
                out_ref[r, lanes] = value
                bias_ref[:, lanes] += jnp.sum(value.astype(F32), axis=0, keepdims=True)


def attend_back(S, C, T, number, q, k, v, o, do, lse, begin, act, wd, riders):
    rows, wide = q.shape
    K, D, n = act.shape[1], wd.shape[0], rows // (S * T)

    def kernel(ride, ins, outs, scratch):
        _, _, row, col = plane(S)
        greet(S, C, row + [col], other=True, axes=ride.axes)

        def meanwhile():
            ride.start()
            attend_back_work(ins[2:], outs[0], outs[1], scratch[:4])

        sum_over_plane(S, T, ins[0], ins[1], outs[2], scratch[4:], meanwhile)
        ride.wait()

    args = [act.reshape(S * T, n, K), wd, q, k, v, o, do, lse, *turn_tables(rows), begin]
    return comm(
        kernel, S, C, number, "attend_back", args, [IN_VMEM] * len(args),
        [(jax.ShapeDtypeStruct((rows, 3 * wide), BF), IN_VMEM), (jax.ShapeDtypeStruct((1, 3 * wide), F32), IN_VMEM),
         (jax.ShapeDtypeStruct((n, D), F32), IN_VMEM)],
        [pltpu.VMEM((wide, rows), BF)] + [pltpu.VMEM((rows, wide), F32)] * 3 + sum_scratch(S, n, D),
        riders,
    )


def doc_begins(lengths_row, rows):
    row_ids = jnp.arange(rows, dtype=jnp.int32)
    ends = jnp.cumsum(lengths_row, dtype=jnp.int32)
    begins = ends - lengths_row
    inside = (row_ids[:, None] >= begins[None, :]) & (row_ids[:, None] < ends[None, :])
    return jnp.sum(jnp.where(inside, begins[None, :], 0), axis=1, dtype=jnp.int32)


def tiles_of(parts, lead):
    flat = jnp.concatenate([x.astype(F32).reshape(lead + (-1,)) for x in parts], axis=-1)
    flat = jnp.pad(flat, ((0, 0),) * len(lead) + ((0, 1024 - flat.shape[-1]),))
    return flat.reshape(lead + (8, 128))


def make_body(S, C, T):
    assert S == C

    def body(tokens, lengths, w_qkv, b_qkv, w_out, w_gateup, w_down, norm_gain, norm_bias, cotangent):
        p, z, c = lax.axis_index("shard"), lax.axis_index("ctx"), lax.axis_index("tp")
        R, D = tokens.shape
        n = R // T
        nb = D // (S * C)
        L = R * C

        def to_parts(x):
            return x.reshape(n, S, C, nb).transpose(2, 0, 1, 3).reshape(S, n, D // S)

        def parts(x):
            return x.reshape(n, S, D // S).swapaxes(0, 1)

        def unpermute(x):
            return x.reshape(x.shape[0], C, S, nb).swapaxes(1, 2).reshape(x.shape)

        def half_of(x):
            return lax.dynamic_slice_in_dim(x, c * n, n, 0)

        def after(x, y):
            return lax.optimization_barrier((x, y))

        def over_ctx(w):
            return lax.all_gather(w.reshape(S * nb, -1), "ctx", axis=0, tiled=True)

        def sum_ctx(g):
            g = lax.psum_scatter(g.astype(BF), "ctx", scatter_dimension=0, tiled=True)
            return g.reshape(S, nb, -1)

        hn = w_qkv.shape[3] // S
        fn = w_gateup.shape[3] // S
        heads = hn // HEAD
        nf = HEAD // (S * C)

        tile = tiles_of((norm_gain[0].reshape(-1), norm_bias[0].reshape(-1), b_qkv[0].reshape(-1), lengths[0]), ())
        raw = lax.all_gather(w_qkv[0].swapaxes(0, 1).reshape(3 * nb, -1), "ctx", axis=0, tiled=True)
        small, _, tok, wo, wg, wd, cot = exchange(
            S, C, T, 0,
            [
                ("shard", w_out[0].reshape(S, hn, nb).swapaxes(1, 2)),
                ("shard", w_gateup[0].reshape(nb, 2, S, fn).transpose(2, 0, 1, 3).reshape(S, nb, 2 * fn)),
                ("shard", w_down[0].reshape(S, fn, nb).swapaxes(1, 2)),
                ("shard", to_parts(half_of(cotangent))),
            ],
            jnp.broadcast_to(tile, (C, S, 8, 128)),
            to_parts(half_of(tokens)),
        )
        (tok,) = gather_columns(S, C, T, 1, tok)
        wg, wd = over_ctx(wg), over_ctx(wd)

        small = lax.dynamic_index_in_dim(small, c, 0, keepdims=False).reshape(C, S, 1024)
        norms = small[:, :, : 4 * nb].reshape(C * S, 4, nb).swapaxes(0, 1).reshape(4, D)
        gains, shifts = norms[:2], norms[2:]
        nbias = 3 * S * heads * nf
        bias = small[:, :, 4 * nb : 4 * nb + nbias].reshape(C, S, 3, S * heads, nf)
        bias = lax.dynamic_slice_in_dim(bias, p * heads, heads, 3)
        bias = bias.transpose(2, 3, 1, 0, 4).reshape(1, 3 * hn)
        docs = lengths.shape[1]
        lengths_row = lax.dynamic_index_in_dim(
            small[0, :, 4 * nb + nbias : 4 * nb + nbias + docs], z, 0, keepdims=False
        ).astype(jnp.int32)
        begin = doc_begins(lengths_row, L)
        begin = begin[None, :]

        n1, qkv, wq, cot, wo = project(
            S, C, T, 12, tok, raw.reshape(C, 3, nb, -1), gains[:1], shifts[:1], bias,
            [("ctx", cot), ("all", wo.reshape(S * nb, hn))],
        )
        wo = wo.reshape(D, hn)
        gb, q, k, v, o, lse = attend(S, C, T, 4, qkv, begin, cot)
        mid, n2 = sum_norm_gather(S, C, T, 2, o, wo, tok, gains[1:], shifts[1:])
        gu, act = by_rows(
            gates_kernel, "gates", [(True, n2), (False, wg)],
            [jax.ShapeDtypeStruct((L, 2 * fn), F32), jax.ShapeDtypeStruct((L, fn), BF)],
        )
        gw_down = mm(gb, act, 0, 0).astype(BF)
        wd, gw_down = after(wd, gw_down)
        gw_down = sum_ctx(gw_down)

        (dgu,) = by_rows(
            gates_back_kernel, "gates_back", [(True, gb), (False, wd), (True, gu)],
            [jax.ShapeDtypeStruct((L, 2 * fn), BF)],
        )
        gw_gateup = mm(n2, dgu, 0, 0).astype(BF)
        dgu, gw_gateup = after(dgu, gw_gateup)
        gw_gateup = sum_ctx(gw_gateup)
        dmid, gb1, stats2 = sum_back_gather(S, C, T, 6, dgu, wg, mid, gb, gains[1:])
        gw_out = mm(gb1, o, 0, 0).astype(BF)
        gb1, gw_out = after(gb1, gw_out)
        gw_out = sum_ctx(gw_out)
        do = mm(gb1, wo, 1, 0).astype(BF)
        dqkv, gbias, got, gw_down = attend_back(
            S, C, T, 11, q, k, v, o, do, lse, begin, act, wd, [("shard", gw_down)]
        )
        out = parts((mid + got).astype(BF))
        gw_qkv = mm(n1, dqkv, 0, 0).astype(BF)
        dqkv, gw_qkv = after(dqkv, gw_qkv)
        gw_qkv = sum_ctx(gw_qkv)
        low, stats1, out, gw_gateup = sum_back(
            S, C, T, 8, dqkv, wq, tok, dmid, gains[:1], [("shard", out), ("shard", gw_gateup)]
        )
        gtok, out, norms, gbias, gw_gateup, gw_down, gw_qkv, gw_out = finish(
            S, C, T, 10, low, out, [stats1, stats2], gbias, gw_gateup, gw_down, gw_qkv, gw_out
        )
        if not ordered(D, S, C):
            gtok, out = unpermute(gtok), unpermute(out)
        gtok = gtok.astype(F32)
        norms = lax.dynamic_slice_in_dim(norms, (z * S + p) * nb % 128, nb, 1) if nb % 128 else norms
        gbias = gbias.reshape(S, 3, heads, S * C, nf)
        gbias = lax.dynamic_index_in_dim(gbias, p * C + z, 3, keepdims=False)
        gbias = gbias.swapaxes(0, 1).reshape(b_qkv.shape)

        return (
            out,
            gtok,
            gw_qkv.swapaxes(0, 1).reshape(w_qkv.shape),
            gbias,
            gw_out.reshape(w_out.shape),
            gw_gateup.reshape(w_gateup.shape),
            gw_down.reshape(w_down.shape),
            norms[None, :2],
            norms[None, 2:],
        )

    return body


def solution(mesh):
    both = ("shard", "ctx")
    specs = (
        P(None, both, None, "tp"),
        P(None, None, "tp", both),
        P(None, "tp", both),
        P(None, both, None, "tp"),
        P(None, "tp", both),
        P(None, None, both),
        P(None, None, both),
    )
    return jax.shard_map(
        make_body(mesh.shape["shard"], mesh.shape["ctx"], mesh.shape["tp"]),
        mesh=mesh,
        in_specs=(P(both, None), P("shard", None)) + specs + (P(both, None),),
        out_specs=(P(both, None), P(both, None)) + specs,
        check_vma=False,
    )
```

```python
import functools

import jax
import jax.numpy as jnp
import numpy as np
from jax import lax
from jax.experimental import pallas as pl
from jax.experimental.pallas import tpu as pltpu
from jax.sharding import PartitionSpec as P

HEAD = 64
ROT = 16
EPS = 1e-05
NEG = -1e30
BASE = 10000.0
BF = jnp.bfloat16
F32 = jnp.float32
BLK = 256
MESH = pl.DeviceIdType.MESH
DMA = pltpu.SemaphoreType.DMA
ANY = pl.BlockSpec(memory_space=pl.ANY)
IN_VMEM = pl.BlockSpec(memory_space=pltpu.VMEM)


def mm(a, b, ca, cb):
    return lax.dot_general(a, b, (((ca,), (cb,)), ((), ())), preferred_element_type=F32)


def remote(src, dst, send, recv, where):
    return pltpu.make_async_remote_copy(
        src_ref=src, dst_ref=dst, send_sem=send, recv_sem=recv, device_id=where, device_id_type=MESH
    )


def here():
    return lax.axis_index("shard"), lax.axis_index("ctx"), lax.axis_index("tp")


class Riders:
    def __init__(self, S, C, riders):
        self.S, self.C = S, C
        self.axes = [axis for axis, _ in riders]
        self.arrays = [x for _, x in riders]
        self.shapes = [
            jax.ShapeDtypeStruct((C,) + x.shape if axis == "all" else x.shape, x.dtype) for axis, x in riders
        ]
        count, most = len(riders), max(S, C) - 1
        self.scratch = [DMA((count, most)), DMA((count, most)), DMA((count,))] if count else []

    def bind(self, ins, outs, sems):
        self.ins, self.outs, self.sems = ins, outs, sems

    def start(self):
        p, z, c = here()
        self.moves = []
        for n, axis in enumerate(self.axes):
            src, dst = self.ins[n], self.outs[n]
            send, recv, own = self.sems
            if axis == "tp":
                copies = [remote(src, dst, send.at[n, 0], recv.at[n, 0], {"tp": 1 - c})]
            elif axis == "all":
                copies = [
                    remote(src, dst.at[z], send.at[n, k - 1], recv.at[n, k - 1], {"ctx": (z + k) % self.C})
                    for k in range(1, self.C)
                ]
                copies.append(pltpu.make_async_copy(src, dst.at[z], own.at[n]))
            else:
                size, me = (self.S, p) if axis == "shard" else (self.C, z)
                copies = [
                    remote(src.at[(me + k) % size], dst.at[me], send.at[n, k - 1], recv.at[n, k - 1], {axis: (me + k) % size})
                    for k in range(1, size)
                ]
                copies.append(pltpu.make_async_copy(src.at[me], dst.at[me], own.at[n]))
            for copy in copies:
                copy.start()
            self.moves += copies

    def wait(self):
        for copy in self.moves:
            copy.wait()


def greet(S, C, mates=(), line=False, other=False, axes=()):
    p, z, c = here()
    peers = [{"shard": q} for q in ([(p + k) % S for k in range(1, S)] if "shard" in axes else mates)]
    if line or "ctx" in axes or "all" in axes:
        peers += [{"ctx": (z + k) % C} for k in range(1, C)]
    if other or "tp" in axes:
        peers.append({"tp": 1 - c})
    barrier = pltpu.get_barrier_semaphore()
    for where in peers:
        pl.semaphore_signal(barrier, inc=1, device_id=where, device_id_type=MESH)
    pl.semaphore_wait(barrier, len(peers))


def comm(kernel, S, C, number, name, args, in_specs, outs, scratch, riders=()):
    ride = Riders(S, C, riders)
    na, nr, no, ns = len(args), len(ride.axes), len(outs), len(scratch)

    def body(*refs):
        ins, refs = refs[:na], refs[na:]
        rins, refs = refs[:nr], refs[nr:]
        os, refs = refs[:no], refs[no:]
        routs, refs = refs[:nr], refs[nr:]
        ride.bind(rins, routs, refs[ns:])
        kernel(ride, ins, os, refs[:ns])

    return pl.pallas_call(
        body,
        out_shape=[shape for shape, _ in outs] + ride.shapes,
        in_specs=list(in_specs) + [IN_VMEM] * nr,
        out_specs=[spec for _, spec in outs] + [ANY] * nr,
        scratch_shapes=list(scratch) + ride.scratch,
        compiler_params=pltpu.CompilerParams(
            collective_id=number, has_side_effects=True, vmem_limit_bytes=56 << 20
        ),
        cost_estimate=pl.CostEstimate(flops=0, bytes_accessed=120_000_000, transcendentals=0),
        name=name,
    )(*args, *ride.arrays)


def exchange(S, C, T, number, riders, tiles, rows=None):
    def kernel(ride, ins, outs, scratch):
        tile, got = ins[0], outs[0]
        send, recv, bsend, brecv, own = scratch[:5]
        p, z, c = here()
        everyone = [(i, j) for i in range(C) for j in range(S) if i or j]
        barrier = pltpu.get_barrier_semaphore()
        peers = [{"shard": (p + j) % S, "ctx": (z + i) % C} for i, j in everyone] + [{"tp": 1 - c}]
        for where in peers:
            pl.semaphore_signal(barrier, inc=1, device_id=where, device_id_type=MESH)
        pl.semaphore_wait(barrier, len(peers))

        def turn_over(source, target, k, axis, size, me):
            ssem, rsem, local = scratch[5:]
            hop = [pltpu.make_async_copy(source.at[me], target.at[me], local.at[k])]
            for j in range(1, size):
                q = (me + j) % size
                hop.append(remote(source.at[q], target.at[me], ssem.at[k, j - 1], rsem.at[k, j - 1], {axis: q}))
            for copy in hop:
                copy.start()
            return hop

        if rows is not None:
            first = turn_over(ins[1], outs[1], 0, "shard", S, p)
        local = pltpu.make_async_copy(tile.at[z, p], got.at[c, z, p], own)
        local.start()
        copies = []
        for at, (where, (i, j)) in enumerate(zip(peers, everyone)):
            q, g = (p + j) % S, (z + i) % C
            copies.append(remote(tile.at[g, q], got.at[c, z, p], send.at[at], recv.at[at], where))
            copies[-1].start()
        ride.start()
        if rows is not None:
            for copy in first:
                copy.wait()
            second = turn_over(outs[1], outs[2], 1, "ctx", C, z)
        local.wait()
        for copy in copies:
            copy.wait()
        back = remote(got.at[c], got.at[c], bsend, brecv, {"tp": 1 - c})
        back.start()
        back.wait_send()
        remote(got.at[1 - c], got.at[1 - c], bsend, brecv, {"tp": 1 - c}).wait_recv()
        if rows is not None:
            for copy in second:
                copy.wait()
        ride.wait()

    count, most = C * S - 1, max(S, C) - 1
    args, outs = [tiles], [(jax.ShapeDtypeStruct((T,) + tiles.shape, tiles.dtype), ANY)]
    scratch = [DMA((count,)), DMA((count,)), DMA, DMA, DMA]
    if rows is not None:
        args.append(rows)
        outs += [(jax.ShapeDtypeStruct(rows.shape, rows.dtype), IN_VMEM)] * 2
        scratch += [DMA((2, most)), DMA((2, most)), DMA((2,))]
    return comm(kernel, S, C, number, "exchange", args, [IN_VMEM] * len(args), outs, scratch, riders)


def plane(S):
    p, _, c = here()
    B = S // 2
    a, b = p // B, p % B
    return a, b, [a * B + (b + j) % B for j in range(1, B)], (1 - a) * B + b


def spread_sems(S):
    count = 4 + 4 * (S // 2 - 1)
    return [DMA((2 * count,)), DMA((2 * count,))]


def spread(S, own, region, send, recv, work=(None, None)):
    p, _, c = here()
    B = S // 2
    a, b, rows, col = plane(S)
    rows, col, other = [{"shard": q} for q in rows], {"shard": col}, {"tp": 1 - c}
    per = 4 + 4 * (B - 1)
    OWN, ROW, COL, VIA_COL, VIA_ROW = 0, 2, 2 + 2 * (B - 1), 4 + 2 * (B - 1), 4 + 3 * (B - 1)
    started = []

    def push(q, h, sem, where, first=False):
        view = region(q, h, c)
        copy = remote(own(h) if first else view, view, send.at[sem], recv.at[sem], where)
        copy.start()
        started.append(copy)

    def came(q, h, sem, core):
        view = region(q, h, core)
        remote(view, view, send.at[sem], recv.at[sem], other).wait_recv()

    for h in range(2):
        for j in range(1, B):
            push(p, h, ROW + 2 * (j - 1) + h, rows[j - 1], True)
    for h in (1, 0):
        push(p, h, COL + h, col, True)
    for h in range(2):
        push(p, h, per + OWN + h, other, True)

    def from_row(j, h):
        q = a * B + (b - j) % B
        came(q, h, ROW + 2 * (j - 1) + h, c)
        push(q, h, per + ROW + 2 * (j - 1) + h, other)
        return q

    def from_col(h):
        q = (1 - a) * B + b
        came(q, h, COL + h, c)
        push(q, h, per + COL + h, other)
        return q

    if work[0] is not None:
        work[0]()
    for j in range(1, B):
        q = from_row(j, 0)
        push(q, 0, VIA_COL + j - 1, col)
    q = from_col(1)
    for j in range(1, B):
        push(q, 1, VIA_ROW + j - 1, rows[j - 1])
    if work[1] is not None:
        work[1]()
    for j in range(1, B):
        from_row(j, 1)
    from_col(0)
    for j in range(1, B):
        q = (1 - a) * B + (b - j) % B
        came(q, 0, VIA_COL + j - 1, c)
        push(q, 0, per + VIA_COL + j - 1, other)
        came(q, 1, VIA_ROW + j - 1, c)
        push(q, 1, per + VIA_ROW + j - 1, other)
    for h in range(2):
        came(p, h, per + OWN + h, 1 - c)
        came((1 - a) * B + b, h, per + COL + h, 1 - c)
    for j in range(1, B):
        for h in range(2):
            came(a * B + (b - j) % B, h, per + ROW + 2 * (j - 1) + h, 1 - c)
        q = (1 - a) * B + (b - j) % B
        came(q, 0, per + VIA_COL + j - 1, 1 - c)
        came(q, 1, per + VIA_ROW + j - 1, 1 - c)
    for copy in started:
        copy.wait_send()


def gather_columns(S, C, T, number, x, riders=(), extra=None):
    _, n, wide = x.shape
    more, more_specs, more_outs, more_scratch, task = extra or ((), (), (), (), None)

    def kernel(ride, ins, outs, scratch):
        x_ref, out_ref = ins[0], outs[0]
        send, recv, own = scratch[:3]
        p, _, c = here()
        _, _, rows, col = plane(S)

        def region(q, h, core):
            part = pl.ds(pl.multiple_of(q * wide, 128), wide)
            return out_ref.at[pl.ds(h * (C // 2), C // 2), core, :, part]

        local = [
            pltpu.make_async_copy(x_ref.at[pl.ds(h * (C // 2), C // 2)], region(p, h, c), own.at[h]) for h in range(2)
        ]
        for copy in local:
            copy.start()
        if task is not None:
            task(ins[1:], outs[1:], scratch[3:], None)
        greet(S, C, rows + [col], other=True, axes=ride.axes)
        ride.start()
        work = [None, None]
        if task is not None:
            work = [functools.partial(task, ins[1:], outs[1:], scratch[3:], piece) for piece in range(2)]
        spread(S, lambda h: x_ref.at[pl.ds(h * (C // 2), C // 2)], region, send, recv, work)
        for copy in local:
            copy.wait()
        ride.wait()

    out, *rest = comm(
        kernel, S, C, number, "gather_columns", [x, *more], [IN_VMEM, *more_specs],
        [(jax.ShapeDtypeStruct((C, T, n, wide * S), x.dtype), ANY), *more_outs],
        spread_sems(S) + [DMA((2,)), *more_scratch], riders,
    )
    return [out.reshape(C * T * n, wide * S)] + rest


CHUNK = 512
ROWS = 32


def sum_scratch(S, n, D):
    half, B = n // 2, S // 2

    def vm(*shape):
        return pltpu.VMEM(shape, BF)

    return [
        vm(S, n, D), vm(S, n, D), vm(S, n, D), vm(B - 1, 2, half, D), vm(B, half, D),
        vm(B - 1, half, D), vm(half, D), vm(half, D), vm(B - 1, half, D),
        DMA((S,)), DMA((S,)), DMA((B - 1, 2)), DMA((B - 1, 2)), DMA((B,)), DMA((B,)), DMA((B,)), DMA((B,)),
    ]


def sum_over_plane(S, T, x_ref, w_ref, out_ref, scratch, meanwhile=None):
    away, sib, mine, row1, col1, row2, col2, to_col, to_row = scratch[:9]
    asend, arecv, rsend, rrecv, csend, crecv, fsend, frecv = scratch[9:]
    n, D = out_ref.shape
    half, B = n // 2, S // 2
    _, _, c = here()
    a, b, rows, col = plane(S)
    rows, col, other = [{"shard": q} for q in rows], {"shard": col}, {"tp": 1 - c}

    def chip(e):
        return ((a + e // B) % 2) * B + (b + e % B) % B

    def product(e, core, store):
        x = x_ref[chip(e) * T + core]

        def column(j, _):
            w = pl.ds(pl.multiple_of(j * CHUNK, CHUNK), CHUNK)
            store(w, mm(x, w_ref[w, :], 1, 1))
            return 0

        lax.fori_loop(0, D // CHUNK, column, 0)

    def to_other(e):
        return remote(away.at[e], sib.at[e], asend.at[e], arecv.at[e], other)

    def first(i, _):
        e = S - 1 - i

        def store(w, value):
            away[e, :, w] = value.astype(BF)

        product(e, 1 - c, store)
        to_other(e).start()
        return 0

    lax.fori_loop(0, S, first, 0)

    top, low = pl.ds(0, half), pl.ds(half, half)
    started = []

    def push(src, dst, send, recv, where):
        copy = remote(src, dst, send, recv, where)
        copy.start()
        started.append(copy)

    for e in range(S - 1, -1, -1):
        to_other(e).wait()

        def store(w, value):
            value = value + sib[e, :, w].astype(F32)
            if e:
                mine[e, :, w] = value.astype(BF)
            else:
                out_ref[:, w] = value

        product(e, c, store)
        j = e % B
        if e > B:
            push(mine.at[e, top], row1.at[j - 1, 1], rsend.at[j - 1, 1], rrecv.at[j - 1, 1], rows[j - 1])
            push(mine.at[e, low], col1.at[j], csend.at[j], crecv.at[j], col)
        elif e == B:
            push(mine.at[e, low], col1.at[0], csend.at[0], crecv.at[0], col)
        elif e:
            push(mine.at[e, top], row1.at[j - 1, 0], rsend.at[j - 1, 0], rrecv.at[j - 1, 0], rows[j - 1])

    def came(ref, send, recv):
        remote(ref, ref, send, recv, other).wait_recv()

    if meanwhile is not None:
        meanwhile(0)
    total = mine[B, top, :].astype(F32)
    for j in range(1, B):
        came(row1.at[j - 1, 1], rsend.at[j - 1, 1], rrecv.at[j - 1, 1])
        total = total + row1[j - 1, 1].astype(F32)
    to_col[...] = total.astype(BF)
    push(to_col, col2, fsend.at[0], frecv.at[0], col)
    for j in range(1, B):
        came(col1.at[j], csend.at[j], crecv.at[j])
        to_row[j - 1] = (mine[j, low, :].astype(F32) + col1[j].astype(F32)).astype(BF)
        push(to_row.at[j - 1], row2.at[j - 1], fsend.at[j], frecv.at[j], rows[j - 1])
    if meanwhile is not None:
        meanwhile(1)
    came(col1.at[0], csend.at[0], crecv.at[0])
    upper, lower = out_ref[top, :], out_ref[low, :] + col1[0].astype(F32)
    for j in range(1, B):
        came(row1.at[j - 1, 0], rsend.at[j - 1, 0], rrecv.at[j - 1, 0])
        upper = upper + row1[j - 1, 0].astype(F32)
    came(col2, fsend.at[0], frecv.at[0])
    out_ref[top, :] = upper + col2[...].astype(F32)
    for j in range(1, B):
        came(row2.at[j - 1], fsend.at[j], frecv.at[j])
        lower = lower + row2[j - 1].astype(F32)
    out_ref[low, :] = lower
    for copy in started:
        copy.wait_send()


def project(S, C, T, number, tok, raw, gain, shift, bias):
    L, D = tok.shape
    _, parts, nb, wide = raw.shape
    hn = wide // S
    most = S - 1

    def kernel(ride, ins, outs, scratch):
        tok_ref, raw_ref, gain_ref, shift_ref, bias_ref = ins
        n_ref, out_ref, w_ref = outs
        send, recv, own = scratch
        p, _, _ = here()
        mates = [(p + k) % S for k in range(1, S)]
        greet(S, C, mates)

        def lanes(q):
            return pl.ds(pl.multiple_of(q * hn, 128), hn)

        copies = []
        for part in range(parts):
            dst = w_ref.at[:, p, :, pl.ds(part * hn, hn)]
            for k, q in enumerate(mates):
                copies.append(
                    remote(raw_ref.at[:, part, :, lanes(q)], dst, send.at[k, part], recv.at[k, part], {"shard": q})
                )
            copies.append(pltpu.make_async_copy(raw_ref.at[:, part, :, lanes(p)], dst, own.at[part]))
        for copy in copies:
            copy.start()

        def normed(r):
            n_ref[r, :] = (norm_of(tok_ref[r, :].astype(F32))[0] * gain_ref[...] + shift_ref[...]).astype(BF)

        row_blocks(L, normed)
        for copy in copies:
            copy.wait()
        w = w_ref[...].reshape(D, parts * hn)

        @pl.loop(0, L // BLK)
        def _(i):
            r = pl.ds(pl.multiple_of(i * BLK, BLK), BLK)
            out_ref[r, :] = mm(n_ref[r, :], w, 1, 0) + bias_ref[...]

    n, out, w = comm(
        kernel, S, C, number, "project", [tok, raw, gain, shift, bias], [IN_VMEM] * 5,
        [
            (jax.ShapeDtypeStruct((L, D), BF), IN_VMEM), (jax.ShapeDtypeStruct((L, parts * hn), F32), IN_VMEM),
            (jax.ShapeDtypeStruct((C, S, nb, parts * hn), BF), IN_VMEM),
        ],
        [DMA((most, parts)), DMA((most, parts)), DMA((parts,))],
    )
    return n, out, w.reshape(D, parts * hn)


def gates_back_kernel(gb_ref, wd_ref, gu_ref, dgu_ref):
    dact = mm(gb_ref[...], wd_ref[...], 1, 0)
    both, width = gu_ref[...], dact.shape[1]
    gate, up = both[:, :width], both[:, width:]
    s = jax.nn.sigmoid(gate)
    dgate = dact * up * s * (1.0 + gate * (1.0 - s))
    dgu_ref[...] = jnp.concatenate((dgate, dact * gate * s), axis=1).astype(BF)


def gates_work(ins, outs, scratch, piece):
    gu_ref, act_ref = outs
    n2_ref, wg_ref, sems = scratch
    if piece != 1:
        for i, (x, y) in enumerate(zip(ins, (n2_ref, wg_ref))):
            copy = pltpu.make_async_copy(x, y, sems.at[i])
            copy.wait() if piece == 0 else copy.start()
    if piece is None:
        return
    (rows, width), half = act_ref.shape, act_ref.shape[0] // BLK // 2

    @pl.loop(piece * half, piece * half + half)
    def _(i):
        r = pl.ds(pl.multiple_of(i * BLK, BLK), BLK)
        both = mm(n2_ref[r, :], wg_ref[...], 1, 0)
        gu_ref[r, :] = both
        gate, up = both[:, :width], both[:, width:]
        act_ref[r, :] = (gate * jax.nn.sigmoid(gate) * up).astype(BF)


def gates(S, C, T, number, n2, wg, x):
    L, width = n2.shape[0], wg.shape[1] // 2
    outs = [jax.ShapeDtypeStruct((L, 2 * width), F32), jax.ShapeDtypeStruct((L, width), BF)]
    return gather_columns(
        S, C, T, number, x, (),
        ([n2, wg], [ANY, ANY], [(shape, IN_VMEM) for shape in outs],
         [pltpu.VMEM(n2.shape, BF), pltpu.VMEM(wg.shape, BF), DMA((2,))], gates_work),
    )


def by_rows(kernel, name, arrays, outs):
    L = outs[0].shape[0]

    def spec(width):
        return pl.BlockSpec((BLK, width), lambda i: (i, 0))

    return pl.pallas_call(
        kernel,
        grid=(L // BLK,),
        in_specs=[spec(x.shape[1]) if rows else pl.BlockSpec(x.shape, lambda i: (0, 0)) for rows, x in arrays],
        out_specs=[spec(x.shape[1]) for x in outs],
        out_shape=outs,
        compiler_params=pltpu.CompilerParams(vmem_limit_bytes=48 << 20),
        name=name,
    )(*[x for _, x in arrays])


def row_blocks(n, work):
    @pl.loop(0, n // ROWS)
    def _(i):
        work(pl.ds(pl.multiple_of(i * ROWS, ROWS), ROWS))


def own_rows(T, x_ref, row_ref, sem):
    p, _, c = here()
    copy = pltpu.make_async_copy(x_ref.at[p * T + c], row_ref, sem)
    copy.start()
    return copy


def norm_of(v):
    center = v - jnp.mean(v, axis=-1, keepdims=True)
    inverse = lax.rsqrt(jnp.mean(center * center, axis=-1, keepdims=True) + EPS)
    return center * inverse, inverse


def norm_back(v, g, gain, stats_ref):
    normal, inverse = norm_of(v)
    e = g * gain
    stats_ref[0:1, :] += jnp.sum(g * normal, axis=0, keepdims=True)
    stats_ref[1:2, :] += jnp.sum(g, axis=0, keepdims=True)
    return inverse * (
        e - jnp.mean(e, axis=-1, keepdims=True) - normal * jnp.mean(e * normal, axis=-1, keepdims=True)
    )


def spread_rows(S, T, src, out_ref, send, recv, own):
    p, _, c = here()
    half = src.shape[0] // 2
    local = pltpu.make_async_copy(src, out_ref.at[p * T + c], own)
    local.start()
    spread(
        S,
        lambda h: src.at[pl.ds(h * half, half)],
        lambda q, h, core: out_ref.at[q * T + core, pl.ds(h * half, half)],
        send,
        recv,
    )
    local.wait()


def sum_norm_gather(S, C, T, number, x, w, residual, gain, shift, riders=()):
    L, K = x.shape
    D, n = w.shape[0], L // (S * T)

    def kernel(ride, ins, outs, scratch):
        x_ref, w_ref, all_ref, gain_ref, shift_ref = ins
        v_ref, out_ref = outs
        acc, low, send, recv, own, res_ref, sem = scratch[:7]
        _, _, rows, col = plane(S)
        rest = own_rows(T, all_ref, res_ref, sem)
        greet(S, C, rows + [col], other=True, axes=ride.axes)
        ride.start()
        sum_over_plane(S, T, x_ref, w_ref, acc, scratch[7:])
        rest.wait()

        def work(r):
            v = res_ref[r, :].astype(F32) + acc[r, :]
            v_ref[r, :] = v
            low[r, :] = (norm_of(v)[0] * gain_ref[...] + shift_ref[...]).astype(BF)

        row_blocks(n, work)
        spread_rows(S, T, low, out_ref, send, recv, own)
        ride.wait()

    v, out, *rest = comm(
        kernel, S, C, number, "sum_norm_gather", [x.reshape(S * T, n, K), w, residual.reshape(S * T, n, D), gain, shift],
        [IN_VMEM, IN_VMEM, ANY, IN_VMEM, IN_VMEM],
        [(jax.ShapeDtypeStruct((n, D), F32), IN_VMEM), (jax.ShapeDtypeStruct((S * T, n, D), BF), ANY)],
        [pltpu.VMEM((n, D), F32), pltpu.VMEM((n, D), BF)] + spread_sems(S)
        + [DMA, pltpu.VMEM((n, D), BF), DMA] + sum_scratch(S, n, D),
        riders,
    )
    return [v, out.reshape(L, D)] + rest


def sum_back_gather(S, C, T, number, x, w, v, residual, gain, riders=()):
    L, K = x.shape
    D, n = w.shape[0], L // (S * T)

    def kernel(ride, ins, outs, scratch):
        x_ref, w_ref, in_ref, all_ref, gain_ref = ins
        v_ref, out_ref, stats = outs
        acc, low, send, recv, own, res_ref, sem = scratch[:7]
        _, _, rows, col = plane(S)
        rest = own_rows(T, all_ref, res_ref, sem)
        greet(S, C, rows + [col], other=True, axes=ride.axes)
        ride.start()
        sum_over_plane(S, T, x_ref, w_ref, acc, scratch[7:])
        rest.wait()
        stats[...] = jnp.zeros_like(stats)

        def work(r):
            g = res_ref[r, :].astype(F32) + norm_back(in_ref[r, :], acc[r, :], gain_ref[...], stats)
            v_ref[r, :] = g
            low[r, :] = g.astype(BF)

        row_blocks(n, work)
        spread_rows(S, T, low, out_ref, send, recv, own)
        ride.wait()

    g, out, stats, *rest = comm(
        kernel, S, C, number, "sum_back_gather", [x.reshape(S * T, n, K), w, v, residual.reshape(S * T, n, D), gain],
        [IN_VMEM, IN_VMEM, IN_VMEM, ANY, IN_VMEM],
        [
            (jax.ShapeDtypeStruct((n, D), F32), IN_VMEM), (jax.ShapeDtypeStruct((S * T, n, D), BF), ANY),
            (jax.ShapeDtypeStruct((2, D), F32), IN_VMEM),
        ],
        [pltpu.VMEM((n, D), F32), pltpu.VMEM((n, D), BF)] + spread_sems(S)
        + [DMA, pltpu.VMEM((n, D), BF), DMA] + sum_scratch(S, n, D),
        riders,
    )
    return [g, out.reshape(L, D), stats] + rest


def sum_back(S, C, T, number, x, w, v, residual, gain, riders=()):
    L, K = x.shape
    D, n = w.shape[0], L // (S * T)

    def kernel(ride, ins, outs, scratch):
        x_ref, w_ref, all_ref, res_ref, gain_ref = ins
        low, stats = outs
        acc, in_ref, sem = scratch[:3]
        _, _, rows, col = plane(S)
        rest = own_rows(T, all_ref, in_ref, sem)
        greet(S, C, rows + [col], other=True, axes=ride.axes)
        ride.start()
        sum_over_plane(S, T, x_ref, w_ref, acc, scratch[3:])
        rest.wait()
        stats[...] = jnp.zeros_like(stats)

        def work(r):
            g = res_ref[r, :] + norm_back(in_ref[r, :].astype(F32), acc[r, :], gain_ref[...], stats)
            low[r, :] = g.astype(BF)

        row_blocks(n, work)
        ride.wait()

    return comm(
        kernel, S, C, number, "sum_back", [x.reshape(S * T, n, K), w, v.reshape(S * T, n, D), residual, gain],
        [IN_VMEM, IN_VMEM, ANY, IN_VMEM, IN_VMEM],
        [(jax.ShapeDtypeStruct((n, D), BF), IN_VMEM), (jax.ShapeDtypeStruct((2, D), F32), IN_VMEM)],
        [pltpu.VMEM((n, D), F32), pltpu.VMEM((n, D), BF), DMA] + sum_scratch(S, n, D),
        riders,
    )


def finish(S, C, T, number, x, y, stats, bias, gateup, down, qkv, out):
    n, D = x.shape
    fn, hn = down.shape[2], out.shape[2]
    wide, lines = D // S, bias.shape[1] // 128
    nb = D // (S * C)
    count = sum(z.shape[0] for z in stats)
    tall = -(-(count + lines) // 8) * 8
    many = C * S - 1
    pieces = S if ordered(D, S, C) else 1

    def kernel(ride, ins, outs, scratch):
        x_ref, y_ref, stat_refs, bias_ref = ins[0], ins[1], ins[2:-5], ins[-5]
        gateup_ref, down_ref, qkv_ref, o_ref = ins[-4:]
        x_out, y_out, norm_out, bias_out, gateup_out, down_out, qkv_out, o_out = outs
        xbuf, xbuf2, ybuf2, tile, send, recv, own, psend, precv, pown, lsend, lrecv, tsend, trecv = scratch[:14]
        qkv_buf, o_buf, gsend, grecv, gown, got = scratch[14:]
        p, z, c = here()
        other = {"tp": 1 - c}
        everyone = [(i, j) for i in range(C) for j in range(S) if i or j]
        peers = [{"shard": (p + j) % S, "ctx": (z + i) % C} for i, j in everyone]
        barrier = pltpu.get_barrier_semaphore()
        for where in peers + [other]:
            pl.semaphore_signal(barrier, inc=1, device_id=where, device_id_type=MESH)
        pl.semaphore_wait(barrier, len(peers) + 1)

        def part(q):
            return pl.ds(pl.multiple_of(q * wide, 128), wide)

        def turn_over(source, target, at, size, me, axis):
            hop = [pltpu.make_async_copy(source(me), target, own.at[at])]
            for k in range(1, size):
                q = (me + k) % size
                hop.append(remote(source(q), target, send.at[at, k - 1], recv.at[at, k - 1], {axis: q}))
            for copy in hop:
                copy.start()
            return hop

        def arrive(buf, out, at):
            hop = []
            for i in range(pieces):
                src = pl.ds(i * (wide // pieces), wide // pieces)
                first = (i * C + p) * nb if pieces > 1 else p * wide
                dst = out.at[c, :, pl.ds(pl.multiple_of(first, 128), wide // pieces)]
                hop.append(pltpu.make_async_copy(buf.at[p, :, src], dst, pown.at[at, i]))
                for k in range(1, S):
                    q = (p + k) % S
                    hop.append(
                        remote(buf.at[q, :, src], dst, psend.at[at, k - 1, i], precv.at[at, k - 1, i], {"shard": q})
                    )
            for copy in hop:
                copy.start()
            return hop

        def both(ref, at):
            copy = remote(ref.at[c], ref.at[c], lsend.at[at], lrecv.at[at], other)
            copy.start()
            return copy

        def settle(ref, at, copy):
            copy.wait_send()
            remote(ref.at[1 - c], ref.at[1 - c], lsend.at[at], lrecv.at[at], other).wait_recv()

        x_hop = turn_over(lambda q: x_ref.at[:, part(q)], xbuf.at[p], 0, S, p, "shard")
        y_hop = turn_over(lambda q: y_ref.at[q], ybuf2.at[z], 1, C, z, "ctx")
        moves = []
        for i, (src, dst) in enumerate(((qkv_ref, qkv_buf), (o_ref, o_buf))):
            moves.append(pltpu.make_async_copy(src.at[p], dst.at[p], gown.at[i]))
            for k in range(1, S):
                q = (p + k) % S
                moves.append(remote(src.at[q], dst.at[p], gsend.at[i, k - 1], grecv.at[i, k - 1], {"shard": q}))
        for copy in moves:
            copy.start()
        tile[...] = jnp.zeros_like(tile)
        at = count
        for i, ref in enumerate(stat_refs):
            for j in range(2):
                tile[j * len(stat_refs) + i : j * len(stat_refs) + i + 1, :] = ref[j : j + 1, :]
        for k in range(lines):
            for block in range(D // 128):
                tile[at + k : at + k + 1, pl.ds(block * 128, 128)] = bias_ref[:, pl.ds(k * 128, 128)]

        def columns(g, q):
            return tile.at[:, pl.ds(pl.multiple_of((g * S + q) * nb // 128 * 128, 128), 128)]

        small = [pltpu.make_async_copy(columns(z, p), got.at[c, z, p], own.at[3])]
        for k, (where, (i, j)) in enumerate(zip(peers, everyone)):
            small.append(
                remote(columns((z + i) % C, (p + j) % S), got.at[c, z, p], tsend.at[k], trecv.at[k], where)
            )
        for copy in small:
            copy.start()
        for copy in x_hop:
            copy.wait()
        x_hop = turn_over(lambda q: xbuf.at[q], xbuf2.at[z], 2, C, z, "ctx")
        for q in range(S):
            down_out[q * fn : (q + 1) * fn, :] = down_ref[q].astype(F32).T
        for copy in y_hop:
            copy.wait()
        y_hop = arrive(ybuf2, y_out, 0)
        for copy in small:
            copy.wait()
        small_last = both(got, 0)
        bias_out[...] = jnp.sum(got[c, :, :, count : count + lines, :], axis=0)
        for i in range(2):
            for q in range(S):
                gateup_out[:, i, q * fn : (q + 1) * fn] = gateup_ref[q, :, i * fn : (i + 1) * fn].astype(F32)
        for copy in moves:
            copy.wait()
        for q in range(S):
            o_out[q * hn : (q + 1) * hn, :] = o_buf[q].astype(F32).T
            for i in range(3):
                qkv_out[i, :, q * hn : (q + 1) * hn] = qkv_buf[q, :, i * hn : (i + 1) * hn].astype(F32)
        for copy in x_hop:
            copy.wait()
        x_hop = arrive(xbuf2, x_out, 1)
        for copy in y_hop:
            copy.wait()
        y_last = both(y_out, 1)
        for copy in x_hop:
            copy.wait()
        x_last = both(x_out, 2)
        settle(got, 0, small_last)
        norm_out[...] = jnp.sum(got[:, :, :, :count, :], axis=(0, 1, 2))
        settle(y_out, 1, y_last)
        settle(x_out, 2, x_last)

    args = [x, y, *stats, bias, gateup, down, qkv, out]
    most = max(S, C) - 1
    home = (jax.ShapeDtypeStruct((T, n, D), BF), ANY)
    x, y, *rest = comm(
        kernel, S, C, number, "finish", args, [IN_VMEM] * len(args),
        [home, home]
        + [
            (jax.ShapeDtypeStruct(shape, F32), IN_VMEM)
            for shape in ((count, 128), (S, lines, 128), (nb, 2, S * fn), (S * fn, nb), (3, nb, S * hn), (S * hn, nb))
        ],
        [
            pltpu.VMEM((S, n, wide), BF), pltpu.VMEM((C, n, wide), BF), pltpu.VMEM((C, n, wide), BF),
            pltpu.VMEM((tall, D), F32), DMA((3, most)), DMA((3, most)), DMA((4,)),
            DMA((2, S - 1, pieces)), DMA((2, S - 1, pieces)), DMA((2, pieces)), DMA((3,)), DMA((3,)),
            DMA((many,)), DMA((many,)),
            pltpu.VMEM(qkv.shape, BF), pltpu.VMEM(out.shape, BF), DMA((2, S - 1)), DMA((2, S - 1)), DMA((2,)),
            pltpu.VMEM((T, C, S, tall, 128), F32),
        ],
    )
    return [x.reshape(T * n, D), y.reshape(T * n, D)] + rest


def ordered(D, S, C):
    return D // (S * C) % 128 == 0


def turn_tables(rows):
    feature = np.arange(128) % HEAD
    freq = np.where(feature < ROT, BASE ** (-2.0 * (feature % (ROT // 2)) / ROT), 0.0)
    near = np.arange(BLK)[:, None] * freq
    far = np.arange(0, rows, BLK)[:, None] * freq
    return [jnp.asarray(f(x), F32) for x in (near, far) for f in (np.cos, np.sin)]


def turn(x, i, tables, sign):
    cos, sin, cos_far, sin_far = tables
    far_cos, far_sin = cos_far[pl.ds(i, 1), :], sin_far[pl.ds(i, 1), :]
    cos_t = cos[...] * far_cos - sin[...] * far_sin
    sin_t = sin[...] * far_cos + cos[...] * far_sin
    ahead = lax.broadcasted_iota(jnp.int32, x.shape, 1) % HEAD < ROT // 2
    partner = jnp.where(ahead, -pltpu.roll(x, 128 - ROT // 2, 1), pltpu.roll(x, ROT // 2, 1))
    return x * cos_t + partner * (sin_t * sign)


def two_heads(x, left):
    zero = jnp.zeros_like(x)
    return [jnp.where(left, x, zero), jnp.where(left, zero, x)]


def block_of(rows):
    return next(size for size in (512, 256) if rows % size == 0)


def attend_kernel(
    first_ref, qkv_ref, cos_ref, sin_ref, cosf_ref, sinf_ref, begin_ref,
    qo_ref, ko_ref, vo_ref, o_ref, lse_ref, vt_ref,
):
    rows, wide = qo_ref.shape
    pairs, size = wide // 128, block_of(rows)
    tables = (cos_ref, sin_ref, cosf_ref, sinf_ref)
    left = lax.broadcasted_iota(jnp.int32, (size, 128), 1) < HEAD
    key_at = lax.broadcasted_iota(jnp.int32, (size, size), 0)
    query_at = lax.broadcasted_iota(jnp.int32, (1, size), 1)

    @pl.loop(0, rows // BLK)
    def _(i):
        r = pl.ds(pl.multiple_of(i * BLK, BLK), BLK)
        for t in range(pairs):
            w = pl.ds(t * 128, 128)
            q, k, v = (qkv_ref[r, pl.ds(part * wide + t * 128, 128)] for part in range(3))
            qo_ref[r, w] = turn(q, i, tables, 1.0).astype(BF) * jnp.asarray(HEAD**-0.5, BF)
            ko_ref[r, w] = turn(k, i, tables, 1.0).astype(BF)
            vo_ref[r, w] = v.astype(BF)
            vt_ref[w, r] = v.T.astype(BF)

    @pl.loop(0, rows // size)
    def _(i):
        r = pl.ds(pl.multiple_of(i * size, size), size)
        qs = sum((two_heads(qo_ref[r, pl.ds(t * 128, 128)], left) for t in range(pairs)), [])
        begin = begin_ref[0:1, r]
        here = query_at + i * size

        def step(j, carry):
            w = pl.ds(pl.multiple_of(j * size, size), size)
            key = key_at + j * size
            seen = (key <= here) & (key >= begin)
            out = []
            for h in range(2 * pairs):
                m, l, acc = carry[h]
                s = jnp.where(seen, mm(ko_ref[w, pl.ds(h // 2 * 128, 128)], qs[h], 1, 1), NEG)
                top = jnp.maximum(m, jnp.max(s, axis=0, keepdims=True))
                fade = jnp.exp(m - top)
                e = jnp.exp(s - top)
                acc = acc * fade + mm(vt_ref[pl.ds(h * HEAD, HEAD), w], e.astype(BF), 1, 0)
                out.append((top, l * fade + jnp.sum(e, axis=0, keepdims=True), acc))
            return tuple(out)

        start = (
            jnp.full((1, size), NEG, F32), jnp.zeros((1, size), F32), jnp.zeros((HEAD, size), F32)
        )
        done = lax.fori_loop(first_ref[i], i + 1, step, (start,) * (2 * pairs))
        for t in range(pairs):
            both = []
            for h in (2 * t, 2 * t + 1):
                m, l, acc = done[h]
                both.append(acc / l)
                lse_ref[h : h + 1, r] = m + jnp.log(l)
            o_ref[r, pl.ds(t * 128, 128)] = jnp.concatenate(both, axis=0).T.astype(BF)


def attend(qkv, begin):
    rows, wide = qkv.shape[0], qkv.shape[1] // 3
    size = block_of(rows)
    half = jax.ShapeDtypeStruct((rows, wide), BF)
    return pl.pallas_call(
        attend_kernel,
        in_specs=[pl.BlockSpec(memory_space=pltpu.SMEM)] + [IN_VMEM] * 6,
        out_specs=[IN_VMEM] * 5,
        out_shape=[half] * 4 + [jax.ShapeDtypeStruct((wide // HEAD, rows), F32)],
        scratch_shapes=[pltpu.VMEM((wide, rows), BF)],
        compiler_params=pltpu.CompilerParams(vmem_limit_bytes=48 << 20),
        name="attend",
    )(begin[0, ::size] // size, qkv, *turn_tables(rows), begin)


def attend_back_work(ins, out_ref, bias_ref, scratch, piece):
    q_ref, k_ref, v_ref, o_ref, do_ref, lse_ref, cos_ref, sin_ref, cosf_ref, sinf_ref, begin_ref = ins
    kt_ref, dq_ref, dk_ref, dv_ref = scratch
    rows, wide = q_ref.shape
    pairs, size = wide // 128, block_of(rows)
    tables = (cos_ref, sin_ref, cosf_ref, sinf_ref)
    left = lax.broadcasted_iota(jnp.int32, (size, 128), 1) < HEAD
    key_at = lax.broadcasted_iota(jnp.int32, (size, size), 0)
    query_at = lax.broadcasted_iota(jnp.int32, (1, size), 1)

    last = rows // size - 1
    first, stop = (0, last) if piece == 0 else (last, last + 1)

    def prepare(i):
        r = pl.ds(pl.multiple_of(i * BLK, BLK), BLK)
        for t in range(pairs):
            w = pl.ds(t * 128, 128)
            kt_ref[w, r] = k_ref[r, w].astype(F32).T.astype(BF)
            dk_ref[r, w] = jnp.zeros((BLK, 128), F32)
            dv_ref[r, w] = jnp.zeros((BLK, 128), F32)

    if piece == 0:
        pl.loop(0, rows // BLK)(prepare)

    @pl.loop(first, stop)
    def _(i):
        r = pl.ds(pl.multiple_of(i * size, size), size)
        qs, dos, deltas, lses = [], [], [], []
        for t in range(pairs):
            w = pl.ds(t * 128, 128)
            do = do_ref[r, w]
            qs += two_heads(q_ref[r, w], left)
            dos += two_heads(do, left)
            prod = (do.astype(F32) * o_ref[r, w].astype(F32)).T
            deltas += [jnp.sum(prod[:HEAD], axis=0, keepdims=True), jnp.sum(prod[HEAD:], axis=0, keepdims=True)]
            lses += [lse_ref[2 * t : 2 * t + 1, r], lse_ref[2 * t + 1 : 2 * t + 2, r]]
        begin = begin_ref[0:1, r]
        here = query_at + i * size

        def step(j, carry):
            w = pl.ds(pl.multiple_of(j * size, size), size)
            key = key_at + j * size
            seen = (key <= here) & (key >= begin)
            out = []
            for t in range(pairs):
                lanes = pl.ds(t * 128, 128)
                k, v = k_ref[w, lanes], v_ref[w, lanes]
                dk = dv = None
                for h in (2 * t, 2 * t + 1):
                    prob = jnp.exp(jnp.where(seen, mm(k, qs[h], 1, 1) - lses[h], NEG))
                    ds = (prob * (mm(v, dos[h], 1, 1) - deltas[h])).astype(BF)
                    out.append(carry[h] + mm(kt_ref[pl.ds(h * HEAD, HEAD), w], ds, 1, 0))
                    dk_h, dv_h = mm(ds, qs[h], 1, 0), mm(prob.astype(BF), dos[h], 1, 0)
                    dk, dv = (dk_h, dv_h) if dk is None else (dk + dk_h, dv + dv_h)
                dk_ref[w, lanes] += dk
                dv_ref[w, lanes] += dv
            return tuple(out)

        done = lax.fori_loop(0, i + 1, step, (jnp.zeros((HEAD, size), F32),) * (2 * pairs))
        for t in range(pairs):
            both = jnp.concatenate(done[2 * t : 2 * t + 2], axis=0)
            dq_ref[r, pl.ds(t * 128, 128)] = both.T * (HEAD**-0.5)

    if piece == 0:
        return
    bias_ref[...] = jnp.zeros_like(bias_ref)

    @pl.loop(0, rows // BLK)
    def _(i):
        r = pl.ds(pl.multiple_of(i * BLK, BLK), BLK)
        for t in range(pairs):
            w = pl.ds(t * 128, 128)
            for part, value in enumerate((turn(dq_ref[r, w], i, tables, -1.0), turn(dk_ref[r, w], i, tables, -1.0), dv_ref[r, w])):
                lanes = pl.ds(part * wide + t * 128, 128)
                value = value.astype(BF)
                out_ref[r, lanes] = value
                bias_ref[:, lanes] += jnp.sum(value.astype(F32), axis=0, keepdims=True)


def attend_back(S, C, T, number, q, k, v, o, do, lse, begin, act, wd, riders):
    rows, wide = q.shape
    K, D, n = act.shape[1], wd.shape[0], rows // (S * T)

    def kernel(ride, ins, outs, scratch):
        _, _, row, col = plane(S)
        greet(S, C, row + [col], other=True, axes=ride.axes)

        def meanwhile(piece):
            if piece == 0:
                ride.start()
            attend_back_work(ins[2:], outs[0], outs[1], scratch[:4], piece)

        sum_over_plane(S, T, ins[0], ins[1], outs[2], scratch[4:], meanwhile)
        ride.wait()

    args = [act.reshape(S * T, n, K), wd, q, k, v, o, do, lse, *turn_tables(rows), begin]
    return comm(
        kernel, S, C, number, "attend_back", args, [IN_VMEM] * len(args),
        [(jax.ShapeDtypeStruct((rows, 3 * wide), BF), IN_VMEM), (jax.ShapeDtypeStruct((1, 3 * wide), F32), IN_VMEM),
         (jax.ShapeDtypeStruct((n, D), F32), IN_VMEM)],
        [pltpu.VMEM((wide, rows), BF)] + [pltpu.VMEM((rows, wide), F32)] * 3 + sum_scratch(S, n, D),
        riders,
    )


def doc_begins(lengths_row, rows):
    row_ids = jnp.arange(rows, dtype=jnp.int32)
    ends = jnp.cumsum(lengths_row, dtype=jnp.int32)
    begins = ends - lengths_row
    inside = (row_ids[:, None] >= begins[None, :]) & (row_ids[:, None] < ends[None, :])
    return jnp.sum(jnp.where(inside, begins[None, :], 0), axis=1, dtype=jnp.int32)


def tiles_of(parts, lead):
    flat = jnp.concatenate([x.astype(F32).reshape(lead + (-1,)) for x in parts], axis=-1)
    flat = jnp.pad(flat, ((0, 0),) * len(lead) + ((0, 1024 - flat.shape[-1]),))
    return flat.reshape(lead + (8, 128))


def make_body(S, C, T):
    assert S == C

    def body(tokens, lengths, w_qkv, b_qkv, w_out, w_gateup, w_down, norm_gain, norm_bias, cotangent):
        p, z, c = lax.axis_index("shard"), lax.axis_index("ctx"), lax.axis_index("tp")
        R, D = tokens.shape
        n = R // T
        nb = D // (S * C)
        L = R * C

        def to_parts(x):
            return x.reshape(n, S, C, nb).transpose(2, 0, 1, 3).reshape(S, n, D // S)

        def parts(x):
            return x.reshape(n, S, D // S).swapaxes(0, 1)

        def unpermute(x):
            return x.reshape(x.shape[0], C, S, nb).swapaxes(1, 2).reshape(x.shape)

        def half_of(x):
            return lax.dynamic_slice_in_dim(x, c * n, n, 0)

        def after(x, y):
            return lax.optimization_barrier((x, y))

        def over_ctx(w):
            return lax.all_gather(w.reshape(S * nb, -1), "ctx", axis=0, tiled=True)

        def sum_ctx(g):
            g = lax.psum_scatter(g.astype(BF), "ctx", scatter_dimension=0, tiled=True)
            return g.reshape(S, nb, -1)

        hn = w_qkv.shape[3] // S
        fn = w_gateup.shape[3] // S
        heads = hn // HEAD
        nf = HEAD // (S * C)

        tile = tiles_of((norm_gain[0].reshape(-1), norm_bias[0].reshape(-1), b_qkv[0].reshape(-1), lengths[0]), ())
        raw = lax.all_gather(w_qkv[0].swapaxes(0, 1).reshape(3 * nb, -1), "ctx", axis=0, tiled=True)
        small, _, tok, wo, wg, wd, cot = exchange(
            S, C, T, 0,
            [
                ("shard", w_out[0].reshape(S, hn, nb).swapaxes(1, 2)),
                ("shard", w_gateup[0].reshape(nb, 2, S, fn).transpose(2, 0, 1, 3).reshape(S, nb, 2 * fn)),
                ("shard", w_down[0].reshape(S, fn, nb).swapaxes(1, 2)),
                ("shard", to_parts(half_of(cotangent))),
            ],
            jnp.broadcast_to(tile, (C, S, 8, 128)),
            to_parts(half_of(tokens)),
        )
        tok, wo = gather_columns(S, C, T, 1, tok, [("all", wo.reshape(S * nb, hn))])
        wo, wg, wd = wo.reshape(D, hn), over_ctx(wg), over_ctx(wd)

        small = lax.dynamic_index_in_dim(small, c, 0, keepdims=False).reshape(C, S, 1024)
        norms = small[:, :, : 4 * nb].reshape(C * S, 4, nb).swapaxes(0, 1).reshape(4, D)
        gains, shifts = norms[:2], norms[2:]
        nbias = 3 * S * heads * nf
        bias = small[:, :, 4 * nb : 4 * nb + nbias].reshape(C, S, 3, S * heads, nf)
        bias = lax.dynamic_slice_in_dim(bias, p * heads, heads, 3)
        bias = bias.transpose(2, 3, 1, 0, 4).reshape(1, 3 * hn)
        docs = lengths.shape[1]
        lengths_row = lax.dynamic_index_in_dim(
            small[0, :, 4 * nb + nbias : 4 * nb + nbias + docs], z, 0, keepdims=False
        ).astype(jnp.int32)
        begin = doc_begins(lengths_row, L)
        begin = begin[None, :]

        n1, qkv, wq = project(S, C, T, 12, tok, raw.reshape(C, 3, nb, -1), gains[:1], shifts[:1], bias)
        q, k, v, o, lse = attend(qkv, begin)
        mid, n2, cot = sum_norm_gather(S, C, T, 2, o, wo, tok, gains[1:], shifts[1:], [("ctx", cot)])
        gb, gu, act = gates(S, C, T, 4, n2, wg, cot)
        gw_down = mm(gb, act, 0, 0).astype(BF)
        wd, gw_down = after(wd, gw_down)
        gw_down = sum_ctx(gw_down)

        (dgu,) = by_rows(
            gates_back_kernel, "gates_back", [(True, gb), (False, wd), (True, gu)],
            [jax.ShapeDtypeStruct((L, 2 * fn), BF)],
        )
        gw_gateup = mm(n2, dgu, 0, 0).astype(BF)
        dgu, gw_gateup = after(dgu, gw_gateup)
        gw_gateup = sum_ctx(gw_gateup)
        dmid, gb1, stats2 = sum_back_gather(S, C, T, 6, dgu, wg, mid, gb, gains[1:])
        gw_out = mm(gb1, o, 0, 0).astype(BF)
        gb1, gw_out = after(gb1, gw_out)
        do = mm(gb1, wo, 1, 0).astype(BF)
        dqkv, gbias, got, gw_down, gw_out = attend_back(
            S, C, T, 11, q, k, v, o, do, lse, begin, act, wd,
            [("shard", gw_down), ("ctx", gw_out.reshape(C, S * nb, hn))],
        )
        out = parts((mid + got).astype(BF))
        gw_qkv = mm(n1, dqkv, 0, 0).astype(BF)
        dqkv, gw_qkv = after(dqkv, gw_qkv)
        gw_qkv = sum_ctx(gw_qkv)
        low, stats1, out, gw_gateup = sum_back(
            S, C, T, 8, dqkv, wq, tok, dmid, gains[:1], [("shard", out), ("shard", gw_gateup)]
        )
        gtok, out, norms, gbias, gw_gateup, gw_down, gw_qkv, gw_out = finish(
            S, C, T, 10, low, out, [stats1, stats2], gbias, gw_gateup, gw_down, gw_qkv,
            jnp.sum(gw_out.astype(F32), axis=0).astype(BF).reshape(S, nb, hn),
        )
        if not ordered(D, S, C):
            gtok, out = unpermute(gtok), unpermute(out)
        gtok = gtok.astype(F32)
        norms = lax.dynamic_slice_in_dim(norms, (z * S + p) * nb % 128, nb, 1) if nb % 128 else norms
        gbias = gbias.reshape(S, 3, heads, S * C, nf)
        gbias = lax.dynamic_index_in_dim(gbias, p * C + z, 3, keepdims=False)
        gbias = gbias.swapaxes(0, 1).reshape(b_qkv.shape)

        return (
            out,
            gtok,
            gw_qkv.swapaxes(0, 1).reshape(w_qkv.shape),
            gbias,
            gw_out.reshape(w_out.shape),
            gw_gateup.reshape(w_gateup.shape),
            gw_down.reshape(w_down.shape),
            norms[None, :2],
            norms[None, 2:],
        )

    return body


def solution(mesh):
    both = ("shard", "ctx")
    specs = (
        P(None, both, None, "tp"),
        P(None, None, "tp", both),
        P(None, "tp", both),
        P(None, both, None, "tp"),
        P(None, "tp", both),
        P(None, None, both),
        P(None, None, both),
    )
    return jax.shard_map(
        make_body(mesh.shape["shard"], mesh.shape["ctx"], mesh.shape["tp"]),
        mesh=mesh,
        in_specs=(P(both, None), P("shard", None)) + specs + (P(both, None),),
        out_specs=(P(both, None), P(both, None)) + specs,
        check_vma=False,
    )
```

```python
import functools
import math

import jax
import jax.numpy as jnp
import numpy as np
from jax import lax
from jax.experimental import pallas as pl
from jax.experimental.pallas import tpu as pltpu
from jax.sharding import PartitionSpec as P

HEAD = 64
ROT = 16
EPS = 1e-05
NEG = -1e30
BASE = 10000.0
BF = jnp.bfloat16
F32 = jnp.float32
BLK = 256
MESH = pl.DeviceIdType.MESH
DMA = pltpu.SemaphoreType.DMA
ANY = pl.BlockSpec(memory_space=pl.ANY)
IN_VMEM = pl.BlockSpec(memory_space=pltpu.VMEM)


def mm(a, b, ca, cb):
    return lax.dot_general(a, b, (((ca,), (cb,)), ((), ())), preferred_element_type=F32)


def remote(src, dst, send, recv, where):
    return pltpu.make_async_remote_copy(
        src_ref=src, dst_ref=dst, send_sem=send, recv_sem=recv, device_id=where, device_id_type=MESH
    )


def here():
    return lax.axis_index("shard"), lax.axis_index("ctx"), lax.axis_index("tp")


class Riders:
    def __init__(self, S, C, riders):
        self.S, self.C = S, C
        self.axes = [axis for axis, _ in riders]
        self.arrays = [x for _, x in riders]
        self.shapes = [
            jax.ShapeDtypeStruct((C,) + x.shape if axis == "all" else x.shape, x.dtype) for axis, x in riders
        ]
        count, most = len(riders), max(S, C) - 1
        self.scratch = [DMA((count, most)), DMA((count, most)), DMA((count,))] if count else []

    def bind(self, ins, outs, sems):
        self.ins, self.outs, self.sems = ins, outs, sems

    def start(self):
        p, z, c = here()
        self.moves = []
        for n, axis in enumerate(self.axes):
            src, dst = self.ins[n], self.outs[n]
            send, recv, own = self.sems
            if axis == "tp":
                copies = [remote(src, dst, send.at[n, 0], recv.at[n, 0], {"tp": 1 - c})]
            elif axis == "all":
                copies = [
                    remote(src, dst.at[z], send.at[n, k - 1], recv.at[n, k - 1], {"ctx": (z + k) % self.C})
                    for k in range(1, self.C)
                ]
                copies.append(pltpu.make_async_copy(src, dst.at[z], own.at[n]))
            else:
                size, me = (self.S, p) if axis == "shard" else (self.C, z)
                copies = [
                    remote(src.at[(me + k) % size], dst.at[me], send.at[n, k - 1], recv.at[n, k - 1], {axis: (me + k) % size})
                    for k in range(1, size)
                ]
                copies.append(pltpu.make_async_copy(src.at[me], dst.at[me], own.at[n]))
            for copy in copies:
                copy.start()
            self.moves += copies

    def wait(self):
        for copy in self.moves:
            copy.wait()


def greet(S, C, mates=(), line=False, other=False, axes=()):
    p, z, c = here()
    peers = [{"shard": q} for q in ([(p + k) % S for k in range(1, S)] if "shard" in axes else mates)]
    if line or "ctx" in axes or "all" in axes:
        peers += [{"ctx": (z + k) % C} for k in range(1, C)]
    if other or "tp" in axes:
        peers.append({"tp": 1 - c})
    barrier = pltpu.get_barrier_semaphore()
    for where in peers:
        pl.semaphore_signal(barrier, inc=1, device_id=where, device_id_type=MESH)
    pl.semaphore_wait(barrier, len(peers))


def in_vmem(shape, dtype):
    *lead, tall, wide = (1, 1) + tuple(shape)
    tile = 32 // np.dtype(dtype).itemsize
    return math.prod(lead) * -(-tall // tile) * tile * -(-wide // 128) * 128 * np.dtype(dtype).itemsize


def comm(kernel, S, C, number, name, args, in_specs, outs, scratch, riders=()):
    ride = Riders(S, C, riders)
    held = [x for x, spec in zip(args, in_specs) if spec is IN_VMEM] + [x for x, spec in outs if spec is IN_VMEM]
    held += ride.arrays + [x for x in scratch if getattr(x, "memory_space", None) == pltpu.VMEM]
    room = sum(in_vmem(x.shape, x.dtype) for x in held) + (10 << 20)
    na, nr, no, ns = len(args), len(ride.axes), len(outs), len(scratch)

    def body(*refs):
        ins, refs = refs[:na], refs[na:]
        rins, refs = refs[:nr], refs[nr:]
        os, refs = refs[:no], refs[no:]
        routs, refs = refs[:nr], refs[nr:]
        ride.bind(rins, routs, refs[ns:])
        kernel(ride, ins, os, refs[:ns])

    return pl.pallas_call(
        body,
        out_shape=[shape for shape, _ in outs] + ride.shapes,
        in_specs=list(in_specs) + [IN_VMEM] * nr,
        out_specs=[spec for _, spec in outs] + [ANY] * nr,
        scratch_shapes=list(scratch) + ride.scratch,
        compiler_params=pltpu.CompilerParams(
            collective_id=number, has_side_effects=True, vmem_limit_bytes=min(room, 60 << 20)
        ),
        cost_estimate=pl.CostEstimate(flops=0, bytes_accessed=120_000_000, transcendentals=0),
        name=name,
    )(*args, *ride.arrays)


def exchange(S, C, T, number, riders, tiles, rows=None):
    def kernel(ride, ins, outs, scratch):
        tile, got = ins[0], outs[0]
        send, recv, bsend, brecv, own = scratch[:5]
        p, z, c = here()
        everyone = [(i, j) for i in range(C) for j in range(S) if i or j]
        barrier = pltpu.get_barrier_semaphore()
        peers = [{"shard": (p + j) % S, "ctx": (z + i) % C} for i, j in everyone] + [{"tp": 1 - c}]
        for where in peers:
            pl.semaphore_signal(barrier, inc=1, device_id=where, device_id_type=MESH)
        pl.semaphore_wait(barrier, len(peers))

        def turn_over(source, target, k, axis, size, me):
            ssem, rsem, local = scratch[5:]
            hop = [pltpu.make_async_copy(source.at[me], target.at[me], local.at[k])]
            for j in range(1, size):
                q = (me + j) % size
                hop.append(remote(source.at[q], target.at[me], ssem.at[k, j - 1], rsem.at[k, j - 1], {axis: q}))
            for copy in hop:
                copy.start()
            return hop

        if rows is not None:
            first = turn_over(ins[1], outs[1], 0, "shard", S, p)
        local = pltpu.make_async_copy(tile.at[z, p], got.at[c, z, p], own)
        local.start()
        copies = []
        for at, (where, (i, j)) in enumerate(zip(peers, everyone)):
            q, g = (p + j) % S, (z + i) % C
            copies.append(remote(tile.at[g, q], got.at[c, z, p], send.at[at], recv.at[at], where))
            copies[-1].start()
        ride.start()
        if rows is not None:
            for copy in first:
                copy.wait()
            second = turn_over(outs[1], outs[2], 1, "ctx", C, z)
        local.wait()
        for copy in copies:
            copy.wait()
        back = remote(got.at[c], got.at[c], bsend, brecv, {"tp": 1 - c})
        back.start()
        back.wait_send()
        remote(got.at[1 - c], got.at[1 - c], bsend, brecv, {"tp": 1 - c}).wait_recv()
        if rows is not None:
            for copy in second:
                copy.wait()
        ride.wait()

    count, most = C * S - 1, max(S, C) - 1
    args, outs = [tiles], [(jax.ShapeDtypeStruct((T,) + tiles.shape, tiles.dtype), ANY)]
    scratch = [DMA((count,)), DMA((count,)), DMA, DMA, DMA]
    if rows is not None:
        args.append(rows)
        outs += [(jax.ShapeDtypeStruct(rows.shape, rows.dtype), IN_VMEM)] * 2
        scratch += [DMA((2, most)), DMA((2, most)), DMA((2,))]
    return comm(kernel, S, C, number, "exchange", args, [IN_VMEM] * len(args), outs, scratch, riders)


def plane(S):
    p, _, c = here()
    B = S // 2
    a, b = p // B, p % B
    return a, b, [a * B + (b + j) % B for j in range(1, B)], (1 - a) * B + b


def spread_sems(S):
    count = 4 + 4 * (S // 2 - 1)
    return [DMA((2 * count,)), DMA((2 * count,))]


def spread(S, own, region, send, recv, work=(None, None)):
    p, _, c = here()
    B = S // 2
    a, b, rows, col = plane(S)
    rows, col, other = [{"shard": q} for q in rows], {"shard": col}, {"tp": 1 - c}
    per = 4 + 4 * (B - 1)
    OWN, ROW, COL, VIA_COL, VIA_ROW = 0, 2, 2 + 2 * (B - 1), 4 + 2 * (B - 1), 4 + 3 * (B - 1)
    started = []

    def push(q, h, sem, where, first=False):
        view = region(q, h, c)
        copy = remote(own(h) if first else view, view, send.at[sem], recv.at[sem], where)
        copy.start()
        started.append(copy)

    def came(q, h, sem, core):
        view = region(q, h, core)
        remote(view, view, send.at[sem], recv.at[sem], other).wait_recv()

    for h in range(2):
        for j in range(1, B):
            push(p, h, ROW + 2 * (j - 1) + h, rows[j - 1], True)
    for h in (1, 0):
        push(p, h, COL + h, col, True)
    for h in range(2):
        push(p, h, per + OWN + h, other, True)

    def from_row(j, h):
        q = a * B + (b - j) % B
        came(q, h, ROW + 2 * (j - 1) + h, c)
        push(q, h, per + ROW + 2 * (j - 1) + h, other)
        return q

    def from_col(h):
        q = (1 - a) * B + b
        came(q, h, COL + h, c)
        push(q, h, per + COL + h, other)
        return q

    if work[0] is not None:
        work[0]()
    for j in range(1, B):
        q = from_row(j, 0)
        push(q, 0, VIA_COL + j - 1, col)
    q = from_col(1)
    for j in range(1, B):
        push(q, 1, VIA_ROW + j - 1, rows[j - 1])
    if work[1] is not None:
        work[1]()
    for j in range(1, B):
        from_row(j, 1)
    from_col(0)
    for j in range(1, B):
        q = (1 - a) * B + (b - j) % B
        came(q, 0, VIA_COL + j - 1, c)
        push(q, 0, per + VIA_COL + j - 1, other)
        came(q, 1, VIA_ROW + j - 1, c)
        push(q, 1, per + VIA_ROW + j - 1, other)
    for h in range(2):
        came(p, h, per + OWN + h, 1 - c)
        came((1 - a) * B + b, h, per + COL + h, 1 - c)
    for j in range(1, B):
        for h in range(2):
            came(a * B + (b - j) % B, h, per + ROW + 2 * (j - 1) + h, 1 - c)
        q = (1 - a) * B + (b - j) % B
        came(q, 0, per + VIA_COL + j - 1, 1 - c)
        came(q, 1, per + VIA_ROW + j - 1, 1 - c)
    for copy in started:
        copy.wait_send()


def gather_columns(S, C, T, number, x, riders=(), extra=None):
    _, n, wide = x.shape
    more, more_specs, more_outs, more_scratch, task = extra or ((), (), (), (), None)

    def kernel(ride, ins, outs, scratch):
        x_ref, out_ref = ins[0], outs[0]
        send, recv, own = scratch[:3]
        p, _, c = here()
        _, _, rows, col = plane(S)

        def region(q, h, core):
            part = pl.ds(pl.multiple_of(q * wide, 128), wide)
            return out_ref.at[pl.ds(h * (C // 2), C // 2), core, :, part]

        local = [
            pltpu.make_async_copy(x_ref.at[pl.ds(h * (C // 2), C // 2)], region(p, h, c), own.at[h]) for h in range(2)
        ]
        for copy in local:
            copy.start()
        if task is not None:
            task(ins[1:], outs[1:], scratch[3:], None)
        greet(S, C, rows + [col], other=True, axes=ride.axes)
        ride.start()
        work = [None, None]
        if task is not None:
            work = [functools.partial(task, ins[1:], outs[1:], scratch[3:], piece) for piece in range(2)]
        spread(S, lambda h: x_ref.at[pl.ds(h * (C // 2), C // 2)], region, send, recv, work)
        for copy in local:
            copy.wait()
        ride.wait()

    out, *rest = comm(
        kernel, S, C, number, "gather_columns", [x, *more], [IN_VMEM, *more_specs],
        [(jax.ShapeDtypeStruct((C, T, n, wide * S), x.dtype), ANY), *more_outs],
        spread_sems(S) + [DMA((2,)), *more_scratch], riders,
    )
    return [out.reshape(C * T * n, wide * S)] + rest


CHUNK = 512
ROWS = 32


def sum_scratch(S, n, D):
    half, B = n // 2, S // 2

    def vm(*shape):
        return pltpu.VMEM(shape, BF)

    return [
        vm(S, n, D), vm(S, n, D), vm(S, n, D), vm(B - 1, 2, half, D), vm(B, half, D),
        vm(B - 1, half, D), vm(half, D), vm(half, D), vm(B - 1, half, D),
        DMA((S,)), DMA((S,)), DMA((B - 1, 2)), DMA((B - 1, 2)), DMA((B,)), DMA((B,)), DMA((B,)), DMA((B,)),
    ]


def sum_over_plane(S, T, x_ref, w_ref, out_ref, scratch, meanwhile=None):
    away, sib, mine, row1, col1, row2, col2, to_col, to_row = scratch[:9]
    asend, arecv, rsend, rrecv, csend, crecv, fsend, frecv = scratch[9:]
    n, D = out_ref.shape
    half, B = n // 2, S // 2
    _, _, c = here()
    a, b, rows, col = plane(S)
    rows, col, other = [{"shard": q} for q in rows], {"shard": col}, {"tp": 1 - c}

    def chip(e):
        return ((a + e // B) % 2) * B + (b + e % B) % B

    def product(e, core, store):
        x = x_ref[chip(e) * T + core]

        def column(j, _):
            w = pl.ds(pl.multiple_of(j * CHUNK, CHUNK), CHUNK)
            store(w, mm(x, w_ref[w, :], 1, 1))
            return 0

        lax.fori_loop(0, D // CHUNK, column, 0)

    def to_other(e):
        return remote(away.at[e], sib.at[e], asend.at[e], arecv.at[e], other)

    def for_other(e):
        def store(w, value):
            away[e, :, w] = value.astype(BF)

        product(e, 1 - c, store)
        to_other(e).start()

    for_other(S - 1)
    top, low = pl.ds(0, half), pl.ds(half, half)
    started = []

    def push(src, dst, send, recv, where):
        copy = remote(src, dst, send, recv, where)
        copy.start()
        started.append(copy)

    for e in range(S - 1, -1, -1):
        if e:
            for_other(e - 1)
        to_other(e).wait()

        def store(w, value):
            value = value + sib[e, :, w].astype(F32)
            if e:
                mine[e, :, w] = value.astype(BF)
            else:
                out_ref[:, w] = value

        product(e, c, store)
        j = e % B
        if e > B:
            push(mine.at[e, top], row1.at[j - 1, 1], rsend.at[j - 1, 1], rrecv.at[j - 1, 1], rows[j - 1])
            push(mine.at[e, low], col1.at[j], csend.at[j], crecv.at[j], col)
        elif e == B:
            push(mine.at[e, low], col1.at[0], csend.at[0], crecv.at[0], col)
        elif e:
            push(mine.at[e, top], row1.at[j - 1, 0], rsend.at[j - 1, 0], rrecv.at[j - 1, 0], rows[j - 1])

    def came(ref, send, recv):
        remote(ref, ref, send, recv, other).wait_recv()

    if meanwhile is not None:
        meanwhile(0)
    total = mine[B, top, :].astype(F32)
    for j in range(1, B):
        came(row1.at[j - 1, 1], rsend.at[j - 1, 1], rrecv.at[j - 1, 1])
        total = total + row1[j - 1, 1].astype(F32)
    to_col[...] = total.astype(BF)
    push(to_col, col2, fsend.at[0], frecv.at[0], col)
    for j in range(1, B):
        came(col1.at[j], csend.at[j], crecv.at[j])
        to_row[j - 1] = (mine[j, low, :].astype(F32) + col1[j].astype(F32)).astype(BF)
        push(to_row.at[j - 1], row2.at[j - 1], fsend.at[j], frecv.at[j], rows[j - 1])
    if meanwhile is not None:
        meanwhile(1)
    came(col1.at[0], csend.at[0], crecv.at[0])
    upper, lower = out_ref[top, :], out_ref[low, :] + col1[0].astype(F32)
    for j in range(1, B):
        came(row1.at[j - 1, 0], rsend.at[j - 1, 0], rrecv.at[j - 1, 0])
        upper = upper + row1[j - 1, 0].astype(F32)
    came(col2, fsend.at[0], frecv.at[0])
    out_ref[top, :] = upper + col2[...].astype(F32)
    for j in range(1, B):
        came(row2.at[j - 1], fsend.at[j], frecv.at[j])
        lower = lower + row2[j - 1].astype(F32)
    out_ref[low, :] = lower
    for copy in started:
        copy.wait_send()


def project(S, C, T, number, tok, raw, gain, shift, bias):
    L, D = tok.shape
    _, parts, nb, wide = raw.shape
    hn = wide // S
    most = S - 1

    def kernel(ride, ins, outs, scratch):
        tok_ref, raw_ref, gain_ref, shift_ref, bias_ref = ins
        n_ref, out_ref, w_ref = outs
        send, recv, own = scratch
        p, _, _ = here()
        mates = [(p + k) % S for k in range(1, S)]
        greet(S, C, mates)

        def lanes(q):
            return pl.ds(pl.multiple_of(q * hn, 128), hn)

        copies = []
        for part in range(parts):
            dst = w_ref.at[:, p, :, pl.ds(part * hn, hn)]
            for k, q in enumerate(mates):
                copies.append(
                    remote(raw_ref.at[:, part, :, lanes(q)], dst, send.at[k, part], recv.at[k, part], {"shard": q})
                )
            copies.append(pltpu.make_async_copy(raw_ref.at[:, part, :, lanes(p)], dst, own.at[part]))
        for copy in copies:
            copy.start()

        def normed(r):
            n_ref[r, :] = (norm_of(tok_ref[r, :].astype(F32))[0] * gain_ref[...] + shift_ref[...]).astype(BF)

        row_blocks(L, normed)
        for copy in copies:
            copy.wait()
        w = w_ref[...].reshape(D, parts * hn)

        @pl.loop(0, L // BLK)
        def _(i):
            r = pl.ds(pl.multiple_of(i * BLK, BLK), BLK)
            out_ref[r, :] = mm(n_ref[r, :], w, 1, 0) + bias_ref[...]

    n, out, w = comm(
        kernel, S, C, number, "project", [tok, raw, gain, shift, bias], [IN_VMEM] * 5,
        [
            (jax.ShapeDtypeStruct((L, D), BF), IN_VMEM), (jax.ShapeDtypeStruct((L, parts * hn), F32), IN_VMEM),
            (jax.ShapeDtypeStruct((C, S, nb, parts * hn), BF), IN_VMEM),
        ],
        [DMA((most, parts)), DMA((most, parts)), DMA((parts,))],
    )
    return n, out, w.reshape(D, parts * hn)


def gates_back_kernel(gb_ref, wd_ref, gu_ref, dgu_ref):
    dact = mm(gb_ref[...], wd_ref[...], 1, 0)
    both, width = gu_ref[...], dact.shape[1]
    gate, up = both[:, :width], both[:, width:]
    s = jax.nn.sigmoid(gate)
    dgate = dact * up * s * (1.0 + gate * (1.0 - s))
    dgu_ref[...] = jnp.concatenate((dgate, dact * gate * s), axis=1).astype(BF)


def gates_work(ins, outs, scratch, piece):
    gu_ref, act_ref = outs
    n2_ref, wg_ref, sems = scratch
    if piece != 1:
        for i, (x, y) in enumerate(zip(ins, (n2_ref, wg_ref))):
            copy = pltpu.make_async_copy(x, y, sems.at[i])
            copy.wait() if piece == 0 else copy.start()
    if piece is None:
        return
    (rows, width), half = act_ref.shape, act_ref.shape[0] // BLK // 2

    @pl.loop(piece * half, piece * half + half)
    def _(i):
        r = pl.ds(pl.multiple_of(i * BLK, BLK), BLK)
        both = mm(n2_ref[r, :], wg_ref[...], 1, 0)
        gu_ref[r, :] = both
        gate, up = both[:, :width], both[:, width:]
        act_ref[r, :] = (gate * jax.nn.sigmoid(gate) * up).astype(BF)


def gates(S, C, T, number, n2, wg, x):
    L, width = n2.shape[0], wg.shape[1] // 2
    outs = [jax.ShapeDtypeStruct((L, 2 * width), F32), jax.ShapeDtypeStruct((L, width), BF)]
    return gather_columns(
        S, C, T, number, x, (),
        ([n2, wg], [ANY, ANY], [(shape, IN_VMEM) for shape in outs],
         [pltpu.VMEM(n2.shape, BF), pltpu.VMEM(wg.shape, BF), DMA((2,))], gates_work),
    )


def by_rows(kernel, name, arrays, outs):
    L = outs[0].shape[0]

    def spec(width):
        return pl.BlockSpec((BLK, width), lambda i: (i, 0))

    return pl.pallas_call(
        kernel,
        grid=(L // BLK,),
        in_specs=[spec(x.shape[1]) if rows else pl.BlockSpec(x.shape, lambda i: (0, 0)) for rows, x in arrays],
        out_specs=[spec(x.shape[1]) for x in outs],
        out_shape=outs,
        compiler_params=pltpu.CompilerParams(vmem_limit_bytes=48 << 20),
        name=name,
    )(*[x for _, x in arrays])


def row_blocks(n, work):
    @pl.loop(0, n // ROWS)
    def _(i):
        work(pl.ds(pl.multiple_of(i * ROWS, ROWS), ROWS))


def own_rows(T, x_ref, row_ref, sem):
    p, _, c = here()
    copy = pltpu.make_async_copy(x_ref.at[p * T + c], row_ref, sem)
    copy.start()
    return copy


def norm_of(v):
    center = v - jnp.mean(v, axis=-1, keepdims=True)
    inverse = lax.rsqrt(jnp.mean(center * center, axis=-1, keepdims=True) + EPS)
    return center * inverse, inverse


def norm_back(v, g, gain, stats_ref):
    normal, inverse = norm_of(v)
    e = g * gain
    stats_ref[0:1, :] += jnp.sum(g * normal, axis=0, keepdims=True)
    stats_ref[1:2, :] += jnp.sum(g, axis=0, keepdims=True)
    return inverse * (
        e - jnp.mean(e, axis=-1, keepdims=True) - normal * jnp.mean(e * normal, axis=-1, keepdims=True)
    )


def spread_rows(S, T, src, out_ref, send, recv, own):
    p, _, c = here()
    half = src.shape[0] // 2
    local = pltpu.make_async_copy(src, out_ref.at[p * T + c], own)
    local.start()
    spread(
        S,
        lambda h: src.at[pl.ds(h * half, half)],
        lambda q, h, core: out_ref.at[q * T + core, pl.ds(h * half, half)],
        send,
        recv,
    )
    local.wait()


def sum_norm_gather(S, C, T, number, x, w, residual, gain, shift, riders=()):
    L, K = x.shape
    D, n = w.shape[0], L // (S * T)

    def kernel(ride, ins, outs, scratch):
        x_ref, w_ref, all_ref, gain_ref, shift_ref = ins
        v_ref, out_ref = outs
        acc, low, send, recv, own, res_ref, sem = scratch[:7]
        _, _, rows, col = plane(S)
        rest = own_rows(T, all_ref, res_ref, sem)
        greet(S, C, rows + [col], other=True, axes=ride.axes)
        ride.start()
        sum_over_plane(S, T, x_ref, w_ref, acc, scratch[7:])
        rest.wait()

        def work(r):
            v = res_ref[r, :].astype(F32) + acc[r, :]
            v_ref[r, :] = v
            low[r, :] = (norm_of(v)[0] * gain_ref[...] + shift_ref[...]).astype(BF)

        row_blocks(n, work)
        spread_rows(S, T, low, out_ref, send, recv, own)
        ride.wait()

    v, out, *rest = comm(
        kernel, S, C, number, "sum_norm_gather", [x.reshape(S * T, n, K), w, residual.reshape(S * T, n, D), gain, shift],
        [IN_VMEM, IN_VMEM, ANY, IN_VMEM, IN_VMEM],
        [(jax.ShapeDtypeStruct((n, D), F32), IN_VMEM), (jax.ShapeDtypeStruct((S * T, n, D), BF), ANY)],
        [pltpu.VMEM((n, D), F32), pltpu.VMEM((n, D), BF)] + spread_sems(S)
        + [DMA, pltpu.VMEM((n, D), BF), DMA] + sum_scratch(S, n, D),
        riders,
    )
    return [v, out.reshape(L, D)] + rest


def sum_back_gather(S, C, T, number, x, w, v, residual, gain, riders=()):
    L, K = x.shape
    D, n = w.shape[0], L // (S * T)

    def kernel(ride, ins, outs, scratch):
        x_ref, w_ref, in_ref, all_ref, gain_ref = ins
        v_ref, out_ref, stats = outs
        acc, low, send, recv, own, res_ref, sem = scratch[:7]
        _, _, rows, col = plane(S)
        rest = own_rows(T, all_ref, res_ref, sem)
        greet(S, C, rows + [col], other=True, axes=ride.axes)
        ride.start()
        sum_over_plane(S, T, x_ref, w_ref, acc, scratch[7:])
        rest.wait()
        stats[...] = jnp.zeros_like(stats)

        def work(r):
            g = res_ref[r, :].astype(F32) + norm_back(in_ref[r, :], acc[r, :], gain_ref[...], stats)
            v_ref[r, :] = g
            low[r, :] = g.astype(BF)

        row_blocks(n, work)
        spread_rows(S, T, low, out_ref, send, recv, own)
        ride.wait()

    g, out, stats, *rest = comm(
        kernel, S, C, number, "sum_back_gather", [x.reshape(S * T, n, K), w, v, residual.reshape(S * T, n, D), gain],
        [IN_VMEM, IN_VMEM, IN_VMEM, ANY, IN_VMEM],
        [
            (jax.ShapeDtypeStruct((n, D), F32), IN_VMEM), (jax.ShapeDtypeStruct((S * T, n, D), BF), ANY),
            (jax.ShapeDtypeStruct((2, D), F32), IN_VMEM),
        ],
        [pltpu.VMEM((n, D), F32), pltpu.VMEM((n, D), BF)] + spread_sems(S)
        + [DMA, pltpu.VMEM((n, D), BF), DMA] + sum_scratch(S, n, D),
        riders,
    )
    return [g, out.reshape(L, D), stats] + rest


def sum_back(S, C, T, number, x, w, v, residual, gain, riders=()):
    L, K = x.shape
    D, n = w.shape[0], L // (S * T)

    def kernel(ride, ins, outs, scratch):
        x_ref, w_ref, all_ref, res_ref, gain_ref = ins
        low, stats = outs
        acc, in_ref, sem = scratch[:3]
        _, _, rows, col = plane(S)
        rest = own_rows(T, all_ref, in_ref, sem)
        greet(S, C, rows + [col], other=True, axes=ride.axes)
        ride.start()
        sum_over_plane(S, T, x_ref, w_ref, acc, scratch[3:])
        rest.wait()
        stats[...] = jnp.zeros_like(stats)

        def work(r):
            g = res_ref[r, :] + norm_back(in_ref[r, :].astype(F32), acc[r, :], gain_ref[...], stats)
            low[r, :] = g.astype(BF)

        row_blocks(n, work)
        ride.wait()

    return comm(
        kernel, S, C, number, "sum_back", [x.reshape(S * T, n, K), w, v.reshape(S * T, n, D), residual, gain],
        [IN_VMEM, IN_VMEM, ANY, IN_VMEM, IN_VMEM],
        [(jax.ShapeDtypeStruct((n, D), BF), IN_VMEM), (jax.ShapeDtypeStruct((2, D), F32), IN_VMEM)],
        [pltpu.VMEM((n, D), F32), pltpu.VMEM((n, D), BF), DMA] + sum_scratch(S, n, D),
        riders,
    )


def finish(S, C, T, number, x, y, stats, bias, gateup, down, qkv, out):
    n, D = x.shape
    fn, hn = down.shape[2], out.shape[2]
    wide, lines = D // S, bias.shape[1] // 128
    nb = D // (S * C)
    count = sum(z.shape[0] for z in stats)
    tall = -(-(count + lines) // 8) * 8
    many = C * S - 1
    pieces = S if ordered(D, S, C) else 1

    def kernel(ride, ins, outs, scratch):
        x_ref, y_ref, stat_refs, bias_ref = ins[0], ins[1], ins[2:-5], ins[-5]
        gateup_ref, down_ref, qkv_ref, o_ref = ins[-4:]
        x_out, y_out, norm_out, bias_out, gateup_out, down_out, qkv_out, o_out = outs
        xbuf, xbuf2, ybuf2, tile, send, recv, own, psend, precv, pown, lsend, lrecv, tsend, trecv = scratch[:14]
        qkv_buf, o_buf, gsend, grecv, gown, got = scratch[14:]
        p, z, c = here()
        other = {"tp": 1 - c}
        everyone = [(i, j) for i in range(C) for j in range(S) if i or j]
        peers = [{"shard": (p + j) % S, "ctx": (z + i) % C} for i, j in everyone]
        barrier = pltpu.get_barrier_semaphore()
        for where in peers + [other]:
            pl.semaphore_signal(barrier, inc=1, device_id=where, device_id_type=MESH)
        pl.semaphore_wait(barrier, len(peers) + 1)

        def part(q):
            return pl.ds(pl.multiple_of(q * wide, 128), wide)

        def turn_over(source, target, at, size, me, axis):
            hop = [pltpu.make_async_copy(source(me), target, own.at[at])]
            for k in range(1, size):
                q = (me + k) % size
                hop.append(remote(source(q), target, send.at[at, k - 1], recv.at[at, k - 1], {axis: q}))
            for copy in hop:
                copy.start()
            return hop

        def arrive(buf, out, at):
            hop = []
            for i in range(pieces):
                src = pl.ds(i * (wide // pieces), wide // pieces)
                first = (i * C + p) * nb if pieces > 1 else p * wide
                dst = out.at[c, :, pl.ds(pl.multiple_of(first, 128), wide // pieces)]
                hop.append(pltpu.make_async_copy(buf.at[p, :, src], dst, pown.at[at, i]))
                for k in range(1, S):
                    q = (p + k) % S
                    hop.append(
                        remote(buf.at[q, :, src], dst, psend.at[at, k - 1, i], precv.at[at, k - 1, i], {"shard": q})
                    )
            for copy in hop:
                copy.start()
            return hop

        def both(ref, at):
            copy = remote(ref.at[c], ref.at[c], lsend.at[at], lrecv.at[at], other)
            copy.start()
            return copy

        def settle(ref, at, copy):
            copy.wait_send()
            remote(ref.at[1 - c], ref.at[1 - c], lsend.at[at], lrecv.at[at], other).wait_recv()

        x_hop = turn_over(lambda q: x_ref.at[:, part(q)], xbuf.at[p], 0, S, p, "shard")
        y_hop = turn_over(lambda q: y_ref.at[q], ybuf2.at[z], 1, C, z, "ctx")
        moves = []
        for i, (src, dst) in enumerate(((qkv_ref, qkv_buf), (o_ref, o_buf))):
            moves.append(pltpu.make_async_copy(src.at[p], dst.at[p], gown.at[i]))
            for k in range(1, S):
                q = (p + k) % S
                moves.append(remote(src.at[q], dst.at[p], gsend.at[i, k - 1], grecv.at[i, k - 1], {"shard": q}))
        for copy in moves:
            copy.start()
        tile[...] = jnp.zeros_like(tile)
        at = count
        for i, ref in enumerate(stat_refs):
            for j in range(2):
                tile[j * len(stat_refs) + i : j * len(stat_refs) + i + 1, :] = ref[j : j + 1, :]
        for k in range(lines):
            for block in range(D // 128):
                tile[at + k : at + k + 1, pl.ds(block * 128, 128)] = bias_ref[:, pl.ds(k * 128, 128)]

        def columns(g, q):
            return tile.at[:, pl.ds(pl.multiple_of((g * S + q) * nb // 128 * 128, 128), 128)]

        small = [pltpu.make_async_copy(columns(z, p), got.at[c, z, p], own.at[3])]
        for k, (where, (i, j)) in enumerate(zip(peers, everyone)):
            small.append(
                remote(columns((z + i) % C, (p + j) % S), got.at[c, z, p], tsend.at[k], trecv.at[k], where)
            )
        for copy in small:
            copy.start()
        for copy in x_hop:
            copy.wait()
        x_hop = turn_over(lambda q: xbuf.at[q], xbuf2.at[z], 2, C, z, "ctx")
        for q in range(S):
            down_out[q * fn : (q + 1) * fn, :] = down_ref[q].astype(F32).T
        for copy in y_hop:
            copy.wait()
        y_hop = arrive(ybuf2, y_out, 0)
        for copy in small:
            copy.wait()
        small_last = both(got, 0)
        bias_out[...] = jnp.sum(got[c, :, :, count : count + lines, :], axis=0)
        for i in range(2):
            for q in range(S):
                gateup_out[:, i, q * fn : (q + 1) * fn] = gateup_ref[q, :, i * fn : (i + 1) * fn].astype(F32)
        for copy in x_hop:
            copy.wait()
        x_hop = arrive(xbuf2, x_out, 1)
        for copy in y_hop:
            copy.wait()
        y_last = both(y_out, 1)
        for copy in moves:
            copy.wait()
        for q in range(S):
            o_out[q * hn : (q + 1) * hn, :] = o_buf[q].astype(F32).T
            for i in range(3):
                qkv_out[i, :, q * hn : (q + 1) * hn] = qkv_buf[q, :, i * hn : (i + 1) * hn].astype(F32)
        for copy in x_hop:
            copy.wait()
        x_last = both(x_out, 2)
        settle(got, 0, small_last)
        norm_out[...] = jnp.sum(got[:, :, :, :count, :], axis=(0, 1, 2))
        settle(y_out, 1, y_last)
        settle(x_out, 2, x_last)

    args = [x, y, *stats, bias, gateup, down, qkv, out]
    most = max(S, C) - 1
    home = (jax.ShapeDtypeStruct((T, n, D), BF), ANY)
    x, y, *rest = comm(
        kernel, S, C, number, "finish", args, [IN_VMEM] * len(args),
        [home, home]
        + [
            (jax.ShapeDtypeStruct(shape, F32), IN_VMEM)
            for shape in ((count, 128), (S, lines, 128), (nb, 2, S * fn), (S * fn, nb), (3, nb, S * hn), (S * hn, nb))
        ],
        [
            pltpu.VMEM((S, n, wide), BF), pltpu.VMEM((C, n, wide), BF), pltpu.VMEM((C, n, wide), BF),
            pltpu.VMEM((tall, D), F32), DMA((3, most)), DMA((3, most)), DMA((4,)),
            DMA((2, S - 1, pieces)), DMA((2, S - 1, pieces)), DMA((2, pieces)), DMA((3,)), DMA((3,)),
            DMA((many,)), DMA((many,)),
            pltpu.VMEM(qkv.shape, BF), pltpu.VMEM(out.shape, BF), DMA((2, S - 1)), DMA((2, S - 1)), DMA((2,)),
            pltpu.VMEM((T, C, S, tall, 128), F32),
        ],
    )
    return [x.reshape(T * n, D), y.reshape(T * n, D)] + rest


def ordered(D, S, C):
    return D // (S * C) % 128 == 0


def turn_tables(rows):
    feature = np.arange(128) % HEAD
    freq = np.where(feature < ROT, BASE ** (-2.0 * (feature % (ROT // 2)) / ROT), 0.0)
    near = np.arange(BLK)[:, None] * freq
    far = np.arange(0, rows, BLK)[:, None] * freq
    return [jnp.asarray(f(x), F32) for x in (near, far) for f in (np.cos, np.sin)]


def turn(x, i, tables, sign):
    cos, sin, cos_far, sin_far = tables
    far_cos, far_sin = cos_far[pl.ds(i, 1), :], sin_far[pl.ds(i, 1), :]
    cos_t = cos[...] * far_cos - sin[...] * far_sin
    sin_t = sin[...] * far_cos + cos[...] * far_sin
    ahead = lax.broadcasted_iota(jnp.int32, x.shape, 1) % HEAD < ROT // 2
    partner = jnp.where(ahead, -pltpu.roll(x, 128 - ROT // 2, 1), pltpu.roll(x, ROT // 2, 1))
    return x * cos_t + partner * (sin_t * sign)


def two_heads(x, left):
    zero = jnp.zeros_like(x)
    return [jnp.where(left, x, zero), jnp.where(left, zero, x)]


def block_of(rows):
    return next(size for size in (512, 256) if rows % size == 0)


def attend_kernel(
    first_ref, qkv_ref, cos_ref, sin_ref, cosf_ref, sinf_ref, begin_ref,
    qo_ref, ko_ref, vo_ref, o_ref, lse_ref, vt_ref,
):
    rows, wide = qo_ref.shape
    pairs, size = wide // 128, block_of(rows)
    tables = (cos_ref, sin_ref, cosf_ref, sinf_ref)
    left = lax.broadcasted_iota(jnp.int32, (size, 128), 1) < HEAD
    key_at = lax.broadcasted_iota(jnp.int32, (size, size), 0)
    query_at = lax.broadcasted_iota(jnp.int32, (1, size), 1)

    @pl.loop(0, rows // BLK)
    def _(i):
        r = pl.ds(pl.multiple_of(i * BLK, BLK), BLK)
        for t in range(pairs):
            w = pl.ds(t * 128, 128)
            q, k, v = (qkv_ref[r, pl.ds(part * wide + t * 128, 128)] for part in range(3))
            qo_ref[r, w] = turn(q, i, tables, 1.0).astype(BF) * jnp.asarray(HEAD**-0.5, BF)
            ko_ref[r, w] = turn(k, i, tables, 1.0).astype(BF)
            vo_ref[r, w] = v.astype(BF)
            vt_ref[w, r] = v.T.astype(BF)

    @pl.loop(0, rows // size)
    def _(i):
        r = pl.ds(pl.multiple_of(i * size, size), size)
        qs = sum((two_heads(qo_ref[r, pl.ds(t * 128, 128)], left) for t in range(pairs)), [])
        begin = begin_ref[0:1, r]
        here = query_at + i * size

        def step(j, carry):
            w = pl.ds(pl.multiple_of(j * size, size), size)
            key = key_at + j * size
            seen = (key <= here) & (key >= begin)
            out = []
            for h in range(2 * pairs):
                m, l, acc = carry[h]
                s = jnp.where(seen, mm(ko_ref[w, pl.ds(h // 2 * 128, 128)], qs[h], 1, 1), NEG)
                top = jnp.maximum(m, jnp.max(s, axis=0, keepdims=True))
                fade = jnp.exp(m - top)
                e = jnp.exp(s - top)
                acc = acc * fade + mm(vt_ref[pl.ds(h * HEAD, HEAD), w], e.astype(BF), 1, 0)
                out.append((top, l * fade + jnp.sum(e, axis=0, keepdims=True), acc))
            return tuple(out)

        start = (
            jnp.full((1, size), NEG, F32), jnp.zeros((1, size), F32), jnp.zeros((HEAD, size), F32)
        )
        done = lax.fori_loop(first_ref[i], i + 1, step, (start,) * (2 * pairs))
        for t in range(pairs):
            both = []
            for h in (2 * t, 2 * t + 1):
                m, l, acc = done[h]
                both.append(acc / l)
                lse_ref[h : h + 1, r] = m + jnp.log(l)
            o_ref[r, pl.ds(t * 128, 128)] = jnp.concatenate(both, axis=0).T.astype(BF)


def attend(qkv, begin):
    rows, wide = qkv.shape[0], qkv.shape[1] // 3
    size = block_of(rows)
    half = jax.ShapeDtypeStruct((rows, wide), BF)
    return pl.pallas_call(
        attend_kernel,
        in_specs=[pl.BlockSpec(memory_space=pltpu.SMEM)] + [IN_VMEM] * 6,
        out_specs=[IN_VMEM] * 5,
        out_shape=[half] * 4 + [jax.ShapeDtypeStruct((wide // HEAD, rows), F32)],
        scratch_shapes=[pltpu.VMEM((wide, rows), BF)],
        compiler_params=pltpu.CompilerParams(vmem_limit_bytes=48 << 20),
        name="attend",
    )(begin[0, ::size] // size, qkv, *turn_tables(rows), begin)


def attend_back_work(ins, out_ref, bias_ref, scratch, piece):
    q_ref, k_ref, v_ref, o_ref, do_ref, lse_ref, cos_ref, sin_ref, cosf_ref, sinf_ref, begin_ref = ins
    kt_ref, dq_ref, dk_ref, dv_ref = scratch
    rows, wide = q_ref.shape
    pairs, size = wide // 128, block_of(rows)
    tables = (cos_ref, sin_ref, cosf_ref, sinf_ref)
    left = lax.broadcasted_iota(jnp.int32, (size, 128), 1) < HEAD
    key_at = lax.broadcasted_iota(jnp.int32, (size, size), 0)
    query_at = lax.broadcasted_iota(jnp.int32, (1, size), 1)

    last = rows // size - 1
    first, stop = (0, last) if piece == 0 else (last, last + 1)

    def prepare(i):
        r = pl.ds(pl.multiple_of(i * BLK, BLK), BLK)
        for t in range(pairs):
            w = pl.ds(t * 128, 128)
            kt_ref[w, r] = k_ref[r, w].astype(F32).T.astype(BF)
            dk_ref[r, w] = jnp.zeros((BLK, 128), F32)
            dv_ref[r, w] = jnp.zeros((BLK, 128), F32)

    if piece == 0:
        pl.loop(0, rows // BLK)(prepare)

    @pl.loop(first, stop)
    def _(i):
        r = pl.ds(pl.multiple_of(i * size, size), size)
        qs, dos, deltas, lses = [], [], [], []
        for t in range(pairs):
            w = pl.ds(t * 128, 128)
            do = do_ref[r, w]
            qs += two_heads(q_ref[r, w], left)
            dos += two_heads(do, left)
            prod = (do.astype(F32) * o_ref[r, w].astype(F32)).T
            deltas += [jnp.sum(prod[:HEAD], axis=0, keepdims=True), jnp.sum(prod[HEAD:], axis=0, keepdims=True)]
            lses += [lse_ref[2 * t : 2 * t + 1, r], lse_ref[2 * t + 1 : 2 * t + 2, r]]
        begin = begin_ref[0:1, r]
        here = query_at + i * size

        def step(j, carry):
            w = pl.ds(pl.multiple_of(j * size, size), size)
            key = key_at + j * size
            seen = (key <= here) & (key >= begin)
            out = []
            for t in range(pairs):
                lanes = pl.ds(t * 128, 128)
                k, v = k_ref[w, lanes], v_ref[w, lanes]
                dk = dv = None
                for h in (2 * t, 2 * t + 1):
                    prob = jnp.exp(jnp.where(seen, mm(k, qs[h], 1, 1) - lses[h], NEG))
                    ds = (prob * (mm(v, dos[h], 1, 1) - deltas[h])).astype(BF)
                    out.append(carry[h] + mm(kt_ref[pl.ds(h * HEAD, HEAD), w], ds, 1, 0))
                    dk_h, dv_h = mm(ds, qs[h], 1, 0), mm(prob.astype(BF), dos[h], 1, 0)
                    dk, dv = (dk_h, dv_h) if dk is None else (dk + dk_h, dv + dv_h)
                dk_ref[w, lanes] += dk
                dv_ref[w, lanes] += dv
            return tuple(out)

        done = lax.fori_loop(0, i + 1, step, (jnp.zeros((HEAD, size), F32),) * (2 * pairs))
        for t in range(pairs):
            both = jnp.concatenate(done[2 * t : 2 * t + 2], axis=0)
            dq_ref[r, pl.ds(t * 128, 128)] = both.T * (HEAD**-0.5)

    if piece == 0:
        return
    bias_ref[...] = jnp.zeros_like(bias_ref)

    @pl.loop(0, rows // BLK)
    def _(i):
        r = pl.ds(pl.multiple_of(i * BLK, BLK), BLK)
        for t in range(pairs):
            w = pl.ds(t * 128, 128)
            for part, value in enumerate((turn(dq_ref[r, w], i, tables, -1.0), turn(dk_ref[r, w], i, tables, -1.0), dv_ref[r, w])):
                lanes = pl.ds(part * wide + t * 128, 128)
                value = value.astype(BF)
                out_ref[r, lanes] = value
                bias_ref[:, lanes] += jnp.sum(value.astype(F32), axis=0, keepdims=True)


def attend_back(S, C, T, number, q, k, v, o, do, lse, begin, act, wd, riders):
    rows, wide = q.shape
    K, D, n = act.shape[1], wd.shape[0], rows // (S * T)

    def kernel(ride, ins, outs, scratch):
        _, _, row, col = plane(S)
        greet(S, C, row + [col], other=True, axes=ride.axes)

        def meanwhile(piece):
            if piece == 0:
                ride.start()
            attend_back_work(ins[2:], outs[0], outs[1], scratch[:4], piece)

        sum_over_plane(S, T, ins[0], ins[1], outs[2], scratch[4:], meanwhile)
        ride.wait()

    args = [act.reshape(S * T, n, K), wd, q, k, v, o, do, lse, *turn_tables(rows), begin]
    return comm(
        kernel, S, C, number, "attend_back", args, [IN_VMEM] * len(args),
        [(jax.ShapeDtypeStruct((rows, 3 * wide), BF), IN_VMEM), (jax.ShapeDtypeStruct((1, 3 * wide), F32), IN_VMEM),
         (jax.ShapeDtypeStruct((n, D), F32), IN_VMEM)],
        [pltpu.VMEM((wide, rows), BF)] + [pltpu.VMEM((rows, wide), F32)] * 3 + sum_scratch(S, n, D),
        riders,
    )


def doc_begins(lengths_row, rows):
    row_ids = jnp.arange(rows, dtype=jnp.int32)
    ends = jnp.cumsum(lengths_row, dtype=jnp.int32)
    begins = ends - lengths_row
    inside = (row_ids[:, None] >= begins[None, :]) & (row_ids[:, None] < ends[None, :])
    return jnp.sum(jnp.where(inside, begins[None, :], 0), axis=1, dtype=jnp.int32)


def tiles_of(parts, lead):
    flat = jnp.concatenate([x.astype(F32).reshape(lead + (-1,)) for x in parts], axis=-1)
    flat = jnp.pad(flat, ((0, 0),) * len(lead) + ((0, 1024 - flat.shape[-1]),))
    return flat.reshape(lead + (8, 128))


def make_body(S, C, T):
    assert S == C

    def body(tokens, lengths, w_qkv, b_qkv, w_out, w_gateup, w_down, norm_gain, norm_bias, cotangent):
        p, z, c = lax.axis_index("shard"), lax.axis_index("ctx"), lax.axis_index("tp")
        R, D = tokens.shape
        n = R // T
        nb = D // (S * C)
        L = R * C

        def to_parts(x):
            return x.reshape(n, S, C, nb).transpose(2, 0, 1, 3).reshape(S, n, D // S)

        def parts(x):
            return x.reshape(n, S, D // S).swapaxes(0, 1)

        def unpermute(x):
            return x.reshape(x.shape[0], C, S, nb).swapaxes(1, 2).reshape(x.shape)

        def half_of(x):
            return lax.dynamic_slice_in_dim(x, c * n, n, 0)

        def after(x, y):
            return lax.optimization_barrier((x, y))

        def over_ctx(w):
            return lax.all_gather(w.reshape(S * nb, -1), "ctx", axis=0, tiled=True)

        def sum_ctx(g):
            g = lax.psum_scatter(g.astype(BF), "ctx", scatter_dimension=0, tiled=True)
            return g.reshape(S, nb, -1)

        hn = w_qkv.shape[3] // S
        fn = w_gateup.shape[3] // S
        heads = hn // HEAD
        nf = HEAD // (S * C)

        tile = tiles_of((norm_gain[0].reshape(-1), norm_bias[0].reshape(-1), b_qkv[0].reshape(-1), lengths[0]), ())
        raw = lax.all_gather(w_qkv[0].swapaxes(0, 1).reshape(3 * nb, -1), "ctx", axis=0, tiled=True)
        small, _, tok, wo, wg, wd, cot = exchange(
            S, C, T, 0,
            [
                ("shard", w_out[0].reshape(S, hn, nb).swapaxes(1, 2)),
                ("shard", w_gateup[0].reshape(nb, 2, S, fn).transpose(2, 0, 1, 3).reshape(S, nb, 2 * fn)),
                ("shard", w_down[0].reshape(S, fn, nb).swapaxes(1, 2)),
                ("shard", to_parts(half_of(cotangent))),
            ],
            jnp.broadcast_to(tile, (C, S, 8, 128)),
            to_parts(half_of(tokens)),
        )
        tok, wo = gather_columns(S, C, T, 1, tok, [("all", wo.reshape(S * nb, hn))])
        wo, wg, wd = wo.reshape(D, hn), over_ctx(wg), over_ctx(wd)

        small = lax.dynamic_index_in_dim(small, c, 0, keepdims=False).reshape(C, S, 1024)
        norms = small[:, :, : 4 * nb].reshape(C * S, 4, nb).swapaxes(0, 1).reshape(4, D)
        gains, shifts = norms[:2], norms[2:]
        nbias = 3 * S * heads * nf
        bias = small[:, :, 4 * nb : 4 * nb + nbias].reshape(C, S, 3, S * heads, nf)
        bias = lax.dynamic_slice_in_dim(bias, p * heads, heads, 3)
        bias = bias.transpose(2, 3, 1, 0, 4).reshape(1, 3 * hn)
        docs = lengths.shape[1]
        lengths_row = lax.dynamic_index_in_dim(
            small[0, :, 4 * nb + nbias : 4 * nb + nbias + docs], z, 0, keepdims=False
        ).astype(jnp.int32)
        begin = doc_begins(lengths_row, L)
        begin = begin[None, :]

        n1, qkv, wq = project(S, C, T, 12, tok, raw.reshape(C, 3, nb, -1), gains[:1], shifts[:1], bias)
        q, k, v, o, lse = attend(qkv, begin)
        mid, n2, cot = sum_norm_gather(S, C, T, 2, o, wo, tok, gains[1:], shifts[1:], [("ctx", cot)])
        gb, gu, act = gates(S, C, T, 4, n2, wg, cot)
        gw_down = mm(gb, act, 0, 0).astype(BF)
        wd, gw_down = after(wd, gw_down)
        gw_down = sum_ctx(gw_down)

        (dgu,) = by_rows(
            gates_back_kernel, "gates_back", [(True, gb), (False, wd), (True, gu)],
            [jax.ShapeDtypeStruct((L, 2 * fn), BF)],
        )
        gw_gateup = mm(n2, dgu, 0, 0).astype(BF)
        dgu, gw_gateup = after(dgu, gw_gateup)
        gw_gateup = sum_ctx(gw_gateup)
        dmid, gb1, stats2 = sum_back_gather(S, C, T, 6, dgu, wg, mid, gb, gains[1:])
        gw_out = mm(gb1, o, 0, 0).astype(BF)
        gb1, gw_out = after(gb1, gw_out)
        do = mm(gb1, wo, 1, 0).astype(BF)
        dqkv, gbias, got, gw_down, gw_out = attend_back(
            S, C, T, 11, q, k, v, o, do, lse, begin, act, wd,
            [("shard", gw_down), ("ctx", gw_out.reshape(C, S * nb, hn))],
        )
        out = parts((mid + got).astype(BF))
        gw_qkv = mm(n1, dqkv, 0, 0).astype(BF)
        dqkv, gw_qkv = after(dqkv, gw_qkv)
        gw_qkv = sum_ctx(gw_qkv)
        low, stats1, out, gw_gateup = sum_back(
            S, C, T, 8, dqkv, wq, tok, dmid, gains[:1], [("shard", out), ("shard", gw_gateup)]
        )
        gtok, out, norms, gbias, gw_gateup, gw_down, gw_qkv, gw_out = finish(
            S, C, T, 10, low, out, [stats1, stats2], gbias, gw_gateup, gw_down, gw_qkv,
            jnp.sum(gw_out.astype(F32), axis=0).astype(BF).reshape(S, nb, hn),
        )
        if not ordered(D, S, C):
            gtok, out = unpermute(gtok), unpermute(out)
        gtok = gtok.astype(F32)
        norms = lax.dynamic_slice_in_dim(norms, (z * S + p) * nb % 128, nb, 1) if nb % 128 else norms
        gbias = gbias.reshape(S, 3, heads, S * C, nf)
        gbias = lax.dynamic_index_in_dim(gbias, p * C + z, 3, keepdims=False)
        gbias = gbias.swapaxes(0, 1).reshape(b_qkv.shape)

        return (
            out,
            gtok,
            gw_qkv.swapaxes(0, 1).reshape(w_qkv.shape),
            gbias,
            gw_out.reshape(w_out.shape),
            gw_gateup.reshape(w_gateup.shape),
            gw_down.reshape(w_down.shape),
            norms[None, :2],
            norms[None, 2:],
        )

    return body


def solution(mesh):
    both = ("shard", "ctx")
    specs = (
        P(None, both, None, "tp"),
        P(None, None, "tp", both),
        P(None, "tp", both),
        P(None, both, None, "tp"),
        P(None, "tp", both),
        P(None, None, both),
        P(None, None, both),
    )
    return jax.shard_map(
        make_body(mesh.shape["shard"], mesh.shape["ctx"], mesh.shape["tp"]),
        mesh=mesh,
        in_specs=(P(both, None), P("shard", None)) + specs + (P(both, None),),
        out_specs=(P(both, None), P(both, None)) + specs,
        check_vma=False,
    )
```

```python
import functools

import jax
import jax.numpy as jnp
import numpy as np
from jax import lax
from jax.experimental import pallas as pl
from jax.experimental.pallas import tpu as pltpu
from jax.sharding import PartitionSpec as P

HEAD = 64
ROT = 16
EPS = 1e-05
NEG = -1e30
BASE = 10000.0
BF = jnp.bfloat16
F32 = jnp.float32
BLK = 256
MESH = pl.DeviceIdType.MESH
DMA = pltpu.SemaphoreType.DMA
ANY = pl.BlockSpec(memory_space=pl.ANY)
IN_VMEM = pl.BlockSpec(memory_space=pltpu.VMEM)


def mm(a, b, ca, cb):
    return lax.dot_general(a, b, (((ca,), (cb,)), ((), ())), preferred_element_type=F32)


def remote(src, dst, send, recv, where):
    return pltpu.make_async_remote_copy(
        src_ref=src, dst_ref=dst, send_sem=send, recv_sem=recv, device_id=where, device_id_type=MESH
    )


def here():
    return lax.axis_index("shard"), lax.axis_index("ctx"), lax.axis_index("tp")


class Riders:
    def __init__(self, S, C, riders):
        self.S, self.C = S, C
        self.axes = [axis for axis, _ in riders]
        self.arrays = [x for _, x in riders]
        self.shapes = [
            jax.ShapeDtypeStruct((C,) + x.shape if axis == "all" else x.shape, x.dtype) for axis, x in riders
        ]
        count, most = len(riders), max(S, C) - 1
        self.scratch = [DMA((count, most)), DMA((count, most)), DMA((count,))] if count else []

    def bind(self, ins, outs, sems):
        self.ins, self.outs, self.sems = ins, outs, sems

    def start(self):
        p, z, c = here()
        self.moves = []
        for n, axis in enumerate(self.axes):
            src, dst = self.ins[n], self.outs[n]
            send, recv, own = self.sems
            if axis == "tp":
                copies = [remote(src, dst, send.at[n, 0], recv.at[n, 0], {"tp": 1 - c})]
            elif axis == "all":
                copies = [
                    remote(src, dst.at[z], send.at[n, k - 1], recv.at[n, k - 1], {"ctx": (z + k) % self.C})
                    for k in range(1, self.C)
                ]
                copies.append(pltpu.make_async_copy(src, dst.at[z], own.at[n]))
            else:
                size, me = (self.S, p) if axis == "shard" else (self.C, z)
                copies = [
                    remote(src.at[(me + k) % size], dst.at[me], send.at[n, k - 1], recv.at[n, k - 1], {axis: (me + k) % size})
                    for k in range(1, size)
                ]
                copies.append(pltpu.make_async_copy(src.at[me], dst.at[me], own.at[n]))
            for copy in copies:
                copy.start()
            self.moves += copies

    def wait(self):
        for copy in self.moves:
            copy.wait()


def greet(S, C, mates=(), line=False, other=False, axes=()):
    p, z, c = here()
    peers = [{"shard": q} for q in ([(p + k) % S for k in range(1, S)] if "shard" in axes else mates)]
    if line or "ctx" in axes or "all" in axes:
        peers += [{"ctx": (z + k) % C} for k in range(1, C)]
    if other or "tp" in axes:
        peers.append({"tp": 1 - c})
    barrier = pltpu.get_barrier_semaphore()
    for where in peers:
        pl.semaphore_signal(barrier, inc=1, device_id=where, device_id_type=MESH)
    pl.semaphore_wait(barrier, len(peers))


def comm(kernel, S, C, number, name, args, in_specs, outs, scratch, riders=()):
    ride = Riders(S, C, riders)
    na, nr, no, ns = len(args), len(ride.axes), len(outs), len(scratch)

    def body(*refs):
        ins, refs = refs[:na], refs[na:]
        rins, refs = refs[:nr], refs[nr:]
        os, refs = refs[:no], refs[no:]
        routs, refs = refs[:nr], refs[nr:]
        ride.bind(rins, routs, refs[ns:])
        kernel(ride, ins, os, refs[:ns])

    return pl.pallas_call(
        body,
        out_shape=[shape for shape, _ in outs] + ride.shapes,
        in_specs=list(in_specs) + [IN_VMEM] * nr,
        out_specs=[spec for _, spec in outs] + [ANY] * nr,
        scratch_shapes=list(scratch) + ride.scratch,
        compiler_params=pltpu.CompilerParams(
            collective_id=number, has_side_effects=True, vmem_limit_bytes=62 << 20
        ),
        cost_estimate=pl.CostEstimate(flops=0, bytes_accessed=120_000_000, transcendentals=0),
        name=name,
    )(*args, *ride.arrays)


def exchange(S, C, T, number, riders, tiles, rows=None):
    def kernel(ride, ins, outs, scratch):
        tile, got = ins[0], outs[0]
        send, recv, bsend, brecv, own = scratch[:5]
        p, z, c = here()
        everyone = [(i, j) for i in range(C) for j in range(S) if i or j]
        barrier = pltpu.get_barrier_semaphore()
        peers = [{"shard": (p + j) % S, "ctx": (z + i) % C} for i, j in everyone] + [{"tp": 1 - c}]
        for where in peers:
            pl.semaphore_signal(barrier, inc=1, device_id=where, device_id_type=MESH)
        pl.semaphore_wait(barrier, len(peers))

        def turn_over(source, target, k, axis, size, me):
            ssem, rsem, local = scratch[5:]
            hop = [pltpu.make_async_copy(source.at[me], target.at[me], local.at[k])]
            for j in range(1, size):
                q = (me + j) % size
                hop.append(remote(source.at[q], target.at[me], ssem.at[k, j - 1], rsem.at[k, j - 1], {axis: q}))
            for copy in hop:
                copy.start()
            return hop

        if rows is not None:
            first = turn_over(ins[1], outs[1], 0, "shard", S, p)
        local = pltpu.make_async_copy(tile.at[z, p], got.at[c, z, p], own)
        local.start()
        copies = []
        for at, (where, (i, j)) in enumerate(zip(peers, everyone)):
            q, g = (p + j) % S, (z + i) % C
            copies.append(remote(tile.at[g, q], got.at[c, z, p], send.at[at], recv.at[at], where))
            copies[-1].start()
        ride.start()
        if rows is not None:
            for copy in first:
                copy.wait()
            second = turn_over(outs[1], outs[2], 1, "ctx", C, z)
        local.wait()
        for copy in copies:
            copy.wait()
        back = remote(got.at[c], got.at[c], bsend, brecv, {"tp": 1 - c})
        back.start()
        back.wait_send()
        remote(got.at[1 - c], got.at[1 - c], bsend, brecv, {"tp": 1 - c}).wait_recv()
        if rows is not None:
            for copy in second:
                copy.wait()
        ride.wait()

    count, most = C * S - 1, max(S, C) - 1
    args, outs = [tiles], [(jax.ShapeDtypeStruct((T,) + tiles.shape, tiles.dtype), ANY)]
    scratch = [DMA((count,)), DMA((count,)), DMA, DMA, DMA]
    if rows is not None:
        args.append(rows)
        outs += [(jax.ShapeDtypeStruct(rows.shape, rows.dtype), IN_VMEM)] * 2
        scratch += [DMA((2, most)), DMA((2, most)), DMA((2,))]
    return comm(kernel, S, C, number, "exchange", args, [IN_VMEM] * len(args), outs, scratch, riders)


def plane(S):
    p, _, c = here()
    B = S // 2
    a, b = p // B, p % B
    return a, b, [a * B + (b + j) % B for j in range(1, B)], (1 - a) * B + b


def spread_sems(S):
    count = 4 + 4 * (S // 2 - 1)
    return [DMA((2 * count,)), DMA((2 * count,))]


def spread(S, own, region, send, recv, work=(None, None)):
    p, _, c = here()
    B = S // 2
    a, b, rows, col = plane(S)
    rows, col, other = [{"shard": q} for q in rows], {"shard": col}, {"tp": 1 - c}
    per = 4 + 4 * (B - 1)
    OWN, ROW, COL, VIA_COL, VIA_ROW = 0, 2, 2 + 2 * (B - 1), 4 + 2 * (B - 1), 4 + 3 * (B - 1)
    started = []

    def push(q, h, sem, where, first=False):
        view = region(q, h, c)
        copy = remote(own(h) if first else view, view, send.at[sem], recv.at[sem], where)
        copy.start()
        started.append(copy)

    def came(q, h, sem, core):
        view = region(q, h, core)
        remote(view, view, send.at[sem], recv.at[sem], other).wait_recv()

    for h in range(2):
        for j in range(1, B):
            push(p, h, ROW + 2 * (j - 1) + h, rows[j - 1], True)
    for h in (1, 0):
        push(p, h, COL + h, col, True)
    for h in range(2):
        push(p, h, per + OWN + h, other, True)

    def from_row(j, h):
        q = a * B + (b - j) % B
        came(q, h, ROW + 2 * (j - 1) + h, c)
        push(q, h, per + ROW + 2 * (j - 1) + h, other)
        return q

    def from_col(h):
        q = (1 - a) * B + b
        came(q, h, COL + h, c)
        push(q, h, per + COL + h, other)
        return q

    if work[0] is not None:
        work[0]()
    for j in range(1, B):
        q = from_row(j, 0)
        push(q, 0, VIA_COL + j - 1, col)
    q = from_col(1)
    for j in range(1, B):
        push(q, 1, VIA_ROW + j - 1, rows[j - 1])
    if work[1] is not None:
        work[1]()
    for j in range(1, B):
        from_row(j, 1)
    from_col(0)
    for j in range(1, B):
        q = (1 - a) * B + (b - j) % B
        came(q, 0, VIA_COL + j - 1, c)
        push(q, 0, per + VIA_COL + j - 1, other)
        came(q, 1, VIA_ROW + j - 1, c)
        push(q, 1, per + VIA_ROW + j - 1, other)
    for h in range(2):
        came(p, h, per + OWN + h, 1 - c)
        came((1 - a) * B + b, h, per + COL + h, 1 - c)
    for j in range(1, B):
        for h in range(2):
            came(a * B + (b - j) % B, h, per + ROW + 2 * (j - 1) + h, 1 - c)
        q = (1 - a) * B + (b - j) % B
        came(q, 0, per + VIA_COL + j - 1, 1 - c)
        came(q, 1, per + VIA_ROW + j - 1, 1 - c)
    for copy in started:
        copy.wait_send()


def gather_columns(S, C, T, number, x, riders=(), extra=None):
    _, n, wide = x.shape
    more, more_specs, more_outs, more_scratch, task = extra or ((), (), (), (), None)

    def kernel(ride, ins, outs, scratch):
        x_ref, out_ref = ins[0], outs[0]
        send, recv, own = scratch[:3]
        p, _, c = here()
        _, _, rows, col = plane(S)

        def region(q, h, core):
            part = pl.ds(pl.multiple_of(q * wide, 128), wide)
            return out_ref.at[pl.ds(h * (C // 2), C // 2), core, :, part]

        local = [
            pltpu.make_async_copy(x_ref.at[pl.ds(h * (C // 2), C // 2)], region(p, h, c), own.at[h]) for h in range(2)
        ]
        for copy in local:
            copy.start()
        if task is not None:
            task(ins[1:], outs[1:], scratch[3:], None)
        greet(S, C, rows + [col], other=True, axes=ride.axes)
        ride.start()
        work = [None, None]
        if task is not None:
            work = [functools.partial(task, ins[1:], outs[1:], scratch[3:], piece) for piece in range(2)]
        spread(S, lambda h: x_ref.at[pl.ds(h * (C // 2), C // 2)], region, send, recv, work)
        for copy in local:
            copy.wait()
        ride.wait()

    out, *rest = comm(
        kernel, S, C, number, "gather_columns", [x, *more], [IN_VMEM, *more_specs],
        [(jax.ShapeDtypeStruct((C, T, n, wide * S), x.dtype), ANY), *more_outs],
        spread_sems(S) + [DMA((2,)), *more_scratch], riders,
    )
    return [out.reshape(C * T * n, wide * S)] + rest


CHUNK = 512
ROWS = 32


def sum_scratch(S, n, D):
    half, B = n // 2, S // 2

    def vm(*shape):
        return pltpu.VMEM(shape, BF)

    return [
        vm(S, n, D), vm(S, n, D), vm(S, n, D), vm(B - 1, 2, half, D), vm(B, half, D),
        vm(B - 1, half, D), vm(half, D), vm(half, D), vm(B - 1, half, D),
        DMA((S,)), DMA((S,)), DMA((B - 1, 2)), DMA((B - 1, 2)), DMA((B,)), DMA((B,)), DMA((B,)), DMA((B,)),
    ]


def sum_over_plane(S, T, x_ref, w_ref, out_ref, scratch, meanwhile=None):
    away, sib, mine, row1, col1, row2, col2, to_col, to_row = scratch[:9]
    asend, arecv, rsend, rrecv, csend, crecv, fsend, frecv = scratch[9:]
    n, D = out_ref.shape
    half, B = n // 2, S // 2
    _, _, c = here()
    a, b, rows, col = plane(S)
    rows, col, other = [{"shard": q} for q in rows], {"shard": col}, {"tp": 1 - c}

    def chip(e):
        return ((a + e // B) % 2) * B + (b + e % B) % B

    def product(e, core, store):
        x = x_ref[chip(e) * T + core]

        def column(j, _):
            w = pl.ds(pl.multiple_of(j * CHUNK, CHUNK), CHUNK)
            store(w, mm(x, w_ref[w, :], 1, 1))
            return 0

        lax.fori_loop(0, D // CHUNK, column, 0)

    def to_other(e):
        return remote(away.at[e], sib.at[e], asend.at[e], arecv.at[e], other)

    def for_other(e):
        def store(w, value):
            away[e, :, w] = value.astype(BF)

        product(e, 1 - c, store)
        to_other(e).start()

    for_other(S - 1)
    top, low = pl.ds(0, half), pl.ds(half, half)
    started = []

    def push(src, dst, send, recv, where):
        copy = remote(src, dst, send, recv, where)
        copy.start()
        started.append(copy)

    for e in range(S - 1, -1, -1):
        if e:
            for_other(e - 1)
        to_other(e).wait()

        def store(w, value):
            value = value + sib[e, :, w].astype(F32)
            if e:
                mine[e, :, w] = value.astype(BF)
            else:
                out_ref[:, w] = value

        product(e, c, store)
        j = e % B
        if e > B:
            push(mine.at[e, top], row1.at[j - 1, 1], rsend.at[j - 1, 1], rrecv.at[j - 1, 1], rows[j - 1])
            push(mine.at[e, low], col1.at[j], csend.at[j], crecv.at[j], col)
        elif e == B:
            push(mine.at[e, low], col1.at[0], csend.at[0], crecv.at[0], col)
        elif e:
            push(mine.at[e, top], row1.at[j - 1, 0], rsend.at[j - 1, 0], rrecv.at[j - 1, 0], rows[j - 1])

    def came(ref, send, recv):
        remote(ref, ref, send, recv, other).wait_recv()

    if meanwhile is not None:
        meanwhile(0)
    total = mine[B, top, :].astype(F32)
    for j in range(1, B):
        came(row1.at[j - 1, 1], rsend.at[j - 1, 1], rrecv.at[j - 1, 1])
        total = total + row1[j - 1, 1].astype(F32)
    to_col[...] = total.astype(BF)
    push(to_col, col2, fsend.at[0], frecv.at[0], col)
    for j in range(1, B):
        came(col1.at[j], csend.at[j], crecv.at[j])
        to_row[j - 1] = (mine[j, low, :].astype(F32) + col1[j].astype(F32)).astype(BF)
        push(to_row.at[j - 1], row2.at[j - 1], fsend.at[j], frecv.at[j], rows[j - 1])
    if meanwhile is not None:
        meanwhile(1)
    came(col1.at[0], csend.at[0], crecv.at[0])
    upper, lower = out_ref[top, :], out_ref[low, :] + col1[0].astype(F32)
    for j in range(1, B):
        came(row1.at[j - 1, 0], rsend.at[j - 1, 0], rrecv.at[j - 1, 0])
        upper = upper + row1[j - 1, 0].astype(F32)
    came(col2, fsend.at[0], frecv.at[0])
    out_ref[top, :] = upper + col2[...].astype(F32)
    for j in range(1, B):
        came(row2.at[j - 1], fsend.at[j], frecv.at[j])
        lower = lower + row2[j - 1].astype(F32)
    out_ref[low, :] = lower
    for copy in started:
        copy.wait_send()


def project(S, C, T, number, tok, raw, gain, shift, bias):
    L, D = tok.shape
    _, parts, nb, wide = raw.shape
    hn = wide // S
    most = S - 1

    def kernel(ride, ins, outs, scratch):
        tok_ref, raw_ref, gain_ref, shift_ref, bias_ref = ins
        n_ref, out_ref, w_ref = outs
        send, recv, own = scratch
        p, _, _ = here()
        mates = [(p + k) % S for k in range(1, S)]
        greet(S, C, mates)

        def lanes(q):
            return pl.ds(pl.multiple_of(q * hn, 128), hn)

        copies = []
        for part in range(parts):
            dst = w_ref.at[:, p, :, pl.ds(part * hn, hn)]
            for k, q in enumerate(mates):
                copies.append(
                    remote(raw_ref.at[:, part, :, lanes(q)], dst, send.at[k, part], recv.at[k, part], {"shard": q})
                )
            copies.append(pltpu.make_async_copy(raw_ref.at[:, part, :, lanes(p)], dst, own.at[part]))
        for copy in copies:
            copy.start()

        def normed(r):
            n_ref[r, :] = (norm_of(tok_ref[r, :].astype(F32))[0] * gain_ref[...] + shift_ref[...]).astype(BF)

        row_blocks(L, normed)
        for copy in copies:
            copy.wait()
        w = w_ref[...].reshape(D, parts * hn)

        @pl.loop(0, L // BLK)
        def _(i):
            r = pl.ds(pl.multiple_of(i * BLK, BLK), BLK)
            out_ref[r, :] = mm(n_ref[r, :], w, 1, 0) + bias_ref[...]

    n, out, w = comm(
        kernel, S, C, number, "project", [tok, raw, gain, shift, bias], [IN_VMEM] * 5,
        [
            (jax.ShapeDtypeStruct((L, D), BF), IN_VMEM), (jax.ShapeDtypeStruct((L, parts * hn), F32), IN_VMEM),
            (jax.ShapeDtypeStruct((C, S, nb, parts * hn), BF), IN_VMEM),
        ],
        [DMA((most, parts)), DMA((most, parts)), DMA((parts,))],
    )
    return n, out, w.reshape(D, parts * hn)


def gates_back_kernel(gb_ref, wd_ref, gu_ref, dgu_ref):
    dact = mm(gb_ref[...], wd_ref[...], 1, 0)
    both, width = gu_ref[...], dact.shape[1]
    gate, up = both[:, :width], both[:, width:]
    s = jax.nn.sigmoid(gate)
    dgate = dact * up * s * (1.0 + gate * (1.0 - s))
    dgu_ref[...] = jnp.concatenate((dgate, dact * gate * s), axis=1).astype(BF)


def gates_work(ins, outs, scratch, piece):
    gu_ref, act_ref = outs
    n2_ref, wg_ref, sems = scratch
    if piece != 1:
        for i, (x, y) in enumerate(zip(ins, (n2_ref, wg_ref))):
            copy = pltpu.make_async_copy(x, y, sems.at[i])
            copy.wait() if piece == 0 else copy.start()
    if piece is None:
        return
    (rows, width), half = act_ref.shape, act_ref.shape[0] // BLK // 2

    @pl.loop(piece * half, piece * half + half)
    def _(i):
        r = pl.ds(pl.multiple_of(i * BLK, BLK), BLK)
        both = mm(n2_ref[r, :], wg_ref[...], 1, 0)
        gu_ref[r, :] = both
        gate, up = both[:, :width], both[:, width:]
        act_ref[r, :] = (gate * jax.nn.sigmoid(gate) * up).astype(BF)


def gates(S, C, T, number, n2, wg, x):
    L, width = n2.shape[0], wg.shape[1] // 2
    outs = [jax.ShapeDtypeStruct((L, 2 * width), F32), jax.ShapeDtypeStruct((L, width), BF)]
    return gather_columns(
        S, C, T, number, x, (),
        ([n2, wg], [ANY, ANY], [(shape, IN_VMEM) for shape in outs],
         [pltpu.VMEM(n2.shape, BF), pltpu.VMEM(wg.shape, BF), DMA((2,))], gates_work),
    )


def by_rows(kernel, name, arrays, outs):
    L = outs[0].shape[0]

    def spec(width):
        return pl.BlockSpec((BLK, width), lambda i: (i, 0))

    return pl.pallas_call(
        kernel,
        grid=(L // BLK,),
        in_specs=[spec(x.shape[1]) if rows else pl.BlockSpec(x.shape, lambda i: (0, 0)) for rows, x in arrays],
        out_specs=[spec(x.shape[1]) for x in outs],
        out_shape=outs,
        compiler_params=pltpu.CompilerParams(vmem_limit_bytes=62 << 20),
        name=name,
    )(*[x for _, x in arrays])


def row_blocks(n, work):
    @pl.loop(0, n // ROWS)
    def _(i):
        work(pl.ds(pl.multiple_of(i * ROWS, ROWS), ROWS))


def own_rows(T, x_ref, row_ref, sem):
    p, _, c = here()
    copy = pltpu.make_async_copy(x_ref.at[p * T + c], row_ref, sem)
    copy.start()
    return copy


def norm_of(v):
    center = v - jnp.mean(v, axis=-1, keepdims=True)
    inverse = lax.rsqrt(jnp.mean(center * center, axis=-1, keepdims=True) + EPS)
    return center * inverse, inverse


def norm_back(v, g, gain, stats_ref):
    normal, inverse = norm_of(v)
    e = g * gain
    stats_ref[0:1, :] += jnp.sum(g * normal, axis=0, keepdims=True)
    stats_ref[1:2, :] += jnp.sum(g, axis=0, keepdims=True)
    return inverse * (
        e - jnp.mean(e, axis=-1, keepdims=True) - normal * jnp.mean(e * normal, axis=-1, keepdims=True)
    )


def spread_rows(S, T, src, out_ref, send, recv, own):
    p, _, c = here()
    half = src.shape[0] // 2
    local = pltpu.make_async_copy(src, out_ref.at[p * T + c], own)
    local.start()
    spread(
        S,
        lambda h: src.at[pl.ds(h * half, half)],
        lambda q, h, core: out_ref.at[q * T + core, pl.ds(h * half, half)],
        send,
        recv,
    )
    local.wait()


def sum_norm_gather(S, C, T, number, x, w, residual, gain, shift, riders=()):
    L, K = x.shape
    D, n = w.shape[0], L // (S * T)

    def kernel(ride, ins, outs, scratch):
        x_ref, w_ref, all_ref, gain_ref, shift_ref = ins
        v_ref, out_ref = outs
        acc, low, send, recv, own, res_ref, sem = scratch[:7]
        _, _, rows, col = plane(S)
        rest = own_rows(T, all_ref, res_ref, sem)
        greet(S, C, rows + [col], other=True, axes=ride.axes)
        ride.start()
        sum_over_plane(S, T, x_ref, w_ref, acc, scratch[7:])
        rest.wait()

        def work(r):
            v = res_ref[r, :].astype(F32) + acc[r, :]
            v_ref[r, :] = v
            low[r, :] = (norm_of(v)[0] * gain_ref[...] + shift_ref[...]).astype(BF)

        row_blocks(n, work)
        spread_rows(S, T, low, out_ref, send, recv, own)
        ride.wait()

    v, out, *rest = comm(
        kernel, S, C, number, "sum_norm_gather", [x.reshape(S * T, n, K), w, residual.reshape(S * T, n, D), gain, shift],
        [IN_VMEM, IN_VMEM, ANY, IN_VMEM, IN_VMEM],
        [(jax.ShapeDtypeStruct((n, D), F32), IN_VMEM), (jax.ShapeDtypeStruct((S * T, n, D), BF), ANY)],
        [pltpu.VMEM((n, D), F32), pltpu.VMEM((n, D), BF)] + spread_sems(S)
        + [DMA, pltpu.VMEM((n, D), BF), DMA] + sum_scratch(S, n, D),
        riders,
    )
    return [v, out.reshape(L, D)] + rest


def sum_back_gather(S, C, T, number, x, w, v, residual, gain, riders=()):
    L, K = x.shape
    D, n = w.shape[0], L // (S * T)

    def kernel(ride, ins, outs, scratch):
        x_ref, w_ref, in_ref, all_ref, gain_ref = ins
        v_ref, out_ref, stats = outs
        acc, low, send, recv, own, res_ref, sem = scratch[:7]
        _, _, rows, col = plane(S)
        rest = own_rows(T, all_ref, res_ref, sem)
        greet(S, C, rows + [col], other=True, axes=ride.axes)
        ride.start()
        sum_over_plane(S, T, x_ref, w_ref, acc, scratch[7:])
        rest.wait()
        stats[...] = jnp.zeros_like(stats)

        def work(r):
            g = res_ref[r, :].astype(F32) + norm_back(in_ref[r, :], acc[r, :], gain_ref[...], stats)
            v_ref[r, :] = g
            low[r, :] = g.astype(BF)

        row_blocks(n, work)
        spread_rows(S, T, low, out_ref, send, recv, own)
        ride.wait()

    g, out, stats, *rest = comm(
        kernel, S, C, number, "sum_back_gather", [x.reshape(S * T, n, K), w, v, residual.reshape(S * T, n, D), gain],
        [IN_VMEM, IN_VMEM, IN_VMEM, ANY, IN_VMEM],
        [
            (jax.ShapeDtypeStruct((n, D), F32), IN_VMEM), (jax.ShapeDtypeStruct((S * T, n, D), BF), ANY),
            (jax.ShapeDtypeStruct((2, D), F32), IN_VMEM),
        ],
        [pltpu.VMEM((n, D), F32), pltpu.VMEM((n, D), BF)] + spread_sems(S)
        + [DMA, pltpu.VMEM((n, D), BF), DMA] + sum_scratch(S, n, D),
        riders,
    )
    return [g, out.reshape(L, D), stats] + rest


def sum_back(S, C, T, number, x, w, v, residual, gain, riders=()):
    L, K = x.shape
    D, n = w.shape[0], L // (S * T)

    def kernel(ride, ins, outs, scratch):
        x_ref, w_ref, all_ref, res_ref, gain_ref = ins
        low, stats = outs
        acc, in_ref, sem = scratch[:3]
        _, _, rows, col = plane(S)
        rest = own_rows(T, all_ref, in_ref, sem)
        greet(S, C, rows + [col], other=True, axes=ride.axes)
        ride.start()
        sum_over_plane(S, T, x_ref, w_ref, acc, scratch[3:])
        rest.wait()
        stats[...] = jnp.zeros_like(stats)

        def work(r):
            g = res_ref[r, :] + norm_back(in_ref[r, :].astype(F32), acc[r, :], gain_ref[...], stats)
            low[r, :] = g.astype(BF)

        row_blocks(n, work)
        ride.wait()

    return comm(
        kernel, S, C, number, "sum_back", [x.reshape(S * T, n, K), w, v.reshape(S * T, n, D), residual, gain],
        [IN_VMEM, IN_VMEM, ANY, IN_VMEM, IN_VMEM],
        [(jax.ShapeDtypeStruct((n, D), BF), IN_VMEM), (jax.ShapeDtypeStruct((2, D), F32), IN_VMEM)],
        [pltpu.VMEM((n, D), F32), pltpu.VMEM((n, D), BF), DMA] + sum_scratch(S, n, D),
        riders,
    )


def finish(S, C, T, number, x, y, stats, bias, gateup, down, qkv, out):
    n, D = x.shape
    fn, hn = down.shape[2], out.shape[2]
    wide, lines = D // S, bias.shape[1] // 128
    nb = D // (S * C)
    count = sum(z.shape[0] for z in stats)
    tall = -(-(count + lines) // 8) * 8
    many = C * S - 1
    pieces = S if ordered(D, S, C) else 1

    def kernel(ride, ins, outs, scratch):
        x_ref, y_ref, stat_refs, bias_ref = ins[0], ins[1], ins[2:-5], ins[-5]
        gateup_ref, down_ref, qkv_ref, o_ref = ins[-4:]
        x_out, y_out, norm_out, bias_out, gateup_out, down_out, qkv_out, o_out = outs
        xbuf, xbuf2, ybuf2, tile, send, recv, own, psend, precv, pown, lsend, lrecv, tsend, trecv = scratch[:14]
        qkv_buf, o_buf, gsend, grecv, gown, got = scratch[14:]
        p, z, c = here()
        other = {"tp": 1 - c}
        everyone = [(i, j) for i in range(C) for j in range(S) if i or j]
        peers = [{"shard": (p + j) % S, "ctx": (z + i) % C} for i, j in everyone]
        barrier = pltpu.get_barrier_semaphore()
        for where in peers + [other]:
            pl.semaphore_signal(barrier, inc=1, device_id=where, device_id_type=MESH)
        pl.semaphore_wait(barrier, len(peers) + 1)

        def part(q):
            return pl.ds(pl.multiple_of(q * wide, 128), wide)

        def turn_over(source, target, at, size, me, axis):
            hop = [pltpu.make_async_copy(source(me), target, own.at[at])]
            for k in range(1, size):
                q = (me + k) % size
                hop.append(remote(source(q), target, send.at[at, k - 1], recv.at[at, k - 1], {axis: q}))
            for copy in hop:
                copy.start()
            return hop

        def arrive(buf, out, at):
            hop = []
            for i in range(pieces):
                src = pl.ds(i * (wide // pieces), wide // pieces)
                first = (i * C + p) * nb if pieces > 1 else p * wide
                dst = out.at[c, :, pl.ds(pl.multiple_of(first, 128), wide // pieces)]
                hop.append(pltpu.make_async_copy(buf.at[p, :, src], dst, pown.at[at, i]))
                for k in range(1, S):
                    q = (p + k) % S
                    hop.append(
                        remote(buf.at[q, :, src], dst, psend.at[at, k - 1, i], precv.at[at, k - 1, i], {"shard": q})
                    )
            for copy in hop:
                copy.start()
            return hop

        def both(ref, at):
            copy = remote(ref.at[c], ref.at[c], lsend.at[at], lrecv.at[at], other)
            copy.start()
            return copy

        def settle(ref, at, copy):
            copy.wait_send()
            remote(ref.at[1 - c], ref.at[1 - c], lsend.at[at], lrecv.at[at], other).wait_recv()

        x_hop = turn_over(lambda q: x_ref.at[:, part(q)], xbuf.at[p], 0, S, p, "shard")
        y_hop = turn_over(lambda q: y_ref.at[q], ybuf2.at[z], 1, C, z, "ctx")
        moves = []
        for i, (src, dst) in enumerate(((qkv_ref, qkv_buf), (o_ref, o_buf))):
            moves.append(pltpu.make_async_copy(src.at[p], dst.at[p], gown.at[i]))
            for k in range(1, S):
                q = (p + k) % S
                moves.append(remote(src.at[q], dst.at[p], gsend.at[i, k - 1], grecv.at[i, k - 1], {"shard": q}))
        for copy in moves:
            copy.start()
        tile[...] = jnp.zeros_like(tile)
        at = count
        for i, ref in enumerate(stat_refs):
            for j in range(2):
                tile[j * len(stat_refs) + i : j * len(stat_refs) + i + 1, :] = ref[j : j + 1, :]
        for k in range(lines):
            for block in range(D // 128):
                tile[at + k : at + k + 1, pl.ds(block * 128, 128)] = bias_ref[:, pl.ds(k * 128, 128)]

        def columns(g, q):
            return tile.at[:, pl.ds(pl.multiple_of((g * S + q) * nb // 128 * 128, 128), 128)]

        small = [pltpu.make_async_copy(columns(z, p), got.at[c, z, p], own.at[3])]
        for k, (where, (i, j)) in enumerate(zip(peers, everyone)):
            small.append(
                remote(columns((z + i) % C, (p + j) % S), got.at[c, z, p], tsend.at[k], trecv.at[k], where)
            )
        for copy in small:
            copy.start()
        for copy in x_hop:
            copy.wait()
        x_hop = turn_over(lambda q: xbuf.at[q], xbuf2.at[z], 2, C, z, "ctx")
        for q in range(S):
            down_out[q * fn : (q + 1) * fn, :] = down_ref[q].astype(F32).T
        for copy in y_hop:
            copy.wait()
        y_hop = arrive(ybuf2, y_out, 0)
        for copy in small:
            copy.wait()
        small_last = both(got, 0)
        bias_out[...] = jnp.sum(got[c, :, :, count : count + lines, :], axis=0)
        for i in range(2):
            for q in range(S):
                gateup_out[:, i, q * fn : (q + 1) * fn] = gateup_ref[q, :, i * fn : (i + 1) * fn].astype(F32)
        for copy in x_hop:
            copy.wait()
        x_hop = arrive(xbuf2, x_out, 1)
        for copy in y_hop:
            copy.wait()
        y_last = both(y_out, 1)
        for copy in moves:
            copy.wait()
        for q in range(S):
            o_out[q * hn : (q + 1) * hn, :] = o_buf[q].astype(F32).T
            for i in range(3):
                qkv_out[i, :, q * hn : (q + 1) * hn] = qkv_buf[q, :, i * hn : (i + 1) * hn].astype(F32)
        for copy in x_hop:
            copy.wait()
        x_last = both(x_out, 2)
        settle(got, 0, small_last)
        norm_out[...] = jnp.sum(got[:, :, :, :count, :], axis=(0, 1, 2))
        settle(y_out, 1, y_last)
        settle(x_out, 2, x_last)

    args = [x, y, *stats, bias, gateup, down, qkv, out]
    most = max(S, C) - 1
    home = (jax.ShapeDtypeStruct((T, n, D), BF), ANY)
    x, y, *rest = comm(
        kernel, S, C, number, "finish", args, [IN_VMEM] * len(args),
        [home, home]
        + [
            (jax.ShapeDtypeStruct(shape, F32), IN_VMEM)
            for shape in ((count, 128), (S, lines, 128), (nb, 2, S * fn), (S * fn, nb), (3, nb, S * hn), (S * hn, nb))
        ],
        [
            pltpu.VMEM((S, n, wide), BF), pltpu.VMEM((C, n, wide), BF), pltpu.VMEM((C, n, wide), BF),
            pltpu.VMEM((tall, D), F32), DMA((3, most)), DMA((3, most)), DMA((4,)),
            DMA((2, S - 1, pieces)), DMA((2, S - 1, pieces)), DMA((2, pieces)), DMA((3,)), DMA((3,)),
            DMA((many,)), DMA((many,)),
            pltpu.VMEM(qkv.shape, BF), pltpu.VMEM(out.shape, BF), DMA((2, S - 1)), DMA((2, S - 1)), DMA((2,)),
            pltpu.VMEM((T, C, S, tall, 128), F32),
        ],
    )
    return [x.reshape(T * n, D), y.reshape(T * n, D)] + rest


def ordered(D, S, C):
    return D // (S * C) % 128 == 0


def turn_tables(rows):
    feature = np.arange(128) % HEAD
    freq = np.where(feature < ROT, BASE ** (-2.0 * (feature % (ROT // 2)) / ROT), 0.0)
    near = np.arange(BLK)[:, None] * freq
    far = np.arange(0, rows, BLK)[:, None] * freq
    return [jnp.asarray(f(x), F32) for x in (near, far) for f in (np.cos, np.sin)]


def turn(x, i, tables, sign):
    cos, sin, cos_far, sin_far = tables
    far_cos, far_sin = cos_far[pl.ds(i, 1), :], sin_far[pl.ds(i, 1), :]
    cos_t = cos[...] * far_cos - sin[...] * far_sin
    sin_t = sin[...] * far_cos + cos[...] * far_sin
    ahead = lax.broadcasted_iota(jnp.int32, x.shape, 1) % HEAD < ROT // 2
    partner = jnp.where(ahead, -pltpu.roll(x, 128 - ROT // 2, 1), pltpu.roll(x, ROT // 2, 1))
    return x * cos_t + partner * (sin_t * sign)


def two_heads(x, left):
    zero = jnp.zeros_like(x)
    return [jnp.where(left, x, zero), jnp.where(left, zero, x)]


def block_of(rows):
    return next(size for size in (512, 256) if rows % size == 0)


def attend_kernel(
    first_ref, qkv_ref, cos_ref, sin_ref, cosf_ref, sinf_ref, begin_ref,
    qo_ref, ko_ref, vo_ref, o_ref, lse_ref, vt_ref,
):
    rows, wide = qo_ref.shape
    pairs, size = wide // 128, block_of(rows)
    tables = (cos_ref, sin_ref, cosf_ref, sinf_ref)
    left = lax.broadcasted_iota(jnp.int32, (size, 128), 1) < HEAD
    key_at = lax.broadcasted_iota(jnp.int32, (size, size), 0)
    query_at = lax.broadcasted_iota(jnp.int32, (1, size), 1)

    @pl.loop(0, rows // BLK)
    def _(i):
        r = pl.ds(pl.multiple_of(i * BLK, BLK), BLK)
        for t in range(pairs):
            w = pl.ds(t * 128, 128)
            q, k, v = (qkv_ref[r, pl.ds(part * wide + t * 128, 128)] for part in range(3))
            qo_ref[r, w] = turn(q, i, tables, 1.0).astype(BF) * jnp.asarray(HEAD**-0.5, BF)
            ko_ref[r, w] = turn(k, i, tables, 1.0).astype(BF)
            vo_ref[r, w] = v.astype(BF)
            vt_ref[w, r] = v.T.astype(BF)

    @pl.loop(0, rows // size)
    def _(i):
        r = pl.ds(pl.multiple_of(i * size, size), size)
        qs = sum((two_heads(qo_ref[r, pl.ds(t * 128, 128)], left) for t in range(pairs)), [])
        begin = begin_ref[0:1, r]
        here = query_at + i * size

        def step(j, carry):
            w = pl.ds(pl.multiple_of(j * size, size), size)
            key = key_at + j * size
            seen = (key <= here) & (key >= begin)
            out = []
            for h in range(2 * pairs):
                m, l, acc = carry[h]
                s = jnp.where(seen, mm(ko_ref[w, pl.ds(h // 2 * 128, 128)], qs[h], 1, 1), NEG)
                top = jnp.maximum(m, jnp.max(s, axis=0, keepdims=True))
                fade = jnp.exp(m - top)
                e = jnp.exp(s - top)
                acc = acc * fade + mm(vt_ref[pl.ds(h * HEAD, HEAD), w], e.astype(BF), 1, 0)
                out.append((top, l * fade + jnp.sum(e, axis=0, keepdims=True), acc))
            return tuple(out)

        start = (
            jnp.full((1, size), NEG, F32), jnp.zeros((1, size), F32), jnp.zeros((HEAD, size), F32)
        )
        done = lax.fori_loop(first_ref[i], i + 1, step, (start,) * (2 * pairs))
        for t in range(pairs):
            both = []
            for h in (2 * t, 2 * t + 1):
                m, l, acc = done[h]
                both.append(acc / l)
                lse_ref[h : h + 1, r] = m + jnp.log(l)
            o_ref[r, pl.ds(t * 128, 128)] = jnp.concatenate(both, axis=0).T.astype(BF)


def attend(qkv, begin):
    rows, wide = qkv.shape[0], qkv.shape[1] // 3
    size = block_of(rows)
    half = jax.ShapeDtypeStruct((rows, wide), BF)
    return pl.pallas_call(
        attend_kernel,
        in_specs=[pl.BlockSpec(memory_space=pltpu.SMEM)] + [IN_VMEM] * 6,
        out_specs=[IN_VMEM] * 5,
        out_shape=[half] * 4 + [jax.ShapeDtypeStruct((wide // HEAD, rows), F32)],
        scratch_shapes=[pltpu.VMEM((wide, rows), BF)],
        compiler_params=pltpu.CompilerParams(vmem_limit_bytes=62 << 20),
        name="attend",
    )(begin[0, ::size] // size, qkv, *turn_tables(rows), begin)


def attend_back_work(ins, out_ref, bias_ref, scratch, piece):
    q_ref, k_ref, v_ref, o_ref, do_ref, lse_ref, cos_ref, sin_ref, cosf_ref, sinf_ref, begin_ref = ins
    kt_ref, dq_ref, dk_ref, dv_ref = scratch
    rows, wide = q_ref.shape
    pairs, size = wide // 128, block_of(rows)
    tables = (cos_ref, sin_ref, cosf_ref, sinf_ref)
    left = lax.broadcasted_iota(jnp.int32, (size, 128), 1) < HEAD
    key_at = lax.broadcasted_iota(jnp.int32, (size, size), 0)
    query_at = lax.broadcasted_iota(jnp.int32, (1, size), 1)

    last = rows // size - 1
    first, stop = (0, last) if piece == 0 else (last, last + 1)

    def prepare(i):
        r = pl.ds(pl.multiple_of(i * BLK, BLK), BLK)
        for t in range(pairs):
            w = pl.ds(t * 128, 128)
            kt_ref[w, r] = k_ref[r, w].astype(F32).T.astype(BF)
            dk_ref[r, w] = jnp.zeros((BLK, 128), F32)
            dv_ref[r, w] = jnp.zeros((BLK, 128), F32)

    if piece == 0:
        pl.loop(0, rows // BLK)(prepare)

    @pl.loop(first, stop)
    def _(i):
        r = pl.ds(pl.multiple_of(i * size, size), size)
        qs, dos, deltas, lses = [], [], [], []
        for t in range(pairs):
            w = pl.ds(t * 128, 128)
            do = do_ref[r, w]
            qs += two_heads(q_ref[r, w], left)
            dos += two_heads(do, left)
            prod = (do.astype(F32) * o_ref[r, w].astype(F32)).T
            deltas += [jnp.sum(prod[:HEAD], axis=0, keepdims=True), jnp.sum(prod[HEAD:], axis=0, keepdims=True)]
            lses += [lse_ref[2 * t : 2 * t + 1, r], lse_ref[2 * t + 1 : 2 * t + 2, r]]
        begin = begin_ref[0:1, r]
        here = query_at + i * size

        def step(j, carry):
            w = pl.ds(pl.multiple_of(j * size, size), size)
            key = key_at + j * size
            seen = (key <= here) & (key >= begin)
            out = []
            for t in range(pairs):
                lanes = pl.ds(t * 128, 128)
                k, v = k_ref[w, lanes], v_ref[w, lanes]
                dk = dv = None
                for h in (2 * t, 2 * t + 1):
                    prob = jnp.exp(jnp.where(seen, mm(k, qs[h], 1, 1) - lses[h], NEG))
                    ds = (prob * (mm(v, dos[h], 1, 1) - deltas[h])).astype(BF)
                    out.append(carry[h] + mm(kt_ref[pl.ds(h * HEAD, HEAD), w], ds, 1, 0))
                    dk_h, dv_h = mm(ds, qs[h], 1, 0), mm(prob.astype(BF), dos[h], 1, 0)
                    dk, dv = (dk_h, dv_h) if dk is None else (dk + dk_h, dv + dv_h)
                dk_ref[w, lanes] += dk
                dv_ref[w, lanes] += dv
            return tuple(out)

        done = lax.fori_loop(0, i + 1, step, (jnp.zeros((HEAD, size), F32),) * (2 * pairs))
        for t in range(pairs):
            both = jnp.concatenate(done[2 * t : 2 * t + 2], axis=0)
            dq_ref[r, pl.ds(t * 128, 128)] = both.T * (HEAD**-0.5)

    if piece == 0:
        return
    bias_ref[...] = jnp.zeros_like(bias_ref)

    @pl.loop(0, rows // BLK)
    def _(i):
        r = pl.ds(pl.multiple_of(i * BLK, BLK), BLK)
        for t in range(pairs):
            w = pl.ds(t * 128, 128)
            for part, value in enumerate((turn(dq_ref[r, w], i, tables, -1.0), turn(dk_ref[r, w], i, tables, -1.0), dv_ref[r, w])):
                lanes = pl.ds(part * wide + t * 128, 128)
                value = value.astype(BF)
                out_ref[r, lanes] = value
                bias_ref[:, lanes] += jnp.sum(value.astype(F32), axis=0, keepdims=True)


def attend_back(S, C, T, number, q, k, v, o, do, lse, begin, act, wd, riders):
    rows, wide = q.shape
    K, D, n = act.shape[1], wd.shape[0], rows // (S * T)

    def kernel(ride, ins, outs, scratch):
        _, _, row, col = plane(S)
        greet(S, C, row + [col], other=True, axes=ride.axes)

        def meanwhile(piece):
            if piece == 0:
                ride.start()
            attend_back_work(ins[2:], outs[0], outs[1], scratch[:4], piece)

        sum_over_plane(S, T, ins[0], ins[1], outs[2], scratch[4:], meanwhile)
        ride.wait()

    args = [act.reshape(S * T, n, K), wd, q, k, v, o, do, lse, *turn_tables(rows), begin]
    return comm(
        kernel, S, C, number, "attend_back", args, [IN_VMEM] * len(args),
        [(jax.ShapeDtypeStruct((rows, 3 * wide), BF), IN_VMEM), (jax.ShapeDtypeStruct((1, 3 * wide), F32), IN_VMEM),
         (jax.ShapeDtypeStruct((n, D), F32), IN_VMEM)],
        [pltpu.VMEM((wide, rows), BF)] + [pltpu.VMEM((rows, wide), F32)] * 3 + sum_scratch(S, n, D),
        riders,
    )


def doc_begins(lengths_row, rows):
    row_ids = jnp.arange(rows, dtype=jnp.int32)
    ends = jnp.cumsum(lengths_row, dtype=jnp.int32)
    begins = ends - lengths_row
    inside = (row_ids[:, None] >= begins[None, :]) & (row_ids[:, None] < ends[None, :])
    return jnp.sum(jnp.where(inside, begins[None, :], 0), axis=1, dtype=jnp.int32)


def tiles_of(parts, lead):
    flat = jnp.concatenate([x.astype(F32).reshape(lead + (-1,)) for x in parts], axis=-1)
    flat = jnp.pad(flat, ((0, 0),) * len(lead) + ((0, 1024 - flat.shape[-1]),))
    return flat.reshape(lead + (8, 128))


def make_body(S, C, T):
    assert S == C

    def body(tokens, lengths, w_qkv, b_qkv, w_out, w_gateup, w_down, norm_gain, norm_bias, cotangent):
        p, z, c = lax.axis_index("shard"), lax.axis_index("ctx"), lax.axis_index("tp")
        R, D = tokens.shape
        n = R // T
        nb = D // (S * C)
        L = R * C

        def to_parts(x):
            return x.reshape(n, S, C, nb).transpose(2, 0, 1, 3).reshape(S, n, D // S)

        def parts(x):
            return x.reshape(n, S, D // S).swapaxes(0, 1)

        def unpermute(x):
            return x.reshape(x.shape[0], C, S, nb).swapaxes(1, 2).reshape(x.shape)

        def half_of(x):
            return lax.dynamic_slice_in_dim(x, c * n, n, 0)

        def after(x, y):
            return lax.optimization_barrier((x, y))

        def over_ctx(w):
            return lax.all_gather(w.reshape(S * nb, -1), "ctx", axis=0, tiled=True)

        def sum_ctx(g):
            g = lax.psum_scatter(g.astype(BF), "ctx", scatter_dimension=0, tiled=True)
            return g.reshape(S, nb, -1)

        hn = w_qkv.shape[3] // S
        fn = w_gateup.shape[3] // S
        heads = hn // HEAD
        nf = HEAD // (S * C)

        tile = tiles_of((norm_gain[0].reshape(-1), norm_bias[0].reshape(-1), b_qkv[0].reshape(-1), lengths[0]), ())
        raw = lax.all_gather(w_qkv[0].swapaxes(0, 1).reshape(3 * nb, -1), "ctx", axis=0, tiled=True)
        small, _, tok, wo, wg, wd, cot = exchange(
            S, C, T, 0,
            [
                ("shard", w_out[0].reshape(S, hn, nb).swapaxes(1, 2)),
                ("shard", w_gateup[0].reshape(nb, 2, S, fn).transpose(2, 0, 1, 3).reshape(S, nb, 2 * fn)),
                ("shard", w_down[0].reshape(S, fn, nb).swapaxes(1, 2)),
                ("shard", to_parts(half_of(cotangent))),
            ],
            jnp.broadcast_to(tile, (C, S, 8, 128)),
            to_parts(half_of(tokens)),
        )
        tok, wo = gather_columns(S, C, T, 1, tok, [("all", wo.reshape(S * nb, hn))])
        wo, wg, wd = wo.reshape(D, hn), over_ctx(wg), over_ctx(wd)

        small = lax.dynamic_index_in_dim(small, c, 0, keepdims=False).reshape(C, S, 1024)
        norms = small[:, :, : 4 * nb].reshape(C * S, 4, nb).swapaxes(0, 1).reshape(4, D)
        gains, shifts = norms[:2], norms[2:]
        nbias = 3 * S * heads * nf
        bias = small[:, :, 4 * nb : 4 * nb + nbias].reshape(C, S, 3, S * heads, nf)
        bias = lax.dynamic_slice_in_dim(bias, p * heads, heads, 3)
        bias = bias.transpose(2, 3, 1, 0, 4).reshape(1, 3 * hn)
        docs = lengths.shape[1]
        lengths_row = lax.dynamic_index_in_dim(
            small[0, :, 4 * nb + nbias : 4 * nb + nbias + docs], z, 0, keepdims=False
        ).astype(jnp.int32)
        begin = doc_begins(lengths_row, L)
        begin = begin[None, :]

        n1, qkv, wq = project(S, C, T, 12, tok, raw.reshape(C, 3, nb, -1), gains[:1], shifts[:1], bias)
        q, k, v, o, lse = attend(qkv, begin)
        mid, n2, cot = sum_norm_gather(S, C, T, 2, o, wo, tok, gains[1:], shifts[1:], [("ctx", cot)])
        gb, gu, act = gates(S, C, T, 4, n2, wg, cot)
        gw_down = mm(gb, act, 0, 0).astype(BF)
        wd, gw_down = after(wd, gw_down)
        gw_down = sum_ctx(gw_down)

        (dgu,) = by_rows(
            gates_back_kernel, "gates_back", [(True, gb), (False, wd), (True, gu)],
            [jax.ShapeDtypeStruct((L, 2 * fn), BF)],
        )
        gw_gateup = mm(n2, dgu, 0, 0).astype(BF)
        dgu, gw_gateup = after(dgu, gw_gateup)
        gw_gateup = sum_ctx(gw_gateup)
        dmid, gb1, stats2 = sum_back_gather(S, C, T, 6, dgu, wg, mid, gb, gains[1:])
        gw_out = mm(gb1, o, 0, 0).astype(BF)
        gb1, gw_out = after(gb1, gw_out)
        do = mm(gb1, wo, 1, 0).astype(BF)
        dqkv, gbias, got, gw_down, gw_out = attend_back(
            S, C, T, 11, q, k, v, o, do, lse, begin, act, wd,
            [("shard", gw_down), ("ctx", gw_out.reshape(C, S * nb, hn))],
        )
        out = parts((mid + got).astype(BF))
        gw_qkv = mm(n1, dqkv, 0, 0).astype(BF)
        dqkv, gw_qkv = after(dqkv, gw_qkv)
        gw_qkv = sum_ctx(gw_qkv)
        low, stats1, out, gw_gateup = sum_back(
            S, C, T, 8, dqkv, wq, tok, dmid, gains[:1], [("shard", out), ("shard", gw_gateup)]
        )
        gtok, out, norms, gbias, gw_gateup, gw_down, gw_qkv, gw_out = finish(
            S, C, T, 10, low, out, [stats1, stats2], gbias, gw_gateup, gw_down, gw_qkv,
            jnp.sum(gw_out.astype(F32), axis=0).astype(BF).reshape(S, nb, hn),
        )
        if not ordered(D, S, C):
            gtok, out = unpermute(gtok), unpermute(out)
        gtok = gtok.astype(F32)
        norms = lax.dynamic_slice_in_dim(norms, (z * S + p) * nb % 128, nb, 1) if nb % 128 else norms
        gbias = gbias.reshape(S, 3, heads, S * C, nf)
        gbias = lax.dynamic_index_in_dim(gbias, p * C + z, 3, keepdims=False)
        gbias = gbias.swapaxes(0, 1).reshape(b_qkv.shape)

        return (
            out,
            gtok,
            gw_qkv.swapaxes(0, 1).reshape(w_qkv.shape),
            gbias,
            gw_out.reshape(w_out.shape),
            gw_gateup.reshape(w_gateup.shape),
            gw_down.reshape(w_down.shape),
            norms[None, :2],
            norms[None, 2:],
        )

    return body


def solution(mesh):
    both = ("shard", "ctx")
    specs = (
        P(None, both, None, "tp"),
        P(None, None, "tp", both),
        P(None, "tp", both),
        P(None, both, None, "tp"),
        P(None, "tp", both),
        P(None, None, both),
        P(None, None, both),
    )
    return jax.shard_map(
        make_body(mesh.shape["shard"], mesh.shape["ctx"], mesh.shape["tp"]),
        mesh=mesh,
        in_specs=(P(both, None), P("shard", None)) + specs + (P(both, None),),
        out_specs=(P(both, None), P(both, None)) + specs,
        check_vma=False,
    )
```

```python
import functools

import jax
import jax.numpy as jnp
import numpy as np
from jax import lax
from jax.experimental import pallas as pl
from jax.experimental.pallas import tpu as pltpu
from jax.sharding import PartitionSpec as P

HEAD = 64
ROT = 16
EPS = 1e-05
NEG = -1e30
BASE = 10000.0
BF = jnp.bfloat16
F32 = jnp.float32
BLK = 256
MESH = pl.DeviceIdType.MESH
DMA = pltpu.SemaphoreType.DMA
ANY = pl.BlockSpec(memory_space=pl.ANY)
IN_VMEM = pl.BlockSpec(memory_space=pltpu.VMEM)


def mm(a, b, ca, cb):
    return lax.dot_general(a, b, (((ca,), (cb,)), ((), ())), preferred_element_type=F32)


def remote(src, dst, send, recv, where):
    return pltpu.make_async_remote_copy(
        src_ref=src, dst_ref=dst, send_sem=send, recv_sem=recv, device_id=where, device_id_type=MESH
    )


def here():
    return lax.axis_index("shard"), lax.axis_index("ctx"), lax.axis_index("tp")


class Riders:
    def __init__(self, S, C, riders):
        self.S, self.C = S, C
        self.axes = [axis for axis, _ in riders]
        self.arrays = [x for _, x in riders]
        self.shapes = [
            jax.ShapeDtypeStruct((C,) + x.shape if axis == "all" else x.shape, x.dtype) for axis, x in riders
        ]
        count, most = len(riders), max(S, C) - 1
        self.scratch = [DMA((count, most)), DMA((count, most)), DMA((count,))] if count else []

    def bind(self, ins, outs, sems):
        self.ins, self.outs, self.sems = ins, outs, sems

    def start(self):
        p, z, c = here()
        self.moves = []
        for n, axis in enumerate(self.axes):
            src, dst = self.ins[n], self.outs[n]
            send, recv, own = self.sems
            if axis == "tp":
                copies = [remote(src, dst, send.at[n, 0], recv.at[n, 0], {"tp": 1 - c})]
            elif axis == "all":
                copies = [
                    remote(src, dst.at[z], send.at[n, k - 1], recv.at[n, k - 1], {"ctx": (z + k) % self.C})
                    for k in range(1, self.C)
                ]
                copies.append(pltpu.make_async_copy(src, dst.at[z], own.at[n]))
            else:
                size, me = (self.S, p) if axis == "shard" else (self.C, z)
                copies = [
                    remote(src.at[(me + k) % size], dst.at[me], send.at[n, k - 1], recv.at[n, k - 1], {axis: (me + k) % size})
                    for k in range(1, size)
                ]
                copies.append(pltpu.make_async_copy(src.at[me], dst.at[me], own.at[n]))
            for copy in copies:
                copy.start()
            self.moves += copies

    def wait(self):
        for copy in self.moves:
            copy.wait()


def greet(S, C, mates=(), line=False, other=False, axes=()):
    p, z, c = here()
    peers = [{"shard": q} for q in ([(p + k) % S for k in range(1, S)] if "shard" in axes else mates)]
    if line or "ctx" in axes or "all" in axes:
        peers += [{"ctx": (z + k) % C} for k in range(1, C)]
    if other or "tp" in axes:
        peers.append({"tp": 1 - c})
    barrier = pltpu.get_barrier_semaphore()
    for where in peers:
        pl.semaphore_signal(barrier, inc=1, device_id=where, device_id_type=MESH)
    pl.semaphore_wait(barrier, len(peers))


def comm(kernel, S, C, number, name, args, in_specs, outs, scratch, riders=()):
    ride = Riders(S, C, riders)
    na, nr, no, ns = len(args), len(ride.axes), len(outs), len(scratch)

    def body(*refs):
        ins, refs = refs[:na], refs[na:]
        rins, refs = refs[:nr], refs[nr:]
        os, refs = refs[:no], refs[no:]
        routs, refs = refs[:nr], refs[nr:]
        ride.bind(rins, routs, refs[ns:])
        kernel(ride, ins, os, refs[:ns])

    return pl.pallas_call(
        body,
        out_shape=[shape for shape, _ in outs] + ride.shapes,
        in_specs=list(in_specs) + [IN_VMEM] * nr,
        out_specs=[spec for _, spec in outs] + [ANY] * nr,
        scratch_shapes=list(scratch) + ride.scratch,
        compiler_params=pltpu.CompilerParams(
            collective_id=number, has_side_effects=True, vmem_limit_bytes=62 << 20
        ),
        cost_estimate=pl.CostEstimate(flops=0, bytes_accessed=120_000_000, transcendentals=0),
        name=name,
    )(*args, *ride.arrays)


def exchange(S, C, T, number, riders, tiles, rows, beside, turned):
    R, D = rows.shape
    n, wide, nb = R // T, D // S, D // (S * C)
    pieces = S if ordered(D, S, C) else 1
    p, z, c = here()
    if pieces == 1:
        rows, beside = (
            lax.dynamic_slice_in_dim(x, c * n, n, 0).reshape(n, S, C, nb).transpose(2, 0, 1, 3).reshape(S, n, wide)
            for x in (rows, beside)
        )
    heights = [x.shape[0] // S for x in turned]

    def kernel(ride, ins, outs, scratch):
        tile, x_ref, y_ref, *raws = ins
        got, x_buf, x_out, y_out, *turns = outs
        send, recv, bsend, brecv, own, hsend, hrecv, hown, zsend, zrecv, zown, wsend, wrecv, wown, *stages = scratch
        p, z, c = here()
        mates = [(p + k) % S for k in range(1, S)]
        everyone = [(i, j) for i in range(C) for j in range(S) if i or j]
        peers = [{"shard": (p + j) % S, "ctx": (z + i) % C} for i, j in everyone]
        barrier = pltpu.get_barrier_semaphore()
        for where in peers + [{"tp": 1 - c}]:
            pl.semaphore_signal(barrier, inc=1, device_id=where, device_id_type=MESH)
        pl.semaphore_wait(barrier, len(peers) + 1)

        def columns(ref, q, i):
            if pieces == 1:
                return ref.at[q]
            lanes = pl.ds(pl.multiple_of((i * C + q) * nb, 128), nb)
            return ref.at[pl.ds(pl.multiple_of(c * n, 16), n), lanes]

        def first_hop(ref, out, at):
            hop = []
            for i in range(pieces):
                dst = out.at[p, :, pl.ds(i * (wide // pieces), wide // pieces)]
                hop.append(pltpu.make_async_copy(columns(ref, p, i), dst, hown.at[at, i]))
                for k, q in enumerate(mates):
                    hop.append(
                        remote(columns(ref, q, i), dst, hsend.at[at, k, i], hrecv.at[at, k, i], {"shard": q})
                    )
            for copy in hop:
                copy.start()
            return hop

        x_hop = first_hop(x_ref, x_buf, 0)
        local = pltpu.make_async_copy(tile.at[z, p], got.at[c, z, p], own)
        local.start()
        copies = []
        for at, (where, (i, j)) in enumerate(zip(peers, everyone)):
            q, g = (p + j) % S, (z + i) % C
            copies.append(remote(tile.at[g, q], got.at[c, z, p], send.at[at], recv.at[at], where))
            copies[-1].start()
        ride.start()
        y_hop = first_hop(y_ref, y_out, 1)
        moves = []
        for m, (raw, stage, out, height) in enumerate(zip(raws, stages, turns, heights)):
            for q in range(S):
                stage[q] = raw[q * height : (q + 1) * height, :].astype(F32).T.astype(BF)
            moves.append(pltpu.make_async_copy(stage.at[p], out.at[p], wown.at[m]))
            for k, q in enumerate(mates):
                moves.append(remote(stage.at[q], out.at[p], wsend.at[m, k], wrecv.at[m, k], {"shard": q}))
            for copy in moves[-S:]:
                copy.start()
        for copy in x_hop:
            copy.wait()
        line = [pltpu.make_async_copy(x_buf.at[z], x_out.at[z], zown)]
        for k in range(1, C):
            g = (z + k) % C
            line.append(remote(x_buf.at[g], x_out.at[z], zsend.at[k - 1], zrecv.at[k - 1], {"ctx": g}))
        for copy in line:
            copy.start()
        local.wait()
        for copy in copies:
            copy.wait()
        back = remote(got.at[c], got.at[c], bsend, brecv, {"tp": 1 - c})
        back.start()
        back.wait_send()
        remote(got.at[1 - c], got.at[1 - c], bsend, brecv, {"tp": 1 - c}).wait_recv()
        for copy in line + y_hop + moves:
            copy.wait()
        ride.wait()

    count, m = C * S - 1, len(turned)
    part = jax.ShapeDtypeStruct((S, n, wide), rows.dtype)
    return comm(
        kernel, S, C, number, "exchange", [tiles, rows, beside, *turned],
        [IN_VMEM, ANY, ANY] + [IN_VMEM] * m,
        [(jax.ShapeDtypeStruct((T,) + tiles.shape, tiles.dtype), ANY), (part, IN_VMEM), (part, IN_VMEM), (part, ANY)]
        + [(jax.ShapeDtypeStruct((S, nb, height), BF), ANY) for height in heights],
        [
            DMA((count,)), DMA((count,)), DMA, DMA, DMA,
            DMA((2, S - 1, pieces)), DMA((2, S - 1, pieces)), DMA((2, pieces)),
            DMA((C - 1,)), DMA((C - 1,)), DMA, DMA((m, S - 1)), DMA((m, S - 1)), DMA((m,)),
        ]
        + [pltpu.VMEM((S, nb, height), BF) for height in heights],
        riders,
    )


def plane(S):
    p, _, c = here()
    B = S // 2
    a, b = p // B, p % B
    return a, b, [a * B + (b + j) % B for j in range(1, B)], (1 - a) * B + b


def spread_sems(S):
    count = 4 + 4 * (S // 2 - 1)
    return [DMA((2 * count,)), DMA((2 * count,))]


def spread(S, own, region, send, recv, work=(None, None)):
    p, _, c = here()
    B = S // 2
    a, b, rows, col = plane(S)
    rows, col, other = [{"shard": q} for q in rows], {"shard": col}, {"tp": 1 - c}
    per = 4 + 4 * (B - 1)
    OWN, ROW, COL, VIA_COL, VIA_ROW = 0, 2, 2 + 2 * (B - 1), 4 + 2 * (B - 1), 4 + 3 * (B - 1)
    started = []

    def push(q, h, sem, where, first=False):
        view = region(q, h, c)
        copy = remote(own(h) if first else view, view, send.at[sem], recv.at[sem], where)
        copy.start()
        started.append(copy)

    def came(q, h, sem, core):
        view = region(q, h, core)
        remote(view, view, send.at[sem], recv.at[sem], other).wait_recv()

    for h in range(2):
        for j in range(1, B):
            push(p, h, ROW + 2 * (j - 1) + h, rows[j - 1], True)
    for h in (1, 0):
        push(p, h, COL + h, col, True)
    for h in range(2):
        push(p, h, per + OWN + h, other, True)

    def from_row(j, h):
        q = a * B + (b - j) % B
        came(q, h, ROW + 2 * (j - 1) + h, c)
        push(q, h, per + ROW + 2 * (j - 1) + h, other)
        return q

    def from_col(h):
        q = (1 - a) * B + b
        came(q, h, COL + h, c)
        push(q, h, per + COL + h, other)
        return q

    if work[0] is not None:
        work[0]()
    for j in range(1, B):
        q = from_row(j, 0)
        push(q, 0, VIA_COL + j - 1, col)
    q = from_col(1)
    for j in range(1, B):
        push(q, 1, VIA_ROW + j - 1, rows[j - 1])
    if work[1] is not None:
        work[1]()
    for j in range(1, B):
        from_row(j, 1)
    from_col(0)
    for j in range(1, B):
        q = (1 - a) * B + (b - j) % B
        came(q, 0, VIA_COL + j - 1, c)
        push(q, 0, per + VIA_COL + j - 1, other)
        came(q, 1, VIA_ROW + j - 1, c)
        push(q, 1, per + VIA_ROW + j - 1, other)
    for h in range(2):
        came(p, h, per + OWN + h, 1 - c)
        came((1 - a) * B + b, h, per + COL + h, 1 - c)
    for j in range(1, B):
        for h in range(2):
            came(a * B + (b - j) % B, h, per + ROW + 2 * (j - 1) + h, 1 - c)
        q = (1 - a) * B + (b - j) % B
        came(q, 0, per + VIA_COL + j - 1, 1 - c)
        came(q, 1, per + VIA_ROW + j - 1, 1 - c)
    for copy in started:
        copy.wait_send()


def gather_columns(S, C, T, number, x, riders=(), extra=None):
    _, n, wide = x.shape
    more, more_specs, more_outs, more_scratch, task = extra or ((), (), (), (), None)

    def kernel(ride, ins, outs, scratch):
        x_ref, out_ref = ins[0], outs[0]
        send, recv, own = scratch[:3]
        p, _, c = here()
        _, _, rows, col = plane(S)

        def region(q, h, core):
            part = pl.ds(pl.multiple_of(q * wide, 128), wide)
            return out_ref.at[pl.ds(h * (C // 2), C // 2), core, :, part]

        local = [
            pltpu.make_async_copy(x_ref.at[pl.ds(h * (C // 2), C // 2)], region(p, h, c), own.at[h]) for h in range(2)
        ]
        for copy in local:
            copy.start()
        if task is not None:
            task(ins[1:], outs[1:], scratch[3:], None)
        greet(S, C, rows + [col], other=True, axes=ride.axes)
        ride.start()
        work = [None, None]
        if task is not None:
            work = [functools.partial(task, ins[1:], outs[1:], scratch[3:], piece) for piece in range(2)]
        spread(S, lambda h: x_ref.at[pl.ds(h * (C // 2), C // 2)], region, send, recv, work)
        for copy in local:
            copy.wait()
        ride.wait()

    out, *rest = comm(
        kernel, S, C, number, "gather_columns", [x, *more], [IN_VMEM, *more_specs],
        [(jax.ShapeDtypeStruct((C, T, n, wide * S), x.dtype), ANY), *more_outs],
        spread_sems(S) + [DMA((2,)), *more_scratch], riders,
    )
    return [out.reshape(C * T * n, wide * S)] + rest


CHUNK = 512
ROWS = 32


def sum_scratch(S, n, D):
    half, B = n // 2, S // 2

    def vm(*shape):
        return pltpu.VMEM(shape, BF)

    return [
        vm(S, n, D), vm(S, n, D), vm(S, n, D), vm(B - 1, 2, half, D), vm(B, half, D),
        vm(B - 1, half, D), vm(half, D), vm(half, D), vm(B - 1, half, D),
        DMA((S,)), DMA((S,)), DMA((B - 1, 2)), DMA((B - 1, 2)), DMA((B,)), DMA((B,)), DMA((B,)), DMA((B,)),
    ]


def sum_over_plane(S, T, x_ref, w_ref, out_ref, scratch, meanwhile=None):
    away, sib, mine, row1, col1, row2, col2, to_col, to_row = scratch[:9]
    asend, arecv, rsend, rrecv, csend, crecv, fsend, frecv = scratch[9:]
    n, D = out_ref.shape
    half, B = n // 2, S // 2
    _, _, c = here()
    a, b, rows, col = plane(S)
    rows, col, other = [{"shard": q} for q in rows], {"shard": col}, {"tp": 1 - c}

    def chip(e):
        return ((a + e // B) % 2) * B + (b + e % B) % B

    def product(e, core, store):
        x = x_ref[chip(e) * T + core]

        def column(j, _):
            w = pl.ds(pl.multiple_of(j * CHUNK, CHUNK), CHUNK)
            store(w, mm(x, w_ref[w, :], 1, 1))
            return 0

        lax.fori_loop(0, D // CHUNK, column, 0)

    def to_other(e):
        return remote(away.at[e], sib.at[e], asend.at[e], arecv.at[e], other)

    def for_other(e):
        def store(w, value):
            away[e, :, w] = value.astype(BF)

        product(e, 1 - c, store)
        to_other(e).start()

    for_other(S - 1)
    top, low = pl.ds(0, half), pl.ds(half, half)
    started = []

    def push(src, dst, send, recv, where):
        copy = remote(src, dst, send, recv, where)
        copy.start()
        started.append(copy)

    for e in range(S - 1, -1, -1):
        if e:
            for_other(e - 1)
        to_other(e).wait()

        def store(w, value):
            value = value + sib[e, :, w].astype(F32)
            if e:
                mine[e, :, w] = value.astype(BF)
            else:
                out_ref[:, w] = value

        product(e, c, store)
        j = e % B
        if e > B:
            push(mine.at[e, top], row1.at[j - 1, 1], rsend.at[j - 1, 1], rrecv.at[j - 1, 1], rows[j - 1])
            push(mine.at[e, low], col1.at[j], csend.at[j], crecv.at[j], col)
        elif e == B:
            push(mine.at[e, low], col1.at[0], csend.at[0], crecv.at[0], col)
        elif e:
            push(mine.at[e, top], row1.at[j - 1, 0], rsend.at[j - 1, 0], rrecv.at[j - 1, 0], rows[j - 1])

    def came(ref, send, recv):
        remote(ref, ref, send, recv, other).wait_recv()

    if meanwhile is not None:
        meanwhile(0)
    total = mine[B, top, :].astype(F32)
    for j in range(1, B):
        came(row1.at[j - 1, 1], rsend.at[j - 1, 1], rrecv.at[j - 1, 1])
        total = total + row1[j - 1, 1].astype(F32)
    to_col[...] = total.astype(BF)
    push(to_col, col2, fsend.at[0], frecv.at[0], col)
    for j in range(1, B):
        came(col1.at[j], csend.at[j], crecv.at[j])
        to_row[j - 1] = (mine[j, low, :].astype(F32) + col1[j].astype(F32)).astype(BF)
        push(to_row.at[j - 1], row2.at[j - 1], fsend.at[j], frecv.at[j], rows[j - 1])
    if meanwhile is not None:
        meanwhile(1)
    came(col1.at[0], csend.at[0], crecv.at[0])
    upper, lower = out_ref[top, :], out_ref[low, :] + col1[0].astype(F32)
    for j in range(1, B):
        came(row1.at[j - 1, 0], rsend.at[j - 1, 0], rrecv.at[j - 1, 0])
        upper = upper + row1[j - 1, 0].astype(F32)
    came(col2, fsend.at[0], frecv.at[0])
    out_ref[top, :] = upper + col2[...].astype(F32)
    for j in range(1, B):
        came(row2.at[j - 1], fsend.at[j], frecv.at[j])
        lower = lower + row2[j - 1].astype(F32)
    out_ref[low, :] = lower
    for copy in started:
        copy.wait_send()


def project(S, C, T, number, tok, raw, gain, shift, bias):
    L, D = tok.shape
    _, parts, nb, wide = raw.shape
    hn = wide // S
    most = S - 1

    def kernel(ride, ins, outs, scratch):
        tok_ref, raw_ref, gain_ref, shift_ref, bias_ref = ins
        n_ref, out_ref, w_ref = outs
        send, recv, own = scratch
        p, _, _ = here()
        mates = [(p + k) % S for k in range(1, S)]
        greet(S, C, mates)

        def lanes(q):
            return pl.ds(pl.multiple_of(q * hn, 128), hn)

        copies = []
        for part in range(parts):
            dst = w_ref.at[:, p, :, pl.ds(part * hn, hn)]
            for k, q in enumerate(mates):
                copies.append(
                    remote(raw_ref.at[:, part, :, lanes(q)], dst, send.at[k, part], recv.at[k, part], {"shard": q})
                )
            copies.append(pltpu.make_async_copy(raw_ref.at[:, part, :, lanes(p)], dst, own.at[part]))
        for copy in copies:
            copy.start()

        def normed(r):
            n_ref[r, :] = (norm_of(tok_ref[r, :].astype(F32))[0] * gain_ref[...] + shift_ref[...]).astype(BF)

        row_blocks(L, normed)
        for copy in copies:
            copy.wait()
        w = w_ref[...].reshape(D, parts * hn)

        @pl.loop(0, L // BLK)
        def _(i):
            r = pl.ds(pl.multiple_of(i * BLK, BLK), BLK)
            out_ref[r, :] = mm(n_ref[r, :], w, 1, 0) + bias_ref[...]

    n, out, w = comm(
        kernel, S, C, number, "project", [tok, raw, gain, shift, bias], [IN_VMEM] * 5,
        [
            (jax.ShapeDtypeStruct((L, D), BF), IN_VMEM), (jax.ShapeDtypeStruct((L, parts * hn), F32), IN_VMEM),
            (jax.ShapeDtypeStruct((C, S, nb, parts * hn), BF), IN_VMEM),
        ],
        [DMA((most, parts)), DMA((most, parts)), DMA((parts,))],
    )
    return n, out, w.reshape(D, parts * hn)


def gates_back_kernel(gb_ref, wd_ref, gu_ref, dgu_ref):
    dact = mm(gb_ref[...], wd_ref[...], 1, 0)
    both, width = gu_ref[...], dact.shape[1]
    gate, up = both[:, :width], both[:, width:]
    s = jax.nn.sigmoid(gate)
    dgate = dact * up * s * (1.0 + gate * (1.0 - s))
    dgu_ref[...] = jnp.concatenate((dgate, dact * gate * s), axis=1).astype(BF)


def gates_work(ins, outs, scratch, piece):
    gu_ref, act_ref = outs
    n2_ref, wg_ref, sems = scratch
    if piece != 1:
        for i, (x, y) in enumerate(zip(ins, (n2_ref, wg_ref))):
            copy = pltpu.make_async_copy(x, y, sems.at[i])
            copy.wait() if piece == 0 else copy.start()
    if piece is None:
        return
    (rows, width), half = act_ref.shape, act_ref.shape[0] // BLK // 2

    @pl.loop(piece * half, piece * half + half)
    def _(i):
        r = pl.ds(pl.multiple_of(i * BLK, BLK), BLK)
        both = mm(n2_ref[r, :], wg_ref[...], 1, 0)
        gu_ref[r, :] = both
        gate, up = both[:, :width], both[:, width:]
        act_ref[r, :] = (gate * jax.nn.sigmoid(gate) * up).astype(BF)


def gates(S, C, T, number, n2, wg, x):
    L, width = n2.shape[0], wg.shape[1] // 2
    outs = [jax.ShapeDtypeStruct((L, 2 * width), F32), jax.ShapeDtypeStruct((L, width), BF)]
    return gather_columns(
        S, C, T, number, x, (),
        ([n2, wg], [ANY, ANY], [(shape, IN_VMEM) for shape in outs],
         [pltpu.VMEM(n2.shape, BF), pltpu.VMEM(wg.shape, BF), DMA((2,))], gates_work),
    )


def by_rows(kernel, name, arrays, outs):
    L = outs[0].shape[0]

    def spec(width):
        return pl.BlockSpec((BLK, width), lambda i: (i, 0))

    return pl.pallas_call(
        kernel,
        grid=(L // BLK,),
        in_specs=[spec(x.shape[1]) if rows else pl.BlockSpec(x.shape, lambda i: (0, 0)) for rows, x in arrays],
        out_specs=[spec(x.shape[1]) for x in outs],
        out_shape=outs,
        compiler_params=pltpu.CompilerParams(vmem_limit_bytes=62 << 20),
        name=name,
    )(*[x for _, x in arrays])


def row_blocks(n, work):
    @pl.loop(0, n // ROWS)
    def _(i):
        work(pl.ds(pl.multiple_of(i * ROWS, ROWS), ROWS))


def own_rows(T, x_ref, row_ref, sem):
    p, _, c = here()
    copy = pltpu.make_async_copy(x_ref.at[p * T + c], row_ref, sem)
    copy.start()
    return copy


def norm_of(v):
    center = v - jnp.mean(v, axis=-1, keepdims=True)
    inverse = lax.rsqrt(jnp.mean(center * center, axis=-1, keepdims=True) + EPS)
    return center * inverse, inverse


def norm_back(v, g, gain, stats_ref):
    normal, inverse = norm_of(v)
    e = g * gain
    stats_ref[0:1, :] += jnp.sum(g * normal, axis=0, keepdims=True)
    stats_ref[1:2, :] += jnp.sum(g, axis=0, keepdims=True)
    return inverse * (
        e - jnp.mean(e, axis=-1, keepdims=True) - normal * jnp.mean(e * normal, axis=-1, keepdims=True)
    )


def spread_rows(S, T, src, out_ref, send, recv, own):
    p, _, c = here()
    half = src.shape[0] // 2
    local = pltpu.make_async_copy(src, out_ref.at[p * T + c], own)
    local.start()
    spread(
        S,
        lambda h: src.at[pl.ds(h * half, half)],
        lambda q, h, core: out_ref.at[q * T + core, pl.ds(h * half, half)],
        send,
        recv,
    )
    local.wait()


def sum_norm_gather(S, C, T, number, x, w, residual, gain, shift, riders=()):
    L, K = x.shape
    D, n = w.shape[0], L // (S * T)

    def kernel(ride, ins, outs, scratch):
        x_ref, w_ref, all_ref, gain_ref, shift_ref = ins
        v_ref, out_ref = outs
        acc, low, send, recv, own, res_ref, sem = scratch[:7]
        _, _, rows, col = plane(S)
        rest = own_rows(T, all_ref, res_ref, sem)
        greet(S, C, rows + [col], other=True, axes=ride.axes)
        ride.start()
        sum_over_plane(S, T, x_ref, w_ref, acc, scratch[7:])
        rest.wait()

        def work(r):
            v = res_ref[r, :].astype(F32) + acc[r, :]
            v_ref[r, :] = v
            low[r, :] = (norm_of(v)[0] * gain_ref[...] + shift_ref[...]).astype(BF)

        row_blocks(n, work)
        spread_rows(S, T, low, out_ref, send, recv, own)
        ride.wait()

    v, out, *rest = comm(
        kernel, S, C, number, "sum_norm_gather", [x.reshape(S * T, n, K), w, residual.reshape(S * T, n, D), gain, shift],
        [IN_VMEM, IN_VMEM, ANY, IN_VMEM, IN_VMEM],
        [(jax.ShapeDtypeStruct((n, D), F32), IN_VMEM), (jax.ShapeDtypeStruct((S * T, n, D), BF), ANY)],
        [pltpu.VMEM((n, D), F32), pltpu.VMEM((n, D), BF)] + spread_sems(S)
        + [DMA, pltpu.VMEM((n, D), BF), DMA] + sum_scratch(S, n, D),
        riders,
    )
    return [v, out.reshape(L, D)] + rest


def sum_back_gather(S, C, T, number, x, w, v, residual, gain, riders=()):
    L, K = x.shape
    D, n = w.shape[0], L // (S * T)

    def kernel(ride, ins, outs, scratch):
        x_ref, w_ref, in_ref, all_ref, gain_ref = ins
        v_ref, out_ref, stats = outs
        acc, low, send, recv, own, res_ref, sem = scratch[:7]
        _, _, rows, col = plane(S)
        rest = own_rows(T, all_ref, res_ref, sem)
        greet(S, C, rows + [col], other=True, axes=ride.axes)
        ride.start()
        sum_over_plane(S, T, x_ref, w_ref, acc, scratch[7:])
        rest.wait()
        stats[...] = jnp.zeros_like(stats)

        def work(r):
            g = res_ref[r, :].astype(F32) + norm_back(in_ref[r, :], acc[r, :], gain_ref[...], stats)
            v_ref[r, :] = g
            low[r, :] = g.astype(BF)

        row_blocks(n, work)
        spread_rows(S, T, low, out_ref, send, recv, own)
        ride.wait()

    g, out, stats, *rest = comm(
        kernel, S, C, number, "sum_back_gather", [x.reshape(S * T, n, K), w, v, residual.reshape(S * T, n, D), gain],
        [IN_VMEM, IN_VMEM, IN_VMEM, ANY, IN_VMEM],
        [
            (jax.ShapeDtypeStruct((n, D), F32), IN_VMEM), (jax.ShapeDtypeStruct((S * T, n, D), BF), ANY),
            (jax.ShapeDtypeStruct((2, D), F32), IN_VMEM),
        ],
        [pltpu.VMEM((n, D), F32), pltpu.VMEM((n, D), BF)] + spread_sems(S)
        + [DMA, pltpu.VMEM((n, D), BF), DMA] + sum_scratch(S, n, D),
        riders,
    )
    return [g, out.reshape(L, D), stats] + rest


def sum_back(S, C, T, number, x, w, v, residual, gain, riders=()):
    L, K = x.shape
    D, n = w.shape[0], L // (S * T)

    def kernel(ride, ins, outs, scratch):
        x_ref, w_ref, all_ref, res_ref, gain_ref = ins
        low, stats = outs
        acc, in_ref, sem = scratch[:3]
        _, _, rows, col = plane(S)
        rest = own_rows(T, all_ref, in_ref, sem)
        greet(S, C, rows + [col], other=True, axes=ride.axes)
        ride.start()
        sum_over_plane(S, T, x_ref, w_ref, acc, scratch[3:])
        rest.wait()
        stats[...] = jnp.zeros_like(stats)

        def work(r):
            g = res_ref[r, :] + norm_back(in_ref[r, :].astype(F32), acc[r, :], gain_ref[...], stats)
            low[r, :] = g.astype(BF)

        row_blocks(n, work)
        ride.wait()

    return comm(
        kernel, S, C, number, "sum_back", [x.reshape(S * T, n, K), w, v.reshape(S * T, n, D), residual, gain],
        [IN_VMEM, IN_VMEM, ANY, IN_VMEM, IN_VMEM],
        [(jax.ShapeDtypeStruct((n, D), BF), IN_VMEM), (jax.ShapeDtypeStruct((2, D), F32), IN_VMEM)],
        [pltpu.VMEM((n, D), F32), pltpu.VMEM((n, D), BF), DMA] + sum_scratch(S, n, D),
        riders,
    )


def finish(S, C, T, number, x, y, stats, bias, gateup, down, qkv, out):
    n, D = x.shape
    fn, hn = down.shape[2], out.shape[2]
    wide, lines = D // S, bias.shape[1] // 128
    nb = D // (S * C)
    count = sum(z.shape[0] for z in stats)
    tall = -(-(count + lines) // 8) * 8
    many = C * S - 1
    pieces = S if ordered(D, S, C) else 1

    def kernel(ride, ins, outs, scratch):
        x_ref, y_ref, stat_refs, bias_ref = ins[0], ins[1], ins[2:-5], ins[-5]
        gateup_ref, down_ref, qkv_ref, o_ref = ins[-4:]
        x_out, y_out, norm_out, bias_out, gateup_out, down_out, qkv_out, o_out = outs
        xbuf, xbuf2, ybuf2, tile, send, recv, own, psend, precv, pown, lsend, lrecv, tsend, trecv = scratch[:14]
        qkv_buf, o_buf, gsend, grecv, gown, got = scratch[14:]
        p, z, c = here()
        other = {"tp": 1 - c}
        everyone = [(i, j) for i in range(C) for j in range(S) if i or j]
        peers = [{"shard": (p + j) % S, "ctx": (z + i) % C} for i, j in everyone]
        barrier = pltpu.get_barrier_semaphore()
        for where in peers + [other]:
            pl.semaphore_signal(barrier, inc=1, device_id=where, device_id_type=MESH)
        pl.semaphore_wait(barrier, len(peers) + 1)

        def part(q):
            return pl.ds(pl.multiple_of(q * wide, 128), wide)

        def turn_over(source, target, at, size, me, axis):
            hop = [pltpu.make_async_copy(source(me), target, own.at[at])]
            for k in range(1, size):
                q = (me + k) % size
                hop.append(remote(source(q), target, send.at[at, k - 1], recv.at[at, k - 1], {axis: q}))
            for copy in hop:
                copy.start()
            return hop

        def arrive(buf, out, at):
            hop = []
            for i in range(pieces):
                src = pl.ds(i * (wide // pieces), wide // pieces)
                first = (i * C + p) * nb if pieces > 1 else p * wide
                dst = out.at[c, :, pl.ds(pl.multiple_of(first, 128), wide // pieces)]
                hop.append(pltpu.make_async_copy(buf.at[p, :, src], dst, pown.at[at, i]))
                for k in range(1, S):
                    q = (p + k) % S
                    hop.append(
                        remote(buf.at[q, :, src], dst, psend.at[at, k - 1, i], precv.at[at, k - 1, i], {"shard": q})
                    )
            for copy in hop:
                copy.start()
            return hop

        def both(ref, at):
            copy = remote(ref.at[c], ref.at[c], lsend.at[at], lrecv.at[at], other)
            copy.start()
            return copy

        def settle(ref, at, copy):
            copy.wait_send()
            remote(ref.at[1 - c], ref.at[1 - c], lsend.at[at], lrecv.at[at], other).wait_recv()

        x_hop = turn_over(lambda q: x_ref.at[:, part(q)], xbuf.at[p], 0, S, p, "shard")
        y_hop = turn_over(lambda q: y_ref.at[q], ybuf2.at[z], 1, C, z, "ctx")
        moves = []
        for i, (src, dst) in enumerate(((qkv_ref, qkv_buf), (o_ref, o_buf))):
            moves.append(pltpu.make_async_copy(src.at[p], dst.at[p], gown.at[i]))
            for k in range(1, S):
                q = (p + k) % S
                moves.append(remote(src.at[q], dst.at[p], gsend.at[i, k - 1], grecv.at[i, k - 1], {"shard": q}))
        for copy in moves:
            copy.start()
        tile[...] = jnp.zeros_like(tile)
        at = count
        for i, ref in enumerate(stat_refs):
            for j in range(2):
                tile[j * len(stat_refs) + i : j * len(stat_refs) + i + 1, :] = ref[j : j + 1, :]
        for k in range(lines):
            for block in range(D // 128):
                tile[at + k : at + k + 1, pl.ds(block * 128, 128)] = bias_ref[:, pl.ds(k * 128, 128)]

        def columns(g, q):
            return tile.at[:, pl.ds(pl.multiple_of((g * S + q) * nb // 128 * 128, 128), 128)]

        small = [pltpu.make_async_copy(columns(z, p), got.at[c, z, p], own.at[3])]
        for k, (where, (i, j)) in enumerate(zip(peers, everyone)):
            small.append(
                remote(columns((z + i) % C, (p + j) % S), got.at[c, z, p], tsend.at[k], trecv.at[k], where)
            )
        for copy in small:
            copy.start()
        for copy in x_hop:
            copy.wait()
        x_hop = turn_over(lambda q: xbuf.at[q], xbuf2.at[z], 2, C, z, "ctx")
        for q in range(S):
            down_out[q * fn : (q + 1) * fn, :] = down_ref[q].astype(F32).T
        for copy in y_hop:
            copy.wait()
        y_hop = arrive(ybuf2, y_out, 0)
        for copy in small:
            copy.wait()
        small_last = both(got, 0)
        bias_out[...] = jnp.sum(got[c, :, :, count : count + lines, :], axis=0)
        for i in range(2):
            for q in range(S):
                gateup_out[:, i, q * fn : (q + 1) * fn] = gateup_ref[q, :, i * fn : (i + 1) * fn].astype(F32)
        for copy in x_hop:
            copy.wait()
        x_hop = arrive(xbuf2, x_out, 1)
        for copy in y_hop:
            copy.wait()
        y_last = both(y_out, 1)
        for copy in moves:
            copy.wait()
        for q in range(S):
            o_out[q * hn : (q + 1) * hn, :] = o_buf[q].astype(F32).T
            for i in range(3):
                qkv_out[i, :, q * hn : (q + 1) * hn] = qkv_buf[q, :, i * hn : (i + 1) * hn].astype(F32)
        for copy in x_hop:
            copy.wait()
        x_last = both(x_out, 2)
        settle(got, 0, small_last)
        norm_out[...] = jnp.sum(got[:, :, :, :count, :], axis=(0, 1, 2))
        settle(y_out, 1, y_last)
        settle(x_out, 2, x_last)

    args = [x, y, *stats, bias, gateup, down, qkv, out]
    most = max(S, C) - 1
    home = (jax.ShapeDtypeStruct((T, n, D), BF), ANY)
    x, y, *rest = comm(
        kernel, S, C, number, "finish", args, [IN_VMEM] * len(args),
        [home, home]
        + [
            (jax.ShapeDtypeStruct(shape, F32), IN_VMEM)
            for shape in ((count, 128), (S, lines, 128), (nb, 2, S * fn), (S * fn, nb), (3, nb, S * hn), (S * hn, nb))
        ],
        [
            pltpu.VMEM((S, n, wide), BF), pltpu.VMEM((C, n, wide), BF), pltpu.VMEM((C, n, wide), BF),
            pltpu.VMEM((tall, D), F32), DMA((3, most)), DMA((3, most)), DMA((4,)),
            DMA((2, S - 1, pieces)), DMA((2, S - 1, pieces)), DMA((2, pieces)), DMA((3,)), DMA((3,)),
            DMA((many,)), DMA((many,)),
            pltpu.VMEM(qkv.shape, BF), pltpu.VMEM(out.shape, BF), DMA((2, S - 1)), DMA((2, S - 1)), DMA((2,)),
            pltpu.VMEM((T, C, S, tall, 128), F32),
        ],
    )
    return [x.reshape(T * n, D), y.reshape(T * n, D)] + rest


def ordered(D, S, C):
    return D // (S * C) % 128 == 0


def turn_tables(rows):
    feature = np.arange(128) % HEAD
    freq = np.where(feature < ROT, BASE ** (-2.0 * (feature % (ROT // 2)) / ROT), 0.0)
    near = np.arange(BLK)[:, None] * freq
    far = np.arange(0, rows, BLK)[:, None] * freq
    return [jnp.asarray(f(x), F32) for x in (near, far) for f in (np.cos, np.sin)]


def turn(x, i, tables, sign):
    cos, sin, cos_far, sin_far = tables
    far_cos, far_sin = cos_far[pl.ds(i, 1), :], sin_far[pl.ds(i, 1), :]
    cos_t = cos[...] * far_cos - sin[...] * far_sin
    sin_t = sin[...] * far_cos + cos[...] * far_sin
    ahead = lax.broadcasted_iota(jnp.int32, x.shape, 1) % HEAD < ROT // 2
    partner = jnp.where(ahead, -pltpu.roll(x, 128 - ROT // 2, 1), pltpu.roll(x, ROT // 2, 1))
    return x * cos_t + partner * (sin_t * sign)


def two_heads(x, left):
    zero = jnp.zeros_like(x)
    return [jnp.where(left, x, zero), jnp.where(left, zero, x)]


def block_of(rows):
    return next(size for size in (512, 256) if rows % size == 0)


def attend_kernel(
    first_ref, qkv_ref, cos_ref, sin_ref, cosf_ref, sinf_ref, begin_ref,
    qo_ref, ko_ref, vo_ref, o_ref, lse_ref, vt_ref,
):
    rows, wide = qo_ref.shape
    pairs, size = wide // 128, block_of(rows)
    tables = (cos_ref, sin_ref, cosf_ref, sinf_ref)
    left = lax.broadcasted_iota(jnp.int32, (size, 128), 1) < HEAD
    key_at = lax.broadcasted_iota(jnp.int32, (size, size), 0)
    query_at = lax.broadcasted_iota(jnp.int32, (1, size), 1)

    @pl.loop(0, rows // BLK)
    def _(i):
        r = pl.ds(pl.multiple_of(i * BLK, BLK), BLK)
        for t in range(pairs):
            w = pl.ds(t * 128, 128)
            q, k, v = (qkv_ref[r, pl.ds(part * wide + t * 128, 128)] for part in range(3))
            qo_ref[r, w] = turn(q, i, tables, 1.0).astype(BF) * jnp.asarray(HEAD**-0.5, BF)
            ko_ref[r, w] = turn(k, i, tables, 1.0).astype(BF)
            vo_ref[r, w] = v.astype(BF)
            vt_ref[w, r] = v.T.astype(BF)

    @pl.loop(0, rows // size)
    def _(i):
        r = pl.ds(pl.multiple_of(i * size, size), size)
        qs = sum((two_heads(qo_ref[r, pl.ds(t * 128, 128)], left) for t in range(pairs)), [])
        begin = begin_ref[0:1, r]
        here = query_at + i * size

        def step(j, carry):
            w = pl.ds(pl.multiple_of(j * size, size), size)
            key = key_at + j * size
            seen = (key <= here) & (key >= begin)
            out = []
            for h in range(2 * pairs):
                m, l, acc = carry[h]
                s = jnp.where(seen, mm(ko_ref[w, pl.ds(h // 2 * 128, 128)], qs[h], 1, 1), NEG)
                top = jnp.maximum(m, jnp.max(s, axis=0, keepdims=True))
                fade = jnp.exp(m - top)
                e = jnp.exp(s - top)
                acc = acc * fade + mm(vt_ref[pl.ds(h * HEAD, HEAD), w], e.astype(BF), 1, 0)
                out.append((top, l * fade + jnp.sum(e, axis=0, keepdims=True), acc))
            return tuple(out)

        start = (
            jnp.full((1, size), NEG, F32), jnp.zeros((1, size), F32), jnp.zeros((HEAD, size), F32)
        )
        done = lax.fori_loop(first_ref[i], i + 1, step, (start,) * (2 * pairs))
        for t in range(pairs):
            both = []
            for h in (2 * t, 2 * t + 1):
                m, l, acc = done[h]
                both.append(acc / l)
                lse_ref[h : h + 1, r] = m + jnp.log(l)
            o_ref[r, pl.ds(t * 128, 128)] = jnp.concatenate(both, axis=0).T.astype(BF)


def attend(qkv, begin):
    rows, wide = qkv.shape[0], qkv.shape[1] // 3
    size = block_of(rows)
    half = jax.ShapeDtypeStruct((rows, wide), BF)
    return pl.pallas_call(
        attend_kernel,
        in_specs=[pl.BlockSpec(memory_space=pltpu.SMEM)] + [IN_VMEM] * 6,
        out_specs=[IN_VMEM] * 5,
        out_shape=[half] * 4 + [jax.ShapeDtypeStruct((wide // HEAD, rows), F32)],
        scratch_shapes=[pltpu.VMEM((wide, rows), BF)],
        compiler_params=pltpu.CompilerParams(vmem_limit_bytes=62 << 20),
        name="attend",
    )(begin[0, ::size] // size, qkv, *turn_tables(rows), begin)


def attend_back_work(ins, out_ref, bias_ref, scratch, piece):
    q_ref, k_ref, v_ref, o_ref, do_ref, lse_ref, cos_ref, sin_ref, cosf_ref, sinf_ref, begin_ref = ins
    kt_ref, dq_ref, dk_ref, dv_ref = scratch
    rows, wide = q_ref.shape
    pairs, size = wide // 128, block_of(rows)
    tables = (cos_ref, sin_ref, cosf_ref, sinf_ref)
    left = lax.broadcasted_iota(jnp.int32, (size, 128), 1) < HEAD
    key_at = lax.broadcasted_iota(jnp.int32, (size, size), 0)
    query_at = lax.broadcasted_iota(jnp.int32, (1, size), 1)

    last = rows // size - 1
    first, stop = (0, last) if piece == 0 else (last, last + 1)

    def prepare(i):
        r = pl.ds(pl.multiple_of(i * BLK, BLK), BLK)
        for t in range(pairs):
            w = pl.ds(t * 128, 128)
            kt_ref[w, r] = k_ref[r, w].astype(F32).T.astype(BF)
            dk_ref[r, w] = jnp.zeros((BLK, 128), F32)
            dv_ref[r, w] = jnp.zeros((BLK, 128), F32)

    if piece == 0:
        pl.loop(0, rows // BLK)(prepare)

    @pl.loop(first, stop)
    def _(i):
        r = pl.ds(pl.multiple_of(i * size, size), size)
        qs, dos, deltas, lses = [], [], [], []
        for t in range(pairs):
            w = pl.ds(t * 128, 128)
            do = do_ref[r, w]
            qs += two_heads(q_ref[r, w], left)
            dos += two_heads(do, left)
            prod = (do.astype(F32) * o_ref[r, w].astype(F32)).T
            deltas += [jnp.sum(prod[:HEAD], axis=0, keepdims=True), jnp.sum(prod[HEAD:], axis=0, keepdims=True)]
            lses += [lse_ref[2 * t : 2 * t + 1, r], lse_ref[2 * t + 1 : 2 * t + 2, r]]
        begin = begin_ref[0:1, r]
        here = query_at + i * size

        def step(j, carry):
            w = pl.ds(pl.multiple_of(j * size, size), size)
            key = key_at + j * size
            seen = (key <= here) & (key >= begin)
            out = []
            for t in range(pairs):
                lanes = pl.ds(t * 128, 128)
                k, v = k_ref[w, lanes], v_ref[w, lanes]
                dk = dv = None
                for h in (2 * t, 2 * t + 1):
                    prob = jnp.exp(jnp.where(seen, mm(k, qs[h], 1, 1) - lses[h], NEG))
                    ds = (prob * (mm(v, dos[h], 1, 1) - deltas[h])).astype(BF)
                    out.append(carry[h] + mm(kt_ref[pl.ds(h * HEAD, HEAD), w], ds, 1, 0))
                    dk_h, dv_h = mm(ds, qs[h], 1, 0), mm(prob.astype(BF), dos[h], 1, 0)
                    dk, dv = (dk_h, dv_h) if dk is None else (dk + dk_h, dv + dv_h)
                dk_ref[w, lanes] += dk
                dv_ref[w, lanes] += dv
            return tuple(out)

        done = lax.fori_loop(0, i + 1, step, (jnp.zeros((HEAD, size), F32),) * (2 * pairs))
        for t in range(pairs):
            both = jnp.concatenate(done[2 * t : 2 * t + 2], axis=0)
            dq_ref[r, pl.ds(t * 128, 128)] = both.T * (HEAD**-0.5)

    if piece == 0:
        return
    bias_ref[...] = jnp.zeros_like(bias_ref)

    @pl.loop(0, rows // BLK)
    def _(i):
        r = pl.ds(pl.multiple_of(i * BLK, BLK), BLK)
        for t in range(pairs):
            w = pl.ds(t * 128, 128)
            for part, value in enumerate((turn(dq_ref[r, w], i, tables, -1.0), turn(dk_ref[r, w], i, tables, -1.0), dv_ref[r, w])):
                lanes = pl.ds(part * wide + t * 128, 128)
                value = value.astype(BF)
                out_ref[r, lanes] = value
                bias_ref[:, lanes] += jnp.sum(value.astype(F32), axis=0, keepdims=True)


def attend_back(S, C, T, number, q, k, v, o, do, lse, begin, act, wd, riders):
    rows, wide = q.shape
    K, D, n = act.shape[1], wd.shape[0], rows // (S * T)

    def kernel(ride, ins, outs, scratch):
        _, _, row, col = plane(S)
        greet(S, C, row + [col], other=True, axes=ride.axes)

        def meanwhile(piece):
            if piece == 0:
                ride.start()
            attend_back_work(ins[2:], outs[0], outs[1], scratch[:4], piece)

        sum_over_plane(S, T, ins[0], ins[1], outs[2], scratch[4:], meanwhile)
        ride.wait()

    args = [act.reshape(S * T, n, K), wd, q, k, v, o, do, lse, *turn_tables(rows), begin]
    return comm(
        kernel, S, C, number, "attend_back", args, [IN_VMEM] * len(args),
        [(jax.ShapeDtypeStruct((rows, 3 * wide), BF), IN_VMEM), (jax.ShapeDtypeStruct((1, 3 * wide), F32), IN_VMEM),
         (jax.ShapeDtypeStruct((n, D), F32), IN_VMEM)],
        [pltpu.VMEM((wide, rows), BF)] + [pltpu.VMEM((rows, wide), F32)] * 3 + sum_scratch(S, n, D),
        riders,
    )


def doc_begins(lengths_row, rows):
    row_ids = jnp.arange(rows, dtype=jnp.int32)
    ends = jnp.cumsum(lengths_row, dtype=jnp.int32)
    begins = ends - lengths_row
    inside = (row_ids[:, None] >= begins[None, :]) & (row_ids[:, None] < ends[None, :])
    return jnp.sum(jnp.where(inside, begins[None, :], 0), axis=1, dtype=jnp.int32)


def tiles_of(parts, lead):
    flat = jnp.concatenate([x.astype(F32).reshape(lead + (-1,)) for x in parts], axis=-1)
    flat = jnp.pad(flat, ((0, 0),) * len(lead) + ((0, 1024 - flat.shape[-1]),))
    return flat.reshape(lead + (8, 128))


def make_body(S, C, T):
    assert S == C

    def body(tokens, lengths, w_qkv, b_qkv, w_out, w_gateup, w_down, norm_gain, norm_bias, cotangent):
        p, z, c = lax.axis_index("shard"), lax.axis_index("ctx"), lax.axis_index("tp")
        R, D = tokens.shape
        n = R // T
        nb = D // (S * C)
        L = R * C

        def parts(x):
            return x.reshape(n, S, D // S).swapaxes(0, 1)

        def unpermute(x):
            return x.reshape(x.shape[0], C, S, nb).swapaxes(1, 2).reshape(x.shape)

        def after(x, y):
            return lax.optimization_barrier((x, y))

        def over_ctx(w):
            return lax.all_gather(w.reshape(S * nb, -1), "ctx", axis=0, tiled=True)

        def sum_ctx(g):
            g = lax.psum_scatter(g.astype(BF), "ctx", scatter_dimension=0, tiled=True)
            return g.reshape(S, nb, -1)

        hn = w_qkv.shape[3] // S
        fn = w_gateup.shape[3] // S
        heads = hn // HEAD
        nf = HEAD // (S * C)

        tile = tiles_of((norm_gain[0].reshape(-1), norm_bias[0].reshape(-1), b_qkv[0].reshape(-1), lengths[0]), ())
        raw = lax.all_gather(w_qkv[0].swapaxes(0, 1).reshape(3 * nb, -1), "ctx", axis=0, tiled=True)
        small, _, tok, cot, wo, wd, wg = exchange(
            S, C, T, 0,
            [("shard", w_gateup[0].reshape(nb, 2, S, fn).transpose(2, 0, 1, 3).reshape(S, nb, 2 * fn))],
            jnp.broadcast_to(tile, (C, S, 8, 128)),
            tokens,
            cotangent,
            [w_out[0], w_down[0]],
        )
        tok, wo = gather_columns(S, C, T, 1, tok, [("all", wo.reshape(S * nb, hn))])
        wo, wg, wd = wo.reshape(D, hn), over_ctx(wg), over_ctx(wd)

        small = lax.dynamic_index_in_dim(small, c, 0, keepdims=False).reshape(C, S, 1024)
        norms = small[:, :, : 4 * nb].reshape(C * S, 4, nb).swapaxes(0, 1).reshape(4, D)
        gains, shifts = norms[:2], norms[2:]
        nbias = 3 * S * heads * nf
        bias = small[:, :, 4 * nb : 4 * nb + nbias].reshape(C, S, 3, S * heads, nf)
        bias = lax.dynamic_slice_in_dim(bias, p * heads, heads, 3)
        bias = bias.transpose(2, 3, 1, 0, 4).reshape(1, 3 * hn)
        docs = lengths.shape[1]
        lengths_row = lax.dynamic_index_in_dim(
            small[0, :, 4 * nb + nbias : 4 * nb + nbias + docs], z, 0, keepdims=False
        ).astype(jnp.int32)
        begin = doc_begins(lengths_row, L)
        begin = begin[None, :]

        n1, qkv, wq = project(S, C, T, 12, tok, raw.reshape(C, 3, nb, -1), gains[:1], shifts[:1], bias)
        q, k, v, o, lse = attend(qkv, begin)
        mid, n2, cot = sum_norm_gather(S, C, T, 2, o, wo, tok, gains[1:], shifts[1:], [("ctx", cot)])
        gb, gu, act = gates(S, C, T, 4, n2, wg, cot)
        gw_down = mm(gb, act, 0, 0).astype(BF)
        wd, gw_down = after(wd, gw_down)
        gw_down = sum_ctx(gw_down)

        (dgu,) = by_rows(
            gates_back_kernel, "gates_back", [(True, gb), (False, wd), (True, gu)],
            [jax.ShapeDtypeStruct((L, 2 * fn), BF)],
        )
        gw_gateup = mm(n2, dgu, 0, 0).astype(BF)
        dgu, gw_gateup = after(dgu, gw_gateup)
        gw_gateup = sum_ctx(gw_gateup)
        dmid, gb1, stats2 = sum_back_gather(S, C, T, 6, dgu, wg, mid, gb, gains[1:])
        gw_out = mm(gb1, o, 0, 0).astype(BF)
        gb1, gw_out = after(gb1, gw_out)
        gw_out = sum_ctx(gw_out)
        do = mm(gb1, wo, 1, 0).astype(BF)
        dqkv, gbias, got, gw_down = attend_back(
            S, C, T, 11, q, k, v, o, do, lse, begin, act, wd, [("shard", gw_down)]
        )
        out = parts((mid + got).astype(BF))
        gw_qkv = mm(n1, dqkv, 0, 0).astype(BF)
        dqkv, gw_qkv = after(dqkv, gw_qkv)
        gw_qkv = sum_ctx(gw_qkv)
        low, stats1, out, gw_gateup = sum_back(
            S, C, T, 8, dqkv, wq, tok, dmid, gains[:1], [("shard", out), ("shard", gw_gateup)]
        )
        gtok, out, norms, gbias, gw_gateup, gw_down, gw_qkv, gw_out = finish(
            S, C, T, 10, low, out, [stats1, stats2], gbias, gw_gateup, gw_down, gw_qkv, gw_out
        )
        if not ordered(D, S, C):
            gtok, out = unpermute(gtok), unpermute(out)
        gtok = gtok.astype(F32)
        norms = lax.dynamic_slice_in_dim(norms, (z * S + p) * nb % 128, nb, 1) if nb % 128 else norms
        gbias = gbias.reshape(S, 3, heads, S * C, nf)
        gbias = lax.dynamic_index_in_dim(gbias, p * C + z, 3, keepdims=False)
        gbias = gbias.swapaxes(0, 1).reshape(b_qkv.shape)

        return (
            out,
            gtok,
            gw_qkv.swapaxes(0, 1).reshape(w_qkv.shape),
            gbias,
            gw_out.reshape(w_out.shape),
            gw_gateup.reshape(w_gateup.shape),
            gw_down.reshape(w_down.shape),
            norms[None, :2],
            norms[None, 2:],
        )

    return body


def solution(mesh):
    both = ("shard", "ctx")
    specs = (
        P(None, both, None, "tp"),
        P(None, None, "tp", both),
        P(None, "tp", both),
        P(None, both, None, "tp"),
        P(None, "tp", both),
        P(None, None, both),
        P(None, None, both),
    )
    return jax.shard_map(
        make_body(mesh.shape["shard"], mesh.shape["ctx"], mesh.shape["tp"]),
        mesh=mesh,
        in_specs=(P(both, None), P("shard", None)) + specs + (P(both, None),),
        out_specs=(P(both, None), P(both, None)) + specs,
        check_vma=False,
    )
```

```python
import functools

import jax
import jax.numpy as jnp
import numpy as np
from jax import lax
from jax.experimental import pallas as pl
from jax.experimental.pallas import tpu as pltpu
from jax.sharding import PartitionSpec as P

HEAD = 64
ROT = 16
EPS = 1e-05
NEG = -1e30
BASE = 10000.0
BF = jnp.bfloat16
F32 = jnp.float32
BLK = 256
MESH = pl.DeviceIdType.MESH
DMA = pltpu.SemaphoreType.DMA
ANY = pl.BlockSpec(memory_space=pl.ANY)
IN_VMEM = pl.BlockSpec(memory_space=pltpu.VMEM)


def mm(a, b, ca, cb):
    return lax.dot_general(a, b, (((ca,), (cb,)), ((), ())), preferred_element_type=F32)


def remote(src, dst, send, recv, where):
    return pltpu.make_async_remote_copy(
        src_ref=src, dst_ref=dst, send_sem=send, recv_sem=recv, device_id=where, device_id_type=MESH
    )


def here():
    return lax.axis_index("shard"), lax.axis_index("ctx"), lax.axis_index("tp")


class Riders:
    def __init__(self, S, C, riders):
        self.S, self.C = S, C
        self.axes = [axis for axis, _ in riders]
        self.arrays = [x for _, x in riders]
        self.shapes = [
            jax.ShapeDtypeStruct((C,) + x.shape if axis == "all" else x.shape, x.dtype) for axis, x in riders
        ]
        count, most = len(riders), max(S, C) - 1
        self.scratch = [DMA((count, most)), DMA((count, most)), DMA((count,))] if count else []

    def bind(self, ins, outs, sems):
        self.ins, self.outs, self.sems = ins, outs, sems

    def start(self):
        p, z, c = here()
        self.moves = []
        for n, axis in enumerate(self.axes):
            src, dst = self.ins[n], self.outs[n]
            send, recv, own = self.sems
            if axis == "tp":
                copies = [remote(src, dst, send.at[n, 0], recv.at[n, 0], {"tp": 1 - c})]
            elif axis == "all":
                copies = [
                    remote(src, dst.at[z], send.at[n, k - 1], recv.at[n, k - 1], {"ctx": (z + k) % self.C})
                    for k in range(1, self.C)
                ]
                copies.append(pltpu.make_async_copy(src, dst.at[z], own.at[n]))
            else:
                size, me = (self.S, p) if axis == "shard" else (self.C, z)
                copies = [
                    remote(src.at[(me + k) % size], dst.at[me], send.at[n, k - 1], recv.at[n, k - 1], {axis: (me + k) % size})
                    for k in range(1, size)
                ]
                copies.append(pltpu.make_async_copy(src.at[me], dst.at[me], own.at[n]))
            for copy in copies:
                copy.start()
            self.moves += copies

    def wait(self):
        for copy in self.moves:
            copy.wait()


def greet(S, C, mates=(), line=False, other=False, axes=()):
    p, z, c = here()
    peers = [{"shard": q} for q in ([(p + k) % S for k in range(1, S)] if "shard" in axes else mates)]
    if line or "ctx" in axes or "all" in axes:
        peers += [{"ctx": (z + k) % C} for k in range(1, C)]
    if other or "tp" in axes:
        peers.append({"tp": 1 - c})
    barrier = pltpu.get_barrier_semaphore()
    for where in peers:
        pl.semaphore_signal(barrier, inc=1, device_id=where, device_id_type=MESH)
    pl.semaphore_wait(barrier, len(peers))


def comm(kernel, S, C, number, name, args, in_specs, outs, scratch, riders=()):
    ride = Riders(S, C, riders)
    na, nr, no, ns = len(args), len(ride.axes), len(outs), len(scratch)

    def body(*refs):
        ins, refs = refs[:na], refs[na:]
        rins, refs = refs[:nr], refs[nr:]
        os, refs = refs[:no], refs[no:]
        routs, refs = refs[:nr], refs[nr:]
        ride.bind(rins, routs, refs[ns:])
        kernel(ride, ins, os, refs[:ns])

    return pl.pallas_call(
        body,
        out_shape=[shape for shape, _ in outs] + ride.shapes,
        in_specs=list(in_specs) + [IN_VMEM] * nr,
        out_specs=[spec for _, spec in outs] + [ANY] * nr,
        scratch_shapes=list(scratch) + ride.scratch,
        compiler_params=pltpu.CompilerParams(
            collective_id=number, has_side_effects=True, vmem_limit_bytes=62 << 20
        ),
        cost_estimate=pl.CostEstimate(flops=0, bytes_accessed=120_000_000, transcendentals=0),
        name=name,
    )(*args, *ride.arrays)


def exchange(S, C, T, number, riders, tiles, rows, beside, turned):
    R, D = rows.shape
    n, wide, nb = R // T, D // S, D // (S * C)
    pieces = S if ordered(D, S, C) else 1
    p, z, c = here()
    if pieces == 1:
        rows, beside = (
            lax.dynamic_slice_in_dim(x, c * n, n, 0).reshape(n, S, C, nb).transpose(2, 0, 1, 3).reshape(S, n, wide)
            for x in (rows, beside)
        )
    heights = [x.shape[0] // S for x in turned]

    def kernel(ride, ins, outs, scratch):
        tile, x_ref, y_ref, *raws = ins
        got, x_buf, x_out, y_buf, y_out, *turns = outs
        send, recv, bsend, brecv, own, hsend, hrecv, hown, zsend, zrecv, zown, wsend, wrecv, wown, *stages = scratch
        p, z, c = here()
        mates = [(p + k) % S for k in range(1, S)]
        everyone = [(i, j) for i in range(C) for j in range(S) if i or j]
        peers = [{"shard": (p + j) % S, "ctx": (z + i) % C} for i, j in everyone]
        barrier = pltpu.get_barrier_semaphore()
        for where in peers + [{"tp": 1 - c}]:
            pl.semaphore_signal(barrier, inc=1, device_id=where, device_id_type=MESH)
        pl.semaphore_wait(barrier, len(peers) + 1)

        def columns(ref, q, i):
            if pieces == 1:
                return ref.at[q]
            lanes = pl.ds(pl.multiple_of((i * C + q) * nb, 128), nb)
            return ref.at[pl.ds(pl.multiple_of(c * n, 16), n), lanes]

        def first_hop(ref, out, at):
            hop = []
            for i in range(pieces):
                dst = out.at[p, :, pl.ds(i * (wide // pieces), wide // pieces)]
                hop.append(pltpu.make_async_copy(columns(ref, p, i), dst, hown.at[at, i]))
                for k, q in enumerate(mates):
                    hop.append(
                        remote(columns(ref, q, i), dst, hsend.at[at, k, i], hrecv.at[at, k, i], {"shard": q})
                    )
            for copy in hop:
                copy.start()
            return hop

        x_hop = first_hop(x_ref, x_buf, 0)
        y_hop = first_hop(y_ref, y_buf, 1)
        local = pltpu.make_async_copy(tile.at[z, p], got.at[c, z, p], own)
        local.start()
        copies = []
        for at, (where, (i, j)) in enumerate(zip(peers, everyone)):
            q, g = (p + j) % S, (z + i) % C
            copies.append(remote(tile.at[g, q], got.at[c, z, p], send.at[at], recv.at[at], where))
            copies[-1].start()
        ride.start()
        moves = []
        for m, (raw, stage, out, height) in enumerate(zip(raws, stages, turns, heights)):
            for q in range(S):
                stage[q] = raw[q * height : (q + 1) * height, :].astype(F32).T.astype(BF)
            moves.append(pltpu.make_async_copy(stage.at[p], out.at[p], wown.at[m]))
            for k, q in enumerate(mates):
                moves.append(remote(stage.at[q], out.at[p], wsend.at[m, k], wrecv.at[m, k], {"shard": q}))
            for copy in moves[-S:]:
                copy.start()
        def second_hop(hop, buf, out, at):
            for copy in hop:
                copy.wait()
            line = [pltpu.make_async_copy(buf.at[z], out.at[z], zown.at[at])]
            for k in range(1, C):
                g = (z + k) % C
                line.append(remote(buf.at[g], out.at[z], zsend.at[at, k - 1], zrecv.at[at, k - 1], {"ctx": g}))
            for copy in line:
                copy.start()
            return line

        line = second_hop(x_hop, x_buf, x_out, 0)
        line += second_hop(y_hop, y_buf, y_out, 1)
        local.wait()
        for copy in copies:
            copy.wait()
        back = remote(got.at[c], got.at[c], bsend, brecv, {"tp": 1 - c})
        back.start()
        back.wait_send()
        remote(got.at[1 - c], got.at[1 - c], bsend, brecv, {"tp": 1 - c}).wait_recv()
        for copy in line + moves:
            copy.wait()
        ride.wait()

    count, m = C * S - 1, len(turned)
    part = jax.ShapeDtypeStruct((S, n, wide), rows.dtype)
    return comm(
        kernel, S, C, number, "exchange", [tiles, rows, beside, *turned],
        [IN_VMEM, ANY, ANY] + [IN_VMEM] * m,
        [(jax.ShapeDtypeStruct((T,) + tiles.shape, tiles.dtype), ANY), (part, IN_VMEM), (part, IN_VMEM), (part, IN_VMEM),
         (part, IN_VMEM)]
        + [(jax.ShapeDtypeStruct((S, nb, height), BF), ANY) for height in heights],
        [
            DMA((count,)), DMA((count,)), DMA, DMA, DMA,
            DMA((2, S - 1, pieces)), DMA((2, S - 1, pieces)), DMA((2, pieces)),
            DMA((2, C - 1)), DMA((2, C - 1)), DMA((2,)), DMA((m, S - 1)), DMA((m, S - 1)), DMA((m,)),
        ]
        + [pltpu.VMEM((S, nb, height), BF) for height in heights],
        riders,
    )


def plane(S):
    p, _, c = here()
    B = S // 2
    a, b = p // B, p % B
    return a, b, [a * B + (b + j) % B for j in range(1, B)], (1 - a) * B + b


def spread_sems(S):
    count = 4 + 4 * (S // 2 - 1)
    return [DMA((2 * count,)), DMA((2 * count,))]


def spread(S, own, region, send, recv, work=(None, None)):
    p, _, c = here()
    B = S // 2
    a, b, rows, col = plane(S)
    rows, col, other = [{"shard": q} for q in rows], {"shard": col}, {"tp": 1 - c}
    per = 4 + 4 * (B - 1)
    OWN, ROW, COL, VIA_COL, VIA_ROW = 0, 2, 2 + 2 * (B - 1), 4 + 2 * (B - 1), 4 + 3 * (B - 1)
    started = []

    def push(q, h, sem, where, first=False):
        view = region(q, h, c)
        copy = remote(own(h) if first else view, view, send.at[sem], recv.at[sem], where)
        copy.start()
        started.append(copy)

    def came(q, h, sem, core):
        view = region(q, h, core)
        remote(view, view, send.at[sem], recv.at[sem], other).wait_recv()

    for h in range(2):
        for j in range(1, B):
            push(p, h, ROW + 2 * (j - 1) + h, rows[j - 1], True)
    for h in (1, 0):
        push(p, h, COL + h, col, True)
    for h in range(2):
        push(p, h, per + OWN + h, other, True)

    def from_row(j, h):
        q = a * B + (b - j) % B
        came(q, h, ROW + 2 * (j - 1) + h, c)
        push(q, h, per + ROW + 2 * (j - 1) + h, other)
        return q

    def from_col(h):
        q = (1 - a) * B + b
        came(q, h, COL + h, c)
        push(q, h, per + COL + h, other)
        return q

    if work[0] is not None:
        work[0]()
    for j in range(1, B):
        q = from_row(j, 0)
        push(q, 0, VIA_COL + j - 1, col)
    q = from_col(1)
    for j in range(1, B):
        push(q, 1, VIA_ROW + j - 1, rows[j - 1])
    if work[1] is not None:
        work[1]()
    for j in range(1, B):
        from_row(j, 1)
    from_col(0)
    for j in range(1, B):
        q = (1 - a) * B + (b - j) % B
        came(q, 0, VIA_COL + j - 1, c)
        push(q, 0, per + VIA_COL + j - 1, other)
        came(q, 1, VIA_ROW + j - 1, c)
        push(q, 1, per + VIA_ROW + j - 1, other)
    for h in range(2):
        came(p, h, per + OWN + h, 1 - c)
        came((1 - a) * B + b, h, per + COL + h, 1 - c)
    for j in range(1, B):
        for h in range(2):
            came(a * B + (b - j) % B, h, per + ROW + 2 * (j - 1) + h, 1 - c)
        q = (1 - a) * B + (b - j) % B
        came(q, 0, per + VIA_COL + j - 1, 1 - c)
        came(q, 1, per + VIA_ROW + j - 1, 1 - c)
    for copy in started:
        copy.wait_send()


def gather_columns(S, C, T, number, x, riders=(), extra=None):
    _, n, wide = x.shape
    more, more_specs, more_outs, more_scratch, task = extra or ((), (), (), (), None)

    def kernel(ride, ins, outs, scratch):
        x_ref, out_ref = ins[0], outs[0]
        send, recv, own = scratch[:3]
        p, _, c = here()
        _, _, rows, col = plane(S)

        def region(q, h, core):
            part = pl.ds(pl.multiple_of(q * wide, 128), wide)
            return out_ref.at[pl.ds(h * (C // 2), C // 2), core, :, part]

        local = [
            pltpu.make_async_copy(x_ref.at[pl.ds(h * (C // 2), C // 2)], region(p, h, c), own.at[h]) for h in range(2)
        ]
        for copy in local:
            copy.start()
        if task is not None:
            task(ins[1:], outs[1:], scratch[3:], None)
        greet(S, C, rows + [col], other=True, axes=ride.axes)
        ride.start()
        work = [None, None]
        if task is not None:
            work = [functools.partial(task, ins[1:], outs[1:], scratch[3:], piece) for piece in range(2)]
        spread(S, lambda h: x_ref.at[pl.ds(h * (C // 2), C // 2)], region, send, recv, work)
        for copy in local:
            copy.wait()
        ride.wait()

    out, *rest = comm(
        kernel, S, C, number, "gather_columns", [x, *more], [IN_VMEM, *more_specs],
        [(jax.ShapeDtypeStruct((C, T, n, wide * S), x.dtype), ANY), *more_outs],
        spread_sems(S) + [DMA((2,)), *more_scratch], riders,
    )
    return [out.reshape(C * T * n, wide * S)] + rest


CHUNK = 512
ROWS = 32


def sum_scratch(S, n, D):
    half, B = n // 2, S // 2

    def vm(*shape):
        return pltpu.VMEM(shape, BF)

    return [
        vm(S, n, D), vm(S, n, D), vm(S, n, D), vm(B - 1, 2, half, D), vm(B, half, D),
        vm(B - 1, half, D), vm(half, D), vm(half, D), vm(B - 1, half, D),
        DMA((S,)), DMA((S,)), DMA((B - 1, 2)), DMA((B - 1, 2)), DMA((B,)), DMA((B,)), DMA((B,)), DMA((B,)),
    ]


def sum_over_plane(S, T, x_ref, w_ref, out_ref, scratch, meanwhile=None):
    away, sib, mine, row1, col1, row2, col2, to_col, to_row = scratch[:9]
    asend, arecv, rsend, rrecv, csend, crecv, fsend, frecv = scratch[9:]
    n, D = out_ref.shape
    half, B = n // 2, S // 2
    _, _, c = here()
    a, b, rows, col = plane(S)
    rows, col, other = [{"shard": q} for q in rows], {"shard": col}, {"tp": 1 - c}

    def chip(e):
        return ((a + e // B) % 2) * B + (b + e % B) % B

    def product(e, core, store):
        x = x_ref[chip(e) * T + core]

        def column(j, _):
            w = pl.ds(pl.multiple_of(j * CHUNK, CHUNK), CHUNK)
            store(w, mm(x, w_ref[w, :], 1, 1))
            return 0

        lax.fori_loop(0, D // CHUNK, column, 0)

    def to_other(e):
        return remote(away.at[e], sib.at[e], asend.at[e], arecv.at[e], other)

    def for_other(e):
        def store(w, value):
            away[e, :, w] = value.astype(BF)

        product(e, 1 - c, store)
        to_other(e).start()

    for_other(S - 1)
    top, low = pl.ds(0, half), pl.ds(half, half)
    started = []

    def push(src, dst, send, recv, where):
        copy = remote(src, dst, send, recv, where)
        copy.start()
        started.append(copy)

    for e in range(S - 1, -1, -1):
        if e:
            for_other(e - 1)
        to_other(e).wait()

        def store(w, value):
            value = value + sib[e, :, w].astype(F32)
            if e:
                mine[e, :, w] = value.astype(BF)
            else:
                out_ref[:, w] = value

        product(e, c, store)
        j = e % B
        if e > B:
            push(mine.at[e, top], row1.at[j - 1, 1], rsend.at[j - 1, 1], rrecv.at[j - 1, 1], rows[j - 1])
            push(mine.at[e, low], col1.at[j], csend.at[j], crecv.at[j], col)
        elif e == B:
            push(mine.at[e, low], col1.at[0], csend.at[0], crecv.at[0], col)
        elif e:
            push(mine.at[e, top], row1.at[j - 1, 0], rsend.at[j - 1, 0], rrecv.at[j - 1, 0], rows[j - 1])

    def came(ref, send, recv):
        remote(ref, ref, send, recv, other).wait_recv()

    if meanwhile is not None:
        meanwhile(0)
    total = mine[B, top, :].astype(F32)
    for j in range(1, B):
        came(row1.at[j - 1, 1], rsend.at[j - 1, 1], rrecv.at[j - 1, 1])
        total = total + row1[j - 1, 1].astype(F32)
    to_col[...] = total.astype(BF)
    push(to_col, col2, fsend.at[0], frecv.at[0], col)
    for j in range(1, B):
        came(col1.at[j], csend.at[j], crecv.at[j])
        to_row[j - 1] = (mine[j, low, :].astype(F32) + col1[j].astype(F32)).astype(BF)
        push(to_row.at[j - 1], row2.at[j - 1], fsend.at[j], frecv.at[j], rows[j - 1])
    if meanwhile is not None:
        meanwhile(1)
    came(col1.at[0], csend.at[0], crecv.at[0])
    upper, lower = out_ref[top, :], out_ref[low, :] + col1[0].astype(F32)
    for j in range(1, B):
        came(row1.at[j - 1, 0], rsend.at[j - 1, 0], rrecv.at[j - 1, 0])
        upper = upper + row1[j - 1, 0].astype(F32)
    came(col2, fsend.at[0], frecv.at[0])
    out_ref[top, :] = upper + col2[...].astype(F32)
    for j in range(1, B):
        came(row2.at[j - 1], fsend.at[j], frecv.at[j])
        lower = lower + row2[j - 1].astype(F32)
    out_ref[low, :] = lower
    for copy in started:
        copy.wait_send()


def project(S, C, T, number, tok, raw, gain, shift, bias):
    L, D = tok.shape
    _, parts, nb, wide = raw.shape
    hn = wide // S
    most = S - 1

    def kernel(ride, ins, outs, scratch):
        tok_ref, raw_ref, gain_ref, shift_ref, bias_ref = ins
        n_ref, out_ref, w_ref = outs
        send, recv, own = scratch
        p, _, _ = here()
        mates = [(p + k) % S for k in range(1, S)]
        greet(S, C, mates)

        def lanes(q):
            return pl.ds(pl.multiple_of(q * hn, 128), hn)

        copies = []
        for part in range(parts):
            dst = w_ref.at[:, p, :, pl.ds(part * hn, hn)]
            for k, q in enumerate(mates):
                copies.append(
                    remote(raw_ref.at[:, part, :, lanes(q)], dst, send.at[k, part], recv.at[k, part], {"shard": q})
                )
            copies.append(pltpu.make_async_copy(raw_ref.at[:, part, :, lanes(p)], dst, own.at[part]))
        for copy in copies:
            copy.start()

        def normed(r):
            n_ref[r, :] = (norm_of(tok_ref[r, :].astype(F32))[0] * gain_ref[...] + shift_ref[...]).astype(BF)

        row_blocks(L, normed)
        for copy in copies:
            copy.wait()
        w = w_ref[...].reshape(D, parts * hn)

        @pl.loop(0, L // BLK)
        def _(i):
            r = pl.ds(pl.multiple_of(i * BLK, BLK), BLK)
            out_ref[r, :] = mm(n_ref[r, :], w, 1, 0) + bias_ref[...]

    n, out, w = comm(
        kernel, S, C, number, "project", [tok, raw, gain, shift, bias], [IN_VMEM] * 5,
        [
            (jax.ShapeDtypeStruct((L, D), BF), IN_VMEM), (jax.ShapeDtypeStruct((L, parts * hn), F32), IN_VMEM),
            (jax.ShapeDtypeStruct((C, S, nb, parts * hn), BF), IN_VMEM),
        ],
        [DMA((most, parts)), DMA((most, parts)), DMA((parts,))],
    )
    return n, out, w.reshape(D, parts * hn)


def gates_back_kernel(gb_ref, wd_ref, gu_ref, dgu_ref):
    dact = mm(gb_ref[...], wd_ref[...], 1, 0)
    both, width = gu_ref[...], dact.shape[1]
    gate, up = both[:, :width], both[:, width:]
    s = jax.nn.sigmoid(gate)
    dgate = dact * up * s * (1.0 + gate * (1.0 - s))
    dgu_ref[...] = jnp.concatenate((dgate, dact * gate * s), axis=1).astype(BF)


def gates_work(ins, outs, scratch, piece):
    gu_ref, act_ref = outs
    n2_ref, wg_ref, sems = scratch
    if piece != 1:
        for i, (x, y) in enumerate(zip(ins, (n2_ref, wg_ref))):
            copy = pltpu.make_async_copy(x, y, sems.at[i])
            copy.wait() if piece == 0 else copy.start()
    if piece is None:
        return
    (rows, width), half = act_ref.shape, act_ref.shape[0] // BLK // 2

    @pl.loop(piece * half, piece * half + half)
    def _(i):
        r = pl.ds(pl.multiple_of(i * BLK, BLK), BLK)
        both = mm(n2_ref[r, :], wg_ref[...], 1, 0)
        gu_ref[r, :] = both
        gate, up = both[:, :width], both[:, width:]
        act_ref[r, :] = (gate * jax.nn.sigmoid(gate) * up).astype(BF)


def gates(S, C, T, number, n2, wg, x):
    L, width = n2.shape[0], wg.shape[1] // 2
    outs = [jax.ShapeDtypeStruct((L, 2 * width), F32), jax.ShapeDtypeStruct((L, width), BF)]
    return gather_columns(
        S, C, T, number, x, (),
        ([n2, wg], [ANY, ANY], [(shape, IN_VMEM) for shape in outs],
         [pltpu.VMEM(n2.shape, BF), pltpu.VMEM(wg.shape, BF), DMA((2,))], gates_work),
    )


def by_rows(kernel, name, arrays, outs):
    L = outs[0].shape[0]

    def spec(width):
        return pl.BlockSpec((BLK, width), lambda i: (i, 0))

    return pl.pallas_call(
        kernel,
        grid=(L // BLK,),
        in_specs=[spec(x.shape[1]) if rows else pl.BlockSpec(x.shape, lambda i: (0, 0)) for rows, x in arrays],
        out_specs=[spec(x.shape[1]) for x in outs],
        out_shape=outs,
        compiler_params=pltpu.CompilerParams(vmem_limit_bytes=62 << 20),
        name=name,
    )(*[x for _, x in arrays])


def row_blocks(n, work):
    @pl.loop(0, n // ROWS)
    def _(i):
        work(pl.ds(pl.multiple_of(i * ROWS, ROWS), ROWS))


def own_rows(T, x_ref, row_ref, sem):
    p, _, c = here()
    copy = pltpu.make_async_copy(x_ref.at[p * T + c], row_ref, sem)
    copy.start()
    return copy


def norm_of(v):
    center = v - jnp.mean(v, axis=-1, keepdims=True)
    inverse = lax.rsqrt(jnp.mean(center * center, axis=-1, keepdims=True) + EPS)
    return center * inverse, inverse


def norm_back(v, g, gain, stats_ref):
    normal, inverse = norm_of(v)
    e = g * gain
    stats_ref[0:1, :] += jnp.sum(g * normal, axis=0, keepdims=True)
    stats_ref[1:2, :] += jnp.sum(g, axis=0, keepdims=True)
    return inverse * (
        e - jnp.mean(e, axis=-1, keepdims=True) - normal * jnp.mean(e * normal, axis=-1, keepdims=True)
    )


def spread_rows(S, T, src, out_ref, send, recv, own):
    p, _, c = here()
    half = src.shape[0] // 2
    local = pltpu.make_async_copy(src, out_ref.at[p * T + c], own)
    local.start()
    spread(
        S,
        lambda h: src.at[pl.ds(h * half, half)],
        lambda q, h, core: out_ref.at[q * T + core, pl.ds(h * half, half)],
        send,
        recv,
    )
    local.wait()


def sum_norm_gather(S, C, T, number, x, w, residual, gain, shift, riders=()):
    L, K = x.shape
    D, n = w.shape[0], L // (S * T)

    def kernel(ride, ins, outs, scratch):
        x_ref, w_ref, all_ref, gain_ref, shift_ref = ins
        v_ref, out_ref = outs
        acc, low, send, recv, own, res_ref, sem = scratch[:7]
        _, _, rows, col = plane(S)
        rest = own_rows(T, all_ref, res_ref, sem)
        greet(S, C, rows + [col], other=True, axes=ride.axes)
        ride.start()
        sum_over_plane(S, T, x_ref, w_ref, acc, scratch[7:])
        rest.wait()

        def work(r):
            v = res_ref[r, :].astype(F32) + acc[r, :]
            v_ref[r, :] = v
            low[r, :] = (norm_of(v)[0] * gain_ref[...] + shift_ref[...]).astype(BF)

        row_blocks(n, work)
        spread_rows(S, T, low, out_ref, send, recv, own)
        ride.wait()

    v, out, *rest = comm(
        kernel, S, C, number, "sum_norm_gather", [x.reshape(S * T, n, K), w, residual.reshape(S * T, n, D), gain, shift],
        [IN_VMEM, IN_VMEM, ANY, IN_VMEM, IN_VMEM],
        [(jax.ShapeDtypeStruct((n, D), F32), IN_VMEM), (jax.ShapeDtypeStruct((S * T, n, D), BF), ANY)],
        [pltpu.VMEM((n, D), F32), pltpu.VMEM((n, D), BF)] + spread_sems(S)
        + [DMA, pltpu.VMEM((n, D), BF), DMA] + sum_scratch(S, n, D),
        riders,
    )
    return [v, out.reshape(L, D)] + rest


def sum_back_gather(S, C, T, number, x, w, v, residual, gain, riders=()):
    L, K = x.shape
    D, n = w.shape[0], L // (S * T)

    def kernel(ride, ins, outs, scratch):
        x_ref, w_ref, in_ref, all_ref, gain_ref = ins
        v_ref, out_ref, stats = outs
        acc, low, send, recv, own, res_ref, sem = scratch[:7]
        _, _, rows, col = plane(S)
        rest = own_rows(T, all_ref, res_ref, sem)
        greet(S, C, rows + [col], other=True, axes=ride.axes)
        ride.start()
        sum_over_plane(S, T, x_ref, w_ref, acc, scratch[7:])
        rest.wait()
        stats[...] = jnp.zeros_like(stats)

        def work(r):
            g = res_ref[r, :].astype(F32) + norm_back(in_ref[r, :], acc[r, :], gain_ref[...], stats)
            v_ref[r, :] = g
            low[r, :] = g.astype(BF)

        row_blocks(n, work)
        spread_rows(S, T, low, out_ref, send, recv, own)
        ride.wait()

    g, out, stats, *rest = comm(
        kernel, S, C, number, "sum_back_gather", [x.reshape(S * T, n, K), w, v, residual.reshape(S * T, n, D), gain],
        [IN_VMEM, IN_VMEM, IN_VMEM, ANY, IN_VMEM],
        [
            (jax.ShapeDtypeStruct((n, D), F32), IN_VMEM), (jax.ShapeDtypeStruct((S * T, n, D), BF), ANY),
            (jax.ShapeDtypeStruct((2, D), F32), IN_VMEM),
        ],
        [pltpu.VMEM((n, D), F32), pltpu.VMEM((n, D), BF)] + spread_sems(S)
        + [DMA, pltpu.VMEM((n, D), BF), DMA] + sum_scratch(S, n, D),
        riders,
    )
    return [g, out.reshape(L, D), stats] + rest


def sum_back(S, C, T, number, x, w, v, residual, gain, riders=()):
    L, K = x.shape
    D, n = w.shape[0], L // (S * T)

    def kernel(ride, ins, outs, scratch):
        x_ref, w_ref, all_ref, res_ref, gain_ref = ins
        low, stats = outs
        acc, in_ref, sem = scratch[:3]
        _, _, rows, col = plane(S)
        rest = own_rows(T, all_ref, in_ref, sem)
        greet(S, C, rows + [col], other=True, axes=ride.axes)
        ride.start()
        sum_over_plane(S, T, x_ref, w_ref, acc, scratch[3:])
        rest.wait()
        stats[...] = jnp.zeros_like(stats)

        def work(r):
            g = res_ref[r, :] + norm_back(in_ref[r, :].astype(F32), acc[r, :], gain_ref[...], stats)
            low[r, :] = g.astype(BF)

        row_blocks(n, work)
        ride.wait()

    return comm(
        kernel, S, C, number, "sum_back", [x.reshape(S * T, n, K), w, v.reshape(S * T, n, D), residual, gain],
        [IN_VMEM, IN_VMEM, ANY, IN_VMEM, IN_VMEM],
        [(jax.ShapeDtypeStruct((n, D), BF), IN_VMEM), (jax.ShapeDtypeStruct((2, D), F32), IN_VMEM)],
        [pltpu.VMEM((n, D), F32), pltpu.VMEM((n, D), BF), DMA] + sum_scratch(S, n, D),
        riders,
    )


def finish(S, C, T, number, x, y, stats, bias, qkv, out):
    n, D = x.shape
    hn = out.shape[2]
    wide, lines = D // S, bias.shape[1] // 128
    nb = D // (S * C)
    count = sum(z.shape[0] for z in stats)
    tall = -(-(count + lines) // 8) * 8
    many = C * S - 1
    pieces = S if ordered(D, S, C) else 1

    def kernel(ride, ins, outs, scratch):
        x_ref, y_ref, stat_refs, bias_ref = ins[0], ins[1], ins[2:-3], ins[-3]
        qkv_ref, o_ref = ins[-2:]
        x_out, y_out, norm_out, bias_out, qkv_out, o_out = outs
        xbuf, xbuf2, ybuf2, tile, send, recv, own, psend, precv, pown, lsend, lrecv, tsend, trecv = scratch[:14]
        qkv_buf, o_buf, gsend, grecv, gown, got = scratch[14:]
        p, z, c = here()
        other = {"tp": 1 - c}
        everyone = [(i, j) for i in range(C) for j in range(S) if i or j]
        peers = [{"shard": (p + j) % S, "ctx": (z + i) % C} for i, j in everyone]
        barrier = pltpu.get_barrier_semaphore()
        for where in peers + [other]:
            pl.semaphore_signal(barrier, inc=1, device_id=where, device_id_type=MESH)
        pl.semaphore_wait(barrier, len(peers) + 1)

        def part(q):
            return pl.ds(pl.multiple_of(q * wide, 128), wide)

        def turn_over(source, target, at, size, me, axis):
            hop = [pltpu.make_async_copy(source(me), target, own.at[at])]
            for k in range(1, size):
                q = (me + k) % size
                hop.append(remote(source(q), target, send.at[at, k - 1], recv.at[at, k - 1], {axis: q}))
            for copy in hop:
                copy.start()
            return hop

        def arrive(buf, out, at):
            hop = []
            for i in range(pieces):
                src = pl.ds(i * (wide // pieces), wide // pieces)
                first = (i * C + p) * nb if pieces > 1 else p * wide
                dst = out.at[c, :, pl.ds(pl.multiple_of(first, 128), wide // pieces)]
                hop.append(pltpu.make_async_copy(buf.at[p, :, src], dst, pown.at[at, i]))
                for k in range(1, S):
                    q = (p + k) % S
                    hop.append(
                        remote(buf.at[q, :, src], dst, psend.at[at, k - 1, i], precv.at[at, k - 1, i], {"shard": q})
                    )
            for copy in hop:
                copy.start()
            return hop

        def both(ref, at):
            copy = remote(ref.at[c], ref.at[c], lsend.at[at], lrecv.at[at], other)
            copy.start()
            return copy

        def settle(ref, at, copy):
            copy.wait_send()
            remote(ref.at[1 - c], ref.at[1 - c], lsend.at[at], lrecv.at[at], other).wait_recv()

        x_hop = turn_over(lambda q: x_ref.at[:, part(q)], xbuf.at[p], 0, S, p, "shard")
        y_hop = turn_over(lambda q: y_ref.at[q], ybuf2.at[z], 1, C, z, "ctx")
        moves = []
        for i, (src, dst) in enumerate(((qkv_ref, qkv_buf), (o_ref, o_buf))):
            moves.append(pltpu.make_async_copy(src.at[p], dst.at[p], gown.at[i]))
            for k in range(1, S):
                q = (p + k) % S
                moves.append(remote(src.at[q], dst.at[p], gsend.at[i, k - 1], grecv.at[i, k - 1], {"shard": q}))
        for copy in moves:
            copy.start()
        tile[...] = jnp.zeros_like(tile)
        at = count
        for i, ref in enumerate(stat_refs):
            for j in range(2):
                tile[j * len(stat_refs) + i : j * len(stat_refs) + i + 1, :] = ref[j : j + 1, :]
        for k in range(lines):
            for block in range(D // 128):
                tile[at + k : at + k + 1, pl.ds(block * 128, 128)] = bias_ref[:, pl.ds(k * 128, 128)]

        def columns(g, q):
            return tile.at[:, pl.ds(pl.multiple_of((g * S + q) * nb // 128 * 128, 128), 128)]

        small = [pltpu.make_async_copy(columns(z, p), got.at[c, z, p], own.at[3])]
        for k, (where, (i, j)) in enumerate(zip(peers, everyone)):
            small.append(
                remote(columns((z + i) % C, (p + j) % S), got.at[c, z, p], tsend.at[k], trecv.at[k], where)
            )
        for copy in small:
            copy.start()
        for copy in x_hop:
            copy.wait()
        x_hop = turn_over(lambda q: xbuf.at[q], xbuf2.at[z], 2, C, z, "ctx")
        for copy in y_hop:
            copy.wait()
        y_hop = arrive(ybuf2, y_out, 0)
        for copy in small:
            copy.wait()
        small_last = both(got, 0)
        bias_out[...] = jnp.sum(got[c, :, :, count : count + lines, :], axis=0)
        for copy in x_hop:
            copy.wait()
        x_hop = arrive(xbuf2, x_out, 1)
        for copy in y_hop:
            copy.wait()
        y_last = both(y_out, 1)
        for copy in moves:
            copy.wait()
        for q in range(S):
            o_out[q * hn : (q + 1) * hn, :] = o_buf[q].astype(F32).T
            for i in range(3):
                qkv_out[i, :, q * hn : (q + 1) * hn] = qkv_buf[q, :, i * hn : (i + 1) * hn].astype(F32)
        for copy in x_hop:
            copy.wait()
        x_last = both(x_out, 2)
        settle(got, 0, small_last)
        norm_out[...] = jnp.sum(got[:, :, :, :count, :], axis=(0, 1, 2))
        settle(y_out, 1, y_last)
        settle(x_out, 2, x_last)

    args = [x, y, *stats, bias, qkv, out]
    most = max(S, C) - 1
    home = (jax.ShapeDtypeStruct((T, n, D), BF), ANY)
    x, y, *rest = comm(
        kernel, S, C, number, "finish", args, [IN_VMEM] * len(args),
        [home, home]
        + [
            (jax.ShapeDtypeStruct(shape, F32), IN_VMEM)
            for shape in ((count, 128), (S, lines, 128), (3, nb, S * hn), (S * hn, nb))
        ],
        [
            pltpu.VMEM((S, n, wide), BF), pltpu.VMEM((C, n, wide), BF), pltpu.VMEM((C, n, wide), BF),
            pltpu.VMEM((tall, D), F32), DMA((3, most)), DMA((3, most)), DMA((4,)),
            DMA((2, S - 1, pieces)), DMA((2, S - 1, pieces)), DMA((2, pieces)), DMA((3,)), DMA((3,)),
            DMA((many,)), DMA((many,)),
            pltpu.VMEM(qkv.shape, BF), pltpu.VMEM(out.shape, BF), DMA((2, S - 1)), DMA((2, S - 1)), DMA((2,)),
            pltpu.VMEM((T, C, S, tall, 128), F32),
        ],
    )
    return [x.reshape(T * n, D), y.reshape(T * n, D)] + rest


def final_kernel(gateup_ref, down_ref, gateup_out, down_out):
    S, _, fn = down_ref.shape
    for q in range(S):
        down_out[q * fn : (q + 1) * fn, :] = down_ref[q].astype(F32).T
        for i in range(2):
            gateup_out[:, i, q * fn : (q + 1) * fn] = gateup_ref[q, :, i * fn : (i + 1) * fn].astype(F32)


def final(gateup, down):
    S, nb, fn = down.shape
    return pl.pallas_call(
        final_kernel,
        in_specs=[IN_VMEM] * 2,
        out_specs=[IN_VMEM] * 2,
        out_shape=[jax.ShapeDtypeStruct((nb, 2, S * fn), F32), jax.ShapeDtypeStruct((S * fn, nb), F32)],
        compiler_params=pltpu.CompilerParams(vmem_limit_bytes=62 << 20),
        name="final",
    )(gateup, down)


def ordered(D, S, C):
    return D // (S * C) % 128 == 0


def turn_tables(rows):
    feature = np.arange(128) % HEAD
    freq = np.where(feature < ROT, BASE ** (-2.0 * (feature % (ROT // 2)) / ROT), 0.0)
    near = np.arange(BLK)[:, None] * freq
    far = np.arange(0, rows, BLK)[:, None] * freq
    return [jnp.asarray(f(x), F32) for x in (near, far) for f in (np.cos, np.sin)]


def turn(x, i, tables, sign):
    cos, sin, cos_far, sin_far = tables
    far_cos, far_sin = cos_far[pl.ds(i, 1), :], sin_far[pl.ds(i, 1), :]
    cos_t = cos[...] * far_cos - sin[...] * far_sin
    sin_t = sin[...] * far_cos + cos[...] * far_sin
    ahead = lax.broadcasted_iota(jnp.int32, x.shape, 1) % HEAD < ROT // 2
    partner = jnp.where(ahead, -pltpu.roll(x, 128 - ROT // 2, 1), pltpu.roll(x, ROT // 2, 1))
    return x * cos_t + partner * (sin_t * sign)


def two_heads(x, left):
    zero = jnp.zeros_like(x)
    return [jnp.where(left, x, zero), jnp.where(left, zero, x)]


def block_of(rows):
    return next(size for size in (512, 256) if rows % size == 0)


def attend_kernel(
    first_ref, qkv_ref, cos_ref, sin_ref, cosf_ref, sinf_ref, begin_ref,
    qo_ref, ko_ref, vo_ref, o_ref, lse_ref, vt_ref,
):
    rows, wide = qo_ref.shape
    pairs, size = wide // 128, block_of(rows)
    tables = (cos_ref, sin_ref, cosf_ref, sinf_ref)
    left = lax.broadcasted_iota(jnp.int32, (size, 128), 1) < HEAD
    key_at = lax.broadcasted_iota(jnp.int32, (size, size), 0)
    query_at = lax.broadcasted_iota(jnp.int32, (1, size), 1)

    @pl.loop(0, rows // BLK)
    def _(i):
        r = pl.ds(pl.multiple_of(i * BLK, BLK), BLK)
        for t in range(pairs):
            w = pl.ds(t * 128, 128)
            q, k, v = (qkv_ref[r, pl.ds(part * wide + t * 128, 128)] for part in range(3))
            qo_ref[r, w] = turn(q, i, tables, 1.0).astype(BF) * jnp.asarray(HEAD**-0.5, BF)
            ko_ref[r, w] = turn(k, i, tables, 1.0).astype(BF)
            vo_ref[r, w] = v.astype(BF)
            vt_ref[w, r] = v.T.astype(BF)

    @pl.loop(0, rows // size)
    def _(i):
        r = pl.ds(pl.multiple_of(i * size, size), size)
        qs = sum((two_heads(qo_ref[r, pl.ds(t * 128, 128)], left) for t in range(pairs)), [])
        begin = begin_ref[0:1, r]
        here = query_at + i * size

        def step(j, carry):
            w = pl.ds(pl.multiple_of(j * size, size), size)
            key = key_at + j * size
            seen = (key <= here) & (key >= begin)
            out = []
            for h in range(2 * pairs):
                m, l, acc = carry[h]
                s = jnp.where(seen, mm(ko_ref[w, pl.ds(h // 2 * 128, 128)], qs[h], 1, 1), NEG)
                top = jnp.maximum(m, jnp.max(s, axis=0, keepdims=True))
                fade = jnp.exp(m - top)
                e = jnp.exp(s - top)
                acc = acc * fade + mm(vt_ref[pl.ds(h * HEAD, HEAD), w], e.astype(BF), 1, 0)
                out.append((top, l * fade + jnp.sum(e, axis=0, keepdims=True), acc))
            return tuple(out)

        start = (
            jnp.full((1, size), NEG, F32), jnp.zeros((1, size), F32), jnp.zeros((HEAD, size), F32)
        )
        done = lax.fori_loop(first_ref[i], i + 1, step, (start,) * (2 * pairs))
        for t in range(pairs):
            both = []
            for h in (2 * t, 2 * t + 1):
                m, l, acc = done[h]
                both.append(acc / l)
                lse_ref[h : h + 1, r] = m + jnp.log(l)
            o_ref[r, pl.ds(t * 128, 128)] = jnp.concatenate(both, axis=0).T.astype(BF)


def attend(qkv, begin):
    rows, wide = qkv.shape[0], qkv.shape[1] // 3
    size = block_of(rows)
    half = jax.ShapeDtypeStruct((rows, wide), BF)
    return pl.pallas_call(
        attend_kernel,
        in_specs=[pl.BlockSpec(memory_space=pltpu.SMEM)] + [IN_VMEM] * 6,
        out_specs=[IN_VMEM] * 5,
        out_shape=[half] * 4 + [jax.ShapeDtypeStruct((wide // HEAD, rows), F32)],
        scratch_shapes=[pltpu.VMEM((wide, rows), BF)],
        compiler_params=pltpu.CompilerParams(vmem_limit_bytes=62 << 20),
        name="attend",
    )(begin[0, ::size] // size, qkv, *turn_tables(rows), begin)


def attend_back_work(ins, out_ref, bias_ref, scratch, piece):
    q_ref, k_ref, v_ref, o_ref, do_ref, lse_ref, cos_ref, sin_ref, cosf_ref, sinf_ref, begin_ref = ins
    kt_ref, dq_ref, dk_ref, dv_ref = scratch
    rows, wide = q_ref.shape
    pairs, size = wide // 128, block_of(rows)
    tables = (cos_ref, sin_ref, cosf_ref, sinf_ref)
    left = lax.broadcasted_iota(jnp.int32, (size, 128), 1) < HEAD
    key_at = lax.broadcasted_iota(jnp.int32, (size, size), 0)
    query_at = lax.broadcasted_iota(jnp.int32, (1, size), 1)

    last = rows // size - 1
    first, stop = (0, last) if piece == 0 else (last, last + 1)

    def prepare(i):
        r = pl.ds(pl.multiple_of(i * BLK, BLK), BLK)
        for t in range(pairs):
            w = pl.ds(t * 128, 128)
            kt_ref[w, r] = k_ref[r, w].astype(F32).T.astype(BF)
            dk_ref[r, w] = jnp.zeros((BLK, 128), F32)
            dv_ref[r, w] = jnp.zeros((BLK, 128), F32)

    if piece == 0:
        pl.loop(0, rows // BLK)(prepare)

    @pl.loop(first, stop)
    def _(i):
        r = pl.ds(pl.multiple_of(i * size, size), size)
        qs, dos, deltas, lses = [], [], [], []
        for t in range(pairs):
            w = pl.ds(t * 128, 128)
            do = do_ref[r, w]
            qs += two_heads(q_ref[r, w], left)
            dos += two_heads(do, left)
            prod = (do.astype(F32) * o_ref[r, w].astype(F32)).T
            deltas += [jnp.sum(prod[:HEAD], axis=0, keepdims=True), jnp.sum(prod[HEAD:], axis=0, keepdims=True)]
            lses += [lse_ref[2 * t : 2 * t + 1, r], lse_ref[2 * t + 1 : 2 * t + 2, r]]
        begin = begin_ref[0:1, r]
        here = query_at + i * size

        def step(j, carry):
            w = pl.ds(pl.multiple_of(j * size, size), size)
            key = key_at + j * size
            seen = (key <= here) & (key >= begin)
            out = []
            for t in range(pairs):
                lanes = pl.ds(t * 128, 128)
                k, v = k_ref[w, lanes], v_ref[w, lanes]
                dk = dv = None
                for h in (2 * t, 2 * t + 1):
                    prob = jnp.exp(jnp.where(seen, mm(k, qs[h], 1, 1) - lses[h], NEG))
                    ds = (prob * (mm(v, dos[h], 1, 1) - deltas[h])).astype(BF)
                    out.append(carry[h] + mm(kt_ref[pl.ds(h * HEAD, HEAD), w], ds, 1, 0))
                    dk_h, dv_h = mm(ds, qs[h], 1, 0), mm(prob.astype(BF), dos[h], 1, 0)
                    dk, dv = (dk_h, dv_h) if dk is None else (dk + dk_h, dv + dv_h)
                dk_ref[w, lanes] += dk
                dv_ref[w, lanes] += dv
            return tuple(out)

        done = lax.fori_loop(0, i + 1, step, (jnp.zeros((HEAD, size), F32),) * (2 * pairs))
        for t in range(pairs):
            both = jnp.concatenate(done[2 * t : 2 * t + 2], axis=0)
            dq_ref[r, pl.ds(t * 128, 128)] = both.T * (HEAD**-0.5)

    if piece == 0:
        return
    bias_ref[...] = jnp.zeros_like(bias_ref)

    @pl.loop(0, rows // BLK)
    def _(i):
        r = pl.ds(pl.multiple_of(i * BLK, BLK), BLK)
        for t in range(pairs):
            w = pl.ds(t * 128, 128)
            for part, value in enumerate((turn(dq_ref[r, w], i, tables, -1.0), turn(dk_ref[r, w], i, tables, -1.0), dv_ref[r, w])):
                lanes = pl.ds(part * wide + t * 128, 128)
                value = value.astype(BF)
                out_ref[r, lanes] = value
                bias_ref[:, lanes] += jnp.sum(value.astype(F32), axis=0, keepdims=True)


def attend_back(S, C, T, number, q, k, v, o, do, lse, begin, act, wd, riders):
    rows, wide = q.shape
    K, D, n = act.shape[1], wd.shape[0], rows // (S * T)

    def kernel(ride, ins, outs, scratch):
        _, _, row, col = plane(S)
        greet(S, C, row + [col], other=True, axes=ride.axes)

        def meanwhile(piece):
            if piece == 0:
                ride.start()
            attend_back_work(ins[2:], outs[0], outs[1], scratch[:4], piece)

        sum_over_plane(S, T, ins[0], ins[1], outs[2], scratch[4:], meanwhile)
        ride.wait()

    args = [act.reshape(S * T, n, K), wd, q, k, v, o, do, lse, *turn_tables(rows), begin]
    return comm(
        kernel, S, C, number, "attend_back", args, [IN_VMEM] * len(args),
        [(jax.ShapeDtypeStruct((rows, 3 * wide), BF), IN_VMEM), (jax.ShapeDtypeStruct((1, 3 * wide), F32), IN_VMEM),
         (jax.ShapeDtypeStruct((n, D), F32), IN_VMEM)],
        [pltpu.VMEM((wide, rows), BF)] + [pltpu.VMEM((rows, wide), F32)] * 3 + sum_scratch(S, n, D),
        riders,
    )


def doc_begins(lengths_row, rows):
    row_ids = jnp.arange(rows, dtype=jnp.int32)
    ends = jnp.cumsum(lengths_row, dtype=jnp.int32)
    begins = ends - lengths_row
    inside = (row_ids[:, None] >= begins[None, :]) & (row_ids[:, None] < ends[None, :])
    return jnp.sum(jnp.where(inside, begins[None, :], 0), axis=1, dtype=jnp.int32)


def tiles_of(parts, lead):
    flat = jnp.concatenate([x.astype(F32).reshape(lead + (-1,)) for x in parts], axis=-1)
    flat = jnp.pad(flat, ((0, 0),) * len(lead) + ((0, 1024 - flat.shape[-1]),))
    return flat.reshape(lead + (8, 128))


def make_body(S, C, T):
    assert S == C

    def body(tokens, lengths, w_qkv, b_qkv, w_out, w_gateup, w_down, norm_gain, norm_bias, cotangent):
        p, z, c = lax.axis_index("shard"), lax.axis_index("ctx"), lax.axis_index("tp")
        R, D = tokens.shape
        n = R // T
        nb = D // (S * C)
        L = R * C

        def parts(x):
            return x.reshape(n, S, D // S).swapaxes(0, 1)

        def unpermute(x):
            return x.reshape(x.shape[0], C, S, nb).swapaxes(1, 2).reshape(x.shape)

        def after(x, y):
            return lax.optimization_barrier((x, y))

        def over_ctx(w):
            return lax.all_gather(w.reshape(S * nb, -1), "ctx", axis=0, tiled=True)

        def sum_ctx(g):
            g = lax.psum_scatter(g.astype(BF), "ctx", scatter_dimension=0, tiled=True)
            return g.reshape(S, nb, -1)

        hn = w_qkv.shape[3] // S
        fn = w_gateup.shape[3] // S
        heads = hn // HEAD
        nf = HEAD // (S * C)

        tile = tiles_of((norm_gain[0].reshape(-1), norm_bias[0].reshape(-1), b_qkv[0].reshape(-1), lengths[0]), ())
        raw = lax.all_gather(w_qkv[0].swapaxes(0, 1).reshape(3 * nb, -1), "ctx", axis=0, tiled=True)
        small, _, tok, _, cot, wo, wd, wg = exchange(
            S, C, T, 0,
            [("shard", w_gateup[0].reshape(nb, 2, S, fn).transpose(2, 0, 1, 3).reshape(S, nb, 2 * fn))],
            jnp.broadcast_to(tile, (C, S, 8, 128)),
            tokens,
            cotangent,
            [w_out[0], w_down[0]],
        )
        tok, wo = gather_columns(S, C, T, 1, tok, [("all", wo.reshape(S * nb, hn))])
        wo, wg, wd = wo.reshape(D, hn), over_ctx(wg), over_ctx(wd)

        small = lax.dynamic_index_in_dim(small, c, 0, keepdims=False).reshape(C, S, 1024)
        norms = small[:, :, : 4 * nb].reshape(C * S, 4, nb).swapaxes(0, 1).reshape(4, D)
        gains, shifts = norms[:2], norms[2:]
        nbias = 3 * S * heads * nf
        bias = small[:, :, 4 * nb : 4 * nb + nbias].reshape(C, S, 3, S * heads, nf)
        bias = lax.dynamic_slice_in_dim(bias, p * heads, heads, 3)
        bias = bias.transpose(2, 3, 1, 0, 4).reshape(1, 3 * hn)
        docs = lengths.shape[1]
        lengths_row = lax.dynamic_index_in_dim(
            small[0, :, 4 * nb + nbias : 4 * nb + nbias + docs], z, 0, keepdims=False
        ).astype(jnp.int32)
        begin = doc_begins(lengths_row, L)
        begin = begin[None, :]

        n1, qkv, wq = project(S, C, T, 12, tok, raw.reshape(C, 3, nb, -1), gains[:1], shifts[:1], bias)
        q, k, v, o, lse = attend(qkv, begin)
        mid, n2 = sum_norm_gather(S, C, T, 2, o, wo, tok, gains[1:], shifts[1:])
        gb, gu, act = gates(S, C, T, 4, n2, wg, cot)
        gw_down = mm(gb, act, 0, 0).astype(BF)
        wd, gw_down = after(wd, gw_down)
        gw_down = sum_ctx(gw_down)

        (dgu,) = by_rows(
            gates_back_kernel, "gates_back", [(True, gb), (False, wd), (True, gu)],
            [jax.ShapeDtypeStruct((L, 2 * fn), BF)],
        )
        gw_gateup = mm(n2, dgu, 0, 0).astype(BF)
        dgu, gw_gateup = after(dgu, gw_gateup)
        gw_gateup = sum_ctx(gw_gateup)
        dmid, gb1, stats2 = sum_back_gather(S, C, T, 6, dgu, wg, mid, gb, gains[1:])
        gw_out = mm(gb1, o, 0, 0).astype(BF)
        gb1, gw_out = after(gb1, gw_out)
        gw_out = sum_ctx(gw_out)
        do = mm(gb1, wo, 1, 0).astype(BF)
        dqkv, gbias, got, gw_down = attend_back(
            S, C, T, 11, q, k, v, o, do, lse, begin, act, wd, [("shard", gw_down)]
        )
        out = parts((mid + got).astype(BF))
        gw_qkv = mm(n1, dqkv, 0, 0).astype(BF)
        dqkv, gw_qkv = after(dqkv, gw_qkv)
        gw_qkv = sum_ctx(gw_qkv)
        low, stats1, out, gw_gateup = sum_back(
            S, C, T, 8, dqkv, wq, tok, dmid, gains[:1], [("shard", out), ("shard", gw_gateup)]
        )
        low, gw_gateup, gw_down = lax.optimization_barrier((low, *final(gw_gateup, gw_down)))
        gtok, out, norms, gbias, gw_qkv, gw_out = finish(
            S, C, T, 10, low, out, [stats1, stats2], gbias, gw_qkv, gw_out
        )
        if not ordered(D, S, C):
            gtok, out = unpermute(gtok), unpermute(out)
        gtok = gtok.astype(F32)
        norms = lax.dynamic_slice_in_dim(norms, (z * S + p) * nb % 128, nb, 1) if nb % 128 else norms
        gbias = gbias.reshape(S, 3, heads, S * C, nf)
        gbias = lax.dynamic_index_in_dim(gbias, p * C + z, 3, keepdims=False)
        gbias = gbias.swapaxes(0, 1).reshape(b_qkv.shape)

        return (
            out,
            gtok,
            gw_qkv.swapaxes(0, 1).reshape(w_qkv.shape),
            gbias,
            gw_out.reshape(w_out.shape),
            gw_gateup.reshape(w_gateup.shape),
            gw_down.reshape(w_down.shape),
            norms[None, :2],
            norms[None, 2:],
        )

    return body


def solution(mesh):
    both = ("shard", "ctx")
    specs = (
        P(None, both, None, "tp"),
        P(None, None, "tp", both),
        P(None, "tp", both),
        P(None, both, None, "tp"),
        P(None, "tp", both),
        P(None, None, both),
        P(None, None, both),
    )
    return jax.shard_map(
        make_body(mesh.shape["shard"], mesh.shape["ctx"], mesh.shape["tp"]),
        mesh=mesh,
        in_specs=(P(both, None), P("shard", None)) + specs + (P(both, None),),
        out_specs=(P(both, None), P(both, None)) + specs,
        check_vma=False,
    )
```

```python
import functools

import jax
import jax.numpy as jnp
import numpy as np
from jax import lax
from jax.experimental import pallas as pl
from jax.experimental.pallas import tpu as pltpu
from jax.sharding import PartitionSpec as P

HEAD = 64
ROT = 16
EPS = 1e-05
NEG = -1e30
BASE = 10000.0
BF = jnp.bfloat16
F32 = jnp.float32
BLK = 256
MESH = pl.DeviceIdType.MESH
DMA = pltpu.SemaphoreType.DMA
ANY = pl.BlockSpec(memory_space=pl.ANY)
IN_VMEM = pl.BlockSpec(memory_space=pltpu.VMEM)


def mm(a, b, ca, cb):
    return lax.dot_general(a, b, (((ca,), (cb,)), ((), ())), preferred_element_type=F32)


def remote(src, dst, send, recv, where):
    return pltpu.make_async_remote_copy(
        src_ref=src, dst_ref=dst, send_sem=send, recv_sem=recv, device_id=where, device_id_type=MESH
    )


def here():
    return lax.axis_index("shard"), lax.axis_index("ctx"), lax.axis_index("tp")


class Riders:
    def __init__(self, S, C, riders):
        self.S, self.C = S, C
        self.axes = [axis for axis, _ in riders]
        self.arrays = [x for _, x in riders]
        self.shapes = [
            jax.ShapeDtypeStruct((C,) + x.shape if axis == "all" else x.shape, x.dtype) for axis, x in riders
        ]
        count, most = len(riders), max(S, C) - 1
        self.scratch = [DMA((count, most)), DMA((count, most)), DMA((count,))] if count else []

    def bind(self, ins, outs, sems):
        self.ins, self.outs, self.sems = ins, outs, sems

    def start(self):
        p, z, c = here()
        self.moves = []
        for n, axis in enumerate(self.axes):
            src, dst = self.ins[n], self.outs[n]
            send, recv, own = self.sems
            if axis == "tp":
                copies = [remote(src, dst, send.at[n, 0], recv.at[n, 0], {"tp": 1 - c})]
            elif axis == "all":
                copies = [
                    remote(src, dst.at[z], send.at[n, k - 1], recv.at[n, k - 1], {"ctx": (z + k) % self.C})
                    for k in range(1, self.C)
                ]
                copies.append(pltpu.make_async_copy(src, dst.at[z], own.at[n]))
            else:
                size, me = (self.S, p) if axis == "shard" else (self.C, z)
                copies = [
                    remote(src.at[(me + k) % size], dst.at[me], send.at[n, k - 1], recv.at[n, k - 1], {axis: (me + k) % size})
                    for k in range(1, size)
                ]
                copies.append(pltpu.make_async_copy(src.at[me], dst.at[me], own.at[n]))
            for copy in copies:
                copy.start()
            self.moves += copies

    def wait(self):
        for copy in self.moves:
            copy.wait()


def greet(S, C, mates=(), line=False, other=False, axes=()):
    p, z, c = here()
    peers = [{"shard": q} for q in ([(p + k) % S for k in range(1, S)] if "shard" in axes else mates)]
    if line or "ctx" in axes or "all" in axes:
        peers += [{"ctx": (z + k) % C} for k in range(1, C)]
    if other or "tp" in axes:
        peers.append({"tp": 1 - c})
    barrier = pltpu.get_barrier_semaphore()
    for where in peers:
        pl.semaphore_signal(barrier, inc=1, device_id=where, device_id_type=MESH)
    pl.semaphore_wait(barrier, len(peers))


def comm(kernel, S, C, number, name, args, in_specs, outs, scratch, riders=()):
    ride = Riders(S, C, riders)
    na, nr, no, ns = len(args), len(ride.axes), len(outs), len(scratch)

    def body(*refs):
        ins, refs = refs[:na], refs[na:]
        rins, refs = refs[:nr], refs[nr:]
        os, refs = refs[:no], refs[no:]
        routs, refs = refs[:nr], refs[nr:]
        ride.bind(rins, routs, refs[ns:])
        kernel(ride, ins, os, refs[:ns])

    return pl.pallas_call(
        body,
        out_shape=[shape for shape, _ in outs] + ride.shapes,
        in_specs=list(in_specs) + [IN_VMEM] * nr,
        out_specs=[spec for _, spec in outs] + [ANY] * nr,
        scratch_shapes=list(scratch) + ride.scratch,
        compiler_params=pltpu.CompilerParams(
            collective_id=number, has_side_effects=True, vmem_limit_bytes=62 << 20
        ),
        cost_estimate=pl.CostEstimate(flops=0, bytes_accessed=120_000_000, transcendentals=0),
        name=name,
    )(*args, *ride.arrays)


def exchange(S, C, T, number, riders, tiles, rows, beside, turned):
    R, D = rows.shape
    n, wide, nb = R // T, D // S, D // (S * C)
    pieces = S if ordered(D, S, C) else 1
    p, z, c = here()
    if pieces == 1:
        rows, beside = (
            lax.dynamic_slice_in_dim(x, c * n, n, 0).reshape(n, S, C, nb).transpose(2, 0, 1, 3).reshape(S, n, wide)
            for x in (rows, beside)
        )
    heights = [x.shape[0] // S for x in turned]

    def kernel(ride, ins, outs, scratch):
        tile, x_ref, y_ref, *raws = ins
        got, x_buf, x_out, y_out, *turns = outs
        send, recv, bsend, brecv, own, hsend, hrecv, hown, zsend, zrecv, zown, wsend, wrecv, wown, *stages = scratch
        p, z, c = here()
        mates = [(p + k) % S for k in range(1, S)]
        everyone = [(i, j) for i in range(C) for j in range(S) if i or j]
        peers = [{"shard": (p + j) % S, "ctx": (z + i) % C} for i, j in everyone]
        barrier = pltpu.get_barrier_semaphore()
        for where in peers + [{"tp": 1 - c}]:
            pl.semaphore_signal(barrier, inc=1, device_id=where, device_id_type=MESH)
        pl.semaphore_wait(barrier, len(peers) + 1)

        def columns(ref, q, i):
            if pieces == 1:
                return ref.at[q]
            lanes = pl.ds(pl.multiple_of((i * C + q) * nb, 128), nb)
            return ref.at[pl.ds(pl.multiple_of(c * n, 16), n), lanes]

        def first_hop(ref, out, at):
            hop = []
            for i in range(pieces):
                dst = out.at[p, :, pl.ds(i * (wide // pieces), wide // pieces)]
                hop.append(pltpu.make_async_copy(columns(ref, p, i), dst, hown.at[at, i]))
                for k, q in enumerate(mates):
                    hop.append(
                        remote(columns(ref, q, i), dst, hsend.at[at, k, i], hrecv.at[at, k, i], {"shard": q})
                    )
            for copy in hop:
                copy.start()
            return hop

        x_hop = first_hop(x_ref, x_buf, 0)
        local = pltpu.make_async_copy(tile.at[z, p], got.at[c, z, p], own)
        local.start()
        copies = []
        for at, (where, (i, j)) in enumerate(zip(peers, everyone)):
            q, g = (p + j) % S, (z + i) % C
            copies.append(remote(tile.at[g, q], got.at[c, z, p], send.at[at], recv.at[at], where))
            copies[-1].start()
        ride.start()
        y_hop = first_hop(y_ref, y_out, 1)
        moves = []
        for m, (raw, stage, out, height) in enumerate(zip(raws, stages, turns, heights)):
            for q in range(S):
                stage[q] = raw[q * height : (q + 1) * height, :].astype(F32).T.astype(BF)
            moves.append(pltpu.make_async_copy(stage.at[p], out.at[p], wown.at[m]))
            for k, q in enumerate(mates):
                moves.append(remote(stage.at[q], out.at[p], wsend.at[m, k], wrecv.at[m, k], {"shard": q}))
            for copy in moves[-S:]:
                copy.start()
        for copy in x_hop:
            copy.wait()
        line = [pltpu.make_async_copy(x_buf.at[z], x_out.at[z], zown)]
        for k in range(1, C):
            g = (z + k) % C
            line.append(remote(x_buf.at[g], x_out.at[z], zsend.at[k - 1], zrecv.at[k - 1], {"ctx": g}))
        for copy in line:
            copy.start()
        local.wait()
        for copy in copies:
            copy.wait()
        back = remote(got.at[c], got.at[c], bsend, brecv, {"tp": 1 - c})
        back.start()
        back.wait_send()
        remote(got.at[1 - c], got.at[1 - c], bsend, brecv, {"tp": 1 - c}).wait_recv()
        for copy in line + y_hop + moves:
            copy.wait()
        ride.wait()

    count, m = C * S - 1, len(turned)
    part = jax.ShapeDtypeStruct((S, n, wide), rows.dtype)
    return comm(
        kernel, S, C, number, "exchange", [tiles, rows, beside, *turned],
        [IN_VMEM, ANY, ANY] + [IN_VMEM] * m,
        [(jax.ShapeDtypeStruct((T,) + tiles.shape, tiles.dtype), ANY), (part, IN_VMEM), (part, IN_VMEM), (part, ANY)]
        + [(jax.ShapeDtypeStruct((S, nb, height), BF), ANY) for height in heights],
        [
            DMA((count,)), DMA((count,)), DMA, DMA, DMA,
            DMA((2, S - 1, pieces)), DMA((2, S - 1, pieces)), DMA((2, pieces)),
            DMA((C - 1,)), DMA((C - 1,)), DMA, DMA((m, S - 1)), DMA((m, S - 1)), DMA((m,)),
        ]
        + [pltpu.VMEM((S, nb, height), BF) for height in heights],
        riders,
    )


def plane(S):
    p, _, c = here()
    B = S // 2
    a, b = p // B, p % B
    return a, b, [a * B + (b + j) % B for j in range(1, B)], (1 - a) * B + b


def spread_sems(S):
    count = 4 + 4 * (S // 2 - 1)
    return [DMA((2 * count,)), DMA((2 * count,))]


def spread(S, own, region, send, recv, work=(None, None)):
    p, _, c = here()
    B = S // 2
    a, b, rows, col = plane(S)
    rows, col, other = [{"shard": q} for q in rows], {"shard": col}, {"tp": 1 - c}
    per = 4 + 4 * (B - 1)
    OWN, ROW, COL, VIA_COL, VIA_ROW = 0, 2, 2 + 2 * (B - 1), 4 + 2 * (B - 1), 4 + 3 * (B - 1)
    started = []

    def push(q, h, sem, where, first=False):
        view = region(q, h, c)
        copy = remote(own(h) if first else view, view, send.at[sem], recv.at[sem], where)
        copy.start()
        started.append(copy)

    def came(q, h, sem, core):
        view = region(q, h, core)
        remote(view, view, send.at[sem], recv.at[sem], other).wait_recv()

    for h in range(2):
        for j in range(1, B):
            push(p, h, ROW + 2 * (j - 1) + h, rows[j - 1], True)
    for h in (1, 0):
        push(p, h, COL + h, col, True)
    for h in range(2):
        push(p, h, per + OWN + h, other, True)

    def from_row(j, h):
        q = a * B + (b - j) % B
        came(q, h, ROW + 2 * (j - 1) + h, c)
        push(q, h, per + ROW + 2 * (j - 1) + h, other)
        return q

    def from_col(h):
        q = (1 - a) * B + b
        came(q, h, COL + h, c)
        push(q, h, per + COL + h, other)
        return q

    if work[0] is not None:
        work[0]()
    for j in range(1, B):
        q = from_row(j, 0)
        push(q, 0, VIA_COL + j - 1, col)
    q = from_col(1)
    for j in range(1, B):
        push(q, 1, VIA_ROW + j - 1, rows[j - 1])
    if work[1] is not None:
        work[1]()
    for j in range(1, B):
        from_row(j, 1)
    from_col(0)
    for j in range(1, B):
        q = (1 - a) * B + (b - j) % B
        came(q, 0, VIA_COL + j - 1, c)
        push(q, 0, per + VIA_COL + j - 1, other)
        came(q, 1, VIA_ROW + j - 1, c)
        push(q, 1, per + VIA_ROW + j - 1, other)
    for h in range(2):
        came(p, h, per + OWN + h, 1 - c)
        came((1 - a) * B + b, h, per + COL + h, 1 - c)
    for j in range(1, B):
        for h in range(2):
            came(a * B + (b - j) % B, h, per + ROW + 2 * (j - 1) + h, 1 - c)
        q = (1 - a) * B + (b - j) % B
        came(q, 0, per + VIA_COL + j - 1, 1 - c)
        came(q, 1, per + VIA_ROW + j - 1, 1 - c)
    for copy in started:
        copy.wait_send()


def gather_columns(S, C, T, number, x, riders=(), extra=None):
    _, n, wide = x.shape
    more, more_specs, more_outs, more_scratch, task = extra or ((), (), (), (), None)

    def kernel(ride, ins, outs, scratch):
        x_ref, out_ref = ins[0], outs[0]
        send, recv, own = scratch[:3]
        p, _, c = here()
        _, _, rows, col = plane(S)

        def region(q, h, core):
            part = pl.ds(pl.multiple_of(q * wide, 128), wide)
            return out_ref.at[pl.ds(h * (C // 2), C // 2), core, :, part]

        local = [
            pltpu.make_async_copy(x_ref.at[pl.ds(h * (C // 2), C // 2)], region(p, h, c), own.at[h]) for h in range(2)
        ]
        for copy in local:
            copy.start()
        if task is not None:
            task(ins[1:], outs[1:], scratch[3:], None)
        greet(S, C, rows + [col], other=True, axes=ride.axes)
        ride.start()
        work = [None, None]
        if task is not None:
            work = [functools.partial(task, ins[1:], outs[1:], scratch[3:], piece) for piece in range(2)]
        spread(S, lambda h: x_ref.at[pl.ds(h * (C // 2), C // 2)], region, send, recv, work)
        for copy in local:
            copy.wait()
        ride.wait()

    out, *rest = comm(
        kernel, S, C, number, "gather_columns", [x, *more], [IN_VMEM, *more_specs],
        [(jax.ShapeDtypeStruct((C, T, n, wide * S), x.dtype), ANY), *more_outs],
        spread_sems(S) + [DMA((2,)), *more_scratch], riders,
    )
    return [out.reshape(C * T * n, wide * S)] + rest


CHUNK = 512
ROWS = 32


def sum_scratch(S, n, D):
    half, B = n // 2, S // 2

    def vm(*shape):
        return pltpu.VMEM(shape, BF)

    return [
        vm(S, n, D), vm(S, n, D), vm(S, n, D), vm(B - 1, 2, half, D), vm(B, half, D),
        vm(B - 1, half, D), vm(half, D), vm(half, D), vm(B - 1, half, D),
        DMA((S,)), DMA((S,)), DMA((B - 1, 2)), DMA((B - 1, 2)), DMA((B,)), DMA((B,)), DMA((B,)), DMA((B,)),
    ]


def sum_over_plane(S, T, x_ref, w_ref, out_ref, scratch, meanwhile=None):
    away, sib, mine, row1, col1, row2, col2, to_col, to_row = scratch[:9]
    asend, arecv, rsend, rrecv, csend, crecv, fsend, frecv = scratch[9:]
    n, D = out_ref.shape
    half, B = n // 2, S // 2
    _, _, c = here()
    a, b, rows, col = plane(S)
    rows, col, other = [{"shard": q} for q in rows], {"shard": col}, {"tp": 1 - c}

    def chip(e):
        return ((a + e // B) % 2) * B + (b + e % B) % B

    def product(e, core, store):
        x = x_ref[chip(e) * T + core]

        def column(j, _):
            w = pl.ds(pl.multiple_of(j * CHUNK, CHUNK), CHUNK)
            store(w, mm(x, w_ref[w, :], 1, 1))
            return 0

        lax.fori_loop(0, D // CHUNK, column, 0)

    def to_other(e):
        return remote(away.at[e], sib.at[e], asend.at[e], arecv.at[e], other)

    def for_other(e):
        def store(w, value):
            away[e, :, w] = value.astype(BF)

        product(e, 1 - c, store)
        to_other(e).start()

    for_other(S - 1)
    top, low = pl.ds(0, half), pl.ds(half, half)
    started = []

    def push(src, dst, send, recv, where):
        copy = remote(src, dst, send, recv, where)
        copy.start()
        started.append(copy)

    for e in range(S - 1, -1, -1):
        if e:
            for_other(e - 1)
        to_other(e).wait()

        def store(w, value):
            value = value + sib[e, :, w].astype(F32)
            if e:
                mine[e, :, w] = value.astype(BF)
            else:
                out_ref[:, w] = value

        product(e, c, store)
        j = e % B
        if e > B:
            push(mine.at[e, top], row1.at[j - 1, 1], rsend.at[j - 1, 1], rrecv.at[j - 1, 1], rows[j - 1])
            push(mine.at[e, low], col1.at[j], csend.at[j], crecv.at[j], col)
        elif e == B:
            push(mine.at[e, low], col1.at[0], csend.at[0], crecv.at[0], col)
        elif e:
            push(mine.at[e, top], row1.at[j - 1, 0], rsend.at[j - 1, 0], rrecv.at[j - 1, 0], rows[j - 1])

    def came(ref, send, recv):
        remote(ref, ref, send, recv, other).wait_recv()

    if meanwhile is not None:
        meanwhile(0)
    total = mine[B, top, :].astype(F32)
    for j in range(1, B):
        came(row1.at[j - 1, 1], rsend.at[j - 1, 1], rrecv.at[j - 1, 1])
        total = total + row1[j - 1, 1].astype(F32)
    to_col[...] = total.astype(BF)
    push(to_col, col2, fsend.at[0], frecv.at[0], col)
    for j in range(1, B):
        came(col1.at[j], csend.at[j], crecv.at[j])
        to_row[j - 1] = (mine[j, low, :].astype(F32) + col1[j].astype(F32)).astype(BF)
        push(to_row.at[j - 1], row2.at[j - 1], fsend.at[j], frecv.at[j], rows[j - 1])
    if meanwhile is not None:
        meanwhile(1)
    came(col1.at[0], csend.at[0], crecv.at[0])
    upper, lower = out_ref[top, :], out_ref[low, :] + col1[0].astype(F32)
    for j in range(1, B):
        came(row1.at[j - 1, 0], rsend.at[j - 1, 0], rrecv.at[j - 1, 0])
        upper = upper + row1[j - 1, 0].astype(F32)
    came(col2, fsend.at[0], frecv.at[0])
    out_ref[top, :] = upper + col2[...].astype(F32)
    for j in range(1, B):
        came(row2.at[j - 1], fsend.at[j], frecv.at[j])
        lower = lower + row2[j - 1].astype(F32)
    out_ref[low, :] = lower
    for copy in started:
        copy.wait_send()


def project(S, C, T, number, tok, raw, gain, shift, bias):
    L, D = tok.shape
    _, parts, nb, wide = raw.shape
    hn = wide // S
    most = S - 1

    def kernel(ride, ins, outs, scratch):
        tok_ref, raw_ref, gain_ref, shift_ref, bias_ref = ins
        n_ref, out_ref, w_ref = outs
        send, recv, own = scratch
        p, _, _ = here()
        mates = [(p + k) % S for k in range(1, S)]
        greet(S, C, mates)

        def lanes(q):
            return pl.ds(pl.multiple_of(q * hn, 128), hn)

        copies = []
        for part in range(parts):
            dst = w_ref.at[:, p, :, pl.ds(part * hn, hn)]
            for k, q in enumerate(mates):
                copies.append(
                    remote(raw_ref.at[:, part, :, lanes(q)], dst, send.at[k, part], recv.at[k, part], {"shard": q})
                )
            copies.append(pltpu.make_async_copy(raw_ref.at[:, part, :, lanes(p)], dst, own.at[part]))
        for copy in copies:
            copy.start()

        def normed(r):
            n_ref[r, :] = (norm_of(tok_ref[r, :].astype(F32))[0] * gain_ref[...] + shift_ref[...]).astype(BF)

        row_blocks(L, normed)
        for copy in copies:
            copy.wait()
        w = w_ref[...].reshape(D, parts * hn)

        @pl.loop(0, L // BLK)
        def _(i):
            r = pl.ds(pl.multiple_of(i * BLK, BLK), BLK)
            out_ref[r, :] = mm(n_ref[r, :], w, 1, 0) + bias_ref[...]

    n, out, w = comm(
        kernel, S, C, number, "project", [tok, raw, gain, shift, bias], [IN_VMEM] * 5,
        [
            (jax.ShapeDtypeStruct((L, D), BF), IN_VMEM), (jax.ShapeDtypeStruct((L, parts * hn), F32), IN_VMEM),
            (jax.ShapeDtypeStruct((C, S, nb, parts * hn), BF), IN_VMEM),
        ],
        [DMA((most, parts)), DMA((most, parts)), DMA((parts,))],
    )
    return n, out, w.reshape(D, parts * hn)


def gates_back_kernel(gb_ref, wd_ref, gu_ref, dgu_ref):
    dact = mm(gb_ref[...], wd_ref[...], 1, 0)
    both, width = gu_ref[...], dact.shape[1]
    gate, up = both[:, :width], both[:, width:]
    s = jax.nn.sigmoid(gate)
    dgate = dact * up * s * (1.0 + gate * (1.0 - s))
    dgu_ref[...] = jnp.concatenate((dgate, dact * gate * s), axis=1).astype(BF)


def gates_work(ins, outs, scratch, piece):
    gu_ref, act_ref = outs
    n2_ref, wg_ref, sems = scratch
    if piece != 1:
        for i, (x, y) in enumerate(zip(ins, (n2_ref, wg_ref))):
            copy = pltpu.make_async_copy(x, y, sems.at[i])
            copy.wait() if piece == 0 else copy.start()
    if piece is None:
        return
    (rows, width), half = act_ref.shape, act_ref.shape[0] // BLK // 2

    @pl.loop(piece * half, piece * half + half)
    def _(i):
        r = pl.ds(pl.multiple_of(i * BLK, BLK), BLK)
        both = mm(n2_ref[r, :], wg_ref[...], 1, 0)
        gu_ref[r, :] = both
        gate, up = both[:, :width], both[:, width:]
        act_ref[r, :] = (gate * jax.nn.sigmoid(gate) * up).astype(BF)


def gates(S, C, T, number, n2, wg, x):
    L, width = n2.shape[0], wg.shape[1] // 2
    outs = [jax.ShapeDtypeStruct((L, 2 * width), F32), jax.ShapeDtypeStruct((L, width), BF)]
    return gather_columns(
        S, C, T, number, x, (),
        ([n2, wg], [ANY, ANY], [(shape, IN_VMEM) for shape in outs],
         [pltpu.VMEM(n2.shape, BF), pltpu.VMEM(wg.shape, BF), DMA((2,))], gates_work),
    )


def by_rows(kernel, name, arrays, outs):
    L = outs[0].shape[0]

    def spec(width):
        return pl.BlockSpec((BLK, width), lambda i: (i, 0))

    return pl.pallas_call(
        kernel,
        grid=(L // BLK,),
        in_specs=[spec(x.shape[1]) if rows else pl.BlockSpec(x.shape, lambda i: (0, 0)) for rows, x in arrays],
        out_specs=[spec(x.shape[1]) for x in outs],
        out_shape=outs,
        compiler_params=pltpu.CompilerParams(vmem_limit_bytes=62 << 20),
        name=name,
    )(*[x for _, x in arrays])


def row_blocks(n, work):
    @pl.loop(0, n // ROWS)
    def _(i):
        work(pl.ds(pl.multiple_of(i * ROWS, ROWS), ROWS))


def own_rows(T, x_ref, row_ref, sem):
    p, _, c = here()
    copy = pltpu.make_async_copy(x_ref.at[p * T + c], row_ref, sem)
    copy.start()
    return copy


def norm_of(v):
    center = v - jnp.mean(v, axis=-1, keepdims=True)
    inverse = lax.rsqrt(jnp.mean(center * center, axis=-1, keepdims=True) + EPS)
    return center * inverse, inverse


def norm_back(v, g, gain, stats_ref):
    normal, inverse = norm_of(v)
    e = g * gain
    stats_ref[0:1, :] += jnp.sum(g * normal, axis=0, keepdims=True)
    stats_ref[1:2, :] += jnp.sum(g, axis=0, keepdims=True)
    return inverse * (
        e - jnp.mean(e, axis=-1, keepdims=True) - normal * jnp.mean(e * normal, axis=-1, keepdims=True)
    )


def spread_rows(S, T, src, out_ref, send, recv, own):
    p, _, c = here()
    half = src.shape[0] // 2
    local = pltpu.make_async_copy(src, out_ref.at[p * T + c], own)
    local.start()
    spread(
        S,
        lambda h: src.at[pl.ds(h * half, half)],
        lambda q, h, core: out_ref.at[q * T + core, pl.ds(h * half, half)],
        send,
        recv,
    )
    local.wait()


def sum_norm_gather(S, C, T, number, x, w, residual, gain, shift, riders=()):
    L, K = x.shape
    D, n = w.shape[0], L // (S * T)

    def kernel(ride, ins, outs, scratch):
        x_ref, w_ref, all_ref, gain_ref, shift_ref = ins
        v_ref, out_ref = outs
        acc, low, send, recv, own, res_ref, sem = scratch[:7]
        _, _, rows, col = plane(S)
        rest = own_rows(T, all_ref, res_ref, sem)
        greet(S, C, rows + [col], other=True, axes=ride.axes)
        ride.start()
        sum_over_plane(S, T, x_ref, w_ref, acc, scratch[7:])
        rest.wait()

        def work(r):
            v = res_ref[r, :].astype(F32) + acc[r, :]
            v_ref[r, :] = v
            low[r, :] = (norm_of(v)[0] * gain_ref[...] + shift_ref[...]).astype(BF)

        row_blocks(n, work)
        spread_rows(S, T, low, out_ref, send, recv, own)
        ride.wait()

    v, out, *rest = comm(
        kernel, S, C, number, "sum_norm_gather", [x.reshape(S * T, n, K), w, residual.reshape(S * T, n, D), gain, shift],
        [IN_VMEM, IN_VMEM, ANY, IN_VMEM, IN_VMEM],
        [(jax.ShapeDtypeStruct((n, D), F32), IN_VMEM), (jax.ShapeDtypeStruct((S * T, n, D), BF), ANY)],
        [pltpu.VMEM((n, D), F32), pltpu.VMEM((n, D), BF)] + spread_sems(S)
        + [DMA, pltpu.VMEM((n, D), BF), DMA] + sum_scratch(S, n, D),
        riders,
    )
    return [v, out.reshape(L, D)] + rest


def sum_back_gather(S, C, T, number, x, w, v, residual, gain, riders=()):
    L, K = x.shape
    D, n = w.shape[0], L // (S * T)

    def kernel(ride, ins, outs, scratch):
        x_ref, w_ref, in_ref, all_ref, gain_ref = ins
        v_ref, out_ref, stats = outs
        acc, low, send, recv, own, res_ref, sem = scratch[:7]
        _, _, rows, col = plane(S)
        rest = own_rows(T, all_ref, res_ref, sem)
        greet(S, C, rows + [col], other=True, axes=ride.axes)
        ride.start()
        sum_over_plane(S, T, x_ref, w_ref, acc, scratch[7:])
        rest.wait()
        stats[...] = jnp.zeros_like(stats)

        def work(r):
            g = res_ref[r, :].astype(F32) + norm_back(in_ref[r, :], acc[r, :], gain_ref[...], stats)
            v_ref[r, :] = g
            low[r, :] = g.astype(BF)

        row_blocks(n, work)
        spread_rows(S, T, low, out_ref, send, recv, own)
        ride.wait()

    g, out, stats, *rest = comm(
        kernel, S, C, number, "sum_back_gather", [x.reshape(S * T, n, K), w, v, residual.reshape(S * T, n, D), gain],
        [IN_VMEM, IN_VMEM, IN_VMEM, ANY, IN_VMEM],
        [
            (jax.ShapeDtypeStruct((n, D), F32), IN_VMEM), (jax.ShapeDtypeStruct((S * T, n, D), BF), ANY),
            (jax.ShapeDtypeStruct((2, D), F32), IN_VMEM),
        ],
        [pltpu.VMEM((n, D), F32), pltpu.VMEM((n, D), BF)] + spread_sems(S)
        + [DMA, pltpu.VMEM((n, D), BF), DMA] + sum_scratch(S, n, D),
        riders,
    )
    return [g, out.reshape(L, D), stats] + rest


def sum_back(S, C, T, number, x, w, v, residual, gain, riders=()):
    L, K = x.shape
    D, n = w.shape[0], L // (S * T)

    def kernel(ride, ins, outs, scratch):
        x_ref, w_ref, all_ref, res_ref, gain_ref = ins
        low, stats = outs
        acc, in_ref, sem = scratch[:3]
        _, _, rows, col = plane(S)
        rest = own_rows(T, all_ref, in_ref, sem)
        greet(S, C, rows + [col], other=True, axes=ride.axes)
        ride.start()
        sum_over_plane(S, T, x_ref, w_ref, acc, scratch[3:])
        rest.wait()
        stats[...] = jnp.zeros_like(stats)

        def work(r):
            g = res_ref[r, :] + norm_back(in_ref[r, :].astype(F32), acc[r, :], gain_ref[...], stats)
            low[r, :] = g.astype(BF)

        row_blocks(n, work)
        ride.wait()

    return comm(
        kernel, S, C, number, "sum_back", [x.reshape(S * T, n, K), w, v.reshape(S * T, n, D), residual, gain],
        [IN_VMEM, IN_VMEM, ANY, IN_VMEM, IN_VMEM],
        [(jax.ShapeDtypeStruct((n, D), BF), IN_VMEM), (jax.ShapeDtypeStruct((2, D), F32), IN_VMEM)],
        [pltpu.VMEM((n, D), F32), pltpu.VMEM((n, D), BF), DMA] + sum_scratch(S, n, D),
        riders,
    )


def finish(S, C, T, number, x, y, stats, bias, qkv, out):
    n, D = x.shape
    hn = out.shape[2]
    wide, lines = D // S, bias.shape[1] // 128
    nb = D // (S * C)
    count = sum(z.shape[0] for z in stats)
    tall = -(-(count + lines) // 8) * 8
    many = C * S - 1
    pieces = S if ordered(D, S, C) else 1

    def kernel(ride, ins, outs, scratch):
        x_ref, y_ref, stat_refs, bias_ref = ins[0], ins[1], ins[2:-3], ins[-3]
        qkv_ref, o_ref = ins[-2:]
        x_out, y_out, norm_out, bias_out, qkv_out, o_out = outs
        xbuf, xbuf2, ybuf2, tile, send, recv, own, psend, precv, pown, lsend, lrecv, tsend, trecv = scratch[:14]
        qkv_buf, o_buf, gsend, grecv, gown, got = scratch[14:]
        p, z, c = here()
        other = {"tp": 1 - c}
        everyone = [(i, j) for i in range(C) for j in range(S) if i or j]
        peers = [{"shard": (p + j) % S, "ctx": (z + i) % C} for i, j in everyone]
        barrier = pltpu.get_barrier_semaphore()
        for where in peers + [other]:
            pl.semaphore_signal(barrier, inc=1, device_id=where, device_id_type=MESH)
        pl.semaphore_wait(barrier, len(peers) + 1)

        def part(q):
            return pl.ds(pl.multiple_of(q * wide, 128), wide)

        def turn_over(source, target, at, size, me, axis):
            hop = [pltpu.make_async_copy(source(me), target, own.at[at])]
            for k in range(1, size):
                q = (me + k) % size
                hop.append(remote(source(q), target, send.at[at, k - 1], recv.at[at, k - 1], {axis: q}))
            for copy in hop:
                copy.start()
            return hop

        def arrive(buf, out, at):
            hop = []
            for i in range(pieces):
                src = pl.ds(i * (wide // pieces), wide // pieces)
                first = (i * C + p) * nb if pieces > 1 else p * wide
                dst = out.at[c, :, pl.ds(pl.multiple_of(first, 128), wide // pieces)]
                hop.append(pltpu.make_async_copy(buf.at[p, :, src], dst, pown.at[at, i]))
                for k in range(1, S):
                    q = (p + k) % S
                    hop.append(
                        remote(buf.at[q, :, src], dst, psend.at[at, k - 1, i], precv.at[at, k - 1, i], {"shard": q})
                    )
            for copy in hop:
                copy.start()
            return hop

        def both(ref, at):
            copy = remote(ref.at[c], ref.at[c], lsend.at[at], lrecv.at[at], other)
            copy.start()
            return copy

        def settle(ref, at, copy):
            copy.wait_send()
            remote(ref.at[1 - c], ref.at[1 - c], lsend.at[at], lrecv.at[at], other).wait_recv()

        x_hop = turn_over(lambda q: x_ref.at[:, part(q)], xbuf.at[p], 0, S, p, "shard")
        y_hop = turn_over(lambda q: y_ref.at[q], ybuf2.at[z], 1, C, z, "ctx")
        moves = []
        for i, (src, dst) in enumerate(((qkv_ref, qkv_buf), (o_ref, o_buf))):
            moves.append(pltpu.make_async_copy(src.at[p], dst.at[p], gown.at[i]))
            for k in range(1, S):
                q = (p + k) % S
                moves.append(remote(src.at[q], dst.at[p], gsend.at[i, k - 1], grecv.at[i, k - 1], {"shard": q}))
        for copy in moves:
            copy.start()
        tile[...] = jnp.zeros_like(tile)
        at = count
        for i, ref in enumerate(stat_refs):
            for j in range(2):
                tile[j * len(stat_refs) + i : j * len(stat_refs) + i + 1, :] = ref[j : j + 1, :]
        for k in range(lines):
            for block in range(D // 128):
                tile[at + k : at + k + 1, pl.ds(block * 128, 128)] = bias_ref[:, pl.ds(k * 128, 128)]

        def columns(g, q):
            return tile.at[:, pl.ds(pl.multiple_of((g * S + q) * nb // 128 * 128, 128), 128)]

        small = [pltpu.make_async_copy(columns(z, p), got.at[c, z, p], own.at[3])]
        for k, (where, (i, j)) in enumerate(zip(peers, everyone)):
            small.append(
                remote(columns((z + i) % C, (p + j) % S), got.at[c, z, p], tsend.at[k], trecv.at[k], where)
            )
        for copy in small:
            copy.start()
        for copy in x_hop:
            copy.wait()
        x_hop = turn_over(lambda q: xbuf.at[q], xbuf2.at[z], 2, C, z, "ctx")
        for copy in y_hop:
            copy.wait()
        y_hop = arrive(ybuf2, y_out, 0)
        for copy in small:
            copy.wait()
        small_last = both(got, 0)
        bias_out[...] = jnp.sum(got[c, :, :, count : count + lines, :], axis=0)
        for copy in x_hop:
            copy.wait()
        x_hop = arrive(xbuf2, x_out, 1)
        for copy in y_hop:
            copy.wait()
        y_last = both(y_out, 1)
        for copy in moves:
            copy.wait()
        for q in range(S):
            o_out[q * hn : (q + 1) * hn, :] = o_buf[q].astype(F32).T
            for i in range(3):
                qkv_out[i, :, q * hn : (q + 1) * hn] = qkv_buf[q, :, i * hn : (i + 1) * hn].astype(F32)
        for copy in x_hop:
            copy.wait()
        x_last = both(x_out, 2)
        settle(got, 0, small_last)
        norm_out[...] = jnp.sum(got[:, :, :, :count, :], axis=(0, 1, 2))
        settle(y_out, 1, y_last)
        settle(x_out, 2, x_last)

    args = [x, y, *stats, bias, qkv, out]
    most = max(S, C) - 1
    home = (jax.ShapeDtypeStruct((T, n, D), BF), ANY)
    x, y, *rest = comm(
        kernel, S, C, number, "finish", args, [IN_VMEM] * len(args),
        [home, home]
        + [
            (jax.ShapeDtypeStruct(shape, F32), IN_VMEM)
            for shape in ((count, 128), (S, lines, 128), (3, nb, S * hn), (S * hn, nb))
        ],
        [
            pltpu.VMEM((S, n, wide), BF), pltpu.VMEM((C, n, wide), BF), pltpu.VMEM((C, n, wide), BF),
            pltpu.VMEM((tall, D), F32), DMA((3, most)), DMA((3, most)), DMA((4,)),
            DMA((2, S - 1, pieces)), DMA((2, S - 1, pieces)), DMA((2, pieces)), DMA((3,)), DMA((3,)),
            DMA((many,)), DMA((many,)),
            pltpu.VMEM(qkv.shape, BF), pltpu.VMEM(out.shape, BF), DMA((2, S - 1)), DMA((2, S - 1)), DMA((2,)),
            pltpu.VMEM((T, C, S, tall, 128), F32),
        ],
    )
    return [x.reshape(T * n, D), y.reshape(T * n, D)] + rest


def final_kernel(gateup_ref, down_ref, gateup_out, down_out):
    S, _, fn = down_ref.shape
    for q in range(S):
        down_out[q * fn : (q + 1) * fn, :] = down_ref[q].astype(F32).T
        for i in range(2):
            gateup_out[:, i, q * fn : (q + 1) * fn] = gateup_ref[q, :, i * fn : (i + 1) * fn].astype(F32)


def final(gateup, down):
    S, nb, fn = down.shape
    return pl.pallas_call(
        final_kernel,
        in_specs=[IN_VMEM] * 2,
        out_specs=[IN_VMEM] * 2,
        out_shape=[jax.ShapeDtypeStruct((nb, 2, S * fn), F32), jax.ShapeDtypeStruct((S * fn, nb), F32)],
        compiler_params=pltpu.CompilerParams(vmem_limit_bytes=62 << 20),
        name="final",
    )(gateup, down)


def ordered(D, S, C):
    return D // (S * C) % 128 == 0


def turn_tables(rows):
    feature = np.arange(128) % HEAD
    freq = np.where(feature < ROT, BASE ** (-2.0 * (feature % (ROT // 2)) / ROT), 0.0)
    near = np.arange(BLK)[:, None] * freq
    far = np.arange(0, rows, BLK)[:, None] * freq
    return [jnp.asarray(f(x), F32) for x in (near, far) for f in (np.cos, np.sin)]


def turn(x, i, tables, sign):
    cos, sin, cos_far, sin_far = tables
    far_cos, far_sin = cos_far[pl.ds(i, 1), :], sin_far[pl.ds(i, 1), :]
    cos_t = cos[...] * far_cos - sin[...] * far_sin
    sin_t = sin[...] * far_cos + cos[...] * far_sin
    ahead = lax.broadcasted_iota(jnp.int32, x.shape, 1) % HEAD < ROT // 2
    partner = jnp.where(ahead, -pltpu.roll(x, 128 - ROT // 2, 1), pltpu.roll(x, ROT // 2, 1))
    return x * cos_t + partner * (sin_t * sign)


def two_heads(x, left):
    zero = jnp.zeros_like(x)
    return [jnp.where(left, x, zero), jnp.where(left, zero, x)]


def block_of(rows):
    return next(size for size in (512, 256) if rows % size == 0)


def attend_kernel(
    first_ref, qkv_ref, cos_ref, sin_ref, cosf_ref, sinf_ref, begin_ref,
    qo_ref, ko_ref, vo_ref, o_ref, lse_ref, vt_ref,
):
    rows, wide = qo_ref.shape
    pairs, size = wide // 128, block_of(rows)
    tables = (cos_ref, sin_ref, cosf_ref, sinf_ref)
    left = lax.broadcasted_iota(jnp.int32, (size, 128), 1) < HEAD
    key_at = lax.broadcasted_iota(jnp.int32, (size, size), 0)
    query_at = lax.broadcasted_iota(jnp.int32, (1, size), 1)

    @pl.loop(0, rows // BLK)
    def _(i):
        r = pl.ds(pl.multiple_of(i * BLK, BLK), BLK)
        for t in range(pairs):
            w = pl.ds(t * 128, 128)
            q, k, v = (qkv_ref[r, pl.ds(part * wide + t * 128, 128)] for part in range(3))
            qo_ref[r, w] = turn(q, i, tables, 1.0).astype(BF) * jnp.asarray(HEAD**-0.5, BF)
            ko_ref[r, w] = turn(k, i, tables, 1.0).astype(BF)
            vo_ref[r, w] = v.astype(BF)
            vt_ref[w, r] = v.T.astype(BF)

    @pl.loop(0, rows // size)
    def _(i):
        r = pl.ds(pl.multiple_of(i * size, size), size)
        qs = sum((two_heads(qo_ref[r, pl.ds(t * 128, 128)], left) for t in range(pairs)), [])
        begin = begin_ref[0:1, r]
        here = query_at + i * size

        def step(j, carry):
            w = pl.ds(pl.multiple_of(j * size, size), size)
            key = key_at + j * size
            seen = (key <= here) & (key >= begin)
            out = []
            for h in range(2 * pairs):
                m, l, acc = carry[h]
                s = jnp.where(seen, mm(ko_ref[w, pl.ds(h // 2 * 128, 128)], qs[h], 1, 1), NEG)
                top = jnp.maximum(m, jnp.max(s, axis=0, keepdims=True))
                fade = jnp.exp(m - top)
                e = jnp.exp(s - top)
                acc = acc * fade + mm(vt_ref[pl.ds(h * HEAD, HEAD), w], e.astype(BF), 1, 0)
                out.append((top, l * fade + jnp.sum(e, axis=0, keepdims=True), acc))
            return tuple(out)

        start = (
            jnp.full((1, size), NEG, F32), jnp.zeros((1, size), F32), jnp.zeros((HEAD, size), F32)
        )
        done = lax.fori_loop(first_ref[i], i + 1, step, (start,) * (2 * pairs))
        for t in range(pairs):
            both = []
            for h in (2 * t, 2 * t + 1):
                m, l, acc = done[h]
                both.append(acc / l)
                lse_ref[h : h + 1, r] = m + jnp.log(l)
            o_ref[r, pl.ds(t * 128, 128)] = jnp.concatenate(both, axis=0).T.astype(BF)


def attend(qkv, begin):
    rows, wide = qkv.shape[0], qkv.shape[1] // 3
    size = block_of(rows)
    half = jax.ShapeDtypeStruct((rows, wide), BF)
    return pl.pallas_call(
        attend_kernel,
        in_specs=[pl.BlockSpec(memory_space=pltpu.SMEM)] + [IN_VMEM] * 6,
        out_specs=[IN_VMEM] * 5,
        out_shape=[half] * 4 + [jax.ShapeDtypeStruct((wide // HEAD, rows), F32)],
        scratch_shapes=[pltpu.VMEM((wide, rows), BF)],
        compiler_params=pltpu.CompilerParams(vmem_limit_bytes=62 << 20),
        name="attend",
    )(begin[0, ::size] // size, qkv, *turn_tables(rows), begin)


def attend_back_work(ins, out_ref, bias_ref, scratch, piece):
    q_ref, k_ref, v_ref, o_ref, do_ref, lse_ref, cos_ref, sin_ref, cosf_ref, sinf_ref, begin_ref = ins
    kt_ref, dq_ref, dk_ref, dv_ref = scratch
    rows, wide = q_ref.shape
    pairs, size = wide // 128, block_of(rows)
    tables = (cos_ref, sin_ref, cosf_ref, sinf_ref)
    left = lax.broadcasted_iota(jnp.int32, (size, 128), 1) < HEAD
    key_at = lax.broadcasted_iota(jnp.int32, (size, size), 0)
    query_at = lax.broadcasted_iota(jnp.int32, (1, size), 1)

    last = rows // size - 1
    first, stop = (0, last) if piece == 0 else (last, last + 1)

    def prepare(i):
        r = pl.ds(pl.multiple_of(i * BLK, BLK), BLK)
        for t in range(pairs):
            w = pl.ds(t * 128, 128)
            kt_ref[w, r] = k_ref[r, w].astype(F32).T.astype(BF)
            dk_ref[r, w] = jnp.zeros((BLK, 128), F32)
            dv_ref[r, w] = jnp.zeros((BLK, 128), F32)

    if piece == 0:
        pl.loop(0, rows // BLK)(prepare)

    @pl.loop(first, stop)
    def _(i):
        r = pl.ds(pl.multiple_of(i * size, size), size)
        qs, dos, deltas, lses = [], [], [], []
        for t in range(pairs):
            w = pl.ds(t * 128, 128)
            do = do_ref[r, w]
            qs += two_heads(q_ref[r, w], left)
            dos += two_heads(do, left)
            prod = (do.astype(F32) * o_ref[r, w].astype(F32)).T
            deltas += [jnp.sum(prod[:HEAD], axis=0, keepdims=True), jnp.sum(prod[HEAD:], axis=0, keepdims=True)]
            lses += [lse_ref[2 * t : 2 * t + 1, r], lse_ref[2 * t + 1 : 2 * t + 2, r]]
        begin = begin_ref[0:1, r]
        here = query_at + i * size

        def step(j, carry):
            w = pl.ds(pl.multiple_of(j * size, size), size)
            key = key_at + j * size
            seen = (key <= here) & (key >= begin)
            out = []
            for t in range(pairs):
                lanes = pl.ds(t * 128, 128)
                k, v = k_ref[w, lanes], v_ref[w, lanes]
                dk = dv = None
                for h in (2 * t, 2 * t + 1):
                    prob = jnp.exp(jnp.where(seen, mm(k, qs[h], 1, 1) - lses[h], NEG))
                    ds = (prob * (mm(v, dos[h], 1, 1) - deltas[h])).astype(BF)
                    out.append(carry[h] + mm(kt_ref[pl.ds(h * HEAD, HEAD), w], ds, 1, 0))
                    dk_h, dv_h = mm(ds, qs[h], 1, 0), mm(prob.astype(BF), dos[h], 1, 0)
                    dk, dv = (dk_h, dv_h) if dk is None else (dk + dk_h, dv + dv_h)
                dk_ref[w, lanes] += dk
                dv_ref[w, lanes] += dv
            return tuple(out)

        done = lax.fori_loop(0, i + 1, step, (jnp.zeros((HEAD, size), F32),) * (2 * pairs))
        for t in range(pairs):
            both = jnp.concatenate(done[2 * t : 2 * t + 2], axis=0)
            dq_ref[r, pl.ds(t * 128, 128)] = both.T * (HEAD**-0.5)

    if piece == 0:
        return
    bias_ref[...] = jnp.zeros_like(bias_ref)

    @pl.loop(0, rows // BLK)
    def _(i):
        r = pl.ds(pl.multiple_of(i * BLK, BLK), BLK)
        for t in range(pairs):
            w = pl.ds(t * 128, 128)
            for part, value in enumerate((turn(dq_ref[r, w], i, tables, -1.0), turn(dk_ref[r, w], i, tables, -1.0), dv_ref[r, w])):
                lanes = pl.ds(part * wide + t * 128, 128)
                value = value.astype(BF)
                out_ref[r, lanes] = value
                bias_ref[:, lanes] += jnp.sum(value.astype(F32), axis=0, keepdims=True)


def attend_back(S, C, T, number, q, k, v, o, do, lse, begin, act, wd, riders):
    rows, wide = q.shape
    K, D, n = act.shape[1], wd.shape[0], rows // (S * T)

    def kernel(ride, ins, outs, scratch):
        _, _, row, col = plane(S)
        greet(S, C, row + [col], other=True, axes=ride.axes)

        def meanwhile(piece):
            if piece == 0:
                ride.start()
            attend_back_work(ins[2:], outs[0], outs[1], scratch[:4], piece)

        sum_over_plane(S, T, ins[0], ins[1], outs[2], scratch[4:], meanwhile)
        ride.wait()

    args = [act.reshape(S * T, n, K), wd, q, k, v, o, do, lse, *turn_tables(rows), begin]
    return comm(
        kernel, S, C, number, "attend_back", args, [IN_VMEM] * len(args),
        [(jax.ShapeDtypeStruct((rows, 3 * wide), BF), IN_VMEM), (jax.ShapeDtypeStruct((1, 3 * wide), F32), IN_VMEM),
         (jax.ShapeDtypeStruct((n, D), F32), IN_VMEM)],
        [pltpu.VMEM((wide, rows), BF)] + [pltpu.VMEM((rows, wide), F32)] * 3 + sum_scratch(S, n, D),
        riders,
    )


def doc_begins(lengths_row, rows):
    row_ids = jnp.arange(rows, dtype=jnp.int32)
    ends = jnp.cumsum(lengths_row, dtype=jnp.int32)
    begins = ends - lengths_row
    inside = (row_ids[:, None] >= begins[None, :]) & (row_ids[:, None] < ends[None, :])
    return jnp.sum(jnp.where(inside, begins[None, :], 0), axis=1, dtype=jnp.int32)


def tiles_of(parts, lead):
    flat = jnp.concatenate([x.astype(F32).reshape(lead + (-1,)) for x in parts], axis=-1)
    flat = jnp.pad(flat, ((0, 0),) * len(lead) + ((0, 1024 - flat.shape[-1]),))
    return flat.reshape(lead + (8, 128))


def make_body(S, C, T):
    assert S == C

    def body(tokens, lengths, w_qkv, b_qkv, w_out, w_gateup, w_down, norm_gain, norm_bias, cotangent):
        p, z, c = lax.axis_index("shard"), lax.axis_index("ctx"), lax.axis_index("tp")
        R, D = tokens.shape
        n = R // T
        nb = D // (S * C)
        L = R * C

        def parts(x):
            return x.reshape(n, S, D // S).swapaxes(0, 1)

        def unpermute(x):
            return x.reshape(x.shape[0], C, S, nb).swapaxes(1, 2).reshape(x.shape)

        def after(x, y):
            return lax.optimization_barrier((x, y))

        def over_ctx(w):
            return lax.all_gather(w.reshape(S * nb, -1), "ctx", axis=0, tiled=True)

        def sum_ctx(g):
            g = lax.psum_scatter(g.astype(BF), "ctx", scatter_dimension=0, tiled=True)
            return g.reshape(S, nb, -1)

        hn = w_qkv.shape[3] // S
        fn = w_gateup.shape[3] // S
        heads = hn // HEAD
        nf = HEAD // (S * C)

        tile = tiles_of((norm_gain[0].reshape(-1), norm_bias[0].reshape(-1), b_qkv[0].reshape(-1), lengths[0]), ())
        raw = lax.all_gather(w_qkv[0].swapaxes(0, 1).reshape(3 * nb, -1), "ctx", axis=0, tiled=True)
        small, _, tok, cot, wo, wd, wg = exchange(
            S, C, T, 0,
            [("shard", w_gateup[0].reshape(nb, 2, S, fn).transpose(2, 0, 1, 3).reshape(S, nb, 2 * fn))],
            jnp.broadcast_to(tile, (C, S, 8, 128)),
            tokens,
            cotangent,
            [w_out[0], w_down[0]],
        )
        tok, wo = gather_columns(S, C, T, 1, tok, [("all", wo.reshape(S * nb, hn))])
        wo, wg, wd = wo.reshape(D, hn), over_ctx(wg), over_ctx(wd)

        small = lax.dynamic_index_in_dim(small, c, 0, keepdims=False).reshape(C, S, 1024)
        norms = small[:, :, : 4 * nb].reshape(C * S, 4, nb).swapaxes(0, 1).reshape(4, D)
        gains, shifts = norms[:2], norms[2:]
        nbias = 3 * S * heads * nf
        bias = small[:, :, 4 * nb : 4 * nb + nbias].reshape(C, S, 3, S * heads, nf)
        bias = lax.dynamic_slice_in_dim(bias, p * heads, heads, 3)
        bias = bias.transpose(2, 3, 1, 0, 4).reshape(1, 3 * hn)
        docs = lengths.shape[1]
        lengths_row = lax.dynamic_index_in_dim(
            small[0, :, 4 * nb + nbias : 4 * nb + nbias + docs], z, 0, keepdims=False
        ).astype(jnp.int32)
        begin = doc_begins(lengths_row, L)
        begin = begin[None, :]

        n1, qkv, wq = project(S, C, T, 12, tok, raw.reshape(C, 3, nb, -1), gains[:1], shifts[:1], bias)
        q, k, v, o, lse = attend(qkv, begin)
        mid, n2, cot = sum_norm_gather(S, C, T, 2, o, wo, tok, gains[1:], shifts[1:], [("ctx", cot)])
        gb, gu, act = gates(S, C, T, 4, n2, wg, cot)
        gw_down = mm(gb, act, 0, 0).astype(BF)
        wd, gw_down = after(wd, gw_down)
        gw_down = sum_ctx(gw_down)

        (dgu,) = by_rows(
            gates_back_kernel, "gates_back", [(True, gb), (False, wd), (True, gu)],
            [jax.ShapeDtypeStruct((L, 2 * fn), BF)],
        )
        gw_gateup = mm(n2, dgu, 0, 0).astype(BF)
        dgu, gw_gateup = after(dgu, gw_gateup)
        gw_gateup = sum_ctx(gw_gateup)
        dmid, gb1, stats2 = sum_back_gather(S, C, T, 6, dgu, wg, mid, gb, gains[1:])
        gw_out = mm(gb1, o, 0, 0).astype(BF)
        gb1, gw_out = after(gb1, gw_out)
        gw_out = sum_ctx(gw_out)
        do = mm(gb1, wo, 1, 0).astype(BF)
        dqkv, gbias, got, gw_down = attend_back(
            S, C, T, 11, q, k, v, o, do, lse, begin, act, wd, [("shard", gw_down)]
        )
        out = parts((mid + got).astype(BF))
        gw_qkv = mm(n1, dqkv, 0, 0).astype(BF)
        dqkv, gw_qkv = after(dqkv, gw_qkv)
        gw_qkv = sum_ctx(gw_qkv)
        low, stats1, out, gw_gateup = sum_back(
            S, C, T, 8, dqkv, wq, tok, dmid, gains[:1], [("shard", out), ("shard", gw_gateup)]
        )
        low, gw_gateup, gw_down = lax.optimization_barrier((low, *final(gw_gateup, gw_down)))
        gtok, out, norms, gbias, gw_qkv, gw_out = finish(
            S, C, T, 10, low, out, [stats1, stats2], gbias, gw_qkv, gw_out
        )
        if not ordered(D, S, C):
            gtok, out = unpermute(gtok), unpermute(out)
        gtok = gtok.astype(F32)
        norms = lax.dynamic_slice_in_dim(norms, (z * S + p) * nb % 128, nb, 1) if nb % 128 else norms
        gbias = gbias.reshape(S, 3, heads, S * C, nf)
        gbias = lax.dynamic_index_in_dim(gbias, p * C + z, 3, keepdims=False)
        gbias = gbias.swapaxes(0, 1).reshape(b_qkv.shape)

        return (
            out,
            gtok,
            gw_qkv.swapaxes(0, 1).reshape(w_qkv.shape),
            gbias,
            gw_out.reshape(w_out.shape),
            gw_gateup.reshape(w_gateup.shape),
            gw_down.reshape(w_down.shape),
            norms[None, :2],
            norms[None, 2:],
        )

    return body


def solution(mesh):
    both = ("shard", "ctx")
    specs = (
        P(None, both, None, "tp"),
        P(None, None, "tp", both),
        P(None, "tp", both),
        P(None, both, None, "tp"),
        P(None, "tp", both),
        P(None, None, both),
        P(None, None, both),
    )
    return jax.shard_map(
        make_body(mesh.shape["shard"], mesh.shape["ctx"], mesh.shape["tp"]),
        mesh=mesh,
        in_specs=(P(both, None), P("shard", None)) + specs + (P(both, None),),
        out_specs=(P(both, None), P(both, None)) + specs,
        check_vma=False,
    )
```

```python
import functools

import jax
import jax.numpy as jnp
import numpy as np
from jax import lax
from jax.experimental import pallas as pl
from jax.experimental.pallas import tpu as pltpu
from jax.sharding import PartitionSpec as P

HEAD = 64
ROT = 16
EPS = 1e-05
NEG = -1e30
BASE = 10000.0
BF = jnp.bfloat16
F32 = jnp.float32
BLK = 256
MESH = pl.DeviceIdType.MESH
DMA = pltpu.SemaphoreType.DMA
ANY = pl.BlockSpec(memory_space=pl.ANY)
IN_VMEM = pl.BlockSpec(memory_space=pltpu.VMEM)


def mm(a, b, ca, cb):
    return lax.dot_general(a, b, (((ca,), (cb,)), ((), ())), preferred_element_type=F32)


def remote(src, dst, send, recv, where):
    return pltpu.make_async_remote_copy(
        src_ref=src, dst_ref=dst, send_sem=send, recv_sem=recv, device_id=where, device_id_type=MESH
    )


def here():
    return lax.axis_index("shard"), lax.axis_index("ctx"), lax.axis_index("tp")


class Riders:
    def __init__(self, S, C, riders):
        self.S, self.C = S, C
        self.axes = [axis for axis, _ in riders]
        self.arrays = [x for _, x in riders]
        self.shapes = [
            jax.ShapeDtypeStruct((C,) + x.shape if axis == "all" else x.shape, x.dtype) for axis, x in riders
        ]
        count, most = len(riders), max(S, C) - 1
        self.scratch = [DMA((count, most)), DMA((count, most)), DMA((count,))] if count else []

    def bind(self, ins, outs, sems):
        self.ins, self.outs, self.sems = ins, outs, sems

    def start(self):
        p, z, c = here()
        self.moves = []
        for n, axis in enumerate(self.axes):
            src, dst = self.ins[n], self.outs[n]
            send, recv, own = self.sems
            if axis == "tp":
                copies = [remote(src, dst, send.at[n, 0], recv.at[n, 0], {"tp": 1 - c})]
            elif axis == "all":
                copies = [
                    remote(src, dst.at[z], send.at[n, k - 1], recv.at[n, k - 1], {"ctx": (z + k) % self.C})
                    for k in range(1, self.C)
                ]
                copies.append(pltpu.make_async_copy(src, dst.at[z], own.at[n]))
            else:
                size, me = (self.S, p) if axis == "shard" else (self.C, z)
                copies = [
                    remote(src.at[(me + k) % size], dst.at[me], send.at[n, k - 1], recv.at[n, k - 1], {axis: (me + k) % size})
                    for k in range(1, size)
                ]
                copies.append(pltpu.make_async_copy(src.at[me], dst.at[me], own.at[n]))
            for copy in copies:
                copy.start()
            self.moves += copies

    def wait(self):
        for copy in self.moves:
            copy.wait()


def greet(S, C, mates=(), line=False, other=False, axes=()):
    p, z, c = here()
    peers = [{"shard": q} for q in ([(p + k) % S for k in range(1, S)] if "shard" in axes else mates)]
    if line or "ctx" in axes or "all" in axes:
        peers += [{"ctx": (z + k) % C} for k in range(1, C)]
    if other or "tp" in axes:
        peers.append({"tp": 1 - c})
    barrier = pltpu.get_barrier_semaphore()
    for where in peers:
        pl.semaphore_signal(barrier, inc=1, device_id=where, device_id_type=MESH)
    pl.semaphore_wait(barrier, len(peers))


def comm(kernel, S, C, number, name, args, in_specs, outs, scratch, riders=(), room=62):
    ride = Riders(S, C, riders)
    na, nr, no, ns = len(args), len(ride.axes), len(outs), len(scratch)

    def body(*refs):
        ins, refs = refs[:na], refs[na:]
        rins, refs = refs[:nr], refs[nr:]
        os, refs = refs[:no], refs[no:]
        routs, refs = refs[:nr], refs[nr:]
        ride.bind(rins, routs, refs[ns:])
        kernel(ride, ins, os, refs[:ns])

    return pl.pallas_call(
        body,
        out_shape=[shape for shape, _ in outs] + ride.shapes,
        in_specs=list(in_specs) + [IN_VMEM] * nr,
        out_specs=[spec for _, spec in outs] + [ANY] * nr,
        scratch_shapes=list(scratch) + ride.scratch,
        compiler_params=pltpu.CompilerParams(
            collective_id=number, has_side_effects=True, vmem_limit_bytes=room << 20
        ),
        cost_estimate=pl.CostEstimate(flops=0, bytes_accessed=120_000_000, transcendentals=0),
        name=name,
    )(*args, *ride.arrays)


def exchange(S, C, T, number, riders, tiles, rows, beside, turned):
    R, D = rows.shape
    n, wide, nb = R // T, D // S, D // (S * C)
    pieces = S if ordered(D, S, C) else 1
    p, z, c = here()
    if pieces == 1:
        rows, beside = (
            lax.dynamic_slice_in_dim(x, c * n, n, 0).reshape(n, S, C, nb).transpose(2, 0, 1, 3).reshape(S, n, wide)
            for x in (rows, beside)
        )
    heights = [x.shape[0] // S for x in turned]

    def kernel(ride, ins, outs, scratch):
        tile, x_ref, y_ref, *raws = ins
        got, x_buf, x_out, y_out, *turns = outs
        send, recv, bsend, brecv, own, hsend, hrecv, hown, zsend, zrecv, zown, wsend, wrecv, wown, *stages = scratch
        p, z, c = here()
        mates = [(p + k) % S for k in range(1, S)]
        everyone = [(i, j) for i in range(C) for j in range(S) if i or j]
        peers = [{"shard": (p + j) % S, "ctx": (z + i) % C} for i, j in everyone]
        barrier = pltpu.get_barrier_semaphore()
        for where in peers + [{"tp": 1 - c}]:
            pl.semaphore_signal(barrier, inc=1, device_id=where, device_id_type=MESH)
        pl.semaphore_wait(barrier, len(peers) + 1)

        def columns(ref, q, i):
            if pieces == 1:
                return ref.at[q]
            lanes = pl.ds(pl.multiple_of((i * C + q) * nb, 128), nb)
            return ref.at[pl.ds(pl.multiple_of(c * n, 16), n), lanes]

        def first_hop(ref, out, at):
            hop = []
            for i in range(pieces):
                dst = out.at[p, :, pl.ds(i * (wide // pieces), wide // pieces)]
                hop.append(pltpu.make_async_copy(columns(ref, p, i), dst, hown.at[at, i]))
                for k, q in enumerate(mates):
                    hop.append(
                        remote(columns(ref, q, i), dst, hsend.at[at, k, i], hrecv.at[at, k, i], {"shard": q})
                    )
            for copy in hop:
                copy.start()
            return hop

        x_hop = first_hop(x_ref, x_buf, 0)
        local = pltpu.make_async_copy(tile.at[z, p], got.at[c, z, p], own)
        local.start()
        copies = []
        for at, (where, (i, j)) in enumerate(zip(peers, everyone)):
            q, g = (p + j) % S, (z + i) % C
            copies.append(remote(tile.at[g, q], got.at[c, z, p], send.at[at], recv.at[at], where))
            copies[-1].start()
        ride.start()
        y_hop = first_hop(y_ref, y_out, 1)
        moves = []
        for m, (raw, stage, out, height) in enumerate(zip(raws, stages, turns, heights)):
            for q in range(S):
                stage[q] = raw[q * height : (q + 1) * height, :].astype(F32).T.astype(BF)
            moves.append(pltpu.make_async_copy(stage.at[p], out.at[p], wown.at[m]))
            for k, q in enumerate(mates):
                moves.append(remote(stage.at[q], out.at[p], wsend.at[m, k], wrecv.at[m, k], {"shard": q}))
            for copy in moves[-S:]:
                copy.start()
        for copy in x_hop:
            copy.wait()
        line = [pltpu.make_async_copy(x_buf.at[z], x_out.at[z], zown)]
        for k in range(1, C):
            g = (z + k) % C
            line.append(remote(x_buf.at[g], x_out.at[z], zsend.at[k - 1], zrecv.at[k - 1], {"ctx": g}))
        for copy in line:
            copy.start()
        local.wait()
        for copy in copies:
            copy.wait()
        back = remote(got.at[c], got.at[c], bsend, brecv, {"tp": 1 - c})
        back.start()
        back.wait_send()
        remote(got.at[1 - c], got.at[1 - c], bsend, brecv, {"tp": 1 - c}).wait_recv()
        for copy in line + y_hop + moves:
            copy.wait()
        ride.wait()

    count, m = C * S - 1, len(turned)
    part = jax.ShapeDtypeStruct((S, n, wide), rows.dtype)
    return comm(
        kernel, S, C, number, "exchange", [tiles, rows, beside, *turned],
        [IN_VMEM, ANY, ANY] + [IN_VMEM] * m,
        [(jax.ShapeDtypeStruct((T,) + tiles.shape, tiles.dtype), ANY), (part, IN_VMEM), (part, IN_VMEM), (part, ANY)]
        + [(jax.ShapeDtypeStruct((S, nb, height), BF), ANY) for height in heights],
        [
            DMA((count,)), DMA((count,)), DMA, DMA, DMA,
            DMA((2, S - 1, pieces)), DMA((2, S - 1, pieces)), DMA((2, pieces)),
            DMA((C - 1,)), DMA((C - 1,)), DMA, DMA((m, S - 1)), DMA((m, S - 1)), DMA((m,)),
        ]
        + [pltpu.VMEM((S, nb, height), BF) for height in heights],
        riders,
    )


def plane(S):
    p, _, c = here()
    B = S // 2
    a, b = p // B, p % B
    return a, b, [a * B + (b + j) % B for j in range(1, B)], (1 - a) * B + b


def spread_sems(S):
    count = 4 + 4 * (S // 2 - 1)
    return [DMA((2 * count,)), DMA((2 * count,))]


def spread(S, own, region, send, recv, work=(None, None)):
    p, _, c = here()
    B = S // 2
    a, b, rows, col = plane(S)
    rows, col, other = [{"shard": q} for q in rows], {"shard": col}, {"tp": 1 - c}
    per = 4 + 4 * (B - 1)
    OWN, ROW, COL, VIA_COL, VIA_ROW = 0, 2, 2 + 2 * (B - 1), 4 + 2 * (B - 1), 4 + 3 * (B - 1)
    started = []

    def push(q, h, sem, where, first=False):
        view = region(q, h, c)
        copy = remote(own(h) if first else view, view, send.at[sem], recv.at[sem], where)
        copy.start()
        started.append(copy)

    def came(q, h, sem, core):
        view = region(q, h, core)
        remote(view, view, send.at[sem], recv.at[sem], other).wait_recv()

    for h in range(2):
        for j in range(1, B):
            push(p, h, ROW + 2 * (j - 1) + h, rows[j - 1], True)
    for h in (1, 0):
        push(p, h, COL + h, col, True)
    for h in range(2):
        push(p, h, per + OWN + h, other, True)

    def from_row(j, h):
        q = a * B + (b - j) % B
        came(q, h, ROW + 2 * (j - 1) + h, c)
        push(q, h, per + ROW + 2 * (j - 1) + h, other)
        return q

    def from_col(h):
        q = (1 - a) * B + b
        came(q, h, COL + h, c)
        push(q, h, per + COL + h, other)
        return q

    if work[0] is not None:
        work[0]()
    for j in range(1, B):
        q = from_row(j, 0)
        push(q, 0, VIA_COL + j - 1, col)
    q = from_col(1)
    for j in range(1, B):
        push(q, 1, VIA_ROW + j - 1, rows[j - 1])
    if work[1] is not None:
        work[1]()
    for j in range(1, B):
        from_row(j, 1)
    from_col(0)
    for j in range(1, B):
        q = (1 - a) * B + (b - j) % B
        came(q, 0, VIA_COL + j - 1, c)
        push(q, 0, per + VIA_COL + j - 1, other)
        came(q, 1, VIA_ROW + j - 1, c)
        push(q, 1, per + VIA_ROW + j - 1, other)
    for h in range(2):
        came(p, h, per + OWN + h, 1 - c)
        came((1 - a) * B + b, h, per + COL + h, 1 - c)
    for j in range(1, B):
        for h in range(2):
            came(a * B + (b - j) % B, h, per + ROW + 2 * (j - 1) + h, 1 - c)
        q = (1 - a) * B + (b - j) % B
        came(q, 0, per + VIA_COL + j - 1, 1 - c)
        came(q, 1, per + VIA_ROW + j - 1, 1 - c)
    for copy in started:
        copy.wait_send()


def gather_columns(S, C, T, number, x, riders=(), extra=None, room=62):
    _, n, wide = x.shape
    more, more_specs, more_outs, more_scratch, task = extra or ((), (), (), (), None)

    def kernel(ride, ins, outs, scratch):
        x_ref, out_ref = ins[0], outs[0]
        send, recv, own = scratch[:3]
        p, _, c = here()
        _, _, rows, col = plane(S)

        def region(q, h, core):
            part = pl.ds(pl.multiple_of(q * wide, 128), wide)
            return out_ref.at[pl.ds(h * (C // 2), C // 2), core, :, part]

        local = [
            pltpu.make_async_copy(x_ref.at[pl.ds(h * (C // 2), C // 2)], region(p, h, c), own.at[h]) for h in range(2)
        ]
        for copy in local:
            copy.start()
        if task is not None:
            task(ins[1:], outs[1:], scratch[3:], None)
        greet(S, C, rows + [col], other=True, axes=ride.axes)
        ride.start()
        work = [None, None]
        if task is not None:
            work = [functools.partial(task, ins[1:], outs[1:], scratch[3:], piece) for piece in range(2)]
        spread(S, lambda h: x_ref.at[pl.ds(h * (C // 2), C // 2)], region, send, recv, work)
        for copy in local:
            copy.wait()
        ride.wait()

    out, *rest = comm(
        kernel, S, C, number, "gather_columns", [x, *more], [IN_VMEM, *more_specs],
        [(jax.ShapeDtypeStruct((C, T, n, wide * S), x.dtype), ANY), *more_outs],
        spread_sems(S) + [DMA((2,)), *more_scratch], riders, room,
    )
    return [out.reshape(C * T * n, wide * S)] + rest


CHUNK = 512
ROWS = 32


def sum_scratch(S, n, D):
    half, B = n // 2, S // 2

    def vm(*shape):
        return pltpu.VMEM(shape, BF)

    return [
        vm(S, n, D), vm(S, n, D), vm(S, n, D), vm(B - 1, 2, half, D), vm(B, half, D),
        vm(B - 1, half, D), vm(half, D), vm(half, D), vm(B - 1, half, D),
        DMA((S,)), DMA((S,)), DMA((B - 1, 2)), DMA((B - 1, 2)), DMA((B,)), DMA((B,)), DMA((B,)), DMA((B,)),
    ]


def sum_over_plane(S, T, x_ref, w_ref, out_ref, scratch, meanwhile=None):
    away, sib, mine, row1, col1, row2, col2, to_col, to_row = scratch[:9]
    asend, arecv, rsend, rrecv, csend, crecv, fsend, frecv = scratch[9:]
    n, D = out_ref.shape
    half, B = n // 2, S // 2
    _, _, c = here()
    a, b, rows, col = plane(S)
    rows, col, other = [{"shard": q} for q in rows], {"shard": col}, {"tp": 1 - c}

    def chip(e):
        return ((a + e // B) % 2) * B + (b + e % B) % B

    def product(e, core, store):
        x = x_ref[chip(e) * T + core]

        def column(j, _):
            w = pl.ds(pl.multiple_of(j * CHUNK, CHUNK), CHUNK)
            store(w, mm(x, w_ref[w, :], 1, 1))
            return 0

        lax.fori_loop(0, D // CHUNK, column, 0)

    def to_other(e):
        return remote(away.at[e], sib.at[e], asend.at[e], arecv.at[e], other)

    def for_other(e):
        def store(w, value):
            away[e, :, w] = value.astype(BF)

        product(e, 1 - c, store)
        to_other(e).start()

    for_other(S - 1)
    top, low = pl.ds(0, half), pl.ds(half, half)
    started = []

    def push(src, dst, send, recv, where):
        copy = remote(src, dst, send, recv, where)
        copy.start()
        started.append(copy)

    for e in range(S - 1, -1, -1):
        if e:
            for_other(e - 1)
        to_other(e).wait()

        def store(w, value):
            value = value + sib[e, :, w].astype(F32)
            if e:
                mine[e, :, w] = value.astype(BF)
            else:
                out_ref[:, w] = value

        product(e, c, store)
        j = e % B
        if e > B:
            push(mine.at[e, top], row1.at[j - 1, 1], rsend.at[j - 1, 1], rrecv.at[j - 1, 1], rows[j - 1])
            push(mine.at[e, low], col1.at[j], csend.at[j], crecv.at[j], col)
        elif e == B:
            push(mine.at[e, low], col1.at[0], csend.at[0], crecv.at[0], col)
        elif e:
            push(mine.at[e, top], row1.at[j - 1, 0], rsend.at[j - 1, 0], rrecv.at[j - 1, 0], rows[j - 1])

    def came(ref, send, recv):
        remote(ref, ref, send, recv, other).wait_recv()

    if meanwhile is not None:
        meanwhile(0)
    total = mine[B, top, :].astype(F32)
    for j in range(1, B):
        came(row1.at[j - 1, 1], rsend.at[j - 1, 1], rrecv.at[j - 1, 1])
        total = total + row1[j - 1, 1].astype(F32)
    to_col[...] = total.astype(BF)
    push(to_col, col2, fsend.at[0], frecv.at[0], col)
    for j in range(1, B):
        came(col1.at[j], csend.at[j], crecv.at[j])
        to_row[j - 1] = (mine[j, low, :].astype(F32) + col1[j].astype(F32)).astype(BF)
        push(to_row.at[j - 1], row2.at[j - 1], fsend.at[j], frecv.at[j], rows[j - 1])
    if meanwhile is not None:
        meanwhile(1)
    came(col1.at[0], csend.at[0], crecv.at[0])
    upper, lower = out_ref[top, :], out_ref[low, :] + col1[0].astype(F32)
    for j in range(1, B):
        came(row1.at[j - 1, 0], rsend.at[j - 1, 0], rrecv.at[j - 1, 0])
        upper = upper + row1[j - 1, 0].astype(F32)
    came(col2, fsend.at[0], frecv.at[0])
    out_ref[top, :] = upper + col2[...].astype(F32)
    for j in range(1, B):
        came(row2.at[j - 1], fsend.at[j], frecv.at[j])
        lower = lower + row2[j - 1].astype(F32)
    out_ref[low, :] = lower
    for copy in started:
        copy.wait_send()


def project(S, C, T, number, tok, raw, gain, shift, bias):
    L, D = tok.shape
    _, parts, nb, wide = raw.shape
    hn = wide // S
    most = S - 1

    def kernel(ride, ins, outs, scratch):
        tok_ref, raw_ref, gain_ref, shift_ref, bias_ref = ins
        n_ref, out_ref, w_ref = outs
        send, recv, own = scratch
        p, _, _ = here()
        mates = [(p + k) % S for k in range(1, S)]
        greet(S, C, mates)

        def lanes(q):
            return pl.ds(pl.multiple_of(q * hn, 128), hn)

        copies = []
        for part in range(parts):
            dst = w_ref.at[:, p, :, pl.ds(part * hn, hn)]
            for k, q in enumerate(mates):
                copies.append(
                    remote(raw_ref.at[:, part, :, lanes(q)], dst, send.at[k, part], recv.at[k, part], {"shard": q})
                )
            copies.append(pltpu.make_async_copy(raw_ref.at[:, part, :, lanes(p)], dst, own.at[part]))
        for copy in copies:
            copy.start()

        def normed(r):
            n_ref[r, :] = (norm_of(tok_ref[r, :].astype(F32))[0] * gain_ref[...] + shift_ref[...]).astype(BF)

        row_blocks(L, normed)
        for copy in copies:
            copy.wait()
        w = w_ref[...].reshape(D, parts * hn)

        @pl.loop(0, L // BLK)
        def _(i):
            r = pl.ds(pl.multiple_of(i * BLK, BLK), BLK)
            out_ref[r, :] = mm(n_ref[r, :], w, 1, 0) + bias_ref[...]

    n, out, w = comm(
        kernel, S, C, number, "project", [tok, raw, gain, shift, bias], [IN_VMEM] * 5,
        [
            (jax.ShapeDtypeStruct((L, D), BF), IN_VMEM), (jax.ShapeDtypeStruct((L, parts * hn), F32), IN_VMEM),
            (jax.ShapeDtypeStruct((C, S, nb, parts * hn), BF), IN_VMEM),
        ],
        [DMA((most, parts)), DMA((most, parts)), DMA((parts,))],
    )
    return n, out, w.reshape(D, parts * hn)


def gates_back_kernel(gb_ref, wd_ref, gu_ref, dgu_ref):
    dact = mm(gb_ref[...], wd_ref[...], 1, 0)
    both, width = gu_ref[...], dact.shape[1]
    gate, up = both[:, :width], both[:, width:]
    s = jax.nn.sigmoid(gate)
    dgate = dact * up * s * (1.0 + gate * (1.0 - s))
    dgu_ref[...] = jnp.concatenate((dgate, dact * gate * s), axis=1).astype(BF)


def gates_work(ins, outs, scratch, piece):
    gu_ref, act_ref = outs
    n2_ref, wg_ref, sems = scratch
    if piece != 1:
        for i, (x, y) in enumerate(zip(ins, (n2_ref, wg_ref))):
            copy = pltpu.make_async_copy(x, y, sems.at[i])
            copy.wait() if piece == 0 else copy.start()
    if piece is None:
        return
    (rows, width), half = act_ref.shape, act_ref.shape[0] // BLK // 2

    @pl.loop(piece * half, piece * half + half)
    def _(i):
        r = pl.ds(pl.multiple_of(i * BLK, BLK), BLK)
        both = mm(n2_ref[r, :], wg_ref[...], 1, 0)
        gu_ref[r, :] = both
        gate, up = both[:, :width], both[:, width:]
        act_ref[r, :] = (gate * jax.nn.sigmoid(gate) * up).astype(BF)


def gates(S, C, T, number, n2, wg, x):
    L, width = n2.shape[0], wg.shape[1] // 2
    outs = [jax.ShapeDtypeStruct((L, 2 * width), F32), jax.ShapeDtypeStruct((L, width), BF)]
    return gather_columns(
        S, C, T, number, x, (),
        ([n2, wg], [ANY, ANY], [(shape, IN_VMEM) for shape in outs],
         [pltpu.VMEM(n2.shape, BF), pltpu.VMEM(wg.shape, BF), DMA((2,))], gates_work),
        50,
    )


def by_rows(kernel, name, arrays, outs):
    L = outs[0].shape[0]

    def spec(width):
        return pl.BlockSpec((BLK, width), lambda i: (i, 0))

    return pl.pallas_call(
        kernel,
        grid=(L // BLK,),
        in_specs=[spec(x.shape[1]) if rows else pl.BlockSpec(x.shape, lambda i: (0, 0)) for rows, x in arrays],
        out_specs=[spec(x.shape[1]) for x in outs],
        out_shape=outs,
        compiler_params=pltpu.CompilerParams(vmem_limit_bytes=62 << 20),
        name=name,
    )(*[x for _, x in arrays])


def row_blocks(n, work):
    @pl.loop(0, n // ROWS)
    def _(i):
        work(pl.ds(pl.multiple_of(i * ROWS, ROWS), ROWS))


def own_rows(T, x_ref, row_ref, sem):
    p, _, c = here()
    copy = pltpu.make_async_copy(x_ref.at[p * T + c], row_ref, sem)
    copy.start()
    return copy


def norm_of(v):
    center = v - jnp.mean(v, axis=-1, keepdims=True)
    inverse = lax.rsqrt(jnp.mean(center * center, axis=-1, keepdims=True) + EPS)
    return center * inverse, inverse


def norm_back(v, g, gain, stats_ref):
    normal, inverse = norm_of(v)
    e = g * gain
    stats_ref[0:1, :] += jnp.sum(g * normal, axis=0, keepdims=True)
    stats_ref[1:2, :] += jnp.sum(g, axis=0, keepdims=True)
    return inverse * (
        e - jnp.mean(e, axis=-1, keepdims=True) - normal * jnp.mean(e * normal, axis=-1, keepdims=True)
    )


def spread_rows(S, T, src, out_ref, send, recv, own):
    p, _, c = here()
    half = src.shape[0] // 2
    local = pltpu.make_async_copy(src, out_ref.at[p * T + c], own)
    local.start()
    spread(
        S,
        lambda h: src.at[pl.ds(h * half, half)],
        lambda q, h, core: out_ref.at[q * T + core, pl.ds(h * half, half)],
        send,
        recv,
    )
    local.wait()


def sum_norm_gather(S, C, T, number, x, w, residual, gain, shift, riders=()):
    L, K = x.shape
    D, n = w.shape[0], L // (S * T)

    def kernel(ride, ins, outs, scratch):
        x_ref, w_ref, all_ref, gain_ref, shift_ref = ins
        v_ref, out_ref = outs
        acc, low, send, recv, own, res_ref, sem = scratch[:7]
        _, _, rows, col = plane(S)
        rest = own_rows(T, all_ref, res_ref, sem)
        greet(S, C, rows + [col], other=True, axes=ride.axes)
        ride.start()
        sum_over_plane(S, T, x_ref, w_ref, acc, scratch[7:])
        rest.wait()

        def work(r):
            v = res_ref[r, :].astype(F32) + acc[r, :]
            v_ref[r, :] = v
            low[r, :] = (norm_of(v)[0] * gain_ref[...] + shift_ref[...]).astype(BF)

        row_blocks(n, work)
        spread_rows(S, T, low, out_ref, send, recv, own)
        ride.wait()

    v, out, *rest = comm(
        kernel, S, C, number, "sum_norm_gather", [x.reshape(S * T, n, K), w, residual.reshape(S * T, n, D), gain, shift],
        [IN_VMEM, IN_VMEM, ANY, IN_VMEM, IN_VMEM],
        [(jax.ShapeDtypeStruct((n, D), F32), IN_VMEM), (jax.ShapeDtypeStruct((S * T, n, D), BF), ANY)],
        [pltpu.VMEM((n, D), F32), pltpu.VMEM((n, D), BF)] + spread_sems(S)
        + [DMA, pltpu.VMEM((n, D), BF), DMA] + sum_scratch(S, n, D),
        riders,
    )
    return [v, out.reshape(L, D)] + rest


def sum_back_gather(S, C, T, number, x, w, v, residual, gain, riders=()):
    L, K = x.shape
    D, n = w.shape[0], L // (S * T)

    def kernel(ride, ins, outs, scratch):
        x_ref, w_ref, in_ref, all_ref, gain_ref = ins
        v_ref, out_ref, stats = outs
        acc, low, send, recv, own, res_ref, sem = scratch[:7]
        _, _, rows, col = plane(S)
        rest = own_rows(T, all_ref, res_ref, sem)
        greet(S, C, rows + [col], other=True, axes=ride.axes)
        ride.start()
        sum_over_plane(S, T, x_ref, w_ref, acc, scratch[7:])
        rest.wait()
        stats[...] = jnp.zeros_like(stats)

        def work(r):
            g = res_ref[r, :].astype(F32) + norm_back(in_ref[r, :], acc[r, :], gain_ref[...], stats)
            v_ref[r, :] = g
            low[r, :] = g.astype(BF)

        row_blocks(n, work)
        spread_rows(S, T, low, out_ref, send, recv, own)
        ride.wait()

    g, out, stats, *rest = comm(
        kernel, S, C, number, "sum_back_gather", [x.reshape(S * T, n, K), w, v, residual.reshape(S * T, n, D), gain],
        [IN_VMEM, IN_VMEM, IN_VMEM, ANY, IN_VMEM],
        [
            (jax.ShapeDtypeStruct((n, D), F32), IN_VMEM), (jax.ShapeDtypeStruct((S * T, n, D), BF), ANY),
            (jax.ShapeDtypeStruct((2, D), F32), IN_VMEM),
        ],
        [pltpu.VMEM((n, D), F32), pltpu.VMEM((n, D), BF)] + spread_sems(S)
        + [DMA, pltpu.VMEM((n, D), BF), DMA] + sum_scratch(S, n, D),
        riders,
    )
    return [g, out.reshape(L, D), stats] + rest


def sum_back(S, C, T, number, x, w, v, residual, gain, riders=()):
    L, K = x.shape
    D, n = w.shape[0], L // (S * T)

    def kernel(ride, ins, outs, scratch):
        x_ref, w_ref, all_ref, res_ref, gain_ref = ins
        low, stats = outs
        acc, in_ref, sem = scratch[:3]
        _, _, rows, col = plane(S)
        rest = own_rows(T, all_ref, in_ref, sem)
        greet(S, C, rows + [col], other=True, axes=ride.axes)
        ride.start()
        sum_over_plane(S, T, x_ref, w_ref, acc, scratch[3:])
        rest.wait()
        stats[...] = jnp.zeros_like(stats)

        def work(r):
            g = res_ref[r, :] + norm_back(in_ref[r, :].astype(F32), acc[r, :], gain_ref[...], stats)
            low[r, :] = g.astype(BF)

        row_blocks(n, work)
        ride.wait()

    return comm(
        kernel, S, C, number, "sum_back", [x.reshape(S * T, n, K), w, v.reshape(S * T, n, D), residual, gain],
        [IN_VMEM, IN_VMEM, ANY, IN_VMEM, IN_VMEM],
        [(jax.ShapeDtypeStruct((n, D), BF), IN_VMEM), (jax.ShapeDtypeStruct((2, D), F32), IN_VMEM)],
        [pltpu.VMEM((n, D), F32), pltpu.VMEM((n, D), BF), DMA] + sum_scratch(S, n, D),
        riders,
    )


def finish(S, C, T, number, x, y, stats, bias, qkv, out):
    n, D = x.shape
    hn = out.shape[2]
    wide, lines = D // S, bias.shape[1] // 128
    nb = D // (S * C)
    count = sum(z.shape[0] for z in stats)
    tall = -(-(count + lines) // 8) * 8
    many = C * S - 1
    pieces = S if ordered(D, S, C) else 1

    def kernel(ride, ins, outs, scratch):
        x_ref, y_ref, stat_refs, bias_ref = ins[0], ins[1], ins[2:-3], ins[-3]
        qkv_ref, o_ref = ins[-2:]
        x_out, y_out, norm_out, bias_out, qkv_out, o_out = outs
        xbuf, xbuf2, ybuf2, tile, send, recv, own, psend, precv, pown, lsend, lrecv, tsend, trecv = scratch[:14]
        qkv_buf, o_buf, gsend, grecv, gown, got = scratch[14:]
        p, z, c = here()
        other = {"tp": 1 - c}
        everyone = [(i, j) for i in range(C) for j in range(S) if i or j]
        peers = [{"shard": (p + j) % S, "ctx": (z + i) % C} for i, j in everyone]
        barrier = pltpu.get_barrier_semaphore()
        for where in peers + [other]:
            pl.semaphore_signal(barrier, inc=1, device_id=where, device_id_type=MESH)
        pl.semaphore_wait(barrier, len(peers) + 1)

        def part(q):
            return pl.ds(pl.multiple_of(q * wide, 128), wide)

        def turn_over(source, target, at, size, me, axis):
            hop = [pltpu.make_async_copy(source(me), target, own.at[at])]
            for k in range(1, size):
                q = (me + k) % size
                hop.append(remote(source(q), target, send.at[at, k - 1], recv.at[at, k - 1], {axis: q}))
            for copy in hop:
                copy.start()
            return hop

        def arrive(buf, out, at):
            hop = []
            for i in range(pieces):
                src = pl.ds(i * (wide // pieces), wide // pieces)
                first = (i * C + p) * nb if pieces > 1 else p * wide
                dst = out.at[c, :, pl.ds(pl.multiple_of(first, 128), wide // pieces)]
                hop.append(pltpu.make_async_copy(buf.at[p, :, src], dst, pown.at[at, i]))
                for k in range(1, S):
                    q = (p + k) % S
                    hop.append(
                        remote(buf.at[q, :, src], dst, psend.at[at, k - 1, i], precv.at[at, k - 1, i], {"shard": q})
                    )
            for copy in hop:
                copy.start()
            return hop

        def both(ref, at):
            copy = remote(ref.at[c], ref.at[c], lsend.at[at], lrecv.at[at], other)
            copy.start()
            return copy

        def settle(ref, at, copy):
            copy.wait_send()
            remote(ref.at[1 - c], ref.at[1 - c], lsend.at[at], lrecv.at[at], other).wait_recv()

        x_hop = turn_over(lambda q: x_ref.at[:, part(q)], xbuf.at[p], 0, S, p, "shard")
        y_hop = turn_over(lambda q: y_ref.at[q], ybuf2.at[z], 1, C, z, "ctx")
        moves = []
        for i, (src, dst) in enumerate(((qkv_ref, qkv_buf), (o_ref, o_buf))):
            moves.append(pltpu.make_async_copy(src.at[p], dst.at[p], gown.at[i]))
            for k in range(1, S):
                q = (p + k) % S
                moves.append(remote(src.at[q], dst.at[p], gsend.at[i, k - 1], grecv.at[i, k - 1], {"shard": q}))
        for copy in moves:
            copy.start()
        tile[...] = jnp.zeros_like(tile)
        at = count
        for i, ref in enumerate(stat_refs):
            for j in range(2):
                tile[j * len(stat_refs) + i : j * len(stat_refs) + i + 1, :] = ref[j : j + 1, :]
        for k in range(lines):
            for block in range(D // 128):
                tile[at + k : at + k + 1, pl.ds(block * 128, 128)] = bias_ref[:, pl.ds(k * 128, 128)]

        def columns(g, q):
            return tile.at[:, pl.ds(pl.multiple_of((g * S + q) * nb // 128 * 128, 128), 128)]

        small = [pltpu.make_async_copy(columns(z, p), got.at[c, z, p], own.at[3])]
        for k, (where, (i, j)) in enumerate(zip(peers, everyone)):
            small.append(
                remote(columns((z + i) % C, (p + j) % S), got.at[c, z, p], tsend.at[k], trecv.at[k], where)
            )
        for copy in small:
            copy.start()
        for copy in x_hop:
            copy.wait()
        x_hop = turn_over(lambda q: xbuf.at[q], xbuf2.at[z], 2, C, z, "ctx")
        for copy in y_hop:
            copy.wait()
        y_hop = arrive(ybuf2, y_out, 0)
        for copy in small:
            copy.wait()
        small_last = both(got, 0)
        bias_out[...] = jnp.sum(got[c, :, :, count : count + lines, :], axis=0)
        for copy in x_hop:
            copy.wait()
        x_hop = arrive(xbuf2, x_out, 1)
        for copy in y_hop:
            copy.wait()
        y_last = both(y_out, 1)
        for copy in moves:
            copy.wait()
        for q in range(S):
            o_out[q * hn : (q + 1) * hn, :] = o_buf[q].astype(F32).T
            for i in range(3):
                qkv_out[i, :, q * hn : (q + 1) * hn] = qkv_buf[q, :, i * hn : (i + 1) * hn].astype(F32)
        for copy in x_hop:
            copy.wait()
        x_last = both(x_out, 2)
        settle(got, 0, small_last)
        norm_out[...] = jnp.sum(got[:, :, :, :count, :], axis=(0, 1, 2))
        settle(y_out, 1, y_last)
        settle(x_out, 2, x_last)

    args = [x, y, *stats, bias, qkv, out]
    most = max(S, C) - 1
    home = (jax.ShapeDtypeStruct((T, n, D), BF), ANY)
    x, y, *rest = comm(
        kernel, S, C, number, "finish", args, [IN_VMEM] * len(args),
        [home, home]
        + [
            (jax.ShapeDtypeStruct(shape, F32), IN_VMEM)
            for shape in ((count, 128), (S, lines, 128), (3, nb, S * hn), (S * hn, nb))
        ],
        [
            pltpu.VMEM((S, n, wide), BF), pltpu.VMEM((C, n, wide), BF), pltpu.VMEM((C, n, wide), BF),
            pltpu.VMEM((tall, D), F32), DMA((3, most)), DMA((3, most)), DMA((4,)),
            DMA((2, S - 1, pieces)), DMA((2, S - 1, pieces)), DMA((2, pieces)), DMA((3,)), DMA((3,)),
            DMA((many,)), DMA((many,)),
            pltpu.VMEM(qkv.shape, BF), pltpu.VMEM(out.shape, BF), DMA((2, S - 1)), DMA((2, S - 1)), DMA((2,)),
            pltpu.VMEM((T, C, S, tall, 128), F32),
        ],
    )
    return [x.reshape(T * n, D), y.reshape(T * n, D)] + rest


def final_kernel(gateup_ref, down_ref, gateup_out, down_out):
    S, _, fn = down_ref.shape
    for q in range(S):
        down_out[q * fn : (q + 1) * fn, :] = down_ref[q].astype(F32).T
        for i in range(2):
            gateup_out[:, i, q * fn : (q + 1) * fn] = gateup_ref[q, :, i * fn : (i + 1) * fn].astype(F32)


def final(gateup, down):
    S, nb, fn = down.shape
    return pl.pallas_call(
        final_kernel,
        in_specs=[IN_VMEM] * 2,
        out_specs=[IN_VMEM] * 2,
        out_shape=[jax.ShapeDtypeStruct((nb, 2, S * fn), F32), jax.ShapeDtypeStruct((S * fn, nb), F32)],
        compiler_params=pltpu.CompilerParams(vmem_limit_bytes=62 << 20),
        name="final",
    )(gateup, down)


def ordered(D, S, C):
    return D // (S * C) % 128 == 0


def turn_tables(rows):
    feature = np.arange(128) % HEAD
    freq = np.where(feature < ROT, BASE ** (-2.0 * (feature % (ROT // 2)) / ROT), 0.0)
    near = np.arange(BLK)[:, None] * freq
    far = np.arange(0, rows, BLK)[:, None] * freq
    return [jnp.asarray(f(x), F32) for x in (near, far) for f in (np.cos, np.sin)]


def turn(x, i, tables, sign):
    cos, sin, cos_far, sin_far = tables
    far_cos, far_sin = cos_far[pl.ds(i, 1), :], sin_far[pl.ds(i, 1), :]
    cos_t = cos[...] * far_cos - sin[...] * far_sin
    sin_t = sin[...] * far_cos + cos[...] * far_sin
    ahead = lax.broadcasted_iota(jnp.int32, x.shape, 1) % HEAD < ROT // 2
    partner = jnp.where(ahead, -pltpu.roll(x, 128 - ROT // 2, 1), pltpu.roll(x, ROT // 2, 1))
    return x * cos_t + partner * (sin_t * sign)


def two_heads(x, left):
    zero = jnp.zeros_like(x)
    return [jnp.where(left, x, zero), jnp.where(left, zero, x)]


def block_of(rows):
    return next(size for size in (512, 256) if rows % size == 0)


def attend_kernel(
    first_ref, qkv_ref, cos_ref, sin_ref, cosf_ref, sinf_ref, begin_ref,
    qo_ref, ko_ref, vo_ref, o_ref, lse_ref, vt_ref,
):
    rows, wide = qo_ref.shape
    pairs, size = wide // 128, block_of(rows)
    tables = (cos_ref, sin_ref, cosf_ref, sinf_ref)
    left = lax.broadcasted_iota(jnp.int32, (size, 128), 1) < HEAD
    key_at = lax.broadcasted_iota(jnp.int32, (size, size), 0)
    query_at = lax.broadcasted_iota(jnp.int32, (1, size), 1)

    @pl.loop(0, rows // BLK)
    def _(i):
        r = pl.ds(pl.multiple_of(i * BLK, BLK), BLK)
        for t in range(pairs):
            w = pl.ds(t * 128, 128)
            q, k, v = (qkv_ref[r, pl.ds(part * wide + t * 128, 128)] for part in range(3))
            qo_ref[r, w] = turn(q, i, tables, 1.0).astype(BF) * jnp.asarray(HEAD**-0.5, BF)
            ko_ref[r, w] = turn(k, i, tables, 1.0).astype(BF)
            vo_ref[r, w] = v.astype(BF)
            vt_ref[w, r] = v.T.astype(BF)

    @pl.loop(0, rows // size)
    def _(i):
        r = pl.ds(pl.multiple_of(i * size, size), size)
        qs = sum((two_heads(qo_ref[r, pl.ds(t * 128, 128)], left) for t in range(pairs)), [])
        begin = begin_ref[0:1, r]
        here = query_at + i * size

        def step(j, carry):
            w = pl.ds(pl.multiple_of(j * size, size), size)
            key = key_at + j * size
            seen = (key <= here) & (key >= begin)
            out = []
            for h in range(2 * pairs):
                m, l, acc = carry[h]
                s = jnp.where(seen, mm(ko_ref[w, pl.ds(h // 2 * 128, 128)], qs[h], 1, 1), NEG)
                top = jnp.maximum(m, jnp.max(s, axis=0, keepdims=True))
                fade = jnp.exp(m - top)
                e = jnp.exp(s - top)
                acc = acc * fade + mm(vt_ref[pl.ds(h * HEAD, HEAD), w], e.astype(BF), 1, 0)
                out.append((top, l * fade + jnp.sum(e, axis=0, keepdims=True), acc))
            return tuple(out)

        start = (
            jnp.full((1, size), NEG, F32), jnp.zeros((1, size), F32), jnp.zeros((HEAD, size), F32)
        )
        done = lax.fori_loop(first_ref[i], i + 1, step, (start,) * (2 * pairs))
        for t in range(pairs):
            both = []
            for h in (2 * t, 2 * t + 1):
                m, l, acc = done[h]
                both.append(acc / l)
                lse_ref[h : h + 1, r] = m + jnp.log(l)
            o_ref[r, pl.ds(t * 128, 128)] = jnp.concatenate(both, axis=0).T.astype(BF)


def attend(qkv, begin):
    rows, wide = qkv.shape[0], qkv.shape[1] // 3
    size = block_of(rows)
    half = jax.ShapeDtypeStruct((rows, wide), BF)
    return pl.pallas_call(
        attend_kernel,
        in_specs=[pl.BlockSpec(memory_space=pltpu.SMEM)] + [IN_VMEM] * 6,
        out_specs=[IN_VMEM] * 5,
        out_shape=[half] * 4 + [jax.ShapeDtypeStruct((wide // HEAD, rows), F32)],
        scratch_shapes=[pltpu.VMEM((wide, rows), BF)],
        compiler_params=pltpu.CompilerParams(vmem_limit_bytes=62 << 20),
        name="attend",
    )(begin[0, ::size] // size, qkv, *turn_tables(rows), begin)


def attend_back_work(ins, out_ref, bias_ref, scratch, piece):
    q_ref, k_ref, v_ref, o_ref, do_ref, lse_ref, cos_ref, sin_ref, cosf_ref, sinf_ref, begin_ref = ins
    kt_ref, dq_ref, dk_ref, dv_ref = scratch
    rows, wide = q_ref.shape
    pairs, size = wide // 128, block_of(rows)
    tables = (cos_ref, sin_ref, cosf_ref, sinf_ref)
    left = lax.broadcasted_iota(jnp.int32, (size, 128), 1) < HEAD
    key_at = lax.broadcasted_iota(jnp.int32, (size, size), 0)
    query_at = lax.broadcasted_iota(jnp.int32, (1, size), 1)

    last = rows // size - 1
    first, stop = (0, last) if piece == 0 else (last, last + 1)

    def prepare(i):
        r = pl.ds(pl.multiple_of(i * BLK, BLK), BLK)
        for t in range(pairs):
            w = pl.ds(t * 128, 128)
            kt_ref[w, r] = k_ref[r, w].astype(F32).T.astype(BF)
            dk_ref[r, w] = jnp.zeros((BLK, 128), F32)
            dv_ref[r, w] = jnp.zeros((BLK, 128), F32)

    if piece == 0:
        pl.loop(0, rows // BLK)(prepare)

    @pl.loop(first, stop)
    def _(i):
        r = pl.ds(pl.multiple_of(i * size, size), size)
        qs, dos, deltas, lses = [], [], [], []
        for t in range(pairs):
            w = pl.ds(t * 128, 128)
            do = do_ref[r, w]
            qs += two_heads(q_ref[r, w], left)
            dos += two_heads(do, left)
            prod = (do.astype(F32) * o_ref[r, w].astype(F32)).T
            deltas += [jnp.sum(prod[:HEAD], axis=0, keepdims=True), jnp.sum(prod[HEAD:], axis=0, keepdims=True)]
            lses += [lse_ref[2 * t : 2 * t + 1, r], lse_ref[2 * t + 1 : 2 * t + 2, r]]
        begin = begin_ref[0:1, r]
        here = query_at + i * size

        def step(j, carry):
            w = pl.ds(pl.multiple_of(j * size, size), size)
            key = key_at + j * size
            seen = (key <= here) & (key >= begin)
            out = []
            for t in range(pairs):
                lanes = pl.ds(t * 128, 128)
                k, v = k_ref[w, lanes], v_ref[w, lanes]
                dk = dv = None
                for h in (2 * t, 2 * t + 1):
                    prob = jnp.exp(jnp.where(seen, mm(k, qs[h], 1, 1) - lses[h], NEG))
                    ds = (prob * (mm(v, dos[h], 1, 1) - deltas[h])).astype(BF)
                    out.append(carry[h] + mm(kt_ref[pl.ds(h * HEAD, HEAD), w], ds, 1, 0))
                    dk_h, dv_h = mm(ds, qs[h], 1, 0), mm(prob.astype(BF), dos[h], 1, 0)
                    dk, dv = (dk_h, dv_h) if dk is None else (dk + dk_h, dv + dv_h)
                dk_ref[w, lanes] += dk
                dv_ref[w, lanes] += dv
            return tuple(out)

        done = lax.fori_loop(0, i + 1, step, (jnp.zeros((HEAD, size), F32),) * (2 * pairs))
        for t in range(pairs):
            both = jnp.concatenate(done[2 * t : 2 * t + 2], axis=0)
            dq_ref[r, pl.ds(t * 128, 128)] = both.T * (HEAD**-0.5)

    if piece == 0:
        return
    bias_ref[...] = jnp.zeros_like(bias_ref)

    @pl.loop(0, rows // BLK)
    def _(i):
        r = pl.ds(pl.multiple_of(i * BLK, BLK), BLK)
        for t in range(pairs):
            w = pl.ds(t * 128, 128)
            for part, value in enumerate((turn(dq_ref[r, w], i, tables, -1.0), turn(dk_ref[r, w], i, tables, -1.0), dv_ref[r, w])):
                lanes = pl.ds(part * wide + t * 128, 128)
                value = value.astype(BF)
                out_ref[r, lanes] = value
                bias_ref[:, lanes] += jnp.sum(value.astype(F32), axis=0, keepdims=True)


def attend_back(S, C, T, number, q, k, v, o, do, lse, begin, act, wd, riders):
    rows, wide = q.shape
    K, D, n = act.shape[1], wd.shape[0], rows // (S * T)

    def kernel(ride, ins, outs, scratch):
        _, _, row, col = plane(S)
        greet(S, C, row + [col], other=True, axes=ride.axes)

        def meanwhile(piece):
            if piece == 0:
                ride.start()
            attend_back_work(ins[2:], outs[0], outs[1], scratch[:4], piece)

        sum_over_plane(S, T, ins[0], ins[1], outs[2], scratch[4:], meanwhile)
        ride.wait()

    args = [act.reshape(S * T, n, K), wd, q, k, v, o, do, lse, *turn_tables(rows), begin]
    return comm(
        kernel, S, C, number, "attend_back", args, [IN_VMEM] * len(args),
        [(jax.ShapeDtypeStruct((rows, 3 * wide), BF), IN_VMEM), (jax.ShapeDtypeStruct((1, 3 * wide), F32), IN_VMEM),
         (jax.ShapeDtypeStruct((n, D), F32), IN_VMEM)],
        [pltpu.VMEM((wide, rows), BF)] + [pltpu.VMEM((rows, wide), F32)] * 3 + sum_scratch(S, n, D),
        riders,
    )


def doc_begins(lengths_row, rows):
    row_ids = jnp.arange(rows, dtype=jnp.int32)
    ends = jnp.cumsum(lengths_row, dtype=jnp.int32)
    begins = ends - lengths_row
    inside = (row_ids[:, None] >= begins[None, :]) & (row_ids[:, None] < ends[None, :])
    return jnp.sum(jnp.where(inside, begins[None, :], 0), axis=1, dtype=jnp.int32)


def tiles_of(parts, lead):
    flat = jnp.concatenate([x.astype(F32).reshape(lead + (-1,)) for x in parts], axis=-1)
    flat = jnp.pad(flat, ((0, 0),) * len(lead) + ((0, 1024 - flat.shape[-1]),))
    return flat.reshape(lead + (8, 128))


def make_body(S, C, T):
    assert S == C

    def body(tokens, lengths, w_qkv, b_qkv, w_out, w_gateup, w_down, norm_gain, norm_bias, cotangent):
        p, z, c = lax.axis_index("shard"), lax.axis_index("ctx"), lax.axis_index("tp")
        R, D = tokens.shape
        n = R // T
        nb = D // (S * C)
        L = R * C

        def parts(x):
            return x.reshape(n, S, D // S).swapaxes(0, 1)

        def unpermute(x):
            return x.reshape(x.shape[0], C, S, nb).swapaxes(1, 2).reshape(x.shape)

        def after(x, y):
            return lax.optimization_barrier((x, y))

        def over_ctx(w):
            return lax.all_gather(w.reshape(S * nb, -1), "ctx", axis=0, tiled=True)

        def sum_ctx(g):
            g = lax.psum_scatter(g.astype(BF), "ctx", scatter_dimension=0, tiled=True)
            return g.reshape(S, nb, -1)

        hn = w_qkv.shape[3] // S
        fn = w_gateup.shape[3] // S
        heads = hn // HEAD
        nf = HEAD // (S * C)

        tile = tiles_of((norm_gain[0].reshape(-1), norm_bias[0].reshape(-1), b_qkv[0].reshape(-1), lengths[0]), ())
        raw = lax.all_gather(w_qkv[0].swapaxes(0, 1).reshape(3 * nb, -1), "ctx", axis=0, tiled=True)
        small, _, tok, cot, wo, wd, wg = exchange(
            S, C, T, 0,
            [("shard", w_gateup[0].reshape(nb, 2, S, fn).transpose(2, 0, 1, 3).reshape(S, nb, 2 * fn))],
            jnp.broadcast_to(tile, (C, S, 8, 128)),
            tokens,
            cotangent,
            [w_out[0], w_down[0]],
        )
        tok, wo, cot = gather_columns(S, C, T, 1, tok, [("all", wo.reshape(S * nb, hn)), ("ctx", cot)])
        wg, wd, tok = lax.optimization_barrier((wg, wd, tok))
        wo, wg, wd = wo.reshape(D, hn), over_ctx(wg), over_ctx(wd)

        small = lax.dynamic_index_in_dim(small, c, 0, keepdims=False).reshape(C, S, 1024)
        norms = small[:, :, : 4 * nb].reshape(C * S, 4, nb).swapaxes(0, 1).reshape(4, D)
        gains, shifts = norms[:2], norms[2:]
        nbias = 3 * S * heads * nf
        bias = small[:, :, 4 * nb : 4 * nb + nbias].reshape(C, S, 3, S * heads, nf)
        bias = lax.dynamic_slice_in_dim(bias, p * heads, heads, 3)
        bias = bias.transpose(2, 3, 1, 0, 4).reshape(1, 3 * hn)
        docs = lengths.shape[1]
        lengths_row = lax.dynamic_index_in_dim(
            small[0, :, 4 * nb + nbias : 4 * nb + nbias + docs], z, 0, keepdims=False
        ).astype(jnp.int32)
        begin = doc_begins(lengths_row, L)
        begin = begin[None, :]

        n1, qkv, wq = project(S, C, T, 12, tok, raw.reshape(C, 3, nb, -1), gains[:1], shifts[:1], bias)
        q, k, v, o, lse = attend(qkv, begin)
        mid, n2 = sum_norm_gather(S, C, T, 2, o, wo, tok, gains[1:], shifts[1:])
        gb, gu, act = gates(S, C, T, 4, n2, wg, cot)
        gw_down = mm(gb, act, 0, 0).astype(BF)
        wd, gw_down = after(wd, gw_down)
        gw_down = sum_ctx(gw_down)

        (dgu,) = by_rows(
            gates_back_kernel, "gates_back", [(True, gb), (False, wd), (True, gu)],
            [jax.ShapeDtypeStruct((L, 2 * fn), BF)],
        )
        gw_gateup = mm(n2, dgu, 0, 0).astype(BF)
        dgu, gw_gateup = after(dgu, gw_gateup)
        gw_gateup = sum_ctx(gw_gateup)
        dmid, gb1, stats2 = sum_back_gather(S, C, T, 6, dgu, wg, mid, gb, gains[1:])
        gw_out = mm(gb1, o, 0, 0).astype(BF)
        gb1, gw_out = after(gb1, gw_out)
        gw_out = sum_ctx(gw_out)
        do = mm(gb1, wo, 1, 0).astype(BF)
        dqkv, gbias, got, gw_down = attend_back(
            S, C, T, 11, q, k, v, o, do, lse, begin, act, wd, [("shard", gw_down)]
        )
        out = parts((mid + got).astype(BF))
        gw_qkv = mm(n1, dqkv, 0, 0).astype(BF)
        dqkv, gw_qkv = after(dqkv, gw_qkv)
        gw_qkv = sum_ctx(gw_qkv)
        low, stats1, out, gw_gateup = sum_back(
            S, C, T, 8, dqkv, wq, tok, dmid, gains[:1], [("shard", out), ("shard", gw_gateup)]
        )
        low, gw_gateup, gw_down = lax.optimization_barrier((low, *final(gw_gateup, gw_down)))
        gtok, out, norms, gbias, gw_qkv, gw_out = finish(
            S, C, T, 10, low, out, [stats1, stats2], gbias, gw_qkv, gw_out
        )
        if not ordered(D, S, C):
            gtok, out = unpermute(gtok), unpermute(out)
        gtok = gtok.astype(F32)
        norms = lax.dynamic_slice_in_dim(norms, (z * S + p) * nb % 128, nb, 1) if nb % 128 else norms
        gbias = gbias.reshape(S, 3, heads, S * C, nf)
        gbias = lax.dynamic_index_in_dim(gbias, p * C + z, 3, keepdims=False)
        gbias = gbias.swapaxes(0, 1).reshape(b_qkv.shape)

        return (
            out,
            gtok,
            gw_qkv.swapaxes(0, 1).reshape(w_qkv.shape),
            gbias,
            gw_out.reshape(w_out.shape),
            gw_gateup.reshape(w_gateup.shape),
            gw_down.reshape(w_down.shape),
            norms[None, :2],
            norms[None, 2:],
        )

    return body


def solution(mesh):
    both = ("shard", "ctx")
    specs = (
        P(None, both, None, "tp"),
        P(None, None, "tp", both),
        P(None, "tp", both),
        P(None, both, None, "tp"),
        P(None, "tp", both),
        P(None, None, both),
        P(None, None, both),
    )
    return jax.shard_map(
        make_body(mesh.shape["shard"], mesh.shape["ctx"], mesh.shape["tp"]),
        mesh=mesh,
        in_specs=(P(both, None), P("shard", None)) + specs + (P(both, None),),
        out_specs=(P(both, None), P(both, None)) + specs,
        check_vma=False,
    )
```
